32 devices in a mesh: gx: 4 (over z), gy: 8 (over y, x, core).
Axes of the slice: x: 2, y: 2, z: 4, core: 2. Of those that a mesh axis runs over, the one named last changes fastest.
Arguments:
- velocity: float32 [3, 64, 256, 512], P(None, None, 'gy', 'gx'), may hold values from -6 to 6
- pressure: float32 [64, 256, 512], P(None, 'gy', 'gx'), may hold values from -6 to 6
- memory: float32 [64, 256, 512], P(None, 'gy', 'gx'), may hold values from -4 to 4
- buoyancy: float32 [64, 256, 512], P(None, 'gy', 'gx'), may hold values from 0.1 to 0.4
- modulus: float32 [64, 256, 512], P(None, 'gy', 'gx'), may hold values from 0.1 to 0.4
- relax: float32 [64, 256, 512], P(None, 'gy', 'gx'), may hold values from 0.05 to 0.5
- strength: float32 [64, 256, 512], P(None, 'gy', 'gx'), may hold values from 0.2 to 1
- spectra: float32 [2048, 256], P(('gx', 'gy')), may hold values from -6 to 6
- patch_cell: int32 [2048], P(('gx', 'gy')), may hold values from 0 to 262143
- rupture_patches: int32 [32, 64], replicated, may hold values from -1 to 2047, as said below
- slip_weights: bfloat16 [32, 64, 512], P('gx', 'gy'), may hold values from -1 to 1
Outputs:
- velocity_out: float32 [3, 64, 256, 512], P(None, None, 'gy', 'gx')
- pressure_out: float32 [64, 256, 512], P(None, 'gy', 'gx')
- memory_out: float32 [64, 256, 512], P(None, 'gy', 'gx')
- spectra_out: float32 [2048, 256], P(('gx', 'gy'))
- slip_response: float32 [32, 512, 256], P('gx', 'gy')
The draws below stay inside these ranges and needn't reach their ends.
Inputs may be any that keep to these rules, and one draw needn't show every extreme that they name: `patch_cell`: the cell of a patch is a flat index (z * 32 + y) * 128 + x within its brick. `rupture_patches`: each patch is listed in at most one slot. Slot (r, s) belongs to the owner at index r // 8 of gx and s // 8 of gy; of the 64 patches of one block, at most 2 are listed in the slots of any one owner, and some pairs of block and owner reach 2.
All inputs are finite; a program needn't handle non-finite values.
Results may differ from the reference program's by a relative error of at most 0.0029.
Values may be sent and summed in bfloat16 or wider, within the bound.
A program may use at most 128 MiB of HBM per device.

```python
import math
import jax
import jax.numpy as jnp
from jax import lax

CX = 128
CY = 32
CZ = 64
STEPS = 4
FREQS = 128
VARS = 512
CAP = 2
RUP_GROUP = 8
PATCH_DEV = 64
NX = 512
NY = 256
PATCHES = 2048
SLOT_DEV = 8
SLOTS = 64
RUPTURES = 32
N_GY = 8


def draw_rupture_patches(key, part):
    devs = PATCHES // PATCH_DEV
    groups_y = SLOTS // SLOT_DEV
    keys = jax.random.split(jax.random.fold_in(key, 7), 7)
    sigma = jax.random.permutation(keys[0], devs)
    tau = jax.random.permutation(keys[1], devs)
    offsets = jax.random.permutation(keys[2], devs)[:PATCH_DEV // CAP]
    position = jnp.arange(PATCH_DEV, dtype=jnp.int32)
    group_of = position // CAP
    target = sigma[(tau[:, None] + offsets[None, :]) % devs]
    target_pos = target[:, group_of]
    order = jax.vmap(lambda k: jax.random.permutation(k, PATCH_DEV))(jax.random.split(keys[3], devs))
    patch_global = jnp.arange(devs, dtype=jnp.int32)[:, None] * PATCH_DEV + order.astype(jnp.int32)
    slot_perm = jax.vmap(lambda k: jax.random.permutation(k, PATCH_DEV))(jax.random.split(keys[4], devs))
    local = slot_perm[target_pos, position[None, :]]
    levels = jnp.array([100, 100, 100, 50], dtype=jnp.int32)
    heat = levels[jax.random.randint(keys[5], (devs,), 0, 4)]
    heat = heat.at[sigma[0]].set(100)
    keep = jax.random.randint(keys[6], (devs, PATCH_DEV), 0, 100) < heat[target_pos]
    row = target_pos // groups_y * RUP_GROUP + local // SLOT_DEV
    col = target_pos % groups_y * SLOT_DEV + local % SLOT_DEV
    flat = row * SLOTS + col
    total = RUPTURES * SLOTS
    table = jnp.full((total + 1,), -1, dtype=jnp.int32)
    table = table.at[jnp.where(keep, flat, total).reshape(-1)].set(patch_global.reshape(-1))
    return table[:total].reshape(RUPTURES, SLOTS)


def place_ends(values, own_key, least, top_value):
    place = [jax.random.randint(jax.random.fold_in(own_key, axis), (), 0, length) for axis, length in enumerate(values.shape)]
    longest = values.shape.index(max(values.shape))
    neighbour = place[:longest] + [(place[longest] + 1) % values.shape[longest]] + place[longest + 1:]
    return values.at[tuple(place)].set(least).at[tuple(neighbour)].set(top_value)


def with_spikes(values, own_key, source, target, parts, factor):
    owner, partner = [(jnp.arange(values.shape[dim]) // (values.shape[dim] // parts)).reshape([-1 if axis == dim else 1 for axis in range(values.ndim)]) for dim in (source, target)]
    chosen = jax.random.permutation(own_key, parts)[partner]
    strong = (owner == chosen) | (owner == (partner + parts // 2) % parts)
    return jnp.where(strong, factor * values, values)


def block_levels(key, shape, cuts, least, largest):
    level = 1.0
    for dim, shards_of in cuts:
        heights = jax.random.uniform(jax.random.fold_in(jax.random.fold_in(key, 6), dim), (shards_of,), jnp.float32, least / len(cuts), largest / len(cuts))
        level = level * jnp.repeat(jnp.exp(heights), shape[dim] // shards_of).reshape((-1,) + (1,) * (len(shape) - 1 - dim))
    return level


def scatter_about(own_key, shape, scale, reach, pieces=(), kind=jnp.bfloat16):
    values = jax.random.normal(own_key, shape, jnp.float32) * scale
    if len(pieces) > 0:
        values = block_levels(own_key, shape, pieces, -0.22, 0.18) * values
    return jnp.clip(values, min=-reach, max=reach).astype(kind)


def noise_with(rng, dims, scale, bound, cuts, heavy, kind=jnp.bfloat16):
    values = scale * jax.random.normal(rng, dims, jnp.float32)
    if cuts:
        values = values * block_levels(rng, dims, cuts, -0.22, 0.18)
    return jnp.clip(with_spikes(values, jax.random.fold_in(rng, 3), *heavy), -bound, bound).astype(kind)


def setup_inputs(seed: int = 0) -> dict:
    splits = jax.random.split(jax.random.key(seed), 12)
    velocity = scatter_about(splits[0], (3, CZ, NY, NX), 1.0, 6.0, ((2, 8), (3, 4)), jnp.float32)
    pressure = scatter_about(splits[1], (CZ, NY, NX), 1.0, 6.0, ((1, 8), (2, 4)), jnp.float32)
    memory = scatter_about(splits[2], (CZ, NY, NX), 0.3, 4.0, ((1, 8), (2, 4)), jnp.float32)
    buoyancy = jnp.clip(jnp.exp(math.log(0.4) - 1.3862944 * jax.random.uniform(splits[3], (CZ, NY, NX), jnp.float32) ** block_levels(splits[3], (CZ, NY, NX), ((1, 8), (2, 4)), -0.2, 0.2)), 0.1, 0.4)
    modulus = jnp.clip(jnp.exp(math.log(0.4) - 1.3862944 * jax.random.uniform(splits[4], (CZ, NY, NX), jnp.float32) ** block_levels(splits[4], (CZ, NY, NX), ((1, 8), (2, 4)), -0.2, 0.2)), 0.1, 0.4)
    relax = jnp.clip(jnp.exp(math.log(0.5) - 2.3025851 * jax.random.uniform(splits[5], (CZ, NY, NX), jnp.float32) ** block_levels(splits[5], (CZ, NY, NX), ((1, 8), (2, 4)), -0.2, 0.2)), 0.05, 0.5)
    strength = jnp.clip(0.2 + 0.8 * jax.random.uniform(splits[6], (CZ, NY, NX), jnp.float32) ** block_levels(splits[6], (CZ, NY, NX), ((1, 8), (2, 4)), -0.2, 0.2), 0.2, 1.0)
    spectra = scatter_about(splits[7], (PATCHES, 2 * FREQS), 1.0, 6.0, ((0, 32),), jnp.float32)
    patch_cell = place_ends(jax.random.randint(splits[8], (PATCHES,), 0, CX * CY * CZ), jax.random.fold_in(splits[8], 1), 0, (CX * CY * CZ) - 1).astype(jnp.int32)
    rupture_patches = draw_rupture_patches(jax.random.fold_in(splits[11], 71), 0)
    slip_weights = noise_with(splits[10], (RUPTURES, SLOTS, VARS), SLOTS ** -0.5, 1.0, ((0, 4), (1, 8)), (1, 2, 8, 2.0))
    return {"velocity": velocity, "pressure": pressure, "memory": memory, "buoyancy": buoyancy, "modulus": modulus, "relax": relax, "strength": strength, "spectra": spectra, "patch_cell": patch_cell, "rupture_patches": rupture_patches, "slip_weights": slip_weights}


def centred(field, axis):
    widths = [(0, 0), (0, 0), (0, 0)]
    widths[axis] = (1, 1)
    padded = jnp.pad(field, widths)
    length = field.shape[axis]
    return lax.slice_in_dim(padded, 2, length + 2, axis=axis) - lax.slice_in_dim(padded, 0, length, axis=axis)


def phase_row(freqs, step):
    angle = jnp.pi * (jnp.arange(freqs, dtype=jnp.float32) + 0.5) / freqs * step
    return jnp.concatenate([jnp.cos(angle), -jnp.sin(angle)])


def reference(velocity, pressure, memory, buoyancy, modulus, relax, strength, spectra, patch_cell, rupture_patches, slip_weights):
    speed_x, speed_y, speed_z = velocity[0], velocity[1], velocity[2]
    freqs = spectra.shape[1] // 2
    block = jnp.arange(spectra.shape[0], dtype=jnp.int32) // PATCH_DEV
    col_block = block // N_GY
    row_block = block % N_GY
    depth = patch_cell // (CY * CX)
    rows = row_block * CY + (patch_cell // CX) % CY
    cols = col_block * CX + patch_cell % CX
    for step in range(STEPS):
        speed_x = speed_x - buoyancy * centred(pressure, 2)
        speed_y = speed_y - buoyancy * centred(pressure, 1)
        speed_z = speed_z - buoyancy * centred(pressure, 0)
        spread = centred(speed_x, 2) + centred(speed_y, 1) + centred(speed_z, 0)
        shear = centred(speed_x, 1) + centred(speed_y, 2)
        memory = memory - relax * (memory + strength * spread)
        pressure = pressure - modulus * (spread + memory)
        sample = shear[depth, rows, cols]
        spectra = spectra + sample[:, None] * phase_row(freqs, step + 1)[None, :]
    live = rupture_patches >= 0
    picked = spectra[jnp.where(live, rupture_patches, 0)]
    slot_spectra = jnp.where(live[:, :, None], picked, jnp.zeros_like(picked)).astype(jnp.bfloat16)
    slip = jnp.einsum("rsv,rsf->rvf", slip_weights.astype(jnp.float32), slot_spectra.astype(jnp.float32))
    velocity_out = jnp.stack([speed_x, speed_y, speed_z])
    return velocity_out, pressure, memory, spectra, slip
```

```python
import functools

import jax
import jax.numpy as jnp
import numpy as np
from jax import lax
from jax.experimental import pallas as pl
from jax.experimental.pallas import tpu as pltpu
from jax.sharding import PartitionSpec as P

STEPS = 4
CAP = 2
BATCH = 8


def phase_rows(freqs):
    angle = np.pi * (np.arange(freqs) + 0.5) / freqs
    rows = [np.concatenate([np.cos(angle * n), -np.sin(angle * n)]) for n in range(1, STEPS + 1)]
    return jnp.asarray(np.stack(rows).astype(np.float32))


Y_ROWS = [4] + [3] * (STEPS - 1) + [1]
X_PACKS = [3] + [2] * (STEPS - 1) + [1]


def quotient(value, size):
    if size & (size - 1):
        return lax.div(value, jnp.full_like(value, size))
    return lax.shift_right_logical(value, jnp.full_like(value, size.bit_length() - 1))


def remainder(value, size):
    if size & (size - 1):
        return lax.rem(value, jnp.full_like(value, size))
    return value & (size - 1)


def step_kernel(dims, *refs):
    nz, ny, nx, chunks, zc, per_dev, ngx, ngy = dims
    refs = list(refs)
    take = lambda count: [refs.pop(0) for _ in range(count)]
    vel_in, p_in, m_in, b_in, mod_in, rel_in, str_in, spectra, cell, cell_row, phase = take(11)
    listed, weights = take(2)
    vx, vy, vz, p, m, spectra_out, weights_got, rows_out, group_out = take(9)
    b, mod, rel, stg = take(4)
    ysend, yrecv = (take(STEPS + 1), take(STEPS + 1))
    xsend, xrecv = (take(STEPS + 1), take(STEPS + 1))
    vxh, bxh, hx, vyh, rows_got, samples = take(6)
    placing, rows_send, rows_group = take(3)
    in_sem, send_sem, recv_sem, far_send, far_recv = take(5)

    gx, gy = (lax.axis_index("gx"), lax.axis_index("gy"))
    has = [gy > 0, gy < ngy - 1, gx > 0, gx < ngx - 1]
    peer = [{"gy": gy - 1}, {"gy": gy + 1}, {"gx": gx - 1}, {"gx": gx + 1}]

    loads = [
        pltpu.make_async_copy(src, dst, in_sem.at[i])
        for i, (src, dst) in enumerate(
            [
                (p_in, p.at[pl.ds(1, nz)]),
                (b_in, b.at[pl.ds(0, nz)]),
                (vel_in.at[0], vx),
                (vel_in.at[1], vy),
                (vel_in.at[2], vz.at[pl.ds(1, nz)]),
                (rel_in, rel),
                (m_in, m),
                (str_in, stg),
                (mod_in, mod),
            ]
        )
    ]
    for load in loads:
        load.start()

    along_gx = [lax.rem(gx + k, ngx) for k in range(1, ngx)]
    along_gy = [lax.rem(gy + k, ngy) for k in range(1, ngy)]
    peers = [{"gx": other} for other in along_gx] + [{"gy": other} for other in along_gy]
    barrier = pltpu.get_barrier_semaphore()
    for other in peers:
        pl.semaphore_signal(
            barrier, inc=1, device_id=other, device_id_type=pl.DeviceIdType.MESH
        )

    plane = jnp.zeros((ny, nx), jnp.float32)
    p[0] = plane
    p[nz + 1] = plane
    p[nz + 2] = plane
    vz[0] = plane
    vz[nz + 1] = plane
    b[nz] = plane
    for side in range(4):

        @pl.when(jnp.logical_not(has[side]))
        def _():
            for r in range(STEPS + 1):
                if side < 2:
                    yrecv[r][side] = jnp.zeros(yrecv[r].shape[1:], jnp.float32)
                else:
                    xrecv[r][side - 2] = jnp.zeros(xrecv[r].shape[1:], jnp.float32)

    def copy_to(r, c, side):
        slot = side % 2
        if side < 2:
            src, dst = (ysend[r].at[slot, c], yrecv[r].at[1 - slot, c])
        else:
            src, dst = (xsend[r].at[c], xrecv[r].at[1 - slot, c])
        return pltpu.make_async_remote_copy(
            src_ref=src,
            dst_ref=dst,
            send_sem=send_sem.at[r, c, side],
            recv_sem=recv_sem.at[r, c, side - side % 2 + 1 - slot],
            device_id=peer[side],
            device_id_type=pl.DeviceIdType.MESH,
        )

    def copy_from(r, c, side):
        slot = side % 2
        if side < 2:
            src, dst = (ysend[r].at[slot, c], yrecv[r].at[slot, c])
        else:
            src, dst = (xsend[r].at[c], xrecv[r].at[slot, c])
        return pltpu.make_async_remote_copy(
            src_ref=src,
            dst_ref=dst,
            send_sem=send_sem.at[r, c, side],
            recv_sem=recv_sem.at[r, c, side],
            device_id=peer[side],
            device_id_type=pl.DeviceIdType.MESH,
        )

    def send(r, c):
        for side in range(4):

            @pl.when(has[side])
            def _():
                copy_to(r, c, side).start()

    def receive(r, c):
        for side in range(4):

            @pl.when(has[side])
            def _():
                copy_from(r, c, side).wait_recv()

    lane = lax.broadcasted_iota(jnp.int32, (ny, nx), 1)
    row = lax.broadcasted_iota(jnp.int32, (ny, nx), 0)
    quad, lane4 = (quotient(lane, 4), remainder(lane, 4))
    last_lane, first_lane = (lane == nx - 1, lane == 0)
    last_row, first_row = (row == ny - 1, row == 0)

    def pack(total, slab, zl):
        return jnp.where(quad == zl, pltpu.roll(slab, 4 * zl + 2, 1), total)

    def d_x(slab, halo, zl):
        ends = pltpu.roll(halo, nx - 2 - 4 * zl, 1)
        after = jnp.where(last_lane, ends, pltpu.roll(slab, nx - 1, 1))
        before = jnp.where(first_lane, ends, pltpu.roll(slab, 1, 1))
        return after - before

    def d_y(slab, south, north):
        after = jnp.where(last_row, north, pltpu.roll(slab, ny - 1, 0))
        before = jnp.where(first_row, south, pltpu.roll(slab, 1, 0))
        return after - before

    for load in loads[:4]:
        load.wait()
    for c in range(chunks):

        def edges(i, totals):
            pt, vt, bt = totals
            for j in range(BATCH):
                zl = i * BATCH + j
                z = c * zc + zl
                ps, vs, ws, bs = (p[z + 1], vx[z], vy[z], b[z])
                pt, vt, bt = (pack(pt, ps, zl), pack(vt, vs, zl), pack(bt, bs, zl))
                at = pl.ds(zl, 1)
                ysend[0][0, c, 0, at, :] = ps[0:1]
                ysend[0][0, c, 1, at, :] = ps[1:2]
                ysend[0][0, c, 2, at, :] = ws[0:1]
                ysend[0][0, c, 3, at, :] = bs[0:1]
                ysend[0][1, c, 0, at, :] = ps[ny - 2 : ny - 1]
                ysend[0][1, c, 1, at, :] = ps[ny - 1 : ny]
                ysend[0][1, c, 2, at, :] = ws[ny - 1 : ny]
                ysend[0][1, c, 3, at, :] = bs[ny - 1 : ny]
            return pt, vt, bt

        totals = lax.fori_loop(0, zc // BATCH, edges, (plane, plane, plane))
        for i, total in enumerate(totals):
            xsend[0][c, i] = total
        if c == 0:
            pl.semaphore_wait(barrier, len(peers))
        send(0, c)
    for load in loads[4:]:
        load.wait()

    rup_group, slot_dev, variations = weights.shape
    lanes = weights_got.shape[3]
    group_rows = ngy * CAP
    all_rows = ngx * group_rows

    def weight_block(other):
        block = other * (variations // ngy) // lanes
        return weights.at[:, :, pl.ds(pl.multiple_of(block * lanes, lanes), lanes)]

    def far(kind, k, src, dst):
        axis, size = ("gx", ngx) if kind == 1 else ("gy", ngy)
        return pltpu.make_async_remote_copy(
            src_ref=src,
            dst_ref=dst,
            send_sem=far_send.at[kind, k],
            recv_sem=far_recv.at[kind, k],
            device_id={axis: lax.rem(lax.axis_index(axis) + k, size)},
            device_id_type=pl.DeviceIdType.MESH,
        )

    def rows_of(ref, index, count):
        return ref.at[pl.ds(pl.multiple_of(index * count, count), count)]

    def weights_to(k):
        return far(0, k, weight_block(lax.rem(gy + k, ngy)), weights_got.at[gy])

    def weights_from(k):
        return far(0, k, weight_block(gy), weights_got.at[lax.rem(gy + ngy - k, ngy)])

    def first_to(k):
        src = rows_of(rows_send, lax.rem(gx + k, ngx), group_rows)
        return far(1, k, src, rows_of(rows_group, gx, group_rows))

    def first_from(k):
        src = rows_of(rows_send, gx, group_rows)
        return far(1, k, src, rows_of(rows_group, lax.rem(gx + ngx - k, ngx), group_rows))

    def second_to(k):
        return far(2, k, rows_group, rows_of(rows_out, gy, all_rows))

    def second_from(k):
        return far(2, k, rows_group, rows_of(rows_out, lax.rem(gy + ngy - k, ngy), all_rows))

    for k in range(1, ngy):
        weights_to(k).start()
    own_weights = pltpu.make_async_copy(weight_block(gy), weights_got.at[gy], far_send.at[0, 0])
    own_weights.start()

    square = (per_dev, per_dev)
    eye = lax.broadcasted_iota(jnp.int32, square, 0) == lax.broadcasted_iota(jnp.int32, square, 1)

    def to_row(column):
        return jnp.sum(jnp.where(eye, column, 0.0), axis=0, keepdims=True)

    def to_column(line):
        return jnp.sum(jnp.where(eye, line, 0.0), axis=1, keepdims=True)

    def fill_placing():
        ruptures, slots = listed.shape
        shape = (per_dev, slots)
        own_ids = lax.broadcasted_iota(jnp.int32, shape, 0) + (gx * ngy + gy) * per_dev
        slot_owner = quotient(lax.broadcasted_iota(jnp.int32, shape, 1), slot_dev)

        def body(r, best):
            owner = quotient(r, rup_group) * ngy + slot_owner
            return jnp.where(listed[pl.ds(r, 1), :] == own_ids, owner, best)

        best = lax.fori_loop(0, ruptures, body, jnp.full(shape, -1, jnp.int32))
        target = jnp.max(best.astype(jnp.float32), axis=1, keepdims=True)
        before = lax.broadcasted_iota(jnp.int32, square, 1) < lax.broadcasted_iota(
            jnp.int32, square, 0
        )
        same = (to_row(target) == target) & before
        rank = jnp.sum(jnp.where(same, 1.0, 0.0), axis=1, keepdims=True)
        bucket = to_row(jnp.where(target >= 0.0, target * CAP + rank, -1.0))
        place = lax.broadcasted_iota(jnp.int32, placing.shape, 0).astype(jnp.float32)
        placing[...] = jnp.where(place == bucket, 1.0, 0.0).astype(jnp.bfloat16)

    def halos(r, c):
        def joined(i):
            return jnp.where(lane4 < 2, xrecv[r][0, c, i], xrecv[r][1, c, i])

        def swapped(halo):
            return jnp.where(lane4 == 1, pltpu.roll(halo, nx - 1, 1), pltpu.roll(halo, 1, 1))

        outer, own = (joined(0), xsend[r][c, 0])
        if r == 0:
            vh, bh = (joined(1), joined(2))
            bxh[c] = bh
            vyh[0, c] = yrecv[0][0, c, 2]
            vyh[1, c] = yrecv[0][1, c, 2]
        else:
            vh, bh = (vxh[c], bxh[c])
        slope = jnp.where(
            lane4 == 1,
            pltpu.roll(own, nx - 1, 1) - pltpu.roll(outer, 1, 1),
            pltpu.roll(outer, nx - 1, 1) - pltpu.roll(own, 1, 1),
        )
        vh = vh - bh * slope
        vxh[c] = vh
        hx[0, c] = swapped(outer)
        hx[1, c] = swapped(vh)
        vyh[0, c] = vyh[0, c] - yrecv[0][0, c, 3] * (ysend[r][0, c, 0] - yrecv[r][0, c, 0])
        vyh[1, c] = vyh[1, c] - yrecv[0][1, c, 3] * (yrecv[r][1, c, 1] - ysend[r][1, c, 1])

    def sweep(r, c):
        last = r == STEPS - 1
        n = r + 1

        def body(i, totals):
            pt, wt = totals
            base = i * BATCH
            z0 = c * zc + base
            ps = [p[z0 + 1 + j] for j in range(BATCH + 2)]
            bs = [b[z0 + j] for j in range(BATCH + 1)]
            zs = [vz[z0], vz[z0 + 1]]
            vs, ws, new_p = ([], [], [])
            for j in range(BATCH):
                zl = base + j
                at = pl.ds(zl, 1)
                zs.append(vz[z0 + j + 2] - bs[j + 1] * (ps[j + 2] - ps[j]))
                vs.append(vx[z0 + j] - bs[j] * d_x(ps[j], hx[0, c], zl))
                south, north = (yrecv[r][0, c, 1, at, :], yrecv[r][1, c, 0, at, :])
                ws.append(vy[z0 + j] - bs[j] * d_y(ps[j], south, north))
            for j in range(BATCH):
                zl = base + j
                at = pl.ds(zl, 1)
                spread = d_x(vs[j], hx[1, c], zl) + d_y(ws[j], vyh[0, c, at, :], vyh[1, c, at, :])
                spread = spread + (zs[j + 2] - zs[j])
                mem = m[z0 + j]
                mem = mem - rel[z0 + j] * (mem + stg[z0 + j] * spread)
                m[z0 + j] = mem
                new_p.append(ps[j] - mod[z0 + j] * (spread + mem))
            for j in range(BATCH):
                zl = base + j
                at = pl.ds(zl, 1)
                vz[z0 + j + 2] = zs[j + 2]
                vx[z0 + j] = vs[j]
                vy[z0 + j] = ws[j]
                p[z0 + j + 1] = new_p[j]
                wt = pack(wt, ws[j], zl)
                ysend[n][0, c, 0 if last else 2, at, :] = vs[j][0:1]
                ysend[n][1, c, 0 if last else 2, at, :] = vs[j][ny - 1 : ny]
                if not last:
                    pt = pack(pt, new_p[j], zl)
                    ysend[n][0, c, 0, at, :] = new_p[j][0:1]
                    ysend[n][0, c, 1, at, :] = new_p[j][1:2]
                    ysend[n][1, c, 0, at, :] = new_p[j][ny - 2 : ny - 1]
                    ysend[n][1, c, 1, at, :] = new_p[j][ny - 1 : ny]
            return pt, wt

        pt, wt = lax.fori_loop(0, zc // BATCH, body, (plane, plane))
        if last:
            xsend[n][c, 0] = wt
        else:
            xsend[n][c, 0] = pt
            xsend[n][c, 1] = wt

    fill_placing()
    cells = to_column(cell_row[...].astype(jnp.float32)).astype(jnp.int32)
    cell_z, cell_x = (quotient(cells, ny * nx), remainder(cells, nx))
    cell_y = remainder(quotient(cells, nx), ny)
    patch_lane = lax.broadcasted_iota(jnp.int32, (per_dev, nx), 1)

    def masked(keep, values):
        return jnp.where(keep, values, 0.0)

    def sample_own(n):
        def body(i, carry):
            at = cell[i]
            z, y = (quotient(at, ny * nx), remainder(quotient(at, nx), ny))
            out = pl.ds(i, 1)
            rows_got[0, out, :] = vx[z, pl.ds(jnp.minimum(y + 1, ny - 1), 1), :]
            rows_got[1, out, :] = vx[z, pl.ds(jnp.maximum(y - 1, 0), 1), :]
            rows_got[2, out, :] = vy[z, pl.ds(y, 1), :]
            return carry

        lax.fori_loop(0, per_dev, body, 0, unroll=8)
        along = masked(cell_y < ny - 1, rows_got[0]) - masked(cell_y > 0, rows_got[1])
        across = rows_got[2]
        total = masked(patch_lane == cell_x, along)
        total = total + masked(patch_lane == cell_x + 1, across)
        samples[n - 1] = total - masked(patch_lane == cell_x - 1, across)

    def sample_halo(n):
        which_row, which_pack = (Y_ROWS[n] - 1, X_PACKS[n] - 1)

        def body(i, carry):
            at = cell[i]
            z, y = (quotient(at, ny * nx), remainder(quotient(at, nx), ny))
            c, zl = (quotient(z, zc), remainder(z, zc))
            out = pl.ds(i, 1)
            rows_got[0, out, :] = yrecv[n][0, c, which_row, pl.ds(zl, 1), :]
            rows_got[1, out, :] = yrecv[n][1, c, which_row, pl.ds(zl, 1), :]
            rows_got[2, out, :] = xrecv[n][0, c, which_pack, pl.ds(y, 1), :]
            rows_got[3, out, :] = xrecv[n][1, c, which_pack, pl.ds(y, 1), :]
            return carry

        lax.fori_loop(0, per_dev, body, 0, unroll=8)
        start = 4 * remainder(cell_z, zc)
        here = patch_lane == cell_x
        total = samples[n - 1]
        total = total + masked(here & (cell_y == ny - 1), rows_got[1])
        total = total - masked(here & (cell_y == 0), rows_got[0])
        total = total + masked((patch_lane == start + 2) & (cell_x == nx - 1), rows_got[3])
        total = total - masked((patch_lane == start + 1) & (cell_x == 0), rows_got[2])
        value = jnp.sum(total, axis=1, keepdims=True)
        spectra_out[...] = spectra_out[...] + value * phase[n - 1 : n, :]

    spectra_out[...] = spectra[...]
    rup = pl.ds(pl.multiple_of(gx * rup_group, rup_group), rup_group)
    group_out[...] = listed[rup, :]
    for r in range(STEPS):
        vz[1] = vz[1] - b[0] * (p[2] - p[0])
        for c in range(chunks):
            receive(r, c)
            halos(r, c)
            sweep(r, c)
            send(r + 1, c)
        sample_own(r + 1)
        if r > 0:
            sample_halo(r)
    for c in range(chunks):
        receive(STEPS, c)
    sample_halo(STEPS)
    rows_send[...] = jnp.dot(
        placing[...], spectra_out[...].astype(jnp.bfloat16), preferred_element_type=jnp.float32
    ).astype(jnp.bfloat16)
    for k in range(1, ngx):
        first_to(k).start()
    at = pl.ds(pl.multiple_of(gx * group_rows, group_rows), group_rows)
    rows_group[at, :] = rows_send[at, :]
    for k in range(1, ngx):
        first_from(k).wait_recv()
    for k in range(1, ngy):
        second_to(k).start()
    at = pl.ds(pl.multiple_of(gy * all_rows, all_rows), all_rows)
    rows_out[at, :] = rows_group[...]
    own_weights.wait()
    for k in range(1, ngy):
        weights_from(k).wait_recv()
        weights_to(k).wait_send()
    for k in range(1, ngy):
        second_from(k).wait_recv()
        second_to(k).wait_send()
    for k in range(1, ngx):
        first_to(k).wait_send()
    for r in range(STEPS + 1):
        for c in range(chunks):
            for side in range(4):

                @pl.when(has[side])
                def _():
                    copy_to(r, c, side).wait_send()


def finish_kernel(dims, *refs):
    nz, per_dev, ngx, ngy, slot_dev = dims
    refs = list(refs)
    take = lambda count: [refs.pop(0) for _ in range(count)]
    vx, vy, vz, p, m, spectra, weights, rows, group = take(9)
    vel_out, p_out, m_out, spectra_out, slip_out = take(5)
    table, slots, wide, slip, out_sem, slip_sem = take(6)
    rup_group, slot_count = group.shape
    share, lanes = (slip.shape[1], weights.shape[3])
    inner = pl.ds(1, nz)
    pairs = [
        (vx, vel_out.at[0]),
        (vy, vel_out.at[1]),
        (vz.at[inner], vel_out.at[2]),
        (p.at[inner], p_out),
        (m, m_out),
        (spectra, spectra_out),
    ]
    stores = [
        pltpu.make_async_copy(src, dst, out_sem.at[i]) for i, (src, dst) in enumerate(pairs)
    ]
    for store in stores:
        store.start()

    shape = (rup_group, table.shape[1])
    lane = lax.broadcasted_iota(jnp.int32, shape, 1)
    owner, place = (quotient(lane, slot_dev), remainder(lane, slot_dev))
    table[...] = jnp.full(shape, -1, jnp.int32)
    table[:, :slot_count] = group[...]
    ids = table[...]
    source = quotient(ids, per_dev)
    turned = [ids] + [pltpu.roll(ids, k, 0) for k in range(1, rup_group)]

    def earlier(i, rank):
        shift = i - (slot_dev - 1)
        inside = (place >= shift) & (place < shift + slot_dev)
        turn = jnp.where(shift < 0, shift + shape[1], shift)
        for other in turned:
            other = pltpu.roll(other, turn, 1)
            found = inside & (other < ids) & (quotient(other, per_dev) == source)
            rank = jnp.where(found, 1, rank)
        return rank

    rank = lax.fori_loop(0, 2 * slot_dev - 1, earlier, jnp.zeros(shape, jnp.int32))
    block = remainder(source, ngy) * ngx + quotient(source, ngy)
    table[...] = jnp.where(ids >= 0, (block * ngy + owner) * CAP + rank, -1)

    size = min(slot_count, 128)
    square = (size, size)
    eye = lax.broadcasted_iota(jnp.int32, square, 0) == lax.broadcasted_iota(jnp.int32, square, 1)
    row_at = lax.broadcasted_iota(jnp.int32, (size, rows.shape[0]), 1)
    start = pl.multiple_of(remainder(lax.axis_index("gy") * share, lanes), share)

    def respond(r, carry):
        lines = table[pl.ds(r, 1), :].astype(jnp.float32)
        for k in range(slot_count // size):
            line = lines[:, k * size : (k + 1) * size]
            column = jnp.sum(jnp.where(eye, line, 0.0), axis=1, keepdims=True).astype(jnp.int32)
            chosen = jnp.where(row_at == column, 1.0, 0.0).astype(jnp.bfloat16)
            picked = jnp.dot(chosen, rows[...], preferred_element_type=jnp.float32)
            slots[pl.ds(k * size, size), :] = picked.astype(jnp.bfloat16)
        own = weights[:, r].astype(jnp.float32).reshape(slot_count, lanes).astype(jnp.bfloat16)
        wide[...] = lax.dot_general(
            own, slots[...], (((0,), (0,)), ((), ())), preferred_element_type=jnp.float32
        )
        slip[r] = wide[pl.ds(start, share), :]
        pltpu.make_async_copy(slip.at[r], slip_out.at[r], slip_sem.at[r]).start()
        return carry

    lax.fori_loop(0, rup_group, respond, 0)
    for store in stores:
        store.wait()
    for r in range(rup_group):
        pltpu.make_async_copy(slip.at[r], slip_out.at[r], slip_sem.at[r]).wait()


VMEM_LIMIT = 40 * 1024 * 1024


def in_hbm(x):
    return pltpu.with_memory_space_constraint(x, pltpu.HBM)


def advance(
    velocity, pressure, memory, buoyancy, modulus, relax, strength, spectra, patch_cell, listed, weights
):
    nz, ny, nx = pressure.shape
    per_dev, width = spectra.shape
    zc = nx // 4
    chunks = nz // zc
    ngx, ngy = (lax.axis_size("gx"), lax.axis_size("gy"))
    dims = (nz, ny, nx, chunks, zc, per_dev, ngx, ngy)
    rup_group, slot_dev, variations = weights.shape
    lanes = max(variations // ngy, 128)
    all_rows = ngx * ngy * CAP
    f32 = jnp.float32
    field = lambda planes: pltpu.VMEM((planes, ny, nx), f32)
    rounds = range(STEPS + 1)
    any_spec = pl.BlockSpec(memory_space=pl.ANY)
    vmem_spec = pl.BlockSpec(memory_space=pltpu.VMEM)
    return pl.pallas_call(
        functools.partial(step_kernel, dims),
        out_shape=[
            field(nz),
            field(nz),
            field(nz + 2),
            field(nz + 3),
            field(nz),
            pltpu.VMEM(spectra.shape, f32),
            pltpu.VMEM((ngy, rup_group, slot_dev, lanes), jnp.bfloat16),
            pltpu.VMEM((ngy * all_rows, width), jnp.bfloat16),
            pltpu.VMEM((rup_group, listed.shape[1]), jnp.int32),
        ],
        in_specs=[any_spec] * 7
        + [vmem_spec, pl.BlockSpec(memory_space=pltpu.SMEM)]
        + [vmem_spec] * 4,
        out_specs=[vmem_spec] * 9,
        scratch_shapes=[field(nz + 1), field(nz), field(nz), field(nz)]
        + [pltpu.VMEM((2, chunks, Y_ROWS[r], zc, nx), f32) for r in rounds]
        + [pltpu.VMEM((2, chunks, Y_ROWS[r], zc, nx), f32) for r in rounds]
        + [pltpu.VMEM((chunks, X_PACKS[r], ny, nx), f32) for r in rounds]
        + [pltpu.VMEM((2, chunks, X_PACKS[r], ny, nx), f32) for r in rounds]
        + [
            pltpu.VMEM((chunks, ny, nx), f32),
            pltpu.VMEM((chunks, ny, nx), f32),
            pltpu.VMEM((2, chunks, ny, nx), f32),
            pltpu.VMEM((2, chunks, zc, nx), f32),
            pltpu.VMEM((4, per_dev, nx), f32),
            pltpu.VMEM((STEPS, per_dev, nx), f32),
            pltpu.VMEM((all_rows, per_dev), jnp.bfloat16),
            pltpu.VMEM((all_rows, width), jnp.bfloat16),
            pltpu.VMEM((all_rows, width), jnp.bfloat16),
            pltpu.SemaphoreType.DMA((9,)),
            pltpu.SemaphoreType.DMA((STEPS + 1, chunks, 4)),
            pltpu.SemaphoreType.DMA((STEPS + 1, chunks, 4)),
            pltpu.SemaphoreType.DMA((3, max(ngx, ngy))),
            pltpu.SemaphoreType.DMA((3, max(ngx, ngy))),
        ],
        compiler_params=pltpu.CompilerParams(
            collective_id=0, has_side_effects=True, vmem_limit_bytes=VMEM_LIMIT
        ),
    )(
        *[in_hbm(x) for x in (velocity, pressure, memory, buoyancy, modulus, relax, strength)],
        in_hbm(spectra),
        patch_cell,
        in_hbm(patch_cell.reshape(1, -1)),
        in_hbm(phase_rows(width // 2)),
        in_hbm(listed),
        in_hbm(weights),
    )


def finish(state, velocity, pressure, memory, spectra, weights):
    nz = pressure.shape[0]
    per_dev, width = spectra.shape
    ngx, ngy = (lax.axis_size("gx"), lax.axis_size("gy"))
    rup_group, slot_dev, variations = weights.shape
    slot_count = slot_dev * ngy
    share = variations // ngy
    lanes = max(share, 128)
    f32 = jnp.float32
    any_spec = pl.BlockSpec(memory_space=pl.ANY)
    vmem_spec = pl.BlockSpec(memory_space=pltpu.VMEM)
    return pl.pallas_call(
        functools.partial(finish_kernel, (nz, per_dev, ngx, ngy, slot_dev)),
        out_shape=[
            jax.ShapeDtypeStruct(velocity.shape, f32),
            jax.ShapeDtypeStruct(pressure.shape, f32),
            jax.ShapeDtypeStruct(memory.shape, f32),
            jax.ShapeDtypeStruct(spectra.shape, f32),
            jax.ShapeDtypeStruct((rup_group, share, width), f32),
        ],
        in_specs=[vmem_spec] * len(state),
        out_specs=[any_spec] * 5,
        scratch_shapes=[
            pltpu.VMEM((rup_group, max(slot_count, 128)), jnp.int32),
            pltpu.VMEM((slot_count, width), jnp.bfloat16),
            pltpu.VMEM((lanes, width), f32),
            pltpu.VMEM((rup_group, share, width), f32),
            pltpu.SemaphoreType.DMA((6,)),
            pltpu.SemaphoreType.DMA((rup_group,)),
        ],
        compiler_params=pltpu.CompilerParams(vmem_limit_bytes=VMEM_LIMIT),
    )(*[pltpu.with_memory_space_constraint(x, pltpu.VMEM) for x in state])


def per_device(
    velocity,
    pressure,
    memory,
    buoyancy,
    modulus,
    relax,
    strength,
    spectra,
    patch_cell,
    rupture_patches,
    slip_weights,
):
    state = advance(
        velocity,
        pressure,
        memory,
        buoyancy,
        modulus,
        relax,
        strength,
        spectra,
        patch_cell,
        rupture_patches,
        slip_weights,
    )
    return tuple(finish(state, velocity, pressure, memory, spectra, slip_weights))


def solution(mesh):
    in_specs = (
        P(None, None, "gy", "gx"),
        P(None, "gy", "gx"),
        P(None, "gy", "gx"),
        P(None, "gy", "gx"),
        P(None, "gy", "gx"),
        P(None, "gy", "gx"),
        P(None, "gy", "gx"),
        P(("gx", "gy"), None),
        P(("gx", "gy")),
        P(),
        P("gx", "gy", None),
    )
    out_specs = (
        P(None, None, "gy", "gx"),
        P(None, "gy", "gx"),
        P(None, "gy", "gx"),
        P(("gx", "gy"), None),
        P("gx", "gy", None),
    )
    return jax.shard_map(
        per_device, mesh=mesh, in_specs=in_specs, out_specs=out_specs, check_vma=False
    )
```

```python
import functools

import jax
import jax.numpy as jnp
import numpy as np
from jax import lax
from jax.experimental import pallas as pl
from jax.experimental.pallas import tpu as pltpu
from jax.sharding import PartitionSpec as P

STEPS = 4
CAP = 2
BATCH = 8


def phase_rows(freqs):
    angle = np.pi * (np.arange(freqs) + 0.5) / freqs
    rows = [np.concatenate([np.cos(angle * n), -np.sin(angle * n)]) for n in range(1, STEPS + 1)]
    return jnp.asarray(np.stack(rows).astype(np.float32))


Y_ROWS = [4, 3] + [2] * (STEPS - 2)
X_PACKS = [3, 2] + [1] * (STEPS - 2)


def quotient(value, size):
    if size & (size - 1):
        return lax.div(value, jnp.full_like(value, size))
    return lax.shift_right_logical(value, jnp.full_like(value, size.bit_length() - 1))


def remainder(value, size):
    if size & (size - 1):
        return lax.rem(value, jnp.full_like(value, size))
    return value & (size - 1)


def step_kernel(dims, *refs):
    nz, ny, nx, chunks, zc, per_dev, ngx, ngy = dims
    refs = list(refs)
    take = lambda count: [refs.pop(0) for _ in range(count)]
    vel_in, p_in, m_in, b_in, mod_in, rel_in, str_in = take(7)
    spectra_in, cell_in, cell_row_in, phase_in, listed_in, weights = take(6)
    vx, vy, vz, p, m, spectra_out, weights_got, rows_out, table = take(9)
    b, mod, rel, stg = take(4)
    ysend, yrecv = (take(STEPS), take(STEPS))
    xsend, xrecv = (take(STEPS), take(STEPS))
    csend, crecv = (take(STEPS - 1), take(STEPS - 1))
    cell, cell_row, phase, listed = take(4)
    vxh, bxh, hx, vyh, vyx, xj, got, shear, factors = take(9)
    placing, rows_send, rows_group = take(3)
    in_sem, small_sem, send_sem, recv_sem, far_send, far_recv = take(6)

    gx, gy = (lax.axis_index("gx"), lax.axis_index("gy"))
    has = [gy > 0, gy < ngy - 1, gx > 0, gx < ngx - 1]
    has = has + [has[k // 2] & has[2 + k % 2] for k in range(4)]
    peer = [{"gy": gy - 1}, {"gy": gy + 1}, {"gx": gx - 1}, {"gx": gx + 1}]
    peer = peer + [{**peer[k // 2], **peer[2 + k % 2]} for k in range(4)]

    def load(i, c):
        at = pl.ds(c * zc, zc)
        moved = pl.ds(c * zc + 1, zc)
        src, dst = [
            (p_in.at[at], p.at[moved]),
            (b_in.at[at], b.at[at]),
            (vel_in.at[0, at], vx.at[at]),
            (vel_in.at[1, at], vy.at[at]),
            (vel_in.at[2, at], vz.at[moved]),
            (rel_in.at[at], rel.at[at]),
            (m_in.at[at], m.at[at]),
            (str_in.at[at], stg.at[at]),
            (mod_in.at[at], mod.at[at]),
        ][i]
        return pltpu.make_async_copy(src, dst, in_sem.at[i, c])

    smalls = [
        pltpu.make_async_copy(src, dst, small_sem.at[i])
        for i, (src, dst) in enumerate(
            [
                (cell_in, cell),
                (cell_row_in, cell_row),
                (listed_in, listed),
                (phase_in, phase),
                (spectra_in, spectra_out),
            ]
        )
    ]
    for c in range(chunks):
        for i in range(4):
            load(i, c).start()
    for c in range(chunks):
        for i in range(4, 9):
            load(i, c).start()
    for small in smalls:
        small.start()

    along_gx = [lax.rem(gx + k, ngx) for k in range(1, ngx)]
    along_gy = [lax.rem(gy + k, ngy) for k in range(1, ngy)]
    peers = [{"gx": other} for other in along_gx] + [{"gy": other} for other in along_gy]
    peers = peers + [
        {"gy": lax.rem(gy + ngy + dy, ngy), "gx": lax.rem(gx + ngx + dx, ngx)}
        for dy in (-1, 1)
        for dx in (-1, 1)
    ]
    barrier = pltpu.get_barrier_semaphore()
    for other in peers:
        pl.semaphore_signal(
            barrier, inc=1, device_id=other, device_id_type=pl.DeviceIdType.MESH
        )

    plane = jnp.zeros((ny, nx), jnp.float32)
    p[0] = plane
    p[nz + 1] = plane
    p[nz + 2] = plane
    vz[0] = plane
    vz[nz + 1] = plane
    b[nz] = plane
    for side in range(8):

        @pl.when(jnp.logical_not(has[side]))
        def _():
            for r in range(STEPS):
                if side < 2:
                    yrecv[r][side] = jnp.zeros(yrecv[r].shape[1:], jnp.float32)
                elif side < 4:
                    xrecv[r][side - 2] = jnp.zeros(xrecv[r].shape[1:], jnp.float32)
                elif r > 0:
                    for c in range(chunks):
                        crecv[r - 1][c, side - 4] = jnp.zeros((1, nx), jnp.float32)

    def ends(r, c, side, coming):
        k = side % 4
        if side < 2:
            there = side if coming else 1 - side
            src, dst = (ysend[r].at[side, c], yrecv[r].at[there, c])
            arrives = there
        elif side < 4:
            there = k - 2 if coming else 3 - k
            src, dst = (xsend[r].at[c], xrecv[r].at[there, c])
            arrives = 2 + there
        else:
            there = k if coming else 3 - k
            src, dst = (csend[r - 1].at[c, k // 2], crecv[r - 1].at[c, there])
            arrives = 4 + there
        return pltpu.make_async_remote_copy(
            src_ref=src,
            dst_ref=dst,
            send_sem=send_sem.at[r, c, side],
            recv_sem=recv_sem.at[r, c, arrives],
            device_id=peer[side],
            device_id_type=pl.DeviceIdType.MESH,
        )

    def sides(r):
        return range(4) if r == 0 else range(8)

    def send(r, c):
        for side in sides(r):

            @pl.when(has[side])
            def _():
                ends(r, c, side, False).start()

    def receive(r, c):
        for side in sides(r):

            @pl.when(has[side])
            def _():
                ends(r, c, side, True).wait_recv()

    lane = lax.broadcasted_iota(jnp.int32, (ny, nx), 1)
    row = lax.broadcasted_iota(jnp.int32, (ny, nx), 0)
    quad, lane4 = (quotient(lane, 4), remainder(lane, 4))
    last_lane, first_lane = (lane == nx - 1, lane == 0)
    last_row, first_row = (row == ny - 1, row == 0)
    west_half = remainder(lax.broadcasted_iota(jnp.int32, (1, nx), 1), 4) < 2

    def pack(total, slab, zl):
        return jnp.where(quad == zl, pltpu.roll(slab, 4 * zl + 2, 1), total)

    def d_x(slab, halo, zl):
        ends = pltpu.roll(halo, nx - 2 - 4 * zl, 1)
        after = jnp.where(last_lane, ends, pltpu.roll(slab, nx - 1, 1))
        before = jnp.where(first_lane, ends, pltpu.roll(slab, 1, 1))
        return after - before

    def d_y(slab, south, north):
        after = jnp.where(last_row, north, pltpu.roll(slab, ny - 1, 0))
        before = jnp.where(first_row, south, pltpu.roll(slab, 1, 0))
        return after - before

    for c in range(chunks):
        for i in range(4):
            load(i, c).wait()

        def edges(i, totals):
            pt, vt, bt = totals
            for j in range(BATCH):
                zl = i * BATCH + j
                z = c * zc + zl
                ps, vs, ws, bs = (p[z + 1], vx[z], vy[z], b[z])
                pt, vt, bt = (pack(pt, ps, zl), pack(vt, vs, zl), pack(bt, bs, zl))
                at = pl.ds(zl, 1)
                ysend[0][0, c, 0, at, :] = ps[0:1]
                ysend[0][0, c, 1, at, :] = ps[1:2]
                ysend[0][0, c, 2, at, :] = ws[0:1]
                ysend[0][0, c, 3, at, :] = bs[0:1]
                ysend[0][1, c, 0, at, :] = ps[ny - 2 : ny - 1]
                ysend[0][1, c, 1, at, :] = ps[ny - 1 : ny]
                ysend[0][1, c, 2, at, :] = ws[ny - 1 : ny]
                ysend[0][1, c, 3, at, :] = bs[ny - 1 : ny]
            return pt, vt, bt

        totals = lax.fori_loop(0, zc // BATCH, edges, (plane, plane, plane))
        for i, total in enumerate(totals):
            xsend[0][c, i] = total
        if c == 0:
            pl.semaphore_wait(barrier, len(peers))
        send(0, c)

    rup_group, slot_dev, variations = weights.shape
    lanes = weights_got.shape[3]
    group_rows = ngy * CAP
    all_rows = ngx * group_rows

    def weight_block(other):
        block = other * (variations // ngy) // lanes
        return weights.at[:, :, pl.ds(pl.multiple_of(block * lanes, lanes), lanes)]

    def far(kind, k, src, dst):
        axis, size = ("gx", ngx) if kind == 1 else ("gy", ngy)
        return pltpu.make_async_remote_copy(
            src_ref=src,
            dst_ref=dst,
            send_sem=far_send.at[kind, k],
            recv_sem=far_recv.at[kind, k],
            device_id={axis: lax.rem(lax.axis_index(axis) + k, size)},
            device_id_type=pl.DeviceIdType.MESH,
        )

    def rows_of(ref, index, count):
        return ref.at[pl.ds(pl.multiple_of(index * count, count), count)]

    def weights_to(k):
        return far(0, k, weight_block(lax.rem(gy + k, ngy)), weights_got.at[gy])

    def weights_from(k):
        return far(0, k, weight_block(gy), weights_got.at[lax.rem(gy + ngy - k, ngy)])

    def first_to(k):
        src = rows_of(rows_send, lax.rem(gx + k, ngx), group_rows)
        return far(1, k, src, rows_of(rows_group, gx, group_rows))

    def first_from(k):
        src = rows_of(rows_send, gx, group_rows)
        return far(1, k, src, rows_of(rows_group, lax.rem(gx + ngx - k, ngx), group_rows))

    def second_to(k):
        return far(2, k, rows_group, rows_of(rows_out, gy, all_rows))

    def second_from(k):
        return far(2, k, rows_group, rows_of(rows_out, lax.rem(gy + ngy - k, ngy), all_rows))

    for k in range(1, ngy):
        weights_to(k).start()
    own_weights = pltpu.make_async_copy(weight_block(gy), weights_got.at[gy], far_send.at[0, 0])
    own_weights.start()

    square = (per_dev, per_dev)
    eye = lax.broadcasted_iota(jnp.int32, square, 0) == lax.broadcasted_iota(jnp.int32, square, 1)

    def to_row(column):
        return jnp.sum(jnp.where(eye, column, 0.0), axis=0, keepdims=True)

    def to_column(line):
        return jnp.sum(jnp.where(eye, line, 0.0), axis=1, keepdims=True)

    def fill_placing():
        ruptures, slots = listed.shape
        shape = (per_dev, slots)
        own_ids = lax.broadcasted_iota(jnp.int32, shape, 0) + (gx * ngy + gy) * per_dev
        slot_owner = quotient(lax.broadcasted_iota(jnp.int32, shape, 1), slot_dev)

        def body(r, best):
            owner = quotient(r, rup_group) * ngy + slot_owner
            return jnp.where(listed[pl.ds(r, 1), :] == own_ids, owner, best)

        best = lax.fori_loop(0, ruptures, body, jnp.full(shape, -1, jnp.int32))
        target = jnp.max(best.astype(jnp.float32), axis=1, keepdims=True)
        before = lax.broadcasted_iota(jnp.int32, square, 1) < lax.broadcasted_iota(
            jnp.int32, square, 0
        )
        same = (to_row(target) == target) & before
        rank = jnp.sum(jnp.where(same, 1.0, 0.0), axis=1, keepdims=True)
        bucket = to_row(jnp.where(target >= 0.0, target * CAP + rank, -1.0))
        place = lax.broadcasted_iota(jnp.int32, placing.shape, 0).astype(jnp.float32)
        placing[...] = jnp.where(place == bucket, 1.0, 0.0).astype(jnp.bfloat16)

    def fill_table():
        slot_count = listed.shape[1]
        shape = table.shape
        spot = lax.broadcasted_iota(jnp.int32, shape, 1)
        owner, place = (quotient(spot, slot_dev), remainder(spot, slot_dev))
        table[...] = jnp.full(shape, -1, jnp.int32)
        group = pl.ds(pl.multiple_of(gx * rup_group, rup_group), rup_group)
        table[:, :slot_count] = listed[group, :]
        ids = table[...]
        source = quotient(ids, per_dev)

        def earlier(i, rank):
            shift = i - (slot_dev - 1)
            inside = (place >= shift) & (place < shift + slot_dev)
            turned = pltpu.roll(ids, jnp.where(shift < 0, shift + shape[1], shift), 1)
            for k in range(rup_group):
                other = pltpu.roll(turned, k, 0) if k else turned
                found = inside & (other < ids) & (quotient(other, per_dev) == source)
                rank = jnp.where(found, 1, rank)
            return rank

        shifts = 2 * slot_dev - 1
        unroll = max(k for k in range(1, 16) if shifts % k == 0)
        rank = lax.fori_loop(0, shifts, earlier, jnp.zeros(shape, jnp.int32), unroll=unroll)
        block = remainder(source, ngy) * ngx + quotient(source, ngy)
        table[...] = jnp.where(ids >= 0, (block * ngy + owner) * CAP + rank, -1)

    def halos(r, c):
        def joined(i):
            return jnp.where(lane4 < 2, xrecv[r][0, c, i], xrecv[r][1, c, i])

        def swapped(halo):
            return jnp.where(lane4 == 1, pltpu.roll(halo, nx - 1, 1), pltpu.roll(halo, 1, 1))

        outer, own = (joined(0), xsend[r][c, 0])
        if r == 0:
            vh, bh = (joined(1), joined(2))
            bxh[c] = bh
            vyh[0, c] = yrecv[0][0, c, 2]
            vyh[1, c] = yrecv[0][1, c, 2]
        else:
            vh, bh = (vxh[c], bxh[c])
            corner = crecv[r - 1]
            xj[c, 7:8, :] = jnp.where(west_half, corner[c, 0], corner[c, 1])
            xj[c, 8 : 8 + ny, :] = outer
            xj[c, 8 + ny : 9 + ny, :] = jnp.where(west_half, corner[c, 2], corner[c, 3])
            if r == 1:
                vyx[c] = joined(1)
        slope = jnp.where(
            lane4 == 1,
            pltpu.roll(own, nx - 1, 1) - pltpu.roll(outer, 1, 1),
            pltpu.roll(outer, nx - 1, 1) - pltpu.roll(own, 1, 1),
        )
        vh = vh - bh * slope
        vxh[c] = vh
        hx[0, c] = swapped(outer)
        hx[1, c] = swapped(vh)
        vyh[0, c] = vyh[0, c] - yrecv[0][0, c, 3] * (ysend[r][0, c, 0] - yrecv[r][0, c, 0])
        vyh[1, c] = vyh[1, c] - yrecv[0][1, c, 3] * (yrecv[r][1, c, 1] - ysend[r][1, c, 1])

    def sweep(r, c):
        last, first = (r == STEPS - 1, r == 0)
        n = r + 1

        def body(i, totals):
            totals = list(totals)
            base = i * BATCH
            z0 = c * zc + base
            ps = [p[z0 + 1 + j] for j in range(BATCH + 2)]
            bs = [b[z0 + j] for j in range(BATCH + 1)]
            zs = [vz[z0], vz[z0 + 1]]
            vs, ws, new_p = ([], [], [])
            for j in range(BATCH):
                zl = base + j
                at = pl.ds(zl, 1)
                zs.append(vz[z0 + j + 2] - bs[j + 1] * (ps[j + 2] - ps[j]))
                vs.append(vx[z0 + j] - bs[j] * d_x(ps[j], hx[0, c], zl))
                south, north = (yrecv[r][0, c, 1, at, :], yrecv[r][1, c, 0, at, :])
                ws.append(vy[z0 + j] - bs[j] * d_y(ps[j], south, north))
            for j in range(BATCH):
                zl = base + j
                at = pl.ds(zl, 1)
                spread = d_x(vs[j], hx[1, c], zl) + d_y(ws[j], vyh[0, c, at, :], vyh[1, c, at, :])
                spread = spread + (zs[j + 2] - zs[j])
                mem = m[z0 + j]
                mem = mem - rel[z0 + j] * (mem + stg[z0 + j] * spread)
                m[z0 + j] = mem
                new_p.append(ps[j] - mod[z0 + j] * (spread + mem))
            for j in range(BATCH):
                zl = base + j
                at = pl.ds(zl, 1)
                vz[z0 + j + 2] = zs[j + 2]
                vx[z0 + j] = vs[j]
                vy[z0 + j] = ws[j]
                p[z0 + j + 1] = new_p[j]
                if not last:
                    totals[0] = pack(totals[0], new_p[j], zl)
                    ysend[n][0, c, 0, at, :] = new_p[j][0:1]
                    ysend[n][0, c, 1, at, :] = new_p[j][1:2]
                    ysend[n][1, c, 0, at, :] = new_p[j][ny - 2 : ny - 1]
                    ysend[n][1, c, 1, at, :] = new_p[j][ny - 1 : ny]
                if first:
                    totals[1] = pack(totals[1], ws[j], zl)
                    ysend[n][0, c, 2, at, :] = vs[j][0:1]
                    ysend[n][1, c, 2, at, :] = vs[j][ny - 1 : ny]
            return tuple(totals)

        count = 0 if last else X_PACKS[n]
        totals = lax.fori_loop(0, zc // BATCH, body, (plane,) * count)
        for i, total in enumerate(totals):
            xsend[n][c, i] = total
        if not last:
            csend[n - 1][c, 0] = totals[0][0:1]
            csend[n - 1][c, 1] = totals[0][ny - 1 : ny]

    patch_lane = lax.broadcasted_iota(jnp.int32, (per_dev, nx), 1)

    def masked(keep, values):
        return jnp.where(keep, values, 0.0)

    def gather(first_slot, rows):
        def body(i, carry):
            at = cell[i]
            z, y = (quotient(at, ny * nx), remainder(quotient(at, nx), ny))
            out = pl.ds(i, 1)
            for k, row in enumerate(rows):
                got[first_slot + k, out, :] = row(z, y)
            return carry

        lax.fori_loop(0, per_dev, body, 0, unroll=8)

    def row_up(ref, z, y):
        return ref[z, pl.ds(jnp.minimum(y + 1, ny - 1), 1), :]

    def row_down(ref, z, y):
        return ref[z, pl.ds(jnp.maximum(y - 1, 0), 1), :]

    def row_halo(ref, index, z, y):
        side = jnp.where(y == 0, 0, 1)
        which = 1 - side if index is None else index
        return ref[side, quotient(z, zc), which, pl.ds(remainder(z, zc), 1), :]

    def row_pack(ref, shift, z, y):
        return ref[quotient(z, zc), pl.ds(y + shift, 1), :]

    def own_rows(ref, lift):
        return [lambda z, y: row_up(ref, z + lift, y), lambda z, y: row_down(ref, z + lift, y)]

    def halo_rows(n):
        return [
            lambda z, y: row_halo(yrecv[n], None, z, y),
            lambda z, y: row_pack(xj, 9, z, y),
            lambda z, y: row_pack(xj, 7, z, y),
        ]

    B_OWN, P_OWN, V_OWN, P_HALO, V_HALO, B_HALO = (0, 3, 5, 8, 11, 13)

    def places():
        cells = to_column(cell_row[...].astype(jnp.float32)).astype(jnp.int32)
        cell_z, cell_x = (quotient(cells, ny * nx), remainder(cells, nx))
        return cell_x, remainder(quotient(cells, nx), ny), 4 * remainder(cell_z, zc)

    def along(values):
        return jnp.sum(values, axis=1, keepdims=True)

    def note(n, value):
        shear[...] = jnp.broadcast_to(value, shear.shape)
        spectra_out[...] = spectra_out[...] + value * phase[n - 1 : n, :]

    def first_shear():
        cell_x, cell_y, start = places()
        here = patch_lane == cell_x
        up, down = (cell_y < ny - 1, cell_y > 0)
        ahead, behind = (patch_lane == cell_x + 1, patch_lane == cell_x - 1)
        ahead_out = (patch_lane == start + 2) & (cell_x == nx - 1)
        behind_out = (patch_lane == start + 1) & (cell_x == 0)
        total = masked(here, jnp.where(up, got[V_OWN], got[V_HALO]))
        total = total - masked(here, jnp.where(down, got[V_OWN + 1], got[V_HALO]))
        total = total + masked(ahead, got[V_OWN + 2]) - masked(behind, got[V_OWN + 2])
        total = total + masked(ahead_out, got[V_HALO + 1]) - masked(behind_out, got[V_HALO + 1])
        note(1, along(total))
        b_up = along(masked(here, jnp.where(up, got[B_OWN], got[B_HALO])))
        b_down = along(masked(here, jnp.where(down, got[B_OWN + 1], got[B_HALO])))
        b_mid, b_out = (got[B_OWN + 2], got[B_HALO + 1])
        b_ahead = along(masked(ahead, b_mid) + masked(ahead_out, b_out))
        b_behind = along(masked(behind, b_mid) + masked(behind_out, b_out))
        at_up = masked(behind, b_up + b_behind) - masked(ahead, b_up + b_ahead)
        at_down = masked(ahead, b_down + b_ahead) - masked(behind, b_down + b_behind)
        factors[0] = masked(up, at_up)
        factors[1] = masked(down, at_down)
        factors[2] = jnp.where(up, masked(jnp.logical_not(down), at_down), at_up)
        factors[3] = masked(behind_out, b_up + b_behind) - masked(ahead_out, b_up + b_ahead)
        factors[4] = masked(ahead_out, b_down + b_ahead) - masked(behind_out, b_down + b_behind)

    def next_shear(n):
        rows = [P_OWN, P_OWN + 1, P_HALO, P_HALO + 1, P_HALO + 2]
        total = factors[0] * got[rows[0]]
        for k in range(1, 5):
            total = total + factors[k] * got[rows[k]]
        note(n, shear[:, 0:1] + along(total))

    for small in smalls:
        small.wait()
    fill_placing()
    gather(B_OWN, own_rows(b, 0) + [lambda z, y: b[z, pl.ds(y, 1), :]])
    for c in range(chunks):
        for i in range(4, 9):
            load(i, c).wait()

    def work_after(r):
        if r == 0:
            v_rows = own_rows(vx, 0) + [lambda z, y: vy[z, pl.ds(y, 1), :]]
            gather(P_OWN, own_rows(p, 1) + v_rows)
        elif r == 1:
            gather(
                P_HALO,
                halo_rows(1)
                + [
                    lambda z, y: row_halo(yrecv[1], 2, z, y),
                    lambda z, y: row_pack(vyx, 0, z, y),
                    lambda z, y: row_halo(yrecv[0], 3, z, y),
                    lambda z, y: row_pack(bxh, 0, z, y),
                ],
            )
            first_shear()
            next_shear(2)
            gather(P_OWN, own_rows(p, 1))
        elif r < STEPS - 1:
            gather(P_HALO, halo_rows(r))
            next_shear(r + 1)
            gather(P_OWN, own_rows(p, 1))

    def exchange_first():
        gather(P_HALO, halo_rows(STEPS - 1))
        next_shear(STEPS)
        rows_send[...] = jnp.dot(
            placing[...], spectra_out[...].astype(jnp.bfloat16), preferred_element_type=jnp.float32
        ).astype(jnp.bfloat16)
        for k in range(1, ngx):
            first_to(k).start()
        at = pl.ds(pl.multiple_of(gx * group_rows, group_rows), group_rows)
        rows_group[at, :] = rows_send[at, :]

    for r in range(STEPS):
        vz[1] = vz[1] - b[0] * (p[2] - p[0])
        for c in range(chunks):
            receive(r, c)
            halos(r, c)
            if r == STEPS - 1 and c == chunks - 1:
                exchange_first()
            sweep(r, c)
            if r < STEPS - 1:
                send(r + 1, c)
        work_after(r)
    for k in range(1, ngx):
        first_from(k).wait_recv()
    for k in range(1, ngy):
        second_to(k).start()
    at = pl.ds(pl.multiple_of(gy * all_rows, all_rows), all_rows)
    rows_out[at, :] = rows_group[...]
    fill_table()
    for side in range(8):

        @pl.when(has[side])
        def _():
            for r in range(STEPS):
                if side in sides(r):
                    for c in range(chunks):
                        ends(r, c, side, False).wait_send()

    own_weights.wait()
    for k in range(1, ngy):
        weights_from(k).wait_recv()
        weights_to(k).wait_send()
    for k in range(1, ngx):
        first_to(k).wait_send()
    for k in range(1, ngy):
        second_from(k).wait_recv()
        second_to(k).wait_send()


def finish_kernel(dims, *refs):
    nz, slot_count, share = dims
    refs = list(refs)
    take = lambda count: [refs.pop(0) for _ in range(count)]
    vx, vy, vz, p, m, spectra, weights, rows, table = take(9)
    vel_out, p_out, m_out, spectra_out, slip_out = take(5)
    columns, slots, wide, out_sem, slip_sem = take(5)
    rup_group, lanes = (weights.shape[1], weights.shape[3])
    inner = pl.ds(1, nz)
    pairs = [
        (vx, vel_out.at[0]),
        (vy, vel_out.at[1]),
        (vz.at[inner], vel_out.at[2]),
        (p.at[inner], p_out),
        (m, m_out),
        (spectra, spectra_out),
    ]
    stores = [
        pltpu.make_async_copy(src, dst, out_sem.at[i]) for i, (src, dst) in enumerate(pairs)
    ]
    for store in stores:
        store.start()

    size, depth = (min(rup_group * slot_count, 512), min(rows.shape[0], 512))
    lines = min(slot_count, 128)
    square = (lines, lines)
    eye = lax.broadcasted_iota(jnp.int32, square, 0) == lax.broadcasted_iota(jnp.int32, square, 1)
    row_at = lax.broadcasted_iota(jnp.int32, (size, depth), 1)
    start = pl.multiple_of(remainder(lax.axis_index("gy") * share, lanes), share)

    for r in range(rup_group):
        for k in range(slot_count // lines):
            line = table[r : r + 1, k * lines : (k + 1) * lines].astype(jnp.float32)
            column = jnp.sum(jnp.where(eye, line, 0.0), axis=1, keepdims=True).astype(jnp.int32)
            at = pl.ds(r * slot_count + k * lines, lines)
            columns[at, :] = jnp.broadcast_to(column, (lines, columns.shape[1]))

    def choose(i, carry):
        at = pl.ds(pl.multiple_of(i * size, size), size)
        column = columns[at, 0:1]

        def part(k, total):
            base = pl.multiple_of(k * depth, depth)
            chosen = jnp.where(row_at + base == column, 1.0, 0.0).astype(jnp.bfloat16)
            return total + jnp.dot(
                chosen, rows[pl.ds(base, depth), :], preferred_element_type=jnp.float32
            )

        total = jnp.zeros((size, rows.shape[1]), jnp.float32)
        if rows.shape[0] == depth:
            total = part(0, total)
        else:
            total = lax.fori_loop(0, rows.shape[0] // depth, part, total)
        slots[at, :] = total.astype(jnp.bfloat16)
        return carry

    if slots.shape[0] == size:
        choose(0, 0)
    else:
        lax.fori_loop(0, slots.shape[0] // size, choose, 0)
    for r in range(rup_group):
        own = weights[:, r].astype(jnp.float32).reshape(slot_count, lanes).astype(jnp.bfloat16)
        wide[r] = lax.dot_general(
            own,
            slots[pl.ds(r * slot_count, slot_count), :],
            (((0,), (0,)), ((), ())),
            preferred_element_type=jnp.float32,
        )
        pltpu.make_async_copy(
            wide.at[r, pl.ds(start, share)], slip_out.at[r], slip_sem.at[r]
        ).start()
    for store in stores:
        store.wait()
    for r in range(rup_group):
        pltpu.make_async_copy(
            wide.at[r, pl.ds(start, share)], slip_out.at[r], slip_sem.at[r]
        ).wait()


VMEM_LIMIT = 40 * 1024 * 1024


def in_hbm(x):
    return pltpu.with_memory_space_constraint(x, pltpu.HBM)


def advance(
    velocity, pressure, memory, buoyancy, modulus, relax, strength, spectra, patch_cell, listed, weights
):
    nz, ny, nx = pressure.shape
    per_dev, width = spectra.shape
    zc = nx // 4
    chunks = nz // zc
    ngx, ngy = (lax.axis_size("gx"), lax.axis_size("gy"))
    dims = (nz, ny, nx, chunks, zc, per_dev, ngx, ngy)
    rup_group, slot_dev, variations = weights.shape
    lanes = max(variations // ngy, 128)
    all_rows = ngx * ngy * CAP
    f32 = jnp.float32
    field = lambda planes: pltpu.VMEM((planes, ny, nx), f32)
    rounds = range(STEPS)
    any_spec = pl.BlockSpec(memory_space=pl.ANY)
    vmem_spec = pl.BlockSpec(memory_space=pltpu.VMEM)
    return pl.pallas_call(
        functools.partial(step_kernel, dims),
        out_shape=[
            field(nz),
            field(nz),
            field(nz + 2),
            field(nz + 3),
            field(nz),
            pltpu.VMEM(spectra.shape, f32),
            pltpu.VMEM((ngy, rup_group, slot_dev, lanes), jnp.bfloat16),
            pltpu.VMEM((ngy * all_rows, width), jnp.bfloat16),
            pltpu.VMEM((rup_group, max(listed.shape[1], 128)), jnp.int32),
        ],
        in_specs=[any_spec] * 13,
        out_specs=[vmem_spec] * 9,
        scratch_shapes=[field(nz + 1), field(nz), field(nz), field(nz)]
        + [pltpu.VMEM((2, chunks, Y_ROWS[r], zc, nx), f32) for r in rounds]
        + [pltpu.VMEM((2, chunks, Y_ROWS[r], zc, nx), f32) for r in rounds]
        + [pltpu.VMEM((chunks, X_PACKS[r], ny, nx), f32) for r in rounds]
        + [pltpu.VMEM((2, chunks, X_PACKS[r], ny, nx), f32) for r in rounds]
        + [pltpu.VMEM((chunks, 2, 1, nx), f32) for r in rounds[1:]]
        + [pltpu.VMEM((chunks, 4, 1, nx), f32) for r in rounds[1:]]
        + [
            pltpu.SMEM((per_dev,), jnp.int32),
            pltpu.VMEM((1, per_dev), jnp.int32),
            pltpu.VMEM((STEPS, width), f32),
            pltpu.VMEM(listed.shape, jnp.int32),
            pltpu.VMEM((chunks, ny, nx), f32),
            pltpu.VMEM((chunks, ny, nx), f32),
            pltpu.VMEM((2, chunks, ny, nx), f32),
            pltpu.VMEM((2, chunks, zc, nx), f32),
            pltpu.VMEM((chunks, ny, nx), f32),
            pltpu.VMEM((chunks, ny + 16, nx), f32),
            pltpu.VMEM((15, per_dev, nx), f32),
            pltpu.VMEM((per_dev, nx), f32),
            pltpu.VMEM((5, per_dev, nx), f32),
            pltpu.VMEM((all_rows, per_dev), jnp.bfloat16),
            pltpu.VMEM((all_rows, width), jnp.bfloat16),
            pltpu.VMEM((all_rows, width), jnp.bfloat16),
            pltpu.SemaphoreType.DMA((9, chunks)),
            pltpu.SemaphoreType.DMA((5,)),
            pltpu.SemaphoreType.DMA((STEPS, chunks, 8)),
            pltpu.SemaphoreType.DMA((STEPS, chunks, 8)),
            pltpu.SemaphoreType.DMA((3, max(ngx, ngy))),
            pltpu.SemaphoreType.DMA((3, max(ngx, ngy))),
        ],
        compiler_params=pltpu.CompilerParams(
            collective_id=0, has_side_effects=True, vmem_limit_bytes=VMEM_LIMIT
        ),
    )(
        *[in_hbm(x) for x in (velocity, pressure, memory, buoyancy, modulus, relax, strength)],
        in_hbm(spectra),
        in_hbm(patch_cell),
        in_hbm(patch_cell.reshape(1, -1)),
        in_hbm(phase_rows(width // 2)),
        in_hbm(listed),
        in_hbm(weights),
    )


def finish(state, velocity, pressure, memory, spectra, weights):
    nz = pressure.shape[0]
    width = spectra.shape[1]
    ngy = lax.axis_size("gy")
    rup_group, slot_dev, variations = weights.shape
    slot_count = slot_dev * ngy
    share = variations // ngy
    lanes = max(share, 128)
    f32 = jnp.float32
    any_spec = pl.BlockSpec(memory_space=pl.ANY)
    vmem_spec = pl.BlockSpec(memory_space=pltpu.VMEM)
    return pl.pallas_call(
        functools.partial(finish_kernel, (nz, slot_count, share)),
        out_shape=[
            jax.ShapeDtypeStruct(velocity.shape, f32),
            jax.ShapeDtypeStruct(pressure.shape, f32),
            jax.ShapeDtypeStruct(memory.shape, f32),
            jax.ShapeDtypeStruct(spectra.shape, f32),
            jax.ShapeDtypeStruct((rup_group, share, width), f32),
        ],
        in_specs=[vmem_spec] * len(state),
        out_specs=[any_spec] * 5,
        scratch_shapes=[
            pltpu.VMEM((rup_group * slot_count, 128), jnp.int32),
            pltpu.VMEM((rup_group * slot_count, width), jnp.bfloat16),
            pltpu.VMEM((rup_group, lanes, width), f32),
            pltpu.SemaphoreType.DMA((6,)),
            pltpu.SemaphoreType.DMA((rup_group,)),
        ],
        compiler_params=pltpu.CompilerParams(vmem_limit_bytes=VMEM_LIMIT),
    )(*[pltpu.with_memory_space_constraint(x, pltpu.VMEM) for x in state])


def per_device(
    velocity,
    pressure,
    memory,
    buoyancy,
    modulus,
    relax,
    strength,
    spectra,
    patch_cell,
    rupture_patches,
    slip_weights,
):
    state = advance(
        velocity,
        pressure,
        memory,
        buoyancy,
        modulus,
        relax,
        strength,
        spectra,
        patch_cell,
        rupture_patches,
        slip_weights,
    )
    return tuple(finish(state, velocity, pressure, memory, spectra, slip_weights))


def solution(mesh):
    in_specs = (
        P(None, None, "gy", "gx"),
        P(None, "gy", "gx"),
        P(None, "gy", "gx"),
        P(None, "gy", "gx"),
        P(None, "gy", "gx"),
        P(None, "gy", "gx"),
        P(None, "gy", "gx"),
        P(("gx", "gy"), None),
        P(("gx", "gy")),
        P(),
        P("gx", "gy", None),
    )
    out_specs = (
        P(None, None, "gy", "gx"),
        P(None, "gy", "gx"),
        P(None, "gy", "gx"),
        P(("gx", "gy"), None),
        P("gx", "gy", None),
    )
    return jax.shard_map(
        per_device, mesh=mesh, in_specs=in_specs, out_specs=out_specs, check_vma=False
    )
```

```python
import functools

import jax
import jax.numpy as jnp
import numpy as np
from jax import lax
from jax.experimental import pallas as pl
from jax.experimental.pallas import tpu as pltpu
from jax.sharding import PartitionSpec as P

STEPS = 4
CAP = 2
BATCH = 8


def phase_rows(freqs):
    angle = np.pi * (np.arange(freqs) + 0.5) / freqs
    rows = [np.concatenate([np.cos(angle * n), -np.sin(angle * n)]) for n in range(1, STEPS + 1)]
    rows = rows + [np.zeros(2 * freqs)] * (8 - STEPS)
    return jnp.asarray(np.stack(rows).astype(np.float32))


Y_ROWS = [4, 3] + [2] * (STEPS - 2)
X_PACKS = [3, 2] + [1] * (STEPS - 2)


def quotient(value, size):
    if size & (size - 1):
        return lax.div(value, jnp.full_like(value, size))
    return lax.shift_right_logical(value, jnp.full_like(value, size.bit_length() - 1))


def remainder(value, size):
    if size & (size - 1):
        return lax.rem(value, jnp.full_like(value, size))
    return value & (size - 1)


def step_kernel(dims, *refs):
    nz, ny, nx, chunks, zc, per_dev, ngx, ngy = dims
    refs = list(refs)
    take = lambda count: [refs.pop(0) for _ in range(count)]
    vel_in, p_in, m_in, b_in, mod_in, rel_in, str_in = take(7)
    spectra_in, cell_in, cell_row_in, phase_in, listed_in, weights = take(6)
    vx, vy, vz, p, m, spectra_out, weights_got, rows_out, table, heard, phase = take(11)
    b, mod, rel, stg = take(4)
    ysend, yrecv = (take(STEPS), take(STEPS))
    xsend, xrecv = (take(STEPS), take(STEPS))
    csend, crecv = (take(STEPS - 1), take(STEPS - 1))
    cell, cell_row, listed = take(3)
    vxh, bxh, hx, vyh, vyx, xj, got, shear, factors = take(9)
    placing, placed, rows_send, rows_group, told = take(5)
    in_sem, small_sem, send_sem, recv_sem, far_send, far_recv = take(6)
    pass_send, pass_recv, tell_sem, hear_sem = take(4)

    gx, gy = (lax.axis_index("gx"), lax.axis_index("gy"))
    has = [gy > 0, gy < ngy - 1, gx > 0, gx < ngx - 1]
    has = has + [has[k // 2] & has[2 + k % 2] for k in range(4)]
    peer = [{"gy": gy - 1}, {"gy": gy + 1}, {"gx": gx - 1}, {"gx": gx + 1}]
    peer = peer + [{**peer[k // 2], **peer[2 + k % 2]} for k in range(4)]

    def load(i, c):
        at = pl.ds(c * zc, zc)
        moved = pl.ds(c * zc + 1, zc)
        src, dst = [
            (p_in.at[at], p.at[moved]),
            (b_in.at[at], b.at[at]),
            (vel_in.at[0, at], vx.at[at]),
            (vel_in.at[1, at], vy.at[at]),
            (vel_in.at[2, at], vz.at[moved]),
            (rel_in.at[at], rel.at[at]),
            (m_in.at[at], m.at[at]),
            (str_in.at[at], stg.at[at]),
            (mod_in.at[at], mod.at[at]),
        ][i]
        return pltpu.make_async_copy(src, dst, in_sem.at[i, c])

    smalls = [
        pltpu.make_async_copy(src, dst, small_sem.at[i])
        for i, (src, dst) in enumerate(
            [
                (cell_in, cell),
                (cell_row_in, cell_row),
                (listed_in, listed),
                (phase_in, phase),
                (spectra_in, spectra_out),
            ]
        )
    ]
    for c in range(chunks):
        for i in range(4):
            load(i, c).start()
    for c in range(chunks):
        for i in range(4, 9):
            load(i, c).start()
    for small in smalls:
        small.start()

    devices = ngx * ngy
    me = gx * ngy + gy
    mine = gy * ngx + gx

    def other_device(k):
        other = lax.rem(me + k, devices)
        return {"gx": lax.div(other, ngy), "gy": lax.rem(other, ngy)}

    def flip(j):
        index = gy
        for bit in range(j.bit_length()):
            if (j >> bit) & 1:
                step = 2**bit
                index = index + step * (1 - 2 * lax.rem(lax.div(index, step), 2))
        return index

    barrier = pltpu.get_barrier_semaphore()

    def greet(k, carry):
        pl.semaphore_signal(
            barrier, inc=1, device_id=other_device(k), device_id_type=pl.DeviceIdType.MESH
        )
        return carry

    lax.fori_loop(1, devices, greet, 0)

    plane = jnp.zeros((ny, nx), jnp.float32)
    p[0] = plane
    p[nz + 1] = plane
    p[nz + 2] = plane
    vz[0] = plane
    vz[nz + 1] = plane
    b[nz] = plane
    for side in range(8):

        @pl.when(jnp.logical_not(has[side]))
        def _():
            for r in range(STEPS):
                if side < 2:
                    yrecv[r][side] = jnp.zeros(yrecv[r].shape[1:], jnp.float32)
                elif side < 4:
                    xrecv[r][side - 2] = jnp.zeros(xrecv[r].shape[1:], jnp.float32)
                elif r > 0:
                    for c in range(chunks):
                        crecv[r - 1][c, side - 4] = jnp.zeros((1, nx), jnp.float32)

    def ends(r, c, side, coming):
        k = side % 4
        if side < 2:
            there = side if coming else 1 - side
            src, dst = (ysend[r].at[side, c], yrecv[r].at[there, c])
            arrives = there
        elif side < 4:
            there = k - 2 if coming else 3 - k
            src, dst = (xsend[r].at[c], xrecv[r].at[there, c])
            arrives = 2 + there
        else:
            there = k if coming else 3 - k
            src, dst = (csend[r - 1].at[c, k // 2], crecv[r - 1].at[c, there])
            arrives = 4 + there
        return pltpu.make_async_remote_copy(
            src_ref=src,
            dst_ref=dst,
            send_sem=send_sem.at[r, c, side],
            recv_sem=recv_sem.at[r, c, arrives],
            device_id=peer[side],
            device_id_type=pl.DeviceIdType.MESH,
        )

    def sides(r):
        return range(4) if r == 0 else range(8)

    def send(r, c):
        for side in sides(r):

            @pl.when(has[side])
            def _():
                ends(r, c, side, False).start()

    def receive(r, c):
        for side in sides(r):

            @pl.when(has[side])
            def _():
                ends(r, c, side, True).wait_recv()

    lane = lax.broadcasted_iota(jnp.int32, (ny, nx), 1)
    row = lax.broadcasted_iota(jnp.int32, (ny, nx), 0)
    quad, lane4 = (quotient(lane, 4), remainder(lane, 4))
    last_lane, first_lane = (lane == nx - 1, lane == 0)
    last_row, first_row = (row == ny - 1, row == 0)
    west_half = remainder(lax.broadcasted_iota(jnp.int32, (1, nx), 1), 4) < 2

    def pack(total, slab, zl):
        return jnp.where(quad == zl, pltpu.roll(slab, 4 * zl + 2, 1), total)

    def d_x(slab, halo, zl):
        ends = pltpu.roll(halo, nx - 2 - 4 * zl, 1)
        after = jnp.where(last_lane, ends, pltpu.roll(slab, nx - 1, 1))
        before = jnp.where(first_lane, ends, pltpu.roll(slab, 1, 1))
        return after - before

    def d_y(slab, south, north):
        after = jnp.where(last_row, north, pltpu.roll(slab, ny - 1, 0))
        before = jnp.where(first_row, south, pltpu.roll(slab, 1, 0))
        return after - before

    for c in range(chunks):
        for i in range(4):
            load(i, c).wait()

        def edges(i, totals):
            pt, vt, bt = totals
            for j in range(BATCH):
                zl = i * BATCH + j
                z = c * zc + zl
                ps, vs, ws, bs = (p[z + 1], vx[z], vy[z], b[z])
                pt, vt, bt = (pack(pt, ps, zl), pack(vt, vs, zl), pack(bt, bs, zl))
                at = pl.ds(zl, 1)
                ysend[0][0, c, 0, at, :] = ps[0:1]
                ysend[0][0, c, 1, at, :] = ps[1:2]
                ysend[0][0, c, 2, at, :] = ws[0:1]
                ysend[0][0, c, 3, at, :] = bs[0:1]
                ysend[0][1, c, 0, at, :] = ps[ny - 2 : ny - 1]
                ysend[0][1, c, 1, at, :] = ps[ny - 1 : ny]
                ysend[0][1, c, 2, at, :] = ws[ny - 1 : ny]
                ysend[0][1, c, 3, at, :] = bs[ny - 1 : ny]
            return pt, vt, bt

        totals = lax.fori_loop(0, zc // BATCH, edges, (plane, plane, plane))
        for i, total in enumerate(totals):
            xsend[0][c, i] = total
        if c == 0:
            pl.semaphore_wait(barrier, devices - 1)
        send(0, c)

    rup_group, slot_dev, variations = weights.shape
    lanes = weights_got.shape[3]
    group_rows = ngy * CAP
    all_rows = ngx * group_rows

    def weight_block(other):
        block = other * (variations // ngy) // lanes
        return weights.at[:, :, pl.ds(pl.multiple_of(block * lanes, lanes), lanes)]

    def far(kind, k, src, dst):
        axis, size = ("gx", ngx) if kind == 1 else ("gy", ngy)
        return pltpu.make_async_remote_copy(
            src_ref=src,
            dst_ref=dst,
            send_sem=far_send.at[kind, k],
            recv_sem=far_recv.at[kind, k],
            device_id={axis: lax.rem(lax.axis_index(axis) + k, size)},
            device_id_type=pl.DeviceIdType.MESH,
        )

    def rows_of(ref, index, count):
        return ref.at[pl.ds(pl.multiple_of(index * count, count), count)]

    def weights_to(k):
        return far(0, k, weight_block(lax.rem(gy + k, ngy)), weights_got.at[gy])

    def weights_from(k):
        return far(0, k, weight_block(gy), weights_got.at[lax.rem(gy + ngy - k, ngy)])

    def first_to(k):
        src = rows_of(rows_send, lax.rem(gx + k, ngx), group_rows)
        return far(1, k, src, rows_of(rows_group, gx, group_rows))

    def first_from(k):
        src = rows_of(rows_send, gx, group_rows)
        return far(1, k, src, rows_of(rows_group, lax.rem(gx + ngx - k, ngx), group_rows))

    half = all_rows // 2

    def block_rows(owner, h):
        at = pl.multiple_of(owner * all_rows + h * half, half)
        return rows_out.at[pl.ds(at, half)]

    def carry_over(j, h, src, dst, partner):
        return pltpu.make_async_remote_copy(
            src_ref=src,
            dst_ref=dst,
            send_sem=pass_send.at[j, h],
            recv_sem=pass_recv.at[j, h],
            device_id={"gy": partner},
            device_id_type=pl.DeviceIdType.MESH,
        )

    def direct_to(j, h):
        return carry_over(
            j, h, rows_group.at[pl.ds(h * half, half)], block_rows(gy, h), flip(j)
        )

    def pass_on(j, h):
        block = block_rows(flip(j), h)
        return carry_over(j + 1, h, block, block, flip(1))

    def block_from(j, h):
        block = block_rows(flip(j), h)
        return carry_over(j, h, block, block, flip(1 if j % 2 else j))

    def tell(k):
        where = other_device(k)
        return pltpu.make_async_remote_copy(
            src_ref=told.at[where["gx"]],
            dst_ref=heard.at[mine],
            send_sem=tell_sem.at[0],
            recv_sem=hear_sem.at[0],
            device_id=where,
            device_id_type=pl.DeviceIdType.MESH,
        )

    own_weights = pltpu.make_async_copy(weight_block(gy), weights_got.at[gy], far_send.at[0, 0])
    own_told = pltpu.make_async_copy(told.at[gx], heard.at[mine], hear_sem.at[0])

    square = (per_dev, per_dev)
    eye = lax.broadcasted_iota(jnp.int32, square, 0) == lax.broadcasted_iota(jnp.int32, square, 1)

    def to_row(column):
        return jnp.sum(jnp.where(eye, column, 0.0), axis=0, keepdims=True)

    def to_column(line):
        return jnp.sum(jnp.where(eye, line, 0.0), axis=1, keepdims=True)

    def fill_placing():
        ruptures, slots = listed.shape
        shape = (per_dev, slots)
        own_ids = lax.broadcasted_iota(jnp.int32, shape, 0) + (gx * ngy + gy) * per_dev
        slot_owner = quotient(lax.broadcasted_iota(jnp.int32, shape, 1), slot_dev)

        def body(r, best):
            owner = quotient(r, rup_group) * ngy + slot_owner
            return jnp.where(listed[pl.ds(r, 1), :] == own_ids, owner, best)

        best = lax.fori_loop(0, ruptures, body, jnp.full(shape, -1, jnp.int32))
        target = jnp.max(best.astype(jnp.float32), axis=1, keepdims=True)
        before = lax.broadcasted_iota(jnp.int32, square, 1) < lax.broadcasted_iota(
            jnp.int32, square, 0
        )
        same = (to_row(target) == target) & before
        rank = jnp.sum(jnp.where(same, 1.0, 0.0), axis=1, keepdims=True)
        bucket = jnp.where(target >= 0.0, target * CAP + rank, -1.0)
        spot = lax.broadcasted_iota(jnp.int32, placed.shape, 1).astype(jnp.float32)
        placed[...] = jnp.where(spot == bucket, 1.0, 0.0)
        place = lax.broadcasted_iota(jnp.int32, placing.shape, 0).astype(jnp.float32)
        placing[...] = jnp.where(place == to_row(bucket), 1.0, 0.0)

    def fill_table():
        slot_count = listed.shape[1]
        shape = table.shape
        spot = lax.broadcasted_iota(jnp.int32, shape, 1)
        owner, place = (quotient(spot, slot_dev), remainder(spot, slot_dev))
        table[...] = jnp.full(shape, -1, jnp.int32)
        group = pl.ds(pl.multiple_of(gx * rup_group, rup_group), rup_group)
        table[:, :slot_count] = listed[group, :]
        ids = table[...]
        source = quotient(ids, per_dev)

        def earlier(i, rank):
            shift = i - (slot_dev - 1)
            inside = (place >= shift) & (place < shift + slot_dev)
            turned = pltpu.roll(ids, jnp.where(shift < 0, shift + shape[1], shift), 1)
            for k in range(rup_group):
                other = pltpu.roll(turned, k, 0) if k else turned
                found = inside & (other < ids) & (quotient(other, per_dev) == source)
                rank = jnp.where(found, 1, rank)
            return rank

        shifts = 2 * slot_dev - 1
        unroll = max(k for k in range(1, 16) if shifts % k == 0)
        rank = lax.fori_loop(0, shifts, earlier, jnp.zeros(shape, jnp.int32), unroll=unroll)
        block = remainder(source, ngy) * ngx + quotient(source, ngy)
        table[...] = jnp.where(ids >= 0, (block * ngy + owner) * CAP + rank, -1)

    def halos(r, c):
        def joined(i):
            return jnp.where(lane4 < 2, xrecv[r][0, c, i], xrecv[r][1, c, i])

        def swapped(halo):
            return jnp.where(lane4 == 1, pltpu.roll(halo, nx - 1, 1), pltpu.roll(halo, 1, 1))

        outer, own = (joined(0), xsend[r][c, 0])
        if r == 0:
            vh, bh = (joined(1), joined(2))
            bxh[c] = bh
            vyh[0, c] = yrecv[0][0, c, 2]
            vyh[1, c] = yrecv[0][1, c, 2]
        else:
            vh, bh = (vxh[c], bxh[c])
            corner = crecv[r - 1]
            xj[c, 7:8, :] = jnp.where(west_half, corner[c, 0], corner[c, 1])
            xj[c, 8 : 8 + ny, :] = outer
            xj[c, 8 + ny : 9 + ny, :] = jnp.where(west_half, corner[c, 2], corner[c, 3])
            if r == 1:
                vyx[c] = joined(1)
        slope = jnp.where(
            lane4 == 1,
            pltpu.roll(own, nx - 1, 1) - pltpu.roll(outer, 1, 1),
            pltpu.roll(outer, nx - 1, 1) - pltpu.roll(own, 1, 1),
        )
        vh = vh - bh * slope
        vxh[c] = vh
        hx[0, c] = swapped(outer)
        hx[1, c] = swapped(vh)
        vyh[0, c] = vyh[0, c] - yrecv[0][0, c, 3] * (ysend[r][0, c, 0] - yrecv[r][0, c, 0])
        vyh[1, c] = vyh[1, c] - yrecv[0][1, c, 3] * (yrecv[r][1, c, 1] - ysend[r][1, c, 1])

    def sweep(r, c):
        last, first = (r == STEPS - 1, r == 0)
        n = r + 1

        def body(i, totals):
            totals = list(totals)
            base = i * BATCH
            z0 = c * zc + base
            ps = [p[z0 + 1 + j] for j in range(BATCH + 2)]
            bs = [b[z0 + j] for j in range(BATCH + 1)]
            zs = [vz[z0], vz[z0 + 1]]
            vs, ws, new_p = ([], [], [])
            for j in range(BATCH):
                zl = base + j
                at = pl.ds(zl, 1)
                zs.append(vz[z0 + j + 2] - bs[j + 1] * (ps[j + 2] - ps[j]))
                vs.append(vx[z0 + j] - bs[j] * d_x(ps[j], hx[0, c], zl))
                south, north = (yrecv[r][0, c, 1, at, :], yrecv[r][1, c, 0, at, :])
                ws.append(vy[z0 + j] - bs[j] * d_y(ps[j], south, north))
            for j in range(BATCH):
                zl = base + j
                at = pl.ds(zl, 1)
                spread = d_x(vs[j], hx[1, c], zl) + d_y(ws[j], vyh[0, c, at, :], vyh[1, c, at, :])
                spread = spread + (zs[j + 2] - zs[j])
                mem = m[z0 + j]
                mem = mem - rel[z0 + j] * (mem + stg[z0 + j] * spread)
                m[z0 + j] = mem
                new_p.append(ps[j] - mod[z0 + j] * (spread + mem))
            for j in range(BATCH):
                zl = base + j
                at = pl.ds(zl, 1)
                vz[z0 + j + 2] = zs[j + 2]
                vx[z0 + j] = vs[j]
                vy[z0 + j] = ws[j]
                p[z0 + j + 1] = new_p[j]
                if not last:
                    totals[0] = pack(totals[0], new_p[j], zl)
                    ysend[n][0, c, 0, at, :] = new_p[j][0:1]
                    ysend[n][0, c, 1, at, :] = new_p[j][1:2]
                    ysend[n][1, c, 0, at, :] = new_p[j][ny - 2 : ny - 1]
                    ysend[n][1, c, 1, at, :] = new_p[j][ny - 1 : ny]
                if first:
                    totals[1] = pack(totals[1], ws[j], zl)
                    ysend[n][0, c, 2, at, :] = vs[j][0:1]
                    ysend[n][1, c, 2, at, :] = vs[j][ny - 1 : ny]
            return tuple(totals)

        count = 0 if last else X_PACKS[n]
        totals = lax.fori_loop(0, zc // BATCH, body, (plane,) * count)
        for i, total in enumerate(totals):
            xsend[n][c, i] = total
        if not last:
            csend[n - 1][c, 0] = totals[0][0:1]
            csend[n - 1][c, 1] = totals[0][ny - 1 : ny]

    told_lane = lax.broadcasted_iota(jnp.int32, (1, 128), 1)
    in_place = quotient(told_lane, group_rows) == remainder(mine, 128 // group_rows)
    patch_lane = lax.broadcasted_iota(jnp.int32, (per_dev, nx), 1)

    def masked(keep, values):
        return jnp.where(keep, values, 0.0)

    def gather(first_slot, rows):
        def body(i, carry):
            at = cell[i]
            z, y = (quotient(at, ny * nx), remainder(quotient(at, nx), ny))
            out = pl.ds(i, 1)
            for k, row in enumerate(rows):
                got[first_slot + k, out, :] = row(z, y)
            return carry

        lax.fori_loop(0, per_dev, body, 0, unroll=8)

    def row_up(ref, z, y):
        return ref[z, pl.ds(jnp.minimum(y + 1, ny - 1), 1), :]

    def row_down(ref, z, y):
        return ref[z, pl.ds(jnp.maximum(y - 1, 0), 1), :]

    def row_halo(ref, index, z, y):
        side = jnp.where(y == 0, 0, 1)
        which = 1 - side if index is None else index
        return ref[side, quotient(z, zc), which, pl.ds(remainder(z, zc), 1), :]

    def row_pack(ref, shift, z, y):
        return ref[quotient(z, zc), pl.ds(y + shift, 1), :]

    def own_rows(ref, lift):
        return [lambda z, y: row_up(ref, z + lift, y), lambda z, y: row_down(ref, z + lift, y)]

    def halo_rows(n):
        return [
            lambda z, y: row_halo(yrecv[n], None, z, y),
            lambda z, y: row_pack(xj, 9, z, y),
            lambda z, y: row_pack(xj, 7, z, y),
        ]

    B_OWN, P_OWN, V_OWN, P_HALO, V_HALO, B_HALO = (0, 3, 5, 8, 11, 13)

    def places():
        cells = to_column(cell_row[...].astype(jnp.float32)).astype(jnp.int32)
        cell_z, cell_x = (quotient(cells, ny * nx), remainder(cells, nx))
        return cell_x, remainder(quotient(cells, nx), ny), 4 * remainder(cell_z, zc)

    def along(values):
        return jnp.sum(values, axis=1, keepdims=True)

    def note(n, value):
        shear[...] = jnp.broadcast_to(value, shear.shape)
        line = jnp.sum(placed[...] * value, axis=0, keepdims=True)
        for k in range(ngx):
            begin = k * group_rows
            tile = begin - begin % 128
            piece = line[:, tile : tile + 128]
            spread = pltpu.roll(piece, remainder(mine * group_rows + (128 - begin % 128), 128), 1)
            told[k, n - 1 : n, :] = jnp.where(in_place, spread, 0.0)
        spectra_out[...] = spectra_out[...] + value * phase[n - 1 : n, :]

    def first_shear():
        cell_x, cell_y, start = places()
        here = patch_lane == cell_x
        up, down = (cell_y < ny - 1, cell_y > 0)
        ahead, behind = (patch_lane == cell_x + 1, patch_lane == cell_x - 1)
        ahead_out = (patch_lane == start + 2) & (cell_x == nx - 1)
        behind_out = (patch_lane == start + 1) & (cell_x == 0)
        total = masked(here, jnp.where(up, got[V_OWN], got[V_HALO]))
        total = total - masked(here, jnp.where(down, got[V_OWN + 1], got[V_HALO]))
        total = total + masked(ahead, got[V_OWN + 2]) - masked(behind, got[V_OWN + 2])
        total = total + masked(ahead_out, got[V_HALO + 1]) - masked(behind_out, got[V_HALO + 1])
        note(1, along(total))
        b_up = along(masked(here, jnp.where(up, got[B_OWN], got[B_HALO])))
        b_down = along(masked(here, jnp.where(down, got[B_OWN + 1], got[B_HALO])))
        b_mid, b_out = (got[B_OWN + 2], got[B_HALO + 1])
        b_ahead = along(masked(ahead, b_mid) + masked(ahead_out, b_out))
        b_behind = along(masked(behind, b_mid) + masked(behind_out, b_out))
        at_up = masked(behind, b_up + b_behind) - masked(ahead, b_up + b_ahead)
        at_down = masked(ahead, b_down + b_ahead) - masked(behind, b_down + b_behind)
        factors[0] = masked(up, at_up)
        factors[1] = masked(down, at_down)
        factors[2] = jnp.where(up, masked(jnp.logical_not(down), at_down), at_up)
        factors[3] = masked(behind_out, b_up + b_behind) - masked(ahead_out, b_up + b_ahead)
        factors[4] = masked(ahead_out, b_down + b_ahead) - masked(behind_out, b_down + b_behind)

    def next_shear(n):
        rows = [P_OWN, P_OWN + 1, P_HALO, P_HALO + 1, P_HALO + 2]
        total = factors[0] * got[rows[0]]
        for k in range(1, 5):
            total = total + factors[k] * got[rows[k]]
        note(n, shear[:, 0:1] + along(total))

    for small in smalls:
        small.wait()
    told[...] = jnp.zeros(told.shape, jnp.float32)
    fill_placing()
    rows_send[...] = jnp.dot(
        placing[...],
        spectra_out[...],
        preferred_element_type=jnp.float32,
        precision=lax.Precision.HIGHEST,
    )
    for k in range(1, ngx):
        first_to(k).start()
    at = pl.ds(pl.multiple_of(gx * group_rows, group_rows), group_rows)
    rows_group[at, :] = rows_send[at, :]
    gather(B_OWN, own_rows(b, 0) + [lambda z, y: b[z, pl.ds(y, 1), :]])
    for c in range(chunks):
        for i in range(4, 9):
            load(i, c).wait()

    def work_after(r):
        if r == 0:
            v_rows = own_rows(vx, 0) + [lambda z, y: vy[z, pl.ds(y, 1), :]]
            gather(P_OWN, own_rows(p, 1) + v_rows)
        elif r == 1:
            gather(
                P_HALO,
                halo_rows(1)
                + [
                    lambda z, y: row_halo(yrecv[1], 2, z, y),
                    lambda z, y: row_pack(vyx, 0, z, y),
                    lambda z, y: row_halo(yrecv[0], 3, z, y),
                    lambda z, y: row_pack(bxh, 0, z, y),
                ],
            )
            first_shear()
            next_shear(2)
            gather(P_OWN, own_rows(p, 1))
        elif r < STEPS - 1:
            gather(P_HALO, halo_rows(r))
            next_shear(r + 1)
            gather(P_OWN, own_rows(p, 1))

    def last_shear():
        gather(P_HALO, halo_rows(STEPS - 1))
        next_shear(STEPS)
        own_told.start()

        def start(k, carry):
            tell(k).start()
            return carry

        lax.fori_loop(1, devices, start, 0)

    gaps = [(r, c) for r in range(STEPS - 1) for c in range(chunks)][1:]
    jobs = {gap: [] for gap in gaps + [(STEPS - 1, 0), None]}
    order = list(jobs)
    pieces = [(j, h) for j in range(2, ngy, 2) for h in range(2)]

    def enter_rows():
        for k in range(1, ngx):
            first_from(k).wait_recv()
        at = pl.ds(pl.multiple_of(gy * all_rows, all_rows), all_rows)
        rows_out[at, :] = rows_group[...]
        for h in range(2):
            direct_to(1, h).start()
        own_weights.start()

    def leave(j, h):
        direct_to(j, h).start()

    def forward(j, h):
        block_from(j, h).wait_recv()
        pass_on(j, h).start()

    jobs[order[0]].append(enter_rows)
    for i, (j, h) in enumerate(pieces):
        place = i * len(gaps) // len(pieces)
        jobs[order[place]].append(functools.partial(leave, j, h))
        after = order[min(place + 2, len(order) - 1)]
        jobs[after].append(functools.partial(forward, j, h))
    for k in range(1, ngy):
        place = (k - 1) * len(gaps) // (ngy - 1)
        jobs[order[place]].append(lambda k=k: weights_to(k).start())

    for r in range(STEPS):
        vz[1] = vz[1] - b[0] * (p[2] - p[0])
        for c in range(chunks):
            receive(r, c)
            halos(r, c)
            if r == STEPS - 1 and c == chunks - 1:
                last_shear()
            sweep(r, c)
            if r < STEPS - 1:
                send(r + 1, c)
            for job in jobs.get((r, c), []):
                job()
        work_after(r)
    for job in jobs[None]:
        job()
    fill_table()
    for side in range(8):

        @pl.when(has[side])
        def _():
            for r in range(STEPS):
                if side in sides(r):
                    for c in range(chunks):
                        ends(r, c, side, False).wait_send()

    own_weights.wait()
    for k in range(1, ngy):
        weights_from(k).wait_recv()
        weights_to(k).wait_send()
    for k in range(1, ngx):
        first_to(k).wait_send()
    for h in range(2):
        for j in [1] + list(range(2, ngy, 2)):
            direct_to(j, h).wait_send()
        for j in range(2, ngy, 2):
            pass_on(j, h).wait_send()
        for j in range(1, ngy, 2):
            block_from(j, h).wait_recv()
    pltpu.make_async_copy(
        heard.at[pl.ds(1, devices - 1)], heard.at[pl.ds(1, devices - 1)], tell_sem.at[0]
    ).wait()
    pltpu.make_async_copy(heard, heard, hear_sem.at[0]).wait()


def finish_kernel(dims, *refs):
    nz, slot_count, share = dims
    refs = list(refs)
    take = lambda count: [refs.pop(0) for _ in range(count)]
    vx, vy, vz, p, m, spectra, weights, rows, table, heard, phase = take(11)
    vel_out, p_out, m_out, spectra_out, slip_out = take(5)
    columns, slots, wide, exact, out_sem, slip_sem = take(6)
    rup_group, lanes = (weights.shape[1], weights.shape[3])
    inner = pl.ds(1, nz)
    pairs = [
        (vx, vel_out.at[0]),
        (vy, vel_out.at[1]),
        (vz.at[inner], vel_out.at[2]),
        (p.at[inner], p_out),
        (m, m_out),
        (spectra, spectra_out),
    ]
    stores = [
        pltpu.make_async_copy(src, dst, out_sem.at[i]) for i, (src, dst) in enumerate(pairs)
    ]
    for store in stores:
        store.start()

    size, depth = (min(rup_group * slot_count, 512), min(rows.shape[0], 512))
    lines = min(slot_count, 128)
    square = (lines, lines)
    eye = lax.broadcasted_iota(jnp.int32, square, 0) == lax.broadcasted_iota(jnp.int32, square, 1)
    row_at = lax.broadcasted_iota(jnp.int32, (size, depth), 1)
    start = pl.multiple_of(remainder(lax.axis_index("gy") * share, lanes), share)

    for r in range(rup_group):
        for k in range(slot_count // lines):
            line = table[r : r + 1, k * lines : (k + 1) * lines].astype(jnp.float32)
            column = jnp.sum(jnp.where(eye, line, 0.0), axis=1, keepdims=True).astype(jnp.int32)
            at = pl.ds(r * slot_count + k * lines, lines)
            columns[at, :] = jnp.broadcast_to(column, (lines, columns.shape[1]))

    count = heard.shape[0]
    per_tile = count * 128 // rows.shape[0]
    tiles = [
        functools.reduce(jnp.add, [heard[t * per_tile + k] for k in range(per_tile)])
        for t in range(count // per_tile)
    ]
    for t, tile in enumerate(tiles):
        at = pl.ds(t * 128, 128)
        change = lax.dot_general(
            tile,
            phase[...],
            (((0,), (0,)), ((), ())),
            preferred_element_type=jnp.float32,
            precision=lax.Precision.HIGHEST,
        )
        exact[at, :] = (rows[at, :] + change).astype(jnp.bfloat16)

    def choose(i, carry):
        at = pl.ds(pl.multiple_of(i * size, size), size)
        column = columns[at, 0:1]

        def part(k, total):
            base = pl.multiple_of(k * depth, depth)
            chosen = jnp.where(row_at + base == column, 1.0, 0.0).astype(jnp.bfloat16)
            return total + jnp.dot(
                chosen, exact[pl.ds(base, depth), :], preferred_element_type=jnp.float32
            )

        total = jnp.zeros((size, rows.shape[1]), jnp.float32)
        if rows.shape[0] == depth:
            total = part(0, total)
        else:
            total = lax.fori_loop(0, rows.shape[0] // depth, part, total)
        slots[at, :] = total.astype(jnp.bfloat16)
        return carry

    if slots.shape[0] == size:
        choose(0, 0)
    else:
        lax.fori_loop(0, slots.shape[0] // size, choose, 0)
    for r in range(rup_group):
        own = weights[:, r].astype(jnp.float32).reshape(slot_count, lanes).astype(jnp.bfloat16)
        wide[r] = lax.dot_general(
            own,
            slots[pl.ds(r * slot_count, slot_count), :],
            (((0,), (0,)), ((), ())),
            preferred_element_type=jnp.float32,
        )
        pltpu.make_async_copy(
            wide.at[r, pl.ds(start, share)], slip_out.at[r], slip_sem.at[r]
        ).start()
    for store in stores:
        store.wait()
    for r in range(rup_group):
        pltpu.make_async_copy(
            wide.at[r, pl.ds(start, share)], slip_out.at[r], slip_sem.at[r]
        ).wait()


VMEM_LIMIT = 40 * 1024 * 1024


def in_hbm(x):
    return pltpu.with_memory_space_constraint(x, pltpu.HBM)


def advance(
    velocity, pressure, memory, buoyancy, modulus, relax, strength, spectra, patch_cell, listed, weights
):
    nz, ny, nx = pressure.shape
    per_dev, width = spectra.shape
    zc = nx // 4
    chunks = nz // zc
    ngx, ngy = (lax.axis_size("gx"), lax.axis_size("gy"))
    dims = (nz, ny, nx, chunks, zc, per_dev, ngx, ngy)
    rup_group, slot_dev, variations = weights.shape
    lanes = max(variations // ngy, 128)
    all_rows = ngx * ngy * CAP
    f32 = jnp.float32
    field = lambda planes: pltpu.VMEM((planes, ny, nx), f32)
    rounds = range(STEPS)
    any_spec = pl.BlockSpec(memory_space=pl.ANY)
    vmem_spec = pl.BlockSpec(memory_space=pltpu.VMEM)
    return pl.pallas_call(
        functools.partial(step_kernel, dims),
        out_shape=[
            field(nz),
            field(nz),
            field(nz + 2),
            field(nz + 3),
            field(nz),
            pltpu.VMEM(spectra.shape, f32),
            pltpu.VMEM((ngy, rup_group, slot_dev, lanes), jnp.bfloat16),
            pltpu.VMEM((ngy * all_rows, width), f32),
            pltpu.VMEM((rup_group, max(listed.shape[1], 128)), jnp.int32),
            pltpu.VMEM((ngx * ngy, 8, 128), f32),
            pltpu.VMEM((8, width), f32),
        ],
        in_specs=[any_spec] * 13,
        out_specs=[vmem_spec] * 11,
        scratch_shapes=[field(nz + 1), field(nz), field(nz), field(nz)]
        + [pltpu.VMEM((2, chunks, Y_ROWS[r], zc, nx), f32) for r in rounds]
        + [pltpu.VMEM((2, chunks, Y_ROWS[r], zc, nx), f32) for r in rounds]
        + [pltpu.VMEM((chunks, X_PACKS[r], ny, nx), f32) for r in rounds]
        + [pltpu.VMEM((2, chunks, X_PACKS[r], ny, nx), f32) for r in rounds]
        + [pltpu.VMEM((chunks, 2, 1, nx), f32) for r in rounds[1:]]
        + [pltpu.VMEM((chunks, 4, 1, nx), f32) for r in rounds[1:]]
        + [
            pltpu.SMEM((per_dev,), jnp.int32),
            pltpu.VMEM((1, per_dev), jnp.int32),
            pltpu.VMEM(listed.shape, jnp.int32),
            pltpu.VMEM((chunks, ny, nx), f32),
            pltpu.VMEM((chunks, ny, nx), f32),
            pltpu.VMEM((2, chunks, ny, nx), f32),
            pltpu.VMEM((2, chunks, zc, nx), f32),
            pltpu.VMEM((chunks, ny, nx), f32),
            pltpu.VMEM((chunks, ny + 16, nx), f32),
            pltpu.VMEM((15, per_dev, nx), f32),
            pltpu.VMEM((per_dev, nx), f32),
            pltpu.VMEM((5, per_dev, nx), f32),
            pltpu.VMEM((all_rows, per_dev), f32),
            pltpu.VMEM((per_dev, max(all_rows, 128)), f32),
            pltpu.VMEM((all_rows, width), f32),
            pltpu.VMEM((all_rows, width), f32),
            pltpu.VMEM((ngx, 8, 128), f32),
            pltpu.SemaphoreType.DMA((9, chunks)),
            pltpu.SemaphoreType.DMA((5,)),
            pltpu.SemaphoreType.DMA((STEPS, chunks, 8)),
            pltpu.SemaphoreType.DMA((STEPS, chunks, 8)),
            pltpu.SemaphoreType.DMA((2, max(ngx, ngy))),
            pltpu.SemaphoreType.DMA((2, max(ngx, ngy))),
            pltpu.SemaphoreType.DMA((ngy, 2)),
            pltpu.SemaphoreType.DMA((ngy, 2)),
            pltpu.SemaphoreType.DMA((1,)),
            pltpu.SemaphoreType.DMA((1,)),
        ],
        compiler_params=pltpu.CompilerParams(
            collective_id=0, has_side_effects=True, vmem_limit_bytes=VMEM_LIMIT
        ),
    )(
        *[in_hbm(x) for x in (velocity, pressure, memory, buoyancy, modulus, relax, strength)],
        in_hbm(spectra),
        in_hbm(patch_cell),
        in_hbm(patch_cell.reshape(1, -1)),
        in_hbm(phase_rows(width // 2)),
        in_hbm(listed),
        in_hbm(weights),
    )


def finish(state, velocity, pressure, memory, spectra, weights):
    nz = pressure.shape[0]
    width = spectra.shape[1]
    ngy = lax.axis_size("gy")
    rup_group, slot_dev, variations = weights.shape
    slot_count = slot_dev * ngy
    share = variations // ngy
    lanes = max(share, 128)
    f32 = jnp.float32
    any_spec = pl.BlockSpec(memory_space=pl.ANY)
    vmem_spec = pl.BlockSpec(memory_space=pltpu.VMEM)
    return pl.pallas_call(
        functools.partial(finish_kernel, (nz, slot_count, share)),
        out_shape=[
            jax.ShapeDtypeStruct(velocity.shape, f32),
            jax.ShapeDtypeStruct(pressure.shape, f32),
            jax.ShapeDtypeStruct(memory.shape, f32),
            jax.ShapeDtypeStruct(spectra.shape, f32),
            jax.ShapeDtypeStruct((rup_group, share, width), f32),
        ],
        in_specs=[vmem_spec] * len(state),
        out_specs=[any_spec] * 5,
        scratch_shapes=[
            pltpu.VMEM((rup_group * slot_count, 128), jnp.int32),
            pltpu.VMEM((rup_group * slot_count, width), jnp.bfloat16),
            pltpu.VMEM((rup_group, lanes, width), f32),
            pltpu.VMEM(state[7].shape, jnp.bfloat16),
            pltpu.SemaphoreType.DMA((6,)),
            pltpu.SemaphoreType.DMA((rup_group,)),
        ],
        compiler_params=pltpu.CompilerParams(vmem_limit_bytes=VMEM_LIMIT),
    )(*[pltpu.with_memory_space_constraint(x, pltpu.VMEM) for x in state])


def per_device(
    velocity,
    pressure,
    memory,
    buoyancy,
    modulus,
    relax,
    strength,
    spectra,
    patch_cell,
    rupture_patches,
    slip_weights,
):
    state = advance(
        velocity,
        pressure,
        memory,
        buoyancy,
        modulus,
        relax,
        strength,
        spectra,
        patch_cell,
        rupture_patches,
        slip_weights,
    )
    return tuple(finish(state, velocity, pressure, memory, spectra, slip_weights))


def solution(mesh):
    in_specs = (
        P(None, None, "gy", "gx"),
        P(None, "gy", "gx"),
        P(None, "gy", "gx"),
        P(None, "gy", "gx"),
        P(None, "gy", "gx"),
        P(None, "gy", "gx"),
        P(None, "gy", "gx"),
        P(("gx", "gy"), None),
        P(("gx", "gy")),
        P(),
        P("gx", "gy", None),
    )
    out_specs = (
        P(None, None, "gy", "gx"),
        P(None, "gy", "gx"),
        P(None, "gy", "gx"),
        P(("gx", "gy"), None),
        P("gx", "gy", None),
    )
    return jax.shard_map(
        per_device, mesh=mesh, in_specs=in_specs, out_specs=out_specs, check_vma=False
    )
```

```python
import functools

import jax
import jax.numpy as jnp
import numpy as np
from jax import lax
from jax.experimental import pallas as pl
from jax.experimental.pallas import tpu as pltpu
from jax.sharding import PartitionSpec as P

STEPS = 4
CAP = 2
BATCH = 8


def phase_rows(freqs):
    angle = np.pi * (np.arange(freqs) + 0.5) / freqs
    rows = [np.concatenate([np.cos(angle * n), -np.sin(angle * n)]) for n in range(1, STEPS + 1)]
    rows = rows + [np.zeros(2 * freqs)] * (8 - STEPS)
    return jnp.asarray(np.stack(rows).astype(np.float32))


Y_ROWS = [4, 3] + [2] * (STEPS - 2)
X_PACKS = [3, 2] + [1] * (STEPS - 2)


def quotient(value, size):
    if size & (size - 1):
        return lax.div(value, jnp.full_like(value, size))
    return lax.shift_right_logical(value, jnp.full_like(value, size.bit_length() - 1))


def remainder(value, size):
    if size & (size - 1):
        return lax.rem(value, jnp.full_like(value, size))
    return value & (size - 1)


def step_kernel(dims, *refs):
    nz, ny, nx, chunks, zc, per_dev, ngx, ngy = dims
    refs = list(refs)
    take = lambda count: [refs.pop(0) for _ in range(count)]
    vel_in, p_in, m_in, b_in, mod_in, rel_in, str_in = take(7)
    spectra_in, cell_in, cell_row_in, phase_in, listed_in, weights = take(6)
    vx, vy, vz, p, m, spectra_out, weights_got, rows_out, table, heard, heard_last, phase = take(12)
    b, mod, rel, stg = take(4)
    ysend, xsend, csend = take(3)
    yrecv, xrecv, crecv = (take(STEPS), take(STEPS), take(STEPS - 1))
    cell, cell_row, listed = take(3)
    vxh, bxh, hx, vyh, vyx, xj, got, shear, factors = take(9)
    placing, placed, rows_send, rows_group, told, told_last = take(6)
    in_sem, small_sem, send_sem, recv_sem, far_sem, block_sem, tell_sem, hear_sem = take(8)

    gx, gy = (lax.axis_index("gx"), lax.axis_index("gy"))
    has = [gy > 0, gy < ngy - 1, gx > 0, gx < ngx - 1]
    has = has + [has[k // 2] & has[2 + k % 2] for k in range(4)]
    peer = [{"gy": gy - 1}, {"gy": gy + 1}, {"gx": gx - 1}, {"gx": gx + 1}]
    peer = peer + [{**peer[k // 2], **peer[2 + k % 2]} for k in range(4)]

    def load(i, c):
        at = pl.ds(c * zc, zc)
        moved = pl.ds(c * zc + 1, zc)
        src, dst = [
            (p_in.at[at], p.at[moved]),
            (b_in.at[at], b.at[at]),
            (vel_in.at[0, at], vx.at[at]),
            (vel_in.at[1, at], vy.at[at]),
            (vel_in.at[2, at], vz.at[moved]),
            (rel_in.at[at], rel.at[at]),
            (m_in.at[at], m.at[at]),
            (str_in.at[at], stg.at[at]),
            (mod_in.at[at], mod.at[at]),
        ][i]
        return pltpu.make_async_copy(src, dst, in_sem.at[i, c])

    y_row = lambda r, k: sum(Y_ROWS[:r]) + k
    x_row = lambda r, k: sum(X_PACKS[:r]) + k

    smalls = [
        pltpu.make_async_copy(src, dst, small_sem.at[i])
        for i, (src, dst) in enumerate(
            [
                (cell_in, cell),
                (cell_row_in, cell_row),
                (listed_in, listed),
                (phase_in, phase),
                (spectra_in, spectra_out),
            ]
        )
    ]
    for small in smalls:
        small.start()
    for c in range(chunks):
        for i in range(4):
            load(i, c).start()
    for c in range(chunks):
        for i in range(4, 9):
            load(i, c).start()
    devices = ngx * ngy
    me = gx * ngy + gy
    mine = gy * ngx + gx

    def other_device(k):
        other = lax.rem(me + k, devices)
        return {"gx": lax.div(other, ngy), "gy": lax.rem(other, ngy)}

    def flip(j):
        index = gy
        for bit in range(j.bit_length()):
            if (j >> bit) & 1:
                step = 2**bit
                index = index + step * (1 - 2 * lax.rem(lax.div(index, step), 2))
        return index

    barrier = pltpu.get_barrier_semaphore()

    def greet(k, carry):
        pl.semaphore_signal(
            barrier, inc=1, device_id=other_device(k), device_id_type=pl.DeviceIdType.MESH
        )
        return carry

    lax.fori_loop(1, devices, greet, 0)

    plane = jnp.zeros((ny, nx), jnp.float32)
    p[0] = plane
    p[nz + 1] = plane
    p[nz + 2] = plane
    vz[0] = plane
    vz[nz + 1] = plane
    b[nz] = plane
    for side in range(8):

        @pl.when(jnp.logical_not(has[side]))
        def _():
            for r in range(STEPS):
                if side < 2:
                    yrecv[r][side] = jnp.zeros(yrecv[r].shape[1:], jnp.float32)
                elif side < 4:
                    xrecv[r][side - 2] = jnp.zeros(xrecv[r].shape[1:], jnp.float32)
                elif r > 0:
                    for c in range(chunks):
                        crecv[r - 1][c, side - 4] = jnp.zeros((1, nx), jnp.float32)

    def ends(r, c, side, coming):
        k = side % 4
        if side < 2:
            there = side if coming else 1 - side
            src = ysend.at[side, c, pl.ds(y_row(r, 0), Y_ROWS[r])]
            dst = yrecv[r].at[there, c]
            arrives = there
        elif side < 4:
            there = k - 2 if coming else 3 - k
            src = xsend.at[c, pl.ds(x_row(r, 0), X_PACKS[r])]
            dst = xrecv[r].at[there, c]
            arrives = 2 + there
        else:
            there = k if coming else 3 - k
            src = csend.at[k // 2, (r - 1) * chunks + c]
            dst = crecv[r - 1].at[c, there]
            arrives = 4 + there
        return pltpu.make_async_remote_copy(
            src_ref=src,
            dst_ref=dst,
            send_sem=send_sem.at[side],
            recv_sem=recv_sem.at[r % 2, c, arrives],
            device_id=peer[side],
            device_id_type=pl.DeviceIdType.MESH,
        )

    def sides(r):
        return range(4) if r == 0 else range(8)

    def send(r, c):
        for side in sides(r):

            @pl.when(has[side])
            def _():
                ends(r, c, side, False).start()

    def receive(r, c):
        for side in sides(r):

            @pl.when(has[side])
            def _():
                ends(r, c, side, True).wait_recv()

    lane = lax.broadcasted_iota(jnp.int32, (ny, nx), 1)
    row = lax.broadcasted_iota(jnp.int32, (ny, nx), 0)
    quad, lane4 = (quotient(lane, 4), remainder(lane, 4))
    last_lane, first_lane = (lane == nx - 1, lane == 0)
    last_row, first_row = (row == ny - 1, row == 0)
    west_half = remainder(lax.broadcasted_iota(jnp.int32, (1, nx), 1), 4) < 2

    def pack(total, slab, zl):
        return jnp.where(quad == zl, pltpu.roll(slab, 4 * zl + 2, 1), total)

    def d_x(slab, halo, zl):
        ends = pltpu.roll(halo, nx - 2 - 4 * zl, 1)
        after = jnp.where(last_lane, ends, pltpu.roll(slab, nx - 1, 1))
        before = jnp.where(first_lane, ends, pltpu.roll(slab, 1, 1))
        return after - before

    def d_y(slab, south, north):
        after = jnp.where(last_row, north, pltpu.roll(slab, ny - 1, 0))
        before = jnp.where(first_row, south, pltpu.roll(slab, 1, 0))
        return after - before

    for c in range(chunks):
        for i in range(4):
            load(i, c).wait()

        def edges(i, totals):
            pt, vt, bt = totals
            for j in range(BATCH):
                zl = i * BATCH + j
                z = c * zc + zl
                ps, vs, ws, bs = (p[z + 1], vx[z], vy[z], b[z])
                pt, vt, bt = (pack(pt, ps, zl), pack(vt, vs, zl), pack(bt, bs, zl))
                at = pl.ds(zl, 1)
                ysend[0, c, y_row(0, 0), at, :] = ps[0:1]
                ysend[0, c, y_row(0, 1), at, :] = ps[1:2]
                ysend[0, c, y_row(0, 2), at, :] = ws[0:1]
                ysend[0, c, y_row(0, 3), at, :] = bs[0:1]
                ysend[1, c, y_row(0, 0), at, :] = ps[ny - 2 : ny - 1]
                ysend[1, c, y_row(0, 1), at, :] = ps[ny - 1 : ny]
                ysend[1, c, y_row(0, 2), at, :] = ws[ny - 1 : ny]
                ysend[1, c, y_row(0, 3), at, :] = bs[ny - 1 : ny]
            return pt, vt, bt

        totals = lax.fori_loop(0, zc // BATCH, edges, (plane, plane, plane))
        for i, total in enumerate(totals):
            xsend[c, x_row(0, i)] = total
        if c == 0:
            pl.semaphore_wait(barrier, devices - 1)
        send(0, c)

    rup_group, slot_dev, variations = weights.shape
    lanes = weights_got.shape[3]
    group_rows = ngy * CAP
    all_rows = ngx * group_rows

    def weight_block(other):
        block = other * (variations // ngy) // lanes
        return weights.at[:, :, pl.ds(pl.multiple_of(block * lanes, lanes), lanes)]

    def far(kind, k, src, dst):
        axis, size = ("gx", ngx) if kind == 1 else ("gy", ngy)
        return pltpu.make_async_remote_copy(
            src_ref=src,
            dst_ref=dst,
            send_sem=far_sem.at[kind, 0],
            recv_sem=far_sem.at[kind, 1],
            device_id={axis: lax.rem(lax.axis_index(axis) + k, size)},
            device_id_type=pl.DeviceIdType.MESH,
        )

    def settle(ref, sem):
        pltpu.make_async_copy(ref, ref, sem).wait()

    def rows_of(ref, index, count):
        return ref.at[pl.ds(pl.multiple_of(index * count, count), count)]

    def weights_to(k):
        return far(0, k, weight_block(lax.rem(gy + k, ngy)), weights_got.at[gy])

    def first_to(k):
        src = rows_of(rows_send, lax.rem(gx + k, ngx), group_rows)
        return far(1, k, src, rows_of(rows_group, gx, group_rows))

    half = all_rows // 2

    def block_rows(owner, h):
        at = pl.multiple_of(owner * all_rows + h * half, half)
        return rows_out.at[pl.ds(at, half)]

    def carry_over(j, h, src, dst, partner):
        return pltpu.make_async_remote_copy(
            src_ref=src,
            dst_ref=dst,
            send_sem=block_sem.at[0, 1],
            recv_sem=block_sem.at[0, 0] if j % 2 else block_sem.at[j // 2, h],
            device_id={"gy": partner},
            device_id_type=pl.DeviceIdType.MESH,
        )

    def direct_to(j, h):
        return carry_over(
            j, h, rows_group.at[pl.ds(h * half, half)], block_rows(gy, h), flip(j)
        )

    def pass_on(j, h):
        block = block_rows(flip(j), h)
        return carry_over(j + 1, h, block, block, flip(1))

    def block_from(j, h):
        block = block_rows(flip(j), h)
        return carry_over(j, h, block, block, flip(1 if j % 2 else j))

    def tell(k, src, dst, i):
        where = other_device(k)
        return pltpu.make_async_remote_copy(
            src_ref=src.at[where["gx"]],
            dst_ref=dst.at[mine],
            send_sem=tell_sem.at[i],
            recv_sem=hear_sem.at[i],
            device_id=where,
            device_id_type=pl.DeviceIdType.MESH,
        )

    def tell_all(src, dst, i):
        pltpu.make_async_copy(src.at[gx], dst.at[mine], hear_sem.at[i]).start()

        def start(k, carry):
            tell(k, src, dst, i).start()
            return carry

        lax.fori_loop(1, devices, start, 0)

    own_weights = pltpu.make_async_copy(weight_block(gy), weights_got.at[gy], far_sem.at[0, 1])

    square = (per_dev, per_dev)
    eye = lax.broadcasted_iota(jnp.int32, square, 0) == lax.broadcasted_iota(jnp.int32, square, 1)

    def to_row(column):
        return jnp.sum(jnp.where(eye, column, 0.0), axis=0, keepdims=True)

    def to_column(line):
        return jnp.sum(jnp.where(eye, line, 0.0), axis=1, keepdims=True)

    def fill_placing():
        ruptures, slots = listed.shape
        shape = (per_dev, slots)
        own_ids = lax.broadcasted_iota(jnp.int32, shape, 0) + (gx * ngy + gy) * per_dev
        slot_owner = quotient(lax.broadcasted_iota(jnp.int32, shape, 1), slot_dev)

        def body(r, best):
            owner = quotient(r, rup_group) * ngy + slot_owner
            return jnp.where(listed[pl.ds(r, 1), :] == own_ids, owner, best)

        best = lax.fori_loop(0, ruptures, body, jnp.full(shape, -1, jnp.int32))
        target = jnp.max(best.astype(jnp.float32), axis=1, keepdims=True)
        before = lax.broadcasted_iota(jnp.int32, square, 1) < lax.broadcasted_iota(
            jnp.int32, square, 0
        )
        same = (to_row(target) == target) & before
        rank = jnp.sum(jnp.where(same, 1.0, 0.0), axis=1, keepdims=True)
        bucket = jnp.where(target >= 0.0, target * CAP + rank, -1.0)
        spot = lax.broadcasted_iota(jnp.int32, placed.shape, 1).astype(jnp.float32)
        placed[...] = jnp.where(spot == bucket, 1.0, 0.0)
        place = lax.broadcasted_iota(jnp.int32, placing.shape, 0).astype(jnp.float32)
        placing[...] = jnp.where(place == to_row(bucket), 1.0, 0.0)

    def fill_table():
        slot_count = listed.shape[1]
        shape = table.shape
        spot = lax.broadcasted_iota(jnp.int32, shape, 1)
        owner, place = (quotient(spot, slot_dev), remainder(spot, slot_dev))
        table[...] = jnp.full(shape, -1, jnp.int32)
        group = pl.ds(pl.multiple_of(gx * rup_group, rup_group), rup_group)
        table[:, :slot_count] = listed[group, :]
        ids = table[...]
        source = quotient(ids, per_dev)

        def earlier(i, rank):
            shift = i - (slot_dev - 1)
            inside = (place >= shift) & (place < shift + slot_dev)
            turned = pltpu.roll(ids, jnp.where(shift < 0, shift + shape[1], shift), 1)
            for k in range(rup_group):
                other = pltpu.roll(turned, k, 0) if k else turned
                found = inside & (other < ids) & (quotient(other, per_dev) == source)
                rank = jnp.where(found, 1, rank)
            return rank

        shifts = 2 * slot_dev - 1
        unroll = max(k for k in range(1, 16) if shifts % k == 0)
        rank = lax.fori_loop(0, shifts, earlier, jnp.zeros(shape, jnp.int32), unroll=unroll)
        block = remainder(source, ngy) * ngx + quotient(source, ngy)
        table[...] = jnp.where(ids >= 0, (block * ngy + owner) * CAP + rank, -1)

    def halos(r, c):
        def joined(i):
            return jnp.where(lane4 < 2, xrecv[r][0, c, i], xrecv[r][1, c, i])

        def swapped(halo):
            return jnp.where(lane4 == 1, pltpu.roll(halo, nx - 1, 1), pltpu.roll(halo, 1, 1))

        outer, own = (joined(0), xsend[c, x_row(r, 0)])
        if r == 0:
            vh, bh = (joined(1), joined(2))
            bxh[c] = bh
            vyh[0, c] = yrecv[0][0, c, 2]
            vyh[1, c] = yrecv[0][1, c, 2]
        else:
            vh, bh = (vxh[c], bxh[c])
            corner = crecv[r - 1]
            xj[c, 7:8, :] = jnp.where(west_half, corner[c, 0], corner[c, 1])
            xj[c, 8 : 8 + ny, :] = outer
            xj[c, 8 + ny : 9 + ny, :] = jnp.where(west_half, corner[c, 2], corner[c, 3])
            if r == 1:
                vyx[c] = joined(1)
        slope = jnp.where(
            lane4 == 1,
            pltpu.roll(own, nx - 1, 1) - pltpu.roll(outer, 1, 1),
            pltpu.roll(outer, nx - 1, 1) - pltpu.roll(own, 1, 1),
        )
        vh = vh - bh * slope
        vxh[c] = vh
        hx[0, c] = swapped(outer)
        hx[1, c] = swapped(vh)
        vyh[0, c] = vyh[0, c] - yrecv[0][0, c, 3] * (ysend[0, c, y_row(r, 0)] - yrecv[r][0, c, 0])
        vyh[1, c] = vyh[1, c] - yrecv[0][1, c, 3] * (yrecv[r][1, c, 1] - ysend[1, c, y_row(r, 1)])

    def sweep(r, c):
        last, first = (r == STEPS - 1, r == 0)
        n = r + 1

        def body(i, totals):
            totals = list(totals)
            base = i * BATCH
            z0 = c * zc + base
            ps = [p[z0 + 1 + j] for j in range(BATCH + 2)]
            bs = [b[z0 + j] for j in range(BATCH + 1)]
            zs = [vz[z0], vz[z0 + 1]]
            vs, ws, new_p = ([], [], [])
            for j in range(BATCH):
                zl = base + j
                at = pl.ds(zl, 1)
                zs.append(vz[z0 + j + 2] - bs[j + 1] * (ps[j + 2] - ps[j]))
                vs.append(vx[z0 + j] - bs[j] * d_x(ps[j], hx[0, c], zl))
                south, north = (yrecv[r][0, c, 1, at, :], yrecv[r][1, c, 0, at, :])
                ws.append(vy[z0 + j] - bs[j] * d_y(ps[j], south, north))
            for j in range(BATCH):
                zl = base + j
                at = pl.ds(zl, 1)
                spread = d_x(vs[j], hx[1, c], zl) + d_y(ws[j], vyh[0, c, at, :], vyh[1, c, at, :])
                spread = spread + (zs[j + 2] - zs[j])
                mem = m[z0 + j]
                mem = mem - rel[z0 + j] * (mem + stg[z0 + j] * spread)
                m[z0 + j] = mem
                new_p.append(ps[j] - mod[z0 + j] * (spread + mem))
            for j in range(BATCH):
                zl = base + j
                at = pl.ds(zl, 1)
                vz[z0 + j + 2] = zs[j + 2]
                vx[z0 + j] = vs[j]
                vy[z0 + j] = ws[j]
                p[z0 + j + 1] = new_p[j]
                if not last:
                    totals[0] = pack(totals[0], new_p[j], zl)
                    ysend[0, c, y_row(n, 0), at, :] = new_p[j][0:1]
                    ysend[0, c, y_row(n, 1), at, :] = new_p[j][1:2]
                    ysend[1, c, y_row(n, 0), at, :] = new_p[j][ny - 2 : ny - 1]
                    ysend[1, c, y_row(n, 1), at, :] = new_p[j][ny - 1 : ny]
                if first:
                    totals[1] = pack(totals[1], ws[j], zl)
                    ysend[0, c, y_row(n, 2), at, :] = vs[j][0:1]
                    ysend[1, c, y_row(n, 2), at, :] = vs[j][ny - 1 : ny]
            return tuple(totals)

        count = 0 if last else X_PACKS[n]
        totals = lax.fori_loop(0, zc // BATCH, body, (plane,) * count)
        for i, total in enumerate(totals):
            xsend[c, x_row(n, i)] = total
        if not last:
            csend[0, (n - 1) * chunks + c] = totals[0][0:1]
            csend[1, (n - 1) * chunks + c] = totals[0][ny - 1 : ny]

    told_lane = lax.broadcasted_iota(jnp.int32, (1, 128), 1)
    in_place = quotient(told_lane, group_rows) == remainder(mine, 128 // group_rows)
    patch_lane = lax.broadcasted_iota(jnp.int32, (per_dev, nx), 1)

    def masked(keep, values):
        return jnp.where(keep, values, 0.0)

    def gather(first_slot, rows):
        def body(i, carry):
            at = cell[i]
            z, y = (quotient(at, ny * nx), remainder(quotient(at, nx), ny))
            out = pl.ds(i, 1)
            for k, row in enumerate(rows):
                got[first_slot + k, out, :] = row(z, y)
            return carry

        lax.fori_loop(0, per_dev, body, 0, unroll=8)

    def row_up(ref, z, y):
        return ref[z, pl.ds(jnp.minimum(y + 1, ny - 1), 1), :]

    def row_down(ref, z, y):
        return ref[z, pl.ds(jnp.maximum(y - 1, 0), 1), :]

    def row_halo(ref, index, z, y):
        side = jnp.where(y == 0, 0, 1)
        which = 1 - side if index is None else index
        return ref[side, quotient(z, zc), which, pl.ds(remainder(z, zc), 1), :]

    def row_pack(ref, shift, z, y):
        return ref[quotient(z, zc), pl.ds(y + shift, 1), :]

    def own_rows(ref, lift):
        return [lambda z, y: row_up(ref, z + lift, y), lambda z, y: row_down(ref, z + lift, y)]

    def halo_rows(n):
        return [
            lambda z, y: row_halo(yrecv[n], None, z, y),
            lambda z, y: row_pack(xj, 9, z, y),
            lambda z, y: row_pack(xj, 7, z, y),
        ]

    B_OWN, P_OWN, V_OWN, P_HALO, V_HALO, B_HALO = (0, 3, 5, 8, 11, 13)

    def places():
        cells = to_column(cell_row[...].astype(jnp.float32)).astype(jnp.int32)
        cell_z, cell_x = (quotient(cells, ny * nx), remainder(cells, nx))
        return cell_x, remainder(quotient(cells, nx), ny), 4 * remainder(cell_z, zc)

    def along(values):
        return jnp.sum(values, axis=1, keepdims=True)

    def note(n, value):
        shear[...] = jnp.broadcast_to(value, shear.shape)
        line = jnp.sum(placed[...] * value, axis=0, keepdims=True)
        for k in range(ngx):
            begin = k * group_rows
            tile = begin - begin % 128
            piece = line[:, tile : tile + 128]
            spread = pltpu.roll(piece, remainder(mine * group_rows + (128 - begin % 128), 128), 1)
            spread = jnp.where(in_place, spread, 0.0)
            if n < STEPS:
                told[k, n - 1] = spread
            else:
                told_last[k] = spread
        spectra_out[...] = spectra_out[...] + value * phase[n - 1 : n, :]

    def first_shear():
        cell_x, cell_y, start = places()
        here = patch_lane == cell_x
        up, down = (cell_y < ny - 1, cell_y > 0)
        ahead, behind = (patch_lane == cell_x + 1, patch_lane == cell_x - 1)
        ahead_out = (patch_lane == start + 2) & (cell_x == nx - 1)
        behind_out = (patch_lane == start + 1) & (cell_x == 0)
        total = masked(here, jnp.where(up, got[V_OWN], got[V_HALO]))
        total = total - masked(here, jnp.where(down, got[V_OWN + 1], got[V_HALO]))
        total = total + masked(ahead, got[V_OWN + 2]) - masked(behind, got[V_OWN + 2])
        total = total + masked(ahead_out, got[V_HALO + 1]) - masked(behind_out, got[V_HALO + 1])
        note(1, along(total))
        b_up = along(masked(here, jnp.where(up, got[B_OWN], got[B_HALO])))
        b_down = along(masked(here, jnp.where(down, got[B_OWN + 1], got[B_HALO])))
        b_mid, b_out = (got[B_OWN + 2], got[B_HALO + 1])
        b_ahead = along(masked(ahead, b_mid) + masked(ahead_out, b_out))
        b_behind = along(masked(behind, b_mid) + masked(behind_out, b_out))
        at_up = masked(behind, b_up + b_behind) - masked(ahead, b_up + b_ahead)
        at_down = masked(ahead, b_down + b_ahead) - masked(behind, b_down + b_behind)
        factors[0] = masked(up, at_up)
        factors[1] = masked(down, at_down)
        factors[2] = jnp.where(up, masked(jnp.logical_not(down), at_down), at_up)
        factors[3] = masked(behind_out, b_up + b_behind) - masked(ahead_out, b_up + b_ahead)
        factors[4] = masked(ahead_out, b_down + b_ahead) - masked(behind_out, b_down + b_behind)

    def next_shear(n):
        rows = [P_OWN, P_OWN + 1, P_HALO, P_HALO + 1, P_HALO + 2]
        total = factors[0] * got[rows[0]]
        for k in range(1, 5):
            total = total + factors[k] * got[rows[k]]
        note(n, shear[:, 0:1] + along(total))

    for c in range(chunks):
        for i in range(4, 9):
            load(i, c).wait()

    def send_rows():
        fill_placing()
        rows_send[...] = jnp.dot(
            placing[...],
            spectra_out[...],
            preferred_element_type=jnp.float32,
            precision=lax.Precision.HIGHEST,
        )
        for k in range(1, ngx):
            first_to(k).start()
        at = pl.ds(pl.multiple_of(gx * group_rows, group_rows), group_rows)
        rows_group[at, :] = rows_send[at, :]

    def work_after(r):
        if r == 0:
            for small in smalls:
                small.wait()
            send_rows()
            b_rows = own_rows(b, 0) + [lambda z, y: b[z, pl.ds(y, 1), :]]
            v_rows = own_rows(vx, 0) + [lambda z, y: vy[z, pl.ds(y, 1), :]]
            gather(B_OWN, b_rows + own_rows(p, 1) + v_rows)
        elif r == 1:
            gather(
                P_HALO,
                halo_rows(1)
                + [
                    lambda z, y: row_halo(yrecv[1], 2, z, y),
                    lambda z, y: row_pack(vyx, 0, z, y),
                    lambda z, y: row_halo(yrecv[0], 3, z, y),
                    lambda z, y: row_pack(bxh, 0, z, y),
                ],
            )
            first_shear()
            next_shear(2)
            gather(P_OWN, own_rows(p, 1))
        elif r < STEPS - 1:
            gather(P_HALO, halo_rows(r))
            next_shear(r + 1)
            gather(P_OWN, own_rows(p, 1))

    def last_shear():
        gather(P_HALO, halo_rows(STEPS - 1))
        next_shear(STEPS)
        tell_all(told_last, heard_last, 1)

    gaps = [(r, c) for r in range(STEPS - 1) for c in range(chunks)][chunks:]
    jobs = {gap: [] for gap in gaps + [(STEPS - 1, 0), None]}
    order = list(jobs)
    pieces = [(j, h) for j in range(2, ngy, 2) for h in range(2)]

    def enter_rows():
        settle(rows_group.at[pl.ds(0, (ngx - 1) * group_rows)], far_sem.at[1, 1])
        at = pl.ds(pl.multiple_of(gy * all_rows, all_rows), all_rows)
        rows_out[at, :] = rows_group[...]
        for h in range(2):
            direct_to(1, h).start()
        own_weights.start()

    def leave(j, h):
        direct_to(j, h).start()

    def forward(j, h):
        block_from(j, h).wait_recv()
        pass_on(j, h).start()

    jobs[order[0]].append(enter_rows)
    jobs[STEPS - 1, 0].append(lambda: tell_all(told, heard, 0))
    for i, (j, h) in enumerate(pieces):
        place = i * len(gaps) // len(pieces)
        jobs[order[place]].append(functools.partial(leave, j, h))
        after = order[min(place + 2, len(order) - 1)]
        jobs[after].append(functools.partial(forward, j, h))
    for k in range(1, ngy):
        place = (k - 1) * len(gaps) // (ngy - 1)
        jobs[order[place]].append(lambda k=k: weights_to(k).start())

    for r in range(STEPS):
        vz[1] = vz[1] - b[0] * (p[2] - p[0])
        for c in range(chunks):
            receive(r, c)
            halos(r, c)
            if r == STEPS - 1 and c == chunks - 1:
                last_shear()
            sweep(r, c)
            if r < STEPS - 1:
                send(r + 1, c)
            for job in jobs.get((r, c), []):
                job()
        work_after(r)
    for job in jobs[None]:
        job()
    fill_table()
    for side in range(8):

        @pl.when(has[side])
        def _():
            sent = ysend.at[side] if side < 2 else xsend if side < 4 else csend.at[side // 2 - 2]
            settle(sent, send_sem.at[side])

    settle(weights_got.at[pl.ds(0, ngy - 1)], far_sem.at[0, 0])
    settle(weights_got, far_sem.at[0, 1])
    settle(rows_group.at[pl.ds(0, (ngx - 1) * group_rows)], far_sem.at[1, 0])
    settle(rows_out.at[pl.ds(0, (ngy - 1) * all_rows)], block_sem.at[0, 1])
    settle(rows_out.at[pl.ds(0, ngy // 2 * all_rows)], block_sem.at[0, 0])
    for i, ref in enumerate([heard, heard_last]):
        settle(ref.at[pl.ds(1, devices - 1)], tell_sem.at[i])
        settle(ref, hear_sem.at[i])


def finish_kernel(dims, *refs):
    nz, slot_count, share = dims
    refs = list(refs)
    take = lambda count: [refs.pop(0) for _ in range(count)]
    vx, vy, vz, p, m, spectra, weights, rows, table, heard, heard_last, phase = take(12)
    vel_out, p_out, m_out, spectra_out, slip_out = take(5)
    columns, slots, wide, exact, lines_in, out_sem, slip_sem = take(7)
    rup_group, lanes = (weights.shape[1], weights.shape[3])
    inner = pl.ds(1, nz)
    pairs = [
        (vx, vel_out.at[0]),
        (vy, vel_out.at[1]),
        (vz.at[inner], vel_out.at[2]),
        (p.at[inner], p_out),
        (m, m_out),
        (spectra, spectra_out),
    ]
    stores = [
        pltpu.make_async_copy(src, dst, out_sem.at[i]) for i, (src, dst) in enumerate(pairs)
    ]
    for store in stores:
        store.start()

    size, depth = (min(rup_group * slot_count, 512), min(rows.shape[0], 512))
    lines = min(slot_count, 128)
    square = (lines, lines)
    eye = lax.broadcasted_iota(jnp.int32, square, 0) == lax.broadcasted_iota(jnp.int32, square, 1)
    row_at = lax.broadcasted_iota(jnp.int32, (size, depth), 1)
    start = pl.multiple_of(remainder(lax.axis_index("gy") * share, lanes), share)

    for r in range(rup_group):
        for k in range(slot_count // lines):
            line = table[r : r + 1, k * lines : (k + 1) * lines].astype(jnp.float32)
            column = jnp.sum(jnp.where(eye, line, 0.0), axis=1, keepdims=True).astype(jnp.int32)
            at = pl.ds(r * slot_count + k * lines, lines)
            columns[at, :] = jnp.broadcast_to(column, (lines, columns.shape[1]))

    count = heard.shape[0]
    per_tile = count * 128 // rows.shape[0]
    lines_in[...] = jnp.zeros(lines_in.shape, jnp.float32)
    for t in range(count // per_tile):
        at, of = (pl.ds(t * 128, 128), pl.ds(t * per_tile, per_tile))
        for n in range(STEPS):
            told = heard[of, n] if n < STEPS - 1 else heard_last[of]
            lines_in[n : n + 1, :] = jnp.sum(told, axis=0)
        change = lax.dot_general(
            lines_in[...],
            phase[...],
            (((0,), (0,)), ((), ())),
            preferred_element_type=jnp.float32,
            precision=lax.Precision.HIGHEST,
        )
        exact[at, :] = (rows[at, :] + change).astype(jnp.bfloat16)

    def choose(i, carry):
        at = pl.ds(pl.multiple_of(i * size, size), size)
        column = columns[at, 0:1]

        def part(k, total):
            base = pl.multiple_of(k * depth, depth)
            chosen = jnp.where(row_at + base == column, 1.0, 0.0).astype(jnp.bfloat16)
            return total + jnp.dot(
                chosen, exact[pl.ds(base, depth), :], preferred_element_type=jnp.float32
            )

        total = jnp.zeros((size, rows.shape[1]), jnp.float32)
        if rows.shape[0] == depth:
            total = part(0, total)
        else:
            total = lax.fori_loop(0, rows.shape[0] // depth, part, total)
        slots[at, :] = total.astype(jnp.bfloat16)
        return carry

    if slots.shape[0] == size:
        choose(0, 0)
    else:
        lax.fori_loop(0, slots.shape[0] // size, choose, 0)
    for r in range(rup_group):
        own = weights[:, r].astype(jnp.float32).reshape(slot_count, lanes).astype(jnp.bfloat16)
        wide[r] = lax.dot_general(
            own,
            slots[pl.ds(r * slot_count, slot_count), :],
            (((0,), (0,)), ((), ())),
            preferred_element_type=jnp.float32,
        )
        pltpu.make_async_copy(
            wide.at[r, pl.ds(start, share)], slip_out.at[r], slip_sem.at[r]
        ).start()
    for store in stores:
        store.wait()
    for r in range(rup_group):
        pltpu.make_async_copy(
            wide.at[r, pl.ds(start, share)], slip_out.at[r], slip_sem.at[r]
        ).wait()


VMEM_LIMIT = 40 * 1024 * 1024


def in_hbm(x):
    return pltpu.with_memory_space_constraint(x, pltpu.HBM)


def advance(
    velocity, pressure, memory, buoyancy, modulus, relax, strength, spectra, patch_cell, listed, weights
):
    nz, ny, nx = pressure.shape
    per_dev, width = spectra.shape
    zc = nx // 4
    chunks = nz // zc
    ngx, ngy = (lax.axis_size("gx"), lax.axis_size("gy"))
    dims = (nz, ny, nx, chunks, zc, per_dev, ngx, ngy)
    rup_group, slot_dev, variations = weights.shape
    lanes = max(variations // ngy, 128)
    all_rows = ngx * ngy * CAP
    f32 = jnp.float32
    field = lambda planes: pltpu.VMEM((planes, ny, nx), f32)
    rounds = range(STEPS)
    any_spec = pl.BlockSpec(memory_space=pl.ANY)
    vmem_spec = pl.BlockSpec(memory_space=pltpu.VMEM)
    return pl.pallas_call(
        functools.partial(step_kernel, dims),
        out_shape=[
            field(nz),
            field(nz),
            field(nz + 2),
            field(nz + 3),
            field(nz),
            pltpu.VMEM(spectra.shape, f32),
            pltpu.VMEM((ngy, rup_group, slot_dev, lanes), jnp.bfloat16),
            pltpu.VMEM((ngy * all_rows, width), f32),
            pltpu.VMEM((rup_group, max(listed.shape[1], 128)), jnp.int32),
            pltpu.VMEM((ngx * ngy, STEPS - 1, 1, 128), f32),
            pltpu.VMEM((ngx * ngy, 1, 128), f32),
            pltpu.VMEM((8, width), f32),
        ],
        in_specs=[any_spec] * 13,
        out_specs=[vmem_spec] * 12,
        scratch_shapes=[field(nz + 1), field(nz), field(nz), field(nz)]
        + [
            pltpu.VMEM((2, chunks, sum(Y_ROWS), zc, nx), f32),
            pltpu.VMEM((chunks, sum(X_PACKS), ny, nx), f32),
            pltpu.VMEM((2, (STEPS - 1) * chunks, 1, nx), f32),
        ]
        + [pltpu.VMEM((2, chunks, Y_ROWS[r], zc, nx), f32) for r in rounds]
        + [pltpu.VMEM((2, chunks, X_PACKS[r], ny, nx), f32) for r in rounds]
        + [pltpu.VMEM((chunks, 4, 1, nx), f32) for r in rounds[1:]]
        + [
            pltpu.SMEM((per_dev,), jnp.int32),
            pltpu.VMEM((1, per_dev), jnp.int32),
            pltpu.VMEM(listed.shape, jnp.int32),
            pltpu.VMEM((chunks, ny, nx), f32),
            pltpu.VMEM((chunks, ny, nx), f32),
            pltpu.VMEM((2, chunks, ny, nx), f32),
            pltpu.VMEM((2, chunks, zc, nx), f32),
            pltpu.VMEM((chunks, ny, nx), f32),
            pltpu.VMEM((chunks, ny + 16, nx), f32),
            pltpu.VMEM((15, per_dev, nx), f32),
            pltpu.VMEM((per_dev, nx), f32),
            pltpu.VMEM((5, per_dev, nx), f32),
            pltpu.VMEM((all_rows, per_dev), f32),
            pltpu.VMEM((per_dev, max(all_rows, 128)), f32),
            pltpu.VMEM((all_rows, width), f32),
            pltpu.VMEM((all_rows, width), f32),
            pltpu.VMEM((ngx, STEPS - 1, 1, 128), f32),
            pltpu.VMEM((ngx, 1, 128), f32),
            pltpu.SemaphoreType.DMA((9, chunks)),
            pltpu.SemaphoreType.DMA((5,)),
            pltpu.SemaphoreType.DMA((8,)),
            pltpu.SemaphoreType.DMA((2, chunks, 8)),
            pltpu.SemaphoreType.DMA((2, 2)),
            pltpu.SemaphoreType.DMA((ngy // 2, 2)),
            pltpu.SemaphoreType.DMA((2,)),
            pltpu.SemaphoreType.DMA((2,)),
        ],
        compiler_params=pltpu.CompilerParams(
            collective_id=0, has_side_effects=True, vmem_limit_bytes=VMEM_LIMIT
        ),
    )(
        *[in_hbm(x) for x in (velocity, pressure, memory, buoyancy, modulus, relax, strength)],
        in_hbm(spectra),
        in_hbm(patch_cell),
        in_hbm(patch_cell.reshape(1, -1)),
        in_hbm(phase_rows(width // 2)),
        in_hbm(listed),
        in_hbm(weights),
    )


def finish(state, velocity, pressure, memory, spectra, weights):
    nz = pressure.shape[0]
    width = spectra.shape[1]
    ngy = lax.axis_size("gy")
    rup_group, slot_dev, variations = weights.shape
    slot_count = slot_dev * ngy
    share = variations // ngy
    lanes = max(share, 128)
    f32 = jnp.float32
    any_spec = pl.BlockSpec(memory_space=pl.ANY)
    vmem_spec = pl.BlockSpec(memory_space=pltpu.VMEM)
    return pl.pallas_call(
        functools.partial(finish_kernel, (nz, slot_count, share)),
        out_shape=[
            jax.ShapeDtypeStruct(velocity.shape, f32),
            jax.ShapeDtypeStruct(pressure.shape, f32),
            jax.ShapeDtypeStruct(memory.shape, f32),
            jax.ShapeDtypeStruct(spectra.shape, f32),
            jax.ShapeDtypeStruct((rup_group, share, width), f32),
        ],
        in_specs=[vmem_spec] * len(state),
        out_specs=[any_spec] * 5,
        scratch_shapes=[
            pltpu.VMEM((rup_group * slot_count, 128), jnp.int32),
            pltpu.VMEM((rup_group * slot_count, width), jnp.bfloat16),
            pltpu.VMEM((rup_group, lanes, width), f32),
            pltpu.VMEM(state[7].shape, jnp.bfloat16),
            pltpu.VMEM((8, 128), f32),
            pltpu.SemaphoreType.DMA((6,)),
            pltpu.SemaphoreType.DMA((rup_group,)),
        ],
        compiler_params=pltpu.CompilerParams(vmem_limit_bytes=VMEM_LIMIT),
    )(*[pltpu.with_memory_space_constraint(x, pltpu.VMEM) for x in state])


def per_device(
    velocity,
    pressure,
    memory,
    buoyancy,
    modulus,
    relax,
    strength,
    spectra,
    patch_cell,
    rupture_patches,
    slip_weights,
):
    state = advance(
        velocity,
        pressure,
        memory,
        buoyancy,
        modulus,
        relax,
        strength,
        spectra,
        patch_cell,
        rupture_patches,
        slip_weights,
    )
    return tuple(finish(state, velocity, pressure, memory, spectra, slip_weights))


def solution(mesh):
    in_specs = (
        P(None, None, "gy", "gx"),
        P(None, "gy", "gx"),
        P(None, "gy", "gx"),
        P(None, "gy", "gx"),
        P(None, "gy", "gx"),
        P(None, "gy", "gx"),
        P(None, "gy", "gx"),
        P(("gx", "gy"), None),
        P(("gx", "gy")),
        P(),
        P("gx", "gy", None),
    )
    out_specs = (
        P(None, None, "gy", "gx"),
        P(None, "gy", "gx"),
        P(None, "gy", "gx"),
        P(("gx", "gy"), None),
        P("gx", "gy", None),
    )
    return jax.shard_map(
        per_device, mesh=mesh, in_specs=in_specs, out_specs=out_specs, check_vma=False
    )
```

```python
import functools
import math

import jax
import jax.numpy as jnp
import numpy as np
from jax import lax
from jax.experimental import pallas as pl
from jax.experimental.pallas import tpu as pltpu
from jax.sharding import PartitionSpec as P

STEPS = 4
CAP = 2
BATCH = 8


def phase_rows(freqs):
    angle = np.pi * (np.arange(freqs) + 0.5) / freqs
    rows = [np.concatenate([np.cos(angle * n), -np.sin(angle * n)]) for n in range(1, STEPS + 1)]
    rows = rows + [np.zeros(2 * freqs)] * (8 - STEPS)
    return jnp.asarray(np.stack(rows).astype(np.float32))


Y_ROWS = [4, 3] + [2] * (STEPS - 2)
X_PACKS = [3, 2] + [1] * (STEPS - 2)


def quotient(value, size):
    if size & (size - 1):
        return lax.div(value, jnp.full_like(value, size))
    return lax.shift_right_logical(value, jnp.full_like(value, size.bit_length() - 1))


def remainder(value, size):
    if size & (size - 1):
        return lax.rem(value, jnp.full_like(value, size))
    return value & (size - 1)


def step_kernel(dims, *refs):
    nz, ny, nx, chunks, zc, per_dev, ngx, ngy = dims
    refs = list(refs)
    take = lambda count: [refs.pop(0) for _ in range(count)]
    vel_in, p_in, m_in, b_in, mod_in, rel_in, str_in = take(7)
    spectra_in, cell_row_in, phase_in, listed_in, weights = take(5)
    vx, vy, vz, p, m, spectra_out, mixed, rows_out, heard, heard_last, phase = take(11)
    b, mod, rel, stg, vx_old, vy_old, p_old, b_east = take(8)
    ysend, xsend, csend = take(3)
    yrecv, xrecv, crecv = (take(STEPS), take(STEPS), take(STEPS))
    cell_row, listed, index_made, index = take(4)
    vxh, bwh, bxh, hx, hx_old, vyh, vyx, xj, got, shear, factors = take(11)
    hp, hv, hb, weights_got, table, columns, wide = take(7)
    placing, placed, rows_send, rows_group, told, told_last = take(6)
    in_sem, small_sem, send_sem, recv_sem, far_sem, block_sem, tell_sem, hear_sem, index_sem = take(9)

    gx, gy = (lax.axis_index("gx"), lax.axis_index("gy"))
    has = [gy > 0, gy < ngy - 1, gx > 0, gx < ngx - 1]
    has = has + [has[k // 2] & has[2 + k % 2] for k in range(4)]
    peer = [{"gy": gy - 1}, {"gy": gy + 1}, {"gx": gx - 1}, {"gx": gx + 1}]
    peer = peer + [{**peer[k // 2], **peer[2 + k % 2]} for k in range(4)]

    def load(i, c):
        at = pl.ds(c * zc, zc)
        moved = pl.ds(c * zc + 1, zc)
        src, dst = [
            (p_in.at[at], p_old.at[moved]),
            (b_in.at[at], b.at[at]),
            (vel_in.at[0, at], vx_old.at[at]),
            (vel_in.at[1, at], vy_old.at[at]),
            (vel_in.at[2, at], vz.at[moved]),
            (rel_in.at[at], rel.at[at]),
            (m_in.at[at], m.at[at]),
            (str_in.at[at], stg.at[at]),
            (mod_in.at[at], mod.at[at]),
        ][i]
        return pltpu.make_async_copy(src, dst, in_sem.at[i, c])

    y_row = lambda r, k: sum(Y_ROWS[:r]) + k
    x_row = lambda r, k: sum(X_PACKS[:r]) + k

    smalls = [
        pltpu.make_async_copy(src, dst, small_sem.at[i])
        for i, (src, dst) in enumerate(
            [
                (cell_row_in, cell_row),
                (listed_in, listed),
                (phase_in, phase),
                (spectra_in, spectra_out),
            ]
        )
    ]
    for small in smalls:
        small.start()
    for c in range(chunks):
        for i in range(4):
            load(i, c).start()
    for c in range(chunks):
        for i in range(4, 9):
            load(i, c).start()
    devices = ngx * ngy
    me = gx * ngy + gy
    mine = gy * ngx + gx

    def other_device(k):
        other = lax.rem(me + k, devices)
        return {"gx": lax.div(other, ngy), "gy": lax.rem(other, ngy)}

    def flip(j):
        index = gy
        for bit in range(j.bit_length()):
            if (j >> bit) & 1:
                step = 2**bit
                index = index + step * (1 - 2 * lax.rem(lax.div(index, step), 2))
        return index

    barrier = pltpu.get_barrier_semaphore()

    peers = [{"gx": lax.rem(gx + k, ngx)} for k in range(1, ngx)]
    peers = peers + [{"gy": lax.rem(gy + k, ngy)} for k in range(1, ngy)]
    peers = peers + [
        {"gy": lax.rem(gy + ngy + dy, ngy), "gx": lax.rem(gx + ngx + dx, ngx)}
        for dy in (-1, 1)
        for dx in (-1, 1)
    ]
    for other in peers:
        pl.semaphore_signal(
            barrier, inc=1, device_id=other, device_id_type=pl.DeviceIdType.MESH
        )

    plane = jnp.zeros((ny, nx), jnp.float32)
    for field in (p_old, p):
        field[0] = plane
        field[nz + 1] = plane
        field[nz + 2] = plane
    vz[0] = plane
    vz[nz + 1] = plane
    b[nz] = plane
    for side in range(8):

        @pl.when(jnp.logical_not(has[side]))
        def _():
            for r in range(STEPS):
                if side < 2:
                    yrecv[r][side] = jnp.zeros(yrecv[r].shape[1:], jnp.float32)
                elif side < 4:
                    xrecv[r][side - 2] = jnp.zeros(xrecv[r].shape[1:], jnp.float32)
                else:
                    for c in range(chunks):
                        crecv[r][c, side - 4] = jnp.zeros((1, nx), jnp.float32)

    def ends(r, c, side, coming):
        k = side % 4
        if side < 2:
            there = side if coming else 1 - side
            src = ysend.at[side, c, pl.ds(y_row(r, 0), Y_ROWS[r])]
            dst = yrecv[r].at[there, c]
            arrives = there
        elif side < 4:
            there = k - 2 if coming else 3 - k
            src = xsend.at[c, pl.ds(x_row(r, 0), X_PACKS[r])]
            dst = xrecv[r].at[there, c]
            arrives = 2 + there
        else:
            there = k if coming else 3 - k
            src = csend.at[k // 2, r * chunks + c]
            dst = crecv[r].at[c, there]
            arrives = 4 + there
        return pltpu.make_async_remote_copy(
            src_ref=src,
            dst_ref=dst,
            send_sem=send_sem.at[side],
            recv_sem=recv_sem.at[r % 2, c, arrives],
            device_id=peer[side],
            device_id_type=pl.DeviceIdType.MESH,
        )

    def send(r, c):
        for side in range(8):

            @pl.when(has[side])
            def _():
                ends(r, c, side, False).start()

    def receive(r, c):
        for side in range(8):

            @pl.when(has[side])
            def _():
                ends(r, c, side, True).wait_recv()

    lane = lax.broadcasted_iota(jnp.int32, (ny, nx), 1)
    row = lax.broadcasted_iota(jnp.int32, (ny, nx), 0)
    quad, lane4 = (quotient(lane, 4), remainder(lane, 4))
    last_row, first_row = (row == ny - 1, row == 0)
    west_half = remainder(lax.broadcasted_iota(jnp.int32, (1, nx), 1), 4) < 2

    def pack(total, slab, zl):
        return jnp.where(quad == zl, pltpu.roll(slab, 4 * zl + 2, 1), total)

    def d_y(slab, south, north):
        after = jnp.where(last_row, north, pltpu.roll(slab, ny - 1, 0))
        before = jnp.where(first_row, south, pltpu.roll(slab, 1, 0))
        return after - before

    for c in range(chunks):
        for i in range(4):
            load(i, c).wait()

        def edges(i, totals):
            pt, vt, bt = totals
            for j in range(BATCH):
                zl = i * BATCH + j
                z = c * zc + zl
                ps, vs, ws, bs = (p_old[z + 1], vx_old[z], vy_old[z], b[z])
                pt, vt, bt = (pack(pt, ps, zl), pack(vt, vs, zl), pack(bt, bs, zl))
                at = pl.ds(zl, 1)
                ysend[0, c, y_row(0, 0), at, :] = ps[0:1]
                ysend[0, c, y_row(0, 1), at, :] = ps[1:2]
                ysend[0, c, y_row(0, 2), at, :] = ws[0:1]
                ysend[0, c, y_row(0, 3), at, :] = bs[0:1]
                ysend[1, c, y_row(0, 0), at, :] = ps[ny - 2 : ny - 1]
                ysend[1, c, y_row(0, 1), at, :] = ps[ny - 1 : ny]
                ysend[1, c, y_row(0, 2), at, :] = ws[ny - 1 : ny]
                ysend[1, c, y_row(0, 3), at, :] = bs[ny - 1 : ny]
            return pt, vt, bt

        totals = lax.fori_loop(0, zc // BATCH, edges, (plane, plane, plane))
        for i, total in enumerate(totals):
            xsend[c, x_row(0, i)] = total
        csend[0, c] = totals[0][0:1]
        csend[1, c] = totals[0][ny - 1 : ny]
        if c == 0:
            pl.semaphore_wait(barrier, len(peers))
        send(0, c)

    rup_group, slot_dev, variations = weights.shape
    lanes = weights_got.shape[3]
    group_rows = ngy * CAP
    all_rows = ngx * group_rows

    def weight_block(other):
        block = other * (variations // ngy) // lanes
        return weights.at[:, :, pl.ds(pl.multiple_of(block * lanes, lanes), lanes)]

    def far(kind, k, src, dst):
        axis, size = ("gx", ngx) if kind == 1 else ("gy", ngy)
        return pltpu.make_async_remote_copy(
            src_ref=src,
            dst_ref=dst,
            send_sem=far_sem.at[kind, 0],
            recv_sem=far_sem.at[kind, 1],
            device_id={axis: lax.rem(lax.axis_index(axis) + k, size)},
            device_id_type=pl.DeviceIdType.MESH,
        )

    def settle(ref, sem):
        pltpu.make_async_copy(ref, ref, sem).wait()

    def rows_of(ref, index, count):
        return ref.at[pl.ds(pl.multiple_of(index * count, count), count)]

    def weights_to(k):
        return far(0, k, weight_block(lax.rem(gy + k, ngy)), weights_got.at[gy])

    def first_to(k):
        src = rows_of(rows_send, lax.rem(gx + k, ngx), group_rows)
        return far(1, k, src, rows_of(rows_group, gx, group_rows))

    half = all_rows // 2

    def block_rows(owner, h):
        at = pl.multiple_of(owner * all_rows + h * half, half)
        return rows_out.at[pl.ds(at, half)]

    def carry_over(j, h, src, dst, partner):
        return pltpu.make_async_remote_copy(
            src_ref=src,
            dst_ref=dst,
            send_sem=block_sem.at[0, 1],
            recv_sem=block_sem.at[0, 0] if j % 2 else block_sem.at[j // 2, h],
            device_id={"gy": partner},
            device_id_type=pl.DeviceIdType.MESH,
        )

    def direct_to(j, h):
        return carry_over(
            j, h, rows_group.at[pl.ds(h * half, half)], block_rows(gy, h), flip(j)
        )

    def pass_on(j, h):
        block = block_rows(flip(j), h)
        return carry_over(j + 1, h, block, block, flip(1))

    def block_from(j, h):
        block = block_rows(flip(j), h)
        return carry_over(j, h, block, block, flip(1 if j % 2 else j))

    def tell(k, src, dst, i):
        where = other_device(k)
        return pltpu.make_async_remote_copy(
            src_ref=src.at[where["gx"]],
            dst_ref=dst.at[mine],
            send_sem=tell_sem.at[i],
            recv_sem=hear_sem.at[i],
            device_id=where,
            device_id_type=pl.DeviceIdType.MESH,
        )

    def tell_all(src, dst, i):
        pltpu.make_async_copy(src.at[gx], dst.at[mine], hear_sem.at[i]).start()

        def start(k, carry):
            tell(k, src, dst, i).start()
            return carry

        lax.fori_loop(1, devices, start, 0)

    own_weights = pltpu.make_async_copy(weight_block(gy), weights_got.at[gy], far_sem.at[0, 1])

    square = (per_dev, per_dev)
    eye = lax.broadcasted_iota(jnp.int32, square, 0) == lax.broadcasted_iota(jnp.int32, square, 1)

    def to_row(column):
        return jnp.sum(jnp.where(eye, column, 0.0), axis=0, keepdims=True)

    def to_column(line):
        return jnp.sum(jnp.where(eye, line, 0.0), axis=1, keepdims=True)

    def fill_placing():
        ruptures, slots = listed.shape
        shape = (per_dev, slots)
        own_ids = lax.broadcasted_iota(jnp.int32, shape, 0) + (gx * ngy + gy) * per_dev
        slot_owner = quotient(lax.broadcasted_iota(jnp.int32, shape, 1), slot_dev)

        def body(r, best):
            owner = quotient(r, rup_group) * ngy + slot_owner
            return jnp.where(listed[pl.ds(r, 1), :] == own_ids, owner, best)

        best = lax.fori_loop(0, ruptures, body, jnp.full(shape, -1, jnp.int32))
        target = jnp.max(best.astype(jnp.float32), axis=1, keepdims=True)
        before = lax.broadcasted_iota(jnp.int32, square, 1) < lax.broadcasted_iota(
            jnp.int32, square, 0
        )
        same = (to_row(target) == target) & before
        rank = jnp.sum(jnp.where(same, 1.0, 0.0), axis=1, keepdims=True)
        bucket = jnp.where(target >= 0.0, target * CAP + rank, -1.0)
        spot = lax.broadcasted_iota(jnp.int32, placed.shape, 1).astype(jnp.float32)
        placed[...] = jnp.where(spot == bucket, 1.0, 0.0)
        place = lax.broadcasted_iota(jnp.int32, placing.shape, 0).astype(jnp.float32)
        placing[...] = jnp.where(place == to_row(bucket), 1.0, 0.0)

    def fill_table():
        slot_count = listed.shape[1]
        shape = table.shape
        spot = lax.broadcasted_iota(jnp.int32, shape, 1)
        owner, place = (quotient(spot, slot_dev), remainder(spot, slot_dev))
        table[...] = jnp.full(shape, -1, jnp.int32)
        group = pl.ds(pl.multiple_of(gx * rup_group, rup_group), rup_group)
        table[:, :slot_count] = listed[group, :]
        ids = table[...]
        source = quotient(ids, per_dev)

        def earlier(i, rank):
            shift = i - (slot_dev - 1)
            inside = (place >= shift) & (place < shift + slot_dev)
            turned = pltpu.roll(ids, jnp.where(shift < 0, shift + shape[1], shift), 1)
            for k in range(rup_group):
                other = pltpu.roll(turned, k, 0) if k else turned
                found = inside & (other < ids) & (quotient(other, per_dev) == source)
                rank = jnp.where(found, 1, rank)
            return rank

        shifts = 2 * slot_dev - 1
        unroll = max(k for k in range(1, 16) if shifts % k == 0)
        rank = lax.fori_loop(0, shifts, earlier, jnp.zeros(shape, jnp.int32), unroll=unroll)
        block = remainder(source, ngy) * ngx + quotient(source, ngy)
        table[...] = jnp.where(ids >= 0, (block * ngy + owner) * CAP + rank, -1)

    def halos(r, c):
        def joined(i):
            return jnp.where(lane4 < 2, xrecv[r][0, c, i], xrecv[r][1, c, i])

        west, east, own = (xrecv[r][0, c, 0], xrecv[r][1, c, 0], xsend[c, x_row(r, 0)])
        if r == 0:

            def edge(i):
                return jnp.where(lane4 == 1, xrecv[0][0, c, i], xsend[c, x_row(0, i)])

            vh, bh = (pltpu.roll(edge(1), 1, 1), pltpu.roll(edge(2), 1, 1))
            bwh[c] = bh
            bxh[c] = joined(2)
            hx_old[c] = jnp.where(
                lane4 == 1, pltpu.roll(xrecv[0][1, c, 2], nx - 1, 1), xrecv[0][1, c, 1]
            )
            vyh[0, c] = yrecv[0][0, c, 2]
            vyh[1, c] = yrecv[0][1, c, 2]
            for side in range(2):
                hb[side, c] = yrecv[0][side, c, 3]
        else:
            vh, bh = (vxh[c], bwh[c])
            if r == 1:
                vyx[c] = joined(1)
                for side in range(2):
                    hv[side, c] = yrecv[1][side, c, 2]
        for side in range(2):
            hp[r % 2, side, c] = yrecv[r][side, c, 1 - side]
        xj[r % 2, c, 7:8, :] = jnp.where(west_half, crecv[r][c, 0], crecv[r][c, 1])
        xj[r % 2, c, 8 : 8 + ny, :] = joined(0)
        xj[r % 2, c, 8 + ny : 9 + ny, :] = jnp.where(west_half, crecv[r][c, 2], crecv[r][c, 3])
        vh = vh - bh * (own - pltpu.roll(west, 2, 1))
        vxh[c] = vh
        hx[c] = jnp.where(lane4 < 2, pltpu.roll(east, nx - 2, 1), vh)
        vyh[0, c] = vyh[0, c] - yrecv[0][0, c, 3] * (ysend[0, c, y_row(r, 0)] - yrecv[r][0, c, 0])
        vyh[1, c] = vyh[1, c] - yrecv[0][1, c, 3] * (yrecv[r][1, c, 1] - ysend[1, c, y_row(r, 1)])

    def sweep(r, c):
        last, first = (r == STEPS - 1, r == 0)
        n = r + 1

        def body(i, totals):
            totals = list(totals)
            base = i * BATCH
            z0 = c * zc + base
            p_from = p_old if first else p
            ps = [p_from[z0 + 1 + j] for j in range(BATCH + 2)]
            bs = [b[z0 + j] for j in range(BATCH + 1)]
            zs = [vz[z0], vz[z0 + 1]]
            vs, ws, new_p, outer = ([], [], [], [])
            for j in range(BATCH):
                zl = base + j
                at = pl.ds(zl, 1)
                turn = nx - 2 - 4 * zl
                zs.append(vz[z0 + j + 2] - bs[j + 1] * (ps[j + 2] - ps[j]))
                outer.append(pltpu.roll(hx[c], turn, 1))
                ahead = jnp.where(lane >= nx - 2, outer[j], pltpu.roll(ps[j], nx - 2, 1))
                if first:
                    old = pltpu.roll(hx_old[c], turn, 1)
                    shifted = jnp.where(lane == nx - 1, old, pltpu.roll(bs[j], nx - 1, 1))
                    b_east[z0 + j] = shifted
                    speed = pltpu.roll(jnp.where(lane == 0, old, vx_old[z0 + j]), nx - 1, 1)
                else:
                    shifted, speed = (b_east[z0 + j], vx[z0 + j])
                vs.append(speed - shifted * (ahead - ps[j]))
                south, north = (yrecv[r][0, c, 1, at, :], yrecv[r][1, c, 0, at, :])
                side_speed = vy_old[z0 + j] if first else vy[z0 + j]
                ws.append(side_speed - bs[j] * d_y(ps[j], south, north))
            for j in range(BATCH):
                zl = base + j
                at = pl.ds(zl, 1)
                turned = pltpu.roll(vs[j], 2, 1)
                spread = vs[j] - jnp.where(lane < 2, outer[j], turned)
                if last:
                    vs[j] = pltpu.roll(jnp.where(lane == 1, outer[j], turned), nx - 1, 1)
                spread = spread + d_y(ws[j], vyh[0, c, at, :], vyh[1, c, at, :])
                spread = spread + (zs[j + 2] - zs[j])
                mem = m[z0 + j]
                mem = mem - rel[z0 + j] * (mem + stg[z0 + j] * spread)
                m[z0 + j] = mem
                new_p.append(ps[j] - mod[z0 + j] * (spread + mem))
            for j in range(BATCH):
                zl = base + j
                at = pl.ds(zl, 1)
                vz[z0 + j + 2] = zs[j + 2]
                vx[z0 + j] = vs[j]
                vy[z0 + j] = ws[j]
                p[z0 + j + 1] = new_p[j]
                if not last:
                    totals[0] = pack(totals[0], new_p[j], zl)
                    ysend[0, c, y_row(n, 0), at, :] = new_p[j][0:1]
                    ysend[0, c, y_row(n, 1), at, :] = new_p[j][1:2]
                    ysend[1, c, y_row(n, 0), at, :] = new_p[j][ny - 2 : ny - 1]
                    ysend[1, c, y_row(n, 1), at, :] = new_p[j][ny - 1 : ny]
                if first:
                    totals[1] = pack(totals[1], vy_old[z0 + j], zl)
                    ysend[0, c, y_row(n, 2), at, :] = vx_old[z0 + j, 0:1, :]
                    ysend[1, c, y_row(n, 2), at, :] = vx_old[z0 + j, ny - 1 : ny, :]
            return tuple(totals)

        count = 0 if last else X_PACKS[n]
        totals = lax.fori_loop(0, zc // BATCH, body, (plane,) * count)
        for i, total in enumerate(totals):
            xsend[c, x_row(n, i)] = total
        if not last:
            csend[0, n * chunks + c] = totals[0][0:1]
            csend[1, n * chunks + c] = totals[0][ny - 1 : ny]

    told_lane = lax.broadcasted_iota(jnp.int32, (1, 128), 1)
    in_place = quotient(told_lane, group_rows) == remainder(mine, 128 // group_rows)
    patch_lane = lax.broadcasted_iota(jnp.int32, (per_dev, nx), 1)

    def masked(keep, values):
        return jnp.where(keep, values, 0.0)

    def flat(ref):
        return ref.reshape(math.prod(ref.shape[:-1]), ref.shape[-1])

    UP, DOWN, MID, HALO, EDGE, PACK = range(6)

    def make_index():
        cells = cell_row[...]
        z, y = (quotient(cells, ny * nx), remainder(quotient(cells, nx), ny))
        c, zl = (quotient(z, zc), remainder(z, zc))
        side = jnp.where(y == 0, 0, 1)
        rows = [
            z * ny + jnp.minimum(y + 1, ny - 1),
            z * ny + jnp.maximum(y - 1, 0),
            z * ny + y,
            (side * chunks + c) * zc + zl,
            c * (ny + 16) + y,
            c * ny + y,
        ]
        index_made[...] = jnp.zeros(index_made.shape, jnp.int32)
        for k, values in enumerate(rows):
            index_made[k : k + 1, :per_dev] = values

    def gather(*wanted):
        refs = [(slot, flat(ref), which, shift) for slot, ref, which, shift in wanted]

        def body(i, carry):
            at = {which: index[which, i] for which in sorted({w[2] for w in refs})}
            out = pl.ds(i, 1)
            for slot, ref, which, shift in refs:
                got[slot, out, :] = ref[pl.ds(at[which] + shift, 1), :]
            return carry

        lax.fori_loop(0, per_dev, body, 0, unroll=8)

    B_OWN, P_OWN, V_OWN, P_HALO, V_HALO, B_HALO, OLD_OWN, OLD_HALO = (0, 3, 5, 8, 11, 13, 15, 17)

    def own_rows(slot, ref, shift):
        return [(slot, ref, UP, shift), (slot + 1, ref, DOWN, shift)]

    def halo_rows(slot, n):
        edge = xj.at[n % 2]
        return [
            (slot, hp.at[n % 2], HALO, 0),
            (slot + 1, edge, EDGE, 9),
            (slot + 2, edge, EDGE, 7),
        ]

    def places():
        cells = to_column(cell_row[...].astype(jnp.float32)).astype(jnp.int32)
        cell_z, cell_x = (quotient(cells, ny * nx), remainder(cells, nx))
        return cell_x, remainder(quotient(cells, nx), ny), 4 * remainder(cell_z, zc)

    def along(values):
        return jnp.sum(values, axis=1, keepdims=True)

    def note(n, value):
        shear[...] = jnp.broadcast_to(value, shear.shape)
        line = jnp.sum(placed[...] * value, axis=0, keepdims=True)
        for k in range(ngx):
            begin = k * group_rows
            tile = begin - begin % 128
            piece = line[:, tile : tile + 128]
            spread = pltpu.roll(piece, remainder(mine * group_rows + (128 - begin % 128), 128), 1)
            spread = jnp.where(in_place, spread, 0.0)
            if n < STEPS:
                told[k, n - 1] = spread
            else:
                told_last[k] = spread
        spectra_out[...] = spectra_out[...] + value * phase[n - 1 : n, :]

    def marks():
        cell_x, cell_y, start = places()
        here = patch_lane == cell_x
        up, down = (cell_y < ny - 1, cell_y > 0)
        ahead, behind = (patch_lane == cell_x + 1, patch_lane == cell_x - 1)
        ahead_out = (patch_lane == start + 2) & (cell_x == nx - 1)
        behind_out = (patch_lane == start + 1) & (cell_x == 0)
        return here, up, down, ahead, behind, ahead_out, behind_out

    def first_shear():
        here, up, down, ahead, behind, ahead_out, behind_out = marks()
        total = masked(here, jnp.where(up, got[V_OWN], got[V_HALO]))
        total = total - masked(here, jnp.where(down, got[V_OWN + 1], got[V_HALO]))
        total = total + masked(ahead, got[V_OWN + 2]) - masked(behind, got[V_OWN + 2])
        total = total + masked(ahead_out, got[V_HALO + 1]) - masked(behind_out, got[V_HALO + 1])
        shear[...] = jnp.broadcast_to(along(total), shear.shape)

    def make_factors():
        here, up, down, ahead, behind, ahead_out, behind_out = marks()
        b_up = along(masked(here, jnp.where(up, got[B_OWN], got[B_HALO])))
        b_down = along(masked(here, jnp.where(down, got[B_OWN + 1], got[B_HALO])))
        b_mid, b_out = (got[B_OWN + 2], got[B_HALO + 1])
        b_ahead = along(masked(ahead, b_mid) + masked(ahead_out, b_out))
        b_behind = along(masked(behind, b_mid) + masked(behind_out, b_out))
        at_up = masked(behind, b_up + b_behind) - masked(ahead, b_up + b_ahead)
        at_down = masked(ahead, b_down + b_ahead) - masked(behind, b_down + b_behind)
        factors[0] = masked(up, at_up)
        factors[1] = masked(down, at_down)
        factors[2] = jnp.where(up, masked(jnp.logical_not(down), at_down), at_up)
        factors[3] = masked(behind_out, b_up + b_behind) - masked(ahead_out, b_up + b_ahead)
        factors[4] = masked(ahead_out, b_down + b_ahead) - masked(behind_out, b_down + b_behind)

    def next_shear(n, own=P_OWN, halo=P_HALO):
        rows = [own, own + 1, halo, halo + 1, halo + 2]
        total = factors[0] * got[rows[0]]
        for k in range(1, 5):
            total = total + factors[k] * got[rows[k]]
        note(n, shear[:, 0:1] + along(total))

    for small in smalls:
        small.wait()
    make_index()
    index_copy = pltpu.make_async_copy(index_made, index, index_sem.at[0])
    index_copy.start()
    for c in range(chunks):
        for i in range(4, 9):
            load(i, c).wait()

    def send_rows():
        fill_placing()
        rows_send[...] = jnp.dot(
            placing[...],
            spectra_out[...],
            preferred_element_type=jnp.float32,
            precision=lax.Precision.HIGHEST,
        )
        for k in range(1, ngx):
            first_to(k).start()
        at = pl.ds(pl.multiple_of(gx * group_rows, group_rows), group_rows)
        rows_group[at, :] = rows_send[at, :]

    def mix():
        slot_count = slot_dev * ngy
        lines = min(slot_count, 128)
        depth = min(mixed.shape[1], 512)
        share = mixed.shape[0] // rup_group
        begin = pl.multiple_of(lax.rem(gy * share, lanes), share)
        block = (lines, lines)
        own_line = lax.broadcasted_iota(jnp.int32, block, 0) == lax.broadcasted_iota(
            jnp.int32, block, 1
        )
        row_at = lax.broadcasted_iota(jnp.int32, (slot_count, depth), 1)
        for r in range(rup_group):
            for k in range(slot_count // lines):
                line = table[r : r + 1, k * lines : (k + 1) * lines].astype(jnp.float32)
                column = jnp.sum(jnp.where(own_line, line, 0.0), axis=1, keepdims=True)
                at = pl.ds(k * lines, lines)
                columns[r, at, :] = jnp.broadcast_to(
                    column.astype(jnp.int32), (lines, columns.shape[2])
                )

        def blend(r, k):
            base = k * depth
            chosen = jnp.where(row_at + base == columns[r, :, 0:1], 1.0, 0.0).astype(jnp.bfloat16)
            own = weights_got[:, r].astype(jnp.float32).reshape(slot_count, lanes)
            spread = lax.dot_general(
                own.astype(jnp.bfloat16),
                chosen,
                (((0,), (0,)), ((), ())),
                preferred_element_type=jnp.float32,
            )
            wide[r] = spread
            rows = pl.ds(r * share, share)
            mixed[rows, pl.ds(base, depth)] = wide[r, pl.ds(begin, share), :].astype(jnp.bfloat16)

        for r in range(rup_group):
            if mixed.shape[1] == depth:
                blend(r, 0)
            else:

                @pl.loop(0, mixed.shape[1] // depth)
                def _(k):
                    blend(r, k)

    def work_after(r):
        if r == 0:
            send_rows()
            index_copy.wait()
            gather(
                *own_rows(B_OWN, b, 0),
                (B_OWN + 2, b, MID, 0),
                *own_rows(V_OWN, vx_old, 0),
                (V_OWN + 2, vy_old, MID, 0),
                (B_HALO, hb, HALO, 0),
                (B_HALO + 1, bxh, PACK, 0),
                *own_rows(OLD_OWN, p_old, ny),
                *halo_rows(OLD_HALO, 0),
                *own_rows(P_OWN, p, ny),
            )
            make_factors()
        elif r == 1:
            gather(*halo_rows(P_HALO, 1), (V_HALO, hv, HALO, 0), (V_HALO + 1, vyx, PACK, 0))
            first_shear()
            next_shear(1, OLD_OWN, OLD_HALO)
            next_shear(2)
            gather(*own_rows(P_OWN, p, ny))
        elif r < STEPS - 1:
            gather(*halo_rows(P_HALO, r))
            next_shear(r + 1)
            gather(*own_rows(P_OWN, p, ny))

    def last_shear():
        gather(*halo_rows(P_HALO, STEPS - 1))
        next_shear(STEPS)
        tell_all(told_last, heard_last, 1)

    gaps = [(r, c) for r in range(STEPS - 1) for c in range(chunks)][chunks:]
    jobs = {gap: [] for gap in gaps + [(STEPS - 1, 0), None]}
    order = list(jobs)
    pieces = [(j, h) for j in range(2, ngy, 2) for h in range(2)]

    def enter_rows():
        settle(rows_group.at[pl.ds(0, (ngx - 1) * group_rows)], far_sem.at[1, 1])
        at = pl.ds(pl.multiple_of(gy * all_rows, all_rows), all_rows)
        rows_out[at, :] = rows_group[...]
        for h in range(2):
            direct_to(1, h).start()
        own_weights.start()

    def leave(j, h):
        direct_to(j, h).start()

    def forward(j, h):
        block_from(j, h).wait_recv()
        pass_on(j, h).start()

    jobs[order[0]].append(enter_rows)
    jobs[STEPS - 1, 0].append(lambda: tell_all(told, heard, 0))
    for i, (j, h) in enumerate(pieces):
        place = i * len(gaps) // len(pieces)
        jobs[order[place]].append(functools.partial(leave, j, h))
        after = order[min(place + 2, len(order) - 1)]
        jobs[after].append(functools.partial(forward, j, h))
    for k in range(1, ngy):
        place = (k - 1) * len(gaps) // (ngy - 1)
        jobs[order[place]].append(lambda k=k: weights_to(k).start())

    for r in range(STEPS):
        above = p_old if r == 0 else p
        vz[1] = vz[1] - b[0] * (above[2] - above[0])
        for c in range(chunks):
            receive(r, c)
            halos(r, c)
            if r == STEPS - 1 and c == chunks - 1:
                last_shear()
            sweep(r, c)
            if r < STEPS - 1:
                send(r + 1, c)
            for job in jobs.get((r, c), []):
                job()
        work_after(r)
    for job in jobs[None]:
        job()
    fill_table()
    for side in range(8):

        @pl.when(has[side])
        def _():
            sent = ysend.at[side] if side < 2 else xsend if side < 4 else csend.at[side // 2 - 2]
            settle(sent, send_sem.at[side])

    settle(weights_got.at[pl.ds(0, ngy - 1)], far_sem.at[0, 0])
    settle(weights_got, far_sem.at[0, 1])
    mix()
    settle(rows_group.at[pl.ds(0, (ngx - 1) * group_rows)], far_sem.at[1, 0])
    settle(rows_out.at[pl.ds(0, (ngy - 1) * all_rows)], block_sem.at[0, 1])
    settle(rows_out.at[pl.ds(0, ngy // 2 * all_rows)], block_sem.at[0, 0])
    for i, ref in enumerate([heard, heard_last]):
        settle(ref.at[pl.ds(1, devices - 1)], tell_sem.at[i])
        settle(ref, hear_sem.at[i])


def finish_kernel(nz, *refs):
    refs = list(refs)
    take = lambda count: [refs.pop(0) for _ in range(count)]
    vx, vy, vz, p, m, spectra, mixed, rows, heard, heard_last, phase = take(11)
    vel_out, p_out, m_out, spectra_out, slip_out = take(5)
    slip, exact, lines_in, out_sem, slip_sem = take(5)
    inner = pl.ds(1, nz)
    pairs = [
        (vx, vel_out.at[0]),
        (vy, vel_out.at[1]),
        (vz.at[inner], vel_out.at[2]),
        (p.at[inner], p_out),
        (m, m_out),
        (spectra, spectra_out),
    ]
    stores = [
        pltpu.make_async_copy(src, dst, out_sem.at[i]) for i, (src, dst) in enumerate(pairs)
    ]
    for store in stores:
        store.start()

    count = heard.shape[0]
    per_tile = count * 128 // rows.shape[0]
    lines_in[...] = jnp.zeros(lines_in.shape, jnp.float32)
    for t in range(count // per_tile):
        at, of = (pl.ds(t * 128, 128), pl.ds(t * per_tile, per_tile))
        for n in range(STEPS):
            told = heard[of, n] if n < STEPS - 1 else heard_last[of]
            lines_in[n : n + 1, at] = jnp.sum(told, axis=0)
    for t in range(count // per_tile):
        at = pl.ds(t * 128, 128)
        change = lax.dot_general(
            lines_in[:, at],
            phase[...],
            (((0,), (0,)), ((), ())),
            preferred_element_type=jnp.float32,
            precision=lax.Precision.HIGHEST,
        )
        exact[at, :] = (rows[at, :] + change).astype(jnp.bfloat16)
    rup_group, share = slip.shape[:2]
    response = jnp.dot(mixed[...], exact[...], preferred_element_type=jnp.float32)
    slip[...] = response.reshape(slip.shape)
    answer = pltpu.make_async_copy(slip, slip_out, slip_sem.at[0])
    answer.start()
    for store in stores:
        store.wait()
    answer.wait()


VMEM_LIMIT = 40 * 1024 * 1024


def in_hbm(x):
    return pltpu.with_memory_space_constraint(x, pltpu.HBM)


def advance(
    velocity, pressure, memory, buoyancy, modulus, relax, strength, spectra, patch_cell, listed, weights
):
    nz, ny, nx = pressure.shape
    per_dev, width = spectra.shape
    zc = nx // 4
    chunks = nz // zc
    ngx, ngy = (lax.axis_size("gx"), lax.axis_size("gy"))
    dims = (nz, ny, nx, chunks, zc, per_dev, ngx, ngy)
    rup_group, slot_dev, variations = weights.shape
    lanes = max(variations // ngy, 128)
    all_rows = ngx * ngy * CAP
    f32 = jnp.float32
    field = lambda planes: pltpu.VMEM((planes, ny, nx), f32)
    rounds = range(STEPS)
    any_spec = pl.BlockSpec(memory_space=pl.ANY)
    vmem_spec = pl.BlockSpec(memory_space=pltpu.VMEM)
    return pl.pallas_call(
        functools.partial(step_kernel, dims),
        out_shape=[
            field(nz),
            field(nz),
            field(nz + 2),
            field(nz + 3),
            field(nz),
            pltpu.VMEM(spectra.shape, f32),
            pltpu.VMEM((rup_group * (variations // ngy), ngy * all_rows), jnp.bfloat16),
            pltpu.VMEM((ngy * all_rows, width), f32),
            pltpu.VMEM((ngx * ngy, STEPS - 1, 1, 128), f32),
            pltpu.VMEM((ngx * ngy, 1, 128), f32),
            pltpu.VMEM((8, width), f32),
        ],
        in_specs=[any_spec] * 12,
        out_specs=[vmem_spec] * 11,
        scratch_shapes=[field(nz + 1), field(nz), field(nz), field(nz)]
        + [field(nz), field(nz), field(nz + 3), field(nz)]
        + [
            pltpu.VMEM((2, chunks, sum(Y_ROWS), zc, nx), f32),
            pltpu.VMEM((chunks, sum(X_PACKS), ny, nx), f32),
            pltpu.VMEM((2, STEPS * chunks, 1, nx), f32),
        ]
        + [pltpu.VMEM((2, chunks, Y_ROWS[r], zc, nx), f32) for r in rounds]
        + [pltpu.VMEM((2, chunks, X_PACKS[r], ny, nx), f32) for r in rounds]
        + [pltpu.VMEM((chunks, 4, 1, nx), f32) for r in rounds]
        + [
            pltpu.VMEM((1, per_dev), jnp.int32),
            pltpu.VMEM(listed.shape, jnp.int32),
            pltpu.VMEM((8, max(per_dev, 128)), jnp.int32),
            pltpu.SMEM((8, max(per_dev, 128)), jnp.int32),
            pltpu.VMEM((chunks, ny, nx), f32),
            pltpu.VMEM((chunks, ny, nx), f32),
            pltpu.VMEM((chunks, ny, nx), f32),
            pltpu.VMEM((chunks, ny, nx), f32),
            pltpu.VMEM((chunks, ny, nx), f32),
            pltpu.VMEM((2, chunks, zc, nx), f32),
            pltpu.VMEM((chunks, ny, nx), f32),
            pltpu.VMEM((2, chunks, ny + 16, nx), f32),
            pltpu.VMEM((20, per_dev, nx), f32),
            pltpu.VMEM((per_dev, nx), f32),
            pltpu.VMEM((5, per_dev, nx), f32),
            pltpu.VMEM((2, 2, chunks, zc, nx), f32),
            pltpu.VMEM((2, chunks, zc, nx), f32),
            pltpu.VMEM((2, chunks, zc, nx), f32),
            pltpu.VMEM((ngy, rup_group, slot_dev, lanes), jnp.bfloat16),
            pltpu.VMEM((rup_group, max(listed.shape[1], 128)), jnp.int32),
            pltpu.VMEM((rup_group, listed.shape[1], 128), jnp.int32),
            pltpu.VMEM((rup_group, lanes, min(ngy * all_rows, 512)), f32),
            pltpu.VMEM((all_rows, per_dev), f32),
            pltpu.VMEM((per_dev, max(all_rows, 128)), f32),
            pltpu.VMEM((all_rows, width), f32),
            pltpu.VMEM((all_rows, width), f32),
            pltpu.VMEM((ngx, STEPS - 1, 1, 128), f32),
            pltpu.VMEM((ngx, 1, 128), f32),
            pltpu.SemaphoreType.DMA((9, chunks)),
            pltpu.SemaphoreType.DMA((4,)),
            pltpu.SemaphoreType.DMA((8,)),
            pltpu.SemaphoreType.DMA((2, chunks, 8)),
            pltpu.SemaphoreType.DMA((2, 2)),
            pltpu.SemaphoreType.DMA((ngy // 2, 2)),
            pltpu.SemaphoreType.DMA((2,)),
            pltpu.SemaphoreType.DMA((2,)),
            pltpu.SemaphoreType.DMA((1,)),
        ],
        compiler_params=pltpu.CompilerParams(
            collective_id=0, has_side_effects=True, vmem_limit_bytes=VMEM_LIMIT
        ),
    )(
        *[in_hbm(x) for x in (velocity, pressure, memory, buoyancy, modulus, relax, strength)],
        in_hbm(spectra),
        in_hbm(patch_cell.reshape(1, -1)),
        in_hbm(phase_rows(width // 2)),
        in_hbm(listed),
        in_hbm(weights),
    )


def finish(state, velocity, pressure, memory, spectra, weights):
    nz = pressure.shape[0]
    width = spectra.shape[1]
    ngy = lax.axis_size("gy")
    rup_group, slot_dev, variations = weights.shape
    share = variations // ngy
    f32 = jnp.float32
    any_spec = pl.BlockSpec(memory_space=pl.ANY)
    vmem_spec = pl.BlockSpec(memory_space=pltpu.VMEM)
    return pl.pallas_call(
        functools.partial(finish_kernel, nz),
        out_shape=[
            jax.ShapeDtypeStruct(velocity.shape, f32),
            jax.ShapeDtypeStruct(pressure.shape, f32),
            jax.ShapeDtypeStruct(memory.shape, f32),
            jax.ShapeDtypeStruct(spectra.shape, f32),
            jax.ShapeDtypeStruct((rup_group, share, width), f32),
        ],
        in_specs=[vmem_spec] * len(state),
        out_specs=[any_spec] * 5,
        scratch_shapes=[
            pltpu.VMEM((rup_group, share, width), f32),
            pltpu.VMEM(state[7].shape, jnp.bfloat16),
            pltpu.VMEM((8, state[7].shape[0]), f32),
            pltpu.SemaphoreType.DMA((6,)),
            pltpu.SemaphoreType.DMA((1,)),
        ],
        compiler_params=pltpu.CompilerParams(vmem_limit_bytes=VMEM_LIMIT),
    )(*[pltpu.with_memory_space_constraint(x, pltpu.VMEM) for x in state])


def per_device(
    velocity,
    pressure,
    memory,
    buoyancy,
    modulus,
    relax,
    strength,
    spectra,
    patch_cell,
    rupture_patches,
    slip_weights,
):
    state = advance(
        velocity,
        pressure,
        memory,
        buoyancy,
        modulus,
        relax,
        strength,
        spectra,
        patch_cell,
        rupture_patches,
        slip_weights,
    )
    return tuple(finish(state, velocity, pressure, memory, spectra, slip_weights))


def solution(mesh):
    in_specs = (
        P(None, None, "gy", "gx"),
        P(None, "gy", "gx"),
        P(None, "gy", "gx"),
        P(None, "gy", "gx"),
        P(None, "gy", "gx"),
        P(None, "gy", "gx"),
        P(None, "gy", "gx"),
        P(("gx", "gy"), None),
        P(("gx", "gy")),
        P(),
        P("gx", "gy", None),
    )
    out_specs = (
        P(None, None, "gy", "gx"),
        P(None, "gy", "gx"),
        P(None, "gy", "gx"),
        P(("gx", "gy"), None),
        P("gx", "gy", None),
    )
    return jax.shard_map(
        per_device, mesh=mesh, in_specs=in_specs, out_specs=out_specs, check_vma=False
    )
```

```python
import functools
import math

import jax
import jax.numpy as jnp
import numpy as np
from jax import lax
from jax.experimental import pallas as pl
from jax.experimental.pallas import tpu as pltpu
from jax.sharding import PartitionSpec as P

STEPS = 4
CAP = 2
BATCH = 8


def phase_rows(freqs):
    angle = np.pi * (np.arange(freqs) + 0.5) / freqs
    rows = [np.concatenate([np.cos(angle * n), -np.sin(angle * n)]) for n in range(1, STEPS + 1)]
    rows = rows + [np.zeros(2 * freqs)] * (8 - STEPS)
    return jnp.asarray(np.stack(rows).astype(np.float32))


Y_ROWS = [4, 3] + [2] * (STEPS - 2)
X_PACKS = [3, 2] + [1] * (STEPS - 2)


def quotient(value, size):
    if size & (size - 1):
        return lax.div(value, jnp.full_like(value, size))
    return lax.shift_right_logical(value, jnp.full_like(value, size.bit_length() - 1))


def remainder(value, size):
    if size & (size - 1):
        return lax.rem(value, jnp.full_like(value, size))
    return value & (size - 1)


def step_kernel(dims, *refs):
    nz, ny, nx, chunks, zc, per_dev, ngx, ngy = dims
    refs = list(refs)
    take = lambda count: [refs.pop(0) for _ in range(count)]
    vel_in, p_in, m_in, b_in, mod_in, rel_in, str_in = take(7)
    spectra_in, cell_row_in, phase_in, listed_in, weights = take(5)
    vx, vy, vz, p, m, spectra_out, mixed, rows_out, heard, phase = take(10)
    b, mod, rel, stg, vx_old, vy_old, p_old, b_east = take(8)
    ysend, xsend, csend = take(3)
    yrecv, xrecv, crecv = (take(STEPS), take(STEPS), take(STEPS))
    cell_row, listed, index_made, index = take(4)
    vxh, bwh, bxh, hx, hx_old, vyh, vyx, xj, got, shear, factors = take(11)
    hp, hv, hb, weights_got, table, columns, wide = take(7)
    placing, placed, rows_send, rows_group, told = take(5)
    in_sem, small_sem, send_sem, recv_sem, far_sem, block_sem, tell_sem, hear_sem, index_sem = take(9)

    gx, gy = (lax.axis_index("gx"), lax.axis_index("gy"))
    has = [gy > 0, gy < ngy - 1, gx > 0, gx < ngx - 1]
    has = has + [has[k // 2] & has[2 + k % 2] for k in range(4)]
    peer = [{"gy": gy - 1}, {"gy": gy + 1}, {"gx": gx - 1}, {"gx": gx + 1}]
    peer = peer + [{**peer[k // 2], **peer[2 + k % 2]} for k in range(4)]

    def load(i, c):
        at = pl.ds(c * zc, zc)
        moved = pl.ds(c * zc + 1, zc)
        src, dst = [
            (p_in.at[at], p_old.at[moved]),
            (b_in.at[at], b.at[at]),
            (vel_in.at[0, at], vx_old.at[at]),
            (vel_in.at[1, at], vy_old.at[at]),
            (vel_in.at[2, at], vz.at[moved]),
            (rel_in.at[at], rel.at[at]),
            (m_in.at[at], m.at[at]),
            (str_in.at[at], stg.at[at]),
            (mod_in.at[at], mod.at[at]),
        ][i]
        return pltpu.make_async_copy(src, dst, in_sem.at[i, c])

    y_row = lambda r, k: sum(Y_ROWS[:r]) + k
    x_row = lambda r, k: sum(X_PACKS[:r]) + k

    smalls = [
        pltpu.make_async_copy(src, dst, small_sem.at[i])
        for i, (src, dst) in enumerate(
            [
                (cell_row_in, cell_row),
                (listed_in, listed),
                (phase_in, phase),
                (spectra_in, spectra_out),
            ]
        )
    ]
    for small in smalls:
        small.start()
    for c in range(chunks):
        for i in range(4):
            load(i, c).start()
    for c in range(chunks):
        for i in range(4, 9):
            load(i, c).start()
    devices = ngx * ngy
    me = gx * ngy + gy
    mine = gy * ngx + gx

    def other_device(k):
        other = lax.rem(me + k, devices)
        return {"gx": lax.div(other, ngy), "gy": lax.rem(other, ngy)}

    def flip(j):
        index = gy
        for bit in range(j.bit_length()):
            if (j >> bit) & 1:
                step = 2**bit
                index = index + step * (1 - 2 * lax.rem(lax.div(index, step), 2))
        return index

    barrier = pltpu.get_barrier_semaphore()

    peers = [{"gx": lax.rem(gx + k, ngx)} for k in range(1, ngx)]
    peers = peers + [{"gy": lax.rem(gy + k, ngy)} for k in range(1, ngy)]
    peers = peers + [
        {"gy": lax.rem(gy + ngy + dy, ngy), "gx": lax.rem(gx + ngx + dx, ngx)}
        for dy in (-1, 1)
        for dx in (-1, 1)
    ]
    for other in peers:
        pl.semaphore_signal(
            barrier, inc=1, device_id=other, device_id_type=pl.DeviceIdType.MESH
        )

    plane = jnp.zeros((ny, nx), jnp.float32)
    for field in (p_old, p):
        field[0] = plane
        field[nz + 1] = plane
        field[nz + 2] = plane
    vz[0] = plane
    vz[nz + 1] = plane
    b[nz] = plane
    for side in range(8):

        @pl.when(jnp.logical_not(has[side]))
        def _():
            for r in range(STEPS):
                if side < 2:
                    yrecv[r][side] = jnp.zeros(yrecv[r].shape[1:], jnp.float32)
                elif side < 4:
                    xrecv[r][side - 2] = jnp.zeros(xrecv[r].shape[1:], jnp.float32)
                else:
                    for c in range(chunks):
                        crecv[r][c, side - 4] = jnp.zeros((1, nx), jnp.float32)

    def ends(r, c, side, coming):
        k = side % 4
        if side < 2:
            there = side if coming else 1 - side
            src = ysend.at[side, c, pl.ds(y_row(r, 0), Y_ROWS[r])]
            dst = yrecv[r].at[there, c]
            arrives = there
        elif side < 4:
            there = k - 2 if coming else 3 - k
            src = xsend.at[c, pl.ds(x_row(r, 0), X_PACKS[r])]
            dst = xrecv[r].at[there, c]
            arrives = 2 + there
        else:
            there = k if coming else 3 - k
            src = csend.at[k // 2, r * chunks + c]
            dst = crecv[r].at[c, there]
            arrives = 4 + there
        return pltpu.make_async_remote_copy(
            src_ref=src,
            dst_ref=dst,
            send_sem=send_sem.at[side],
            recv_sem=recv_sem.at[r % 2, c, arrives],
            device_id=peer[side],
            device_id_type=pl.DeviceIdType.MESH,
        )

    def send(r, c):
        for side in range(8):

            @pl.when(has[side])
            def _():
                ends(r, c, side, False).start()

    def receive(r, c):
        for side in range(8):

            @pl.when(has[side])
            def _():
                ends(r, c, side, True).wait_recv()

    lane = lax.broadcasted_iota(jnp.int32, (ny, nx), 1)
    row = lax.broadcasted_iota(jnp.int32, (ny, nx), 0)
    quad, lane4 = (quotient(lane, 4), remainder(lane, 4))
    last_row, first_row = (row == ny - 1, row == 0)
    west_half = remainder(lax.broadcasted_iota(jnp.int32, (1, nx), 1), 4) < 2

    def pack(total, slab, zl):
        return jnp.where(quad == zl, pltpu.roll(slab, 4 * zl + 2, 1), total)

    def d_y(slab, south, north):
        after = jnp.where(last_row, north, pltpu.roll(slab, ny - 1, 0))
        before = jnp.where(first_row, south, pltpu.roll(slab, 1, 0))
        return after - before

    for c in range(chunks):
        for i in range(4):
            load(i, c).wait()

        def edges(i, totals):
            pt, vt, bt = totals
            for j in range(8):
                zl = i * 8 + j
                z = c * zc + zl
                ps, vs, ws, bs = (p_old[z + 1], vx_old[z], vy_old[z], b[z])
                pt, vt, bt = (pack(pt, ps, zl), pack(vt, vs, zl), pack(bt, bs, zl))
                at = pl.ds(zl, 1)
                ysend[0, c, y_row(0, 0), at, :] = ps[0:1]
                ysend[0, c, y_row(0, 1), at, :] = ps[1:2]
                ysend[0, c, y_row(0, 2), at, :] = ws[0:1]
                ysend[0, c, y_row(0, 3), at, :] = bs[0:1]
                ysend[1, c, y_row(0, 0), at, :] = ps[ny - 2 : ny - 1]
                ysend[1, c, y_row(0, 1), at, :] = ps[ny - 1 : ny]
                ysend[1, c, y_row(0, 2), at, :] = ws[ny - 1 : ny]
                ysend[1, c, y_row(0, 3), at, :] = bs[ny - 1 : ny]
            return pt, vt, bt

        totals = lax.fori_loop(0, zc // 8, edges, (plane, plane, plane))
        for i, total in enumerate(totals):
            xsend[c, x_row(0, i)] = total
        csend[0, c] = totals[0][0:1]
        csend[1, c] = totals[0][ny - 1 : ny]
        if c == 0:
            pl.semaphore_wait(barrier, len(peers))
        send(0, c)

    rup_group, slot_dev, variations = weights.shape
    lanes = weights_got.shape[3]
    group_rows = ngy * CAP
    all_rows = ngx * group_rows

    def weight_block(other):
        block = other * (variations // ngy) // lanes
        return weights.at[:, :, pl.ds(pl.multiple_of(block * lanes, lanes), lanes)]

    def far(kind, k, src, dst):
        axis, size = ("gx", ngx) if kind == 1 else ("gy", ngy)
        return pltpu.make_async_remote_copy(
            src_ref=src,
            dst_ref=dst,
            send_sem=far_sem.at[kind, 0],
            recv_sem=far_sem.at[kind, 1],
            device_id={axis: lax.rem(lax.axis_index(axis) + k, size)},
            device_id_type=pl.DeviceIdType.MESH,
        )

    def settle(ref, sem):
        pltpu.make_async_copy(ref, ref, sem).wait()

    def rows_of(ref, index, count):
        return ref.at[pl.ds(pl.multiple_of(index * count, count), count)]

    def weights_to(k):
        return far(0, k, weight_block(lax.rem(gy + k, ngy)), weights_got.at[gy])

    def first_to(k):
        src = rows_of(rows_send, lax.rem(gx + k, ngx), group_rows)
        return far(1, k, src, rows_of(rows_group, gx, group_rows))

    half = all_rows // 2

    def block_rows(owner, h):
        at = pl.multiple_of(owner * all_rows + h * half, half)
        return rows_out.at[pl.ds(at, half)]

    def carry_over(j, h, src, dst, partner):
        return pltpu.make_async_remote_copy(
            src_ref=src,
            dst_ref=dst,
            send_sem=block_sem.at[0, 1],
            recv_sem=block_sem.at[0, 0] if j % 2 else block_sem.at[j // 2, h],
            device_id={"gy": partner},
            device_id_type=pl.DeviceIdType.MESH,
        )

    def direct_to(j, h):
        return carry_over(
            j, h, rows_group.at[pl.ds(h * half, half)], block_rows(gy, h), flip(j)
        )

    def pass_on(j, h):
        block = block_rows(flip(j), h)
        return carry_over(j + 1, h, block, block, flip(1))

    def block_from(j, h):
        block = block_rows(flip(j), h)
        return carry_over(j, h, block, block, flip(1 if j % 2 else j))

    def tell(k):
        where = other_device(k)
        return pltpu.make_async_remote_copy(
            src_ref=told.at[where["gx"]],
            dst_ref=heard.at[mine],
            send_sem=tell_sem.at[0],
            recv_sem=hear_sem.at[0],
            device_id=where,
            device_id_type=pl.DeviceIdType.MESH,
        )

    def tell_all():
        pltpu.make_async_copy(told.at[gx], heard.at[mine], hear_sem.at[0]).start()

        def start(k, carry):
            tell(k).start()
            return carry

        lax.fori_loop(1, devices, start, 0)

    own_weights = pltpu.make_async_copy(weight_block(gy), weights_got.at[gy], far_sem.at[0, 1])

    square = (per_dev, per_dev)
    eye = lax.broadcasted_iota(jnp.int32, square, 0) == lax.broadcasted_iota(jnp.int32, square, 1)

    def to_row(column):
        return jnp.sum(jnp.where(eye, column, 0.0), axis=0, keepdims=True)

    def to_column(line):
        return jnp.sum(jnp.where(eye, line, 0.0), axis=1, keepdims=True)

    def fill_placing():
        ruptures, slots = listed.shape
        shape = (per_dev, slots)
        own_ids = lax.broadcasted_iota(jnp.int32, shape, 0) + (gx * ngy + gy) * per_dev
        slot_owner = quotient(lax.broadcasted_iota(jnp.int32, shape, 1), slot_dev)

        def body(r, best):
            owner = quotient(r, rup_group) * ngy + slot_owner
            return jnp.where(listed[pl.ds(r, 1), :] == own_ids, owner, best)

        best = lax.fori_loop(0, ruptures, body, jnp.full(shape, -1, jnp.int32))
        target = jnp.max(best.astype(jnp.float32), axis=1, keepdims=True)
        before = lax.broadcasted_iota(jnp.int32, square, 1) < lax.broadcasted_iota(
            jnp.int32, square, 0
        )
        same = (to_row(target) == target) & before
        rank = jnp.sum(jnp.where(same, 1.0, 0.0), axis=1, keepdims=True)
        bucket = jnp.where(target >= 0.0, target * CAP + rank, -1.0)
        spot = lax.broadcasted_iota(jnp.int32, placed.shape, 1).astype(jnp.float32)
        placed[...] = jnp.where(spot == bucket, 1.0, 0.0)
        place = lax.broadcasted_iota(jnp.int32, placing.shape, 0).astype(jnp.float32)
        placing[...] = jnp.where(place == to_row(bucket), 1.0, 0.0)

    def fill_table():
        slot_count = listed.shape[1]
        shape = table.shape
        spot = lax.broadcasted_iota(jnp.int32, shape, 1)
        owner, place = (quotient(spot, slot_dev), remainder(spot, slot_dev))
        table[...] = jnp.full(shape, -1, jnp.int32)
        group = pl.ds(pl.multiple_of(gx * rup_group, rup_group), rup_group)
        table[:, :slot_count] = listed[group, :]
        ids = table[...]
        source = quotient(ids, per_dev)

        def earlier(i, rank):
            shift = i - (slot_dev - 1)
            inside = (place >= shift) & (place < shift + slot_dev)
            turned = pltpu.roll(ids, jnp.where(shift < 0, shift + shape[1], shift), 1)
            for k in range(rup_group):
                other = pltpu.roll(turned, k, 0) if k else turned
                found = inside & (other < ids) & (quotient(other, per_dev) == source)
                rank = jnp.where(found, 1, rank)
            return rank

        shifts = 2 * slot_dev - 1
        unroll = max(k for k in range(1, 16) if shifts % k == 0)
        rank = lax.fori_loop(0, shifts, earlier, jnp.zeros(shape, jnp.int32), unroll=unroll)
        block = remainder(source, ngy) * ngx + quotient(source, ngy)
        table[...] = jnp.where(ids >= 0, (block * ngy + owner) * CAP + rank, -1)

    def halos(r, c):
        def joined(i):
            return jnp.where(lane4 < 2, xrecv[r][0, c, i], xrecv[r][1, c, i])

        west, east, own = (xrecv[r][0, c, 0], xrecv[r][1, c, 0], xsend[c, x_row(r, 0)])
        if r == 0:

            def edge(i):
                return jnp.where(lane4 == 1, xrecv[0][0, c, i], xsend[c, x_row(0, i)])

            vh, bh = (pltpu.roll(edge(1), 1, 1), pltpu.roll(edge(2), 1, 1))
            bwh[c] = bh
            bxh[c] = joined(2)
            hx_old[0, c] = pltpu.roll(xrecv[0][1, c, 2], nx - 1, 1)
            hx_old[1, c] = pltpu.roll(xrecv[0][1, c, 1], nx - 1, 1)
            vyh[0, c] = yrecv[0][0, c, 2]
            vyh[1, c] = yrecv[0][1, c, 2]
            for side in range(2):
                hb[side, c] = yrecv[0][side, c, 3]
        else:
            vh, bh = (vxh[c], bwh[c])
            if r == 1:
                vyx[c] = joined(1)
                for side in range(2):
                    hv[side, c] = yrecv[1][side, c, 2]
        for side in range(2):
            hp[r % 2, side, c] = yrecv[r][side, c, 1 - side]
        xj[r % 2, c, 7:8, :] = jnp.where(west_half, crecv[r][c, 0], crecv[r][c, 1])
        xj[r % 2, c, 8 : 8 + ny, :] = joined(0)
        xj[r % 2, c, 8 + ny : 9 + ny, :] = jnp.where(west_half, crecv[r][c, 2], crecv[r][c, 3])
        vh = vh - bh * (own - pltpu.roll(west, 2, 1))
        vxh[c] = vh
        hx[c] = jnp.where(lane4 < 2, pltpu.roll(east, nx - 2, 1), vh)
        vyh[0, c] = vyh[0, c] - yrecv[0][0, c, 3] * (ysend[0, c, y_row(r, 0)] - yrecv[r][0, c, 0])
        vyh[1, c] = vyh[1, c] - yrecv[0][1, c, 3] * (yrecv[r][1, c, 1] - ysend[1, c, y_row(r, 1)])

    def sweep(r, c):
        last, first = (r == STEPS - 1, r == 0)
        n = r + 1
        p_from, w_from = (p_old, vy_old) if first else (p, vy)

        def body(i, total):
            base = i * BATCH
            z0 = c * zc + base
            ps = [p_from[z0 + 1 + j] for j in range(BATCH + 2)]
            bs = [b[z0 + j] for j in range(BATCH + 1)]
            zs = [vz[z0], vz[z0 + 1]]
            vs, ws, new_p, outer = ([], [], [], [])
            for j in range(BATCH):
                zl = base + j
                at = pl.ds(zl, 1)
                turn = nx - 2 - 4 * zl
                zs.append(vz[z0 + j + 2] - bs[j + 1] * (ps[j + 2] - ps[j]))
                outer.append(pltpu.roll(hx[c], turn, 1))
                ahead = jnp.where(lane >= nx - 2, outer[j], pltpu.roll(ps[j], nx - 2, 1))
                shifted, speed = (b_east[z0 + j], vx[z0 + j])
                if first:
                    edges_in = [pltpu.roll(hx_old[k, c], turn, 1) for k in range(2)]
                    shifted = jnp.where(lane == nx - 1, edges_in[0], shifted)
                    b_east[z0 + j] = shifted
                    speed = jnp.where(lane == nx - 1, edges_in[1], speed)
                vs.append(speed - shifted * (ahead - ps[j]))
                south, north = (yrecv[r][0, c, 1, at, :], yrecv[r][1, c, 0, at, :])
                ws.append(w_from[z0 + j] - bs[j] * d_y(ps[j], south, north))
            for j in range(BATCH):
                zl = base + j
                at = pl.ds(zl, 1)
                turned = pltpu.roll(vs[j], 2, 1)
                spread = vs[j] - jnp.where(lane < 2, outer[j], turned)
                if last:
                    vs[j] = pltpu.roll(jnp.where(lane == 1, outer[j], turned), nx - 1, 1)
                spread = spread + d_y(ws[j], vyh[0, c, at, :], vyh[1, c, at, :])
                spread = spread + (zs[j + 2] - zs[j])
                mem = m[z0 + j]
                mem = mem - rel[z0 + j] * (mem + stg[z0 + j] * spread)
                m[z0 + j] = mem
                new_p.append(ps[j] - mod[z0 + j] * (spread + mem))
            for j in range(BATCH):
                zl = base + j
                at = pl.ds(zl, 1)
                vz[z0 + j + 2] = zs[j + 2]
                vx[z0 + j] = vs[j]
                vy[z0 + j] = ws[j]
                p[z0 + j + 1] = new_p[j]
                if not last:
                    total = pack(total, new_p[j], zl)
                    ysend[0, c, y_row(n, 0), at, :] = new_p[j][0:1]
                    ysend[0, c, y_row(n, 1), at, :] = new_p[j][1:2]
                    ysend[1, c, y_row(n, 0), at, :] = new_p[j][ny - 2 : ny - 1]
                    ysend[1, c, y_row(n, 1), at, :] = new_p[j][ny - 1 : ny]
            return total

        total = lax.fori_loop(0, zc // BATCH, body, plane)
        if not last:
            xsend[c, x_row(n, 0)] = total
            csend[0, n * chunks + c] = total[0:1]
            csend[1, n * chunks + c] = total[ny - 1 : ny]

    def shift(c):
        def body(i, total):
            for j in range(8):
                zl = i * 8 + j
                z = c * zc + zl
                at = pl.ds(zl, 1)
                old = vx_old[z]
                vx[z] = pltpu.roll(old, nx - 1, 1)
                b_east[z] = pltpu.roll(b[z], nx - 1, 1)
                total = pack(total, vy_old[z], zl)
                ysend[0, c, y_row(1, 2), at, :] = old[0:1]
                ysend[1, c, y_row(1, 2), at, :] = old[ny - 1 : ny]
            return total

        xsend[c, x_row(1, 1)] = lax.fori_loop(0, zc // 8, body, plane)

    told_lane = lax.broadcasted_iota(jnp.int32, (1, 128), 1)
    in_place = quotient(told_lane, group_rows) == remainder(mine, 128 // group_rows)
    patch_lane = lax.broadcasted_iota(jnp.int32, (per_dev, nx), 1)

    def masked(keep, values):
        return jnp.where(keep, values, 0.0)

    def flat(ref):
        return ref.reshape(math.prod(ref.shape[:-1]), ref.shape[-1])

    UP, DOWN, MID, HALO, EDGE, PACK = range(6)

    def make_index():
        cells = cell_row[...]
        z, y = (quotient(cells, ny * nx), remainder(quotient(cells, nx), ny))
        c, zl = (quotient(z, zc), remainder(z, zc))
        side = jnp.where(y == 0, 0, 1)
        rows = [
            z * ny + jnp.minimum(y + 1, ny - 1),
            z * ny + jnp.maximum(y - 1, 0),
            z * ny + y,
            (side * chunks + c) * zc + zl,
            c * (ny + 16) + y,
            c * ny + y,
        ]
        index_made[...] = jnp.zeros(index_made.shape, jnp.int32)
        for k, values in enumerate(rows):
            index_made[k : k + 1, :per_dev] = values

    def gather(*wanted):
        refs = [(slot, flat(ref), which, shift) for slot, ref, which, shift in wanted]

        def body(i, carry):
            at = {which: index[which, i] for which in sorted({w[2] for w in refs})}
            out = pl.ds(i, 1)
            for slot, ref, which, shift in refs:
                got[slot, out, :] = ref[pl.ds(at[which] + shift, 1), :]
            return carry

        lax.fori_loop(0, per_dev, body, 0, unroll=8)

    B_OWN, P_OWN, V_OWN, P_HALO, V_HALO, B_HALO, OLD_OWN, OLD_HALO = (0, 3, 5, 8, 11, 13, 15, 17)

    def own_rows(slot, ref, shift):
        return [(slot, ref, UP, shift), (slot + 1, ref, DOWN, shift)]

    def halo_rows(slot, n):
        edge = xj.at[n % 2]
        return [
            (slot, hp.at[n % 2], HALO, 0),
            (slot + 1, edge, EDGE, 9),
            (slot + 2, edge, EDGE, 7),
        ]

    def places():
        cells = to_column(cell_row[...].astype(jnp.float32)).astype(jnp.int32)
        cell_z, cell_x = (quotient(cells, ny * nx), remainder(cells, nx))
        return cell_x, remainder(quotient(cells, nx), ny), 4 * remainder(cell_z, zc)

    def along(values):
        return jnp.sum(values, axis=1, keepdims=True)

    def note(n, value):
        shear[...] = jnp.broadcast_to(value, shear.shape)
        line = jnp.sum(placed[...] * value, axis=0, keepdims=True)
        for k in range(ngx):
            begin = k * group_rows
            tile = begin - begin % 128
            piece = line[:, tile : tile + 128]
            spread = pltpu.roll(piece, remainder(mine * group_rows + (128 - begin % 128), 128), 1)
            spread = jnp.where(in_place, spread, 0.0)
            told[k, n - 1] = spread
        spectra_out[...] = spectra_out[...] + value * phase[n - 1 : n, :]

    def marks():
        cell_x, cell_y, start = places()
        here = patch_lane == cell_x
        up, down = (cell_y < ny - 1, cell_y > 0)
        ahead, behind = (patch_lane == cell_x + 1, patch_lane == cell_x - 1)
        ahead_out = (patch_lane == start + 2) & (cell_x == nx - 1)
        behind_out = (patch_lane == start + 1) & (cell_x == 0)
        return here, up, down, ahead, behind, ahead_out, behind_out

    def first_shear():
        here, up, down, ahead, behind, ahead_out, behind_out = marks()
        total = masked(here, jnp.where(up, got[V_OWN], got[V_HALO]))
        total = total - masked(here, jnp.where(down, got[V_OWN + 1], got[V_HALO]))
        total = total + masked(ahead, got[V_OWN + 2]) - masked(behind, got[V_OWN + 2])
        total = total + masked(ahead_out, got[V_HALO + 1]) - masked(behind_out, got[V_HALO + 1])
        shear[...] = jnp.broadcast_to(along(total), shear.shape)

    def make_factors():
        here, up, down, ahead, behind, ahead_out, behind_out = marks()
        b_up = along(masked(here, jnp.where(up, got[B_OWN], got[B_HALO])))
        b_down = along(masked(here, jnp.where(down, got[B_OWN + 1], got[B_HALO])))
        b_mid, b_out = (got[B_OWN + 2], got[B_HALO + 1])
        b_ahead = along(masked(ahead, b_mid) + masked(ahead_out, b_out))
        b_behind = along(masked(behind, b_mid) + masked(behind_out, b_out))
        at_up = masked(behind, b_up + b_behind) - masked(ahead, b_up + b_ahead)
        at_down = masked(ahead, b_down + b_ahead) - masked(behind, b_down + b_behind)
        factors[0] = masked(up, at_up)
        factors[1] = masked(down, at_down)
        factors[2] = jnp.where(up, masked(jnp.logical_not(down), at_down), at_up)
        factors[3] = masked(behind_out, b_up + b_behind) - masked(ahead_out, b_up + b_ahead)
        factors[4] = masked(ahead_out, b_down + b_ahead) - masked(behind_out, b_down + b_behind)

    def next_shear(n, own=P_OWN, halo=P_HALO):
        rows = [own, own + 1, halo, halo + 1, halo + 2]
        total = factors[0] * got[rows[0]]
        for k in range(1, 5):
            total = total + factors[k] * got[rows[k]]
        note(n, shear[:, 0:1] + along(total))

    for small in smalls:
        small.wait()
    make_index()
    index_copy = pltpu.make_async_copy(index_made, index, index_sem.at[0])
    index_copy.start()
    for c in range(chunks):
        shift(c)
    for c in range(chunks):
        for i in range(4, 9):
            load(i, c).wait()

    def send_rows():
        fill_placing()
        rows_send[...] = jnp.dot(
            placing[...],
            spectra_out[...],
            preferred_element_type=jnp.float32,
            precision=lax.Precision.HIGHEST,
        )
        for k in range(1, ngx):
            first_to(k).start()
        at = pl.ds(pl.multiple_of(gx * group_rows, group_rows), group_rows)
        rows_group[at, :] = rows_send[at, :]

    def mix():
        slot_count = slot_dev * ngy
        lines = min(slot_count, 128)
        depth = min(mixed.shape[1], 512)
        share = mixed.shape[0] // rup_group
        begin = pl.multiple_of(lax.rem(gy * share, lanes), share)
        block = (lines, lines)
        own_line = lax.broadcasted_iota(jnp.int32, block, 0) == lax.broadcasted_iota(
            jnp.int32, block, 1
        )
        row_at = lax.broadcasted_iota(jnp.int32, (slot_count, depth), 1)
        for r in range(rup_group):
            for k in range(slot_count // lines):
                line = table[r : r + 1, k * lines : (k + 1) * lines].astype(jnp.float32)
                column = jnp.sum(jnp.where(own_line, line, 0.0), axis=1, keepdims=True)
                at = pl.ds(k * lines, lines)
                columns[r, at, :] = jnp.broadcast_to(
                    column.astype(jnp.int32), (lines, columns.shape[2])
                )

        def blend(r, k):
            base = k * depth
            chosen = jnp.where(row_at + base == columns[r, :, 0:1], 1.0, 0.0).astype(jnp.bfloat16)
            own = weights_got[:, r].astype(jnp.float32).reshape(slot_count, lanes)
            spread = lax.dot_general(
                own.astype(jnp.bfloat16),
                chosen,
                (((0,), (0,)), ((), ())),
                preferred_element_type=jnp.float32,
            )
            wide[r] = spread
            rows = pl.ds(r * share, share)
            mixed[rows, pl.ds(base, depth)] = wide[r, pl.ds(begin, share), :].astype(jnp.bfloat16)

        for r in range(rup_group):
            if mixed.shape[1] == depth:
                blend(r, 0)
            else:

                @pl.loop(0, mixed.shape[1] // depth)
                def _(k):
                    blend(r, k)

    def work_after(r):
        if r == 0:
            index_copy.wait()
            gather(
                *own_rows(B_OWN, b, 0),
                (B_OWN + 2, b, MID, 0),
                *own_rows(V_OWN, vx_old, 0),
                (V_OWN + 2, vy_old, MID, 0),
                (B_HALO, hb, HALO, 0),
                (B_HALO + 1, bxh, PACK, 0),
                *own_rows(OLD_OWN, p_old, ny),
                *halo_rows(OLD_HALO, 0),
                *own_rows(P_OWN, p, ny),
            )
            make_factors()
        elif r == 1:
            gather(*halo_rows(P_HALO, 1), (V_HALO, hv, HALO, 0), (V_HALO + 1, vyx, PACK, 0))
            first_shear()
            next_shear(1, OLD_OWN, OLD_HALO)
            next_shear(2)
            gather(*own_rows(P_OWN, p, ny))
        elif r < STEPS - 1:
            gather(*halo_rows(P_HALO, r))
            next_shear(r + 1)
            gather(*own_rows(P_OWN, p, ny))

    def last_shear():
        gather(*halo_rows(P_HALO, STEPS - 1))
        next_shear(STEPS)
        tell_all()

    gaps = [(r, c) for r in range(STEPS - 1) for c in range(chunks)][chunks:]
    jobs = {gap: [] for gap in gaps + [None]}
    order = list(jobs)
    pieces = [(j, h) for j in range(2, ngy, 2) for h in range(2)]

    def enter_rows():
        settle(rows_group.at[pl.ds(0, (ngx - 1) * group_rows)], far_sem.at[1, 1])
        at = pl.ds(pl.multiple_of(gy * all_rows, all_rows), all_rows)
        rows_out[at, :] = rows_group[...]
        for h in range(2):
            direct_to(1, h).start()
        own_weights.start()

    def leave(j, h):
        direct_to(j, h).start()

    def forward(j, h):
        block_from(j, h).wait_recv()
        pass_on(j, h).start()

    jobs[order[0]].append(enter_rows)
    for i, (j, h) in enumerate(pieces):
        place = i * len(gaps) // len(pieces)
        jobs[order[place]].append(functools.partial(leave, j, h))
        after = order[min(place + 2, len(order) - 1)]
        jobs[after].append(functools.partial(forward, j, h))
    for k in range(1, ngy):
        place = (k - 1) * len(gaps) // (ngy - 1)
        jobs[order[place]].append(lambda k=k: weights_to(k).start())

    send_rows()
    for r in range(STEPS):
        above = p_old if r == 0 else p
        vz[1] = vz[1] - b[0] * (above[2] - above[0])
        for c in range(chunks):
            receive(r, c)
            halos(r, c)
            if r == STEPS - 1 and c == chunks - 1:
                last_shear()
            sweep(r, c)
            if r < STEPS - 1:
                send(r + 1, c)
            for job in jobs.get((r, c), []):
                job()
        work_after(r)
    for job in jobs[None]:
        job()
    fill_table()
    for side in range(8):

        @pl.when(has[side])
        def _():
            sent = ysend.at[side] if side < 2 else xsend if side < 4 else csend.at[side // 2 - 2]
            settle(sent, send_sem.at[side])

    settle(weights_got.at[pl.ds(0, ngy - 1)], far_sem.at[0, 0])
    settle(weights_got, far_sem.at[0, 1])
    mix()
    settle(rows_group.at[pl.ds(0, (ngx - 1) * group_rows)], far_sem.at[1, 0])
    settle(rows_out.at[pl.ds(0, (ngy - 1) * all_rows)], block_sem.at[0, 1])
    settle(rows_out.at[pl.ds(0, ngy // 2 * all_rows)], block_sem.at[0, 0])
    settle(heard.at[pl.ds(1, devices - 1)], tell_sem.at[0])
    settle(heard, hear_sem.at[0])


def finish_kernel(nz, *refs):
    refs = list(refs)
    take = lambda count: [refs.pop(0) for _ in range(count)]
    vx, vy, vz, p, m, spectra, mixed, rows, heard, phase = take(10)
    vel_out, p_out, m_out, spectra_out, slip_out = take(5)
    slip, exact, lines_in, out_sem, slip_sem = take(5)
    inner = pl.ds(1, nz)
    pairs = [
        (vx, vel_out.at[0]),
        (vy, vel_out.at[1]),
        (vz.at[inner], vel_out.at[2]),
        (p.at[inner], p_out),
        (m, m_out),
        (spectra, spectra_out),
    ]
    stores = [
        pltpu.make_async_copy(src, dst, out_sem.at[i]) for i, (src, dst) in enumerate(pairs)
    ]
    for store in stores:
        store.start()

    count = heard.shape[0]
    per_tile = count * 128 // rows.shape[0]
    lines_in[...] = jnp.zeros(lines_in.shape, jnp.float32)
    for t in range(count // per_tile):
        at, of = (pl.ds(t * 128, 128), pl.ds(t * per_tile, per_tile))
        for n in range(STEPS):
            lines_in[n : n + 1, at] = jnp.sum(heard[of, n], axis=0)
    for t in range(count // per_tile):
        at = pl.ds(t * 128, 128)
        change = lax.dot_general(
            lines_in[:, at],
            phase[...],
            (((0,), (0,)), ((), ())),
            preferred_element_type=jnp.float32,
            precision=lax.Precision.HIGHEST,
        )
        exact[at, :] = (rows[at, :] + change).astype(jnp.bfloat16)
    rup_group, share = slip.shape[:2]
    response = jnp.dot(mixed[...], exact[...], preferred_element_type=jnp.float32)
    slip[...] = response.reshape(slip.shape)
    answer = pltpu.make_async_copy(slip, slip_out, slip_sem.at[0])
    answer.start()
    for store in stores:
        store.wait()
    answer.wait()


VMEM_LIMIT = 40 * 1024 * 1024


def in_hbm(x):
    return pltpu.with_memory_space_constraint(x, pltpu.HBM)


def advance(
    velocity, pressure, memory, buoyancy, modulus, relax, strength, spectra, patch_cell, listed, weights
):
    nz, ny, nx = pressure.shape
    per_dev, width = spectra.shape
    zc = nx // 4
    chunks = nz // zc
    ngx, ngy = (lax.axis_size("gx"), lax.axis_size("gy"))
    dims = (nz, ny, nx, chunks, zc, per_dev, ngx, ngy)
    rup_group, slot_dev, variations = weights.shape
    lanes = max(variations // ngy, 128)
    all_rows = ngx * ngy * CAP
    f32 = jnp.float32
    field = lambda planes: pltpu.VMEM((planes, ny, nx), f32)
    rounds = range(STEPS)
    any_spec = pl.BlockSpec(memory_space=pl.ANY)
    vmem_spec = pl.BlockSpec(memory_space=pltpu.VMEM)
    return pl.pallas_call(
        functools.partial(step_kernel, dims),
        out_shape=[
            field(nz),
            field(nz),
            field(nz + 2),
            field(nz + 3),
            field(nz),
            pltpu.VMEM(spectra.shape, f32),
            pltpu.VMEM((rup_group * (variations // ngy), ngy * all_rows), jnp.bfloat16),
            pltpu.VMEM((ngy * all_rows, width), f32),
            pltpu.VMEM((ngx * ngy, STEPS, 1, 128), f32),
            pltpu.VMEM((8, width), f32),
        ],
        in_specs=[any_spec] * 12,
        out_specs=[vmem_spec] * 10,
        scratch_shapes=[field(nz + 1), field(nz), field(nz), field(nz)]
        + [field(nz), field(nz), field(nz + 3), field(nz)]
        + [
            pltpu.VMEM((2, chunks, sum(Y_ROWS), zc, nx), f32),
            pltpu.VMEM((chunks, sum(X_PACKS), ny, nx), f32),
            pltpu.VMEM((2, STEPS * chunks, 1, nx), f32),
        ]
        + [pltpu.VMEM((2, chunks, Y_ROWS[r], zc, nx), f32) for r in rounds]
        + [pltpu.VMEM((2, chunks, X_PACKS[r], ny, nx), f32) for r in rounds]
        + [pltpu.VMEM((chunks, 4, 1, nx), f32) for r in rounds]
        + [
            pltpu.VMEM((1, per_dev), jnp.int32),
            pltpu.VMEM(listed.shape, jnp.int32),
            pltpu.VMEM((8, max(per_dev, 128)), jnp.int32),
            pltpu.SMEM((8, max(per_dev, 128)), jnp.int32),
            pltpu.VMEM((chunks, ny, nx), f32),
            pltpu.VMEM((chunks, ny, nx), f32),
            pltpu.VMEM((chunks, ny, nx), f32),
            pltpu.VMEM((chunks, ny, nx), f32),
            pltpu.VMEM((2, chunks, ny, nx), f32),
            pltpu.VMEM((2, chunks, zc, nx), f32),
            pltpu.VMEM((chunks, ny, nx), f32),
            pltpu.VMEM((2, chunks, ny + 16, nx), f32),
            pltpu.VMEM((20, per_dev, nx), f32),
            pltpu.VMEM((per_dev, nx), f32),
            pltpu.VMEM((5, per_dev, nx), f32),
            pltpu.VMEM((2, 2, chunks, zc, nx), f32),
            pltpu.VMEM((2, chunks, zc, nx), f32),
            pltpu.VMEM((2, chunks, zc, nx), f32),
            pltpu.VMEM((ngy, rup_group, slot_dev, lanes), jnp.bfloat16),
            pltpu.VMEM((rup_group, max(listed.shape[1], 128)), jnp.int32),
            pltpu.VMEM((rup_group, listed.shape[1], 128), jnp.int32),
            pltpu.VMEM((rup_group, lanes, min(ngy * all_rows, 512)), f32),
            pltpu.VMEM((all_rows, per_dev), f32),
            pltpu.VMEM((per_dev, max(all_rows, 128)), f32),
            pltpu.VMEM((all_rows, width), f32),
            pltpu.VMEM((all_rows, width), f32),
            pltpu.VMEM((ngx, STEPS, 1, 128), f32),
            pltpu.SemaphoreType.DMA((9, chunks)),
            pltpu.SemaphoreType.DMA((4,)),
            pltpu.SemaphoreType.DMA((8,)),
            pltpu.SemaphoreType.DMA((2, chunks, 8)),
            pltpu.SemaphoreType.DMA((2, 2)),
            pltpu.SemaphoreType.DMA((ngy // 2, 2)),
            pltpu.SemaphoreType.DMA((1,)),
            pltpu.SemaphoreType.DMA((1,)),
            pltpu.SemaphoreType.DMA((1,)),
        ],
        compiler_params=pltpu.CompilerParams(
            collective_id=0, has_side_effects=True, vmem_limit_bytes=VMEM_LIMIT
        ),
    )(
        *[in_hbm(x) for x in (velocity, pressure, memory, buoyancy, modulus, relax, strength)],
        in_hbm(spectra),
        in_hbm(patch_cell.reshape(1, -1)),
        in_hbm(phase_rows(width // 2)),
        in_hbm(listed),
        in_hbm(weights),
    )


def finish(state, velocity, pressure, memory, spectra, weights):
    nz = pressure.shape[0]
    width = spectra.shape[1]
    ngy = lax.axis_size("gy")
    rup_group, slot_dev, variations = weights.shape
    share = variations // ngy
    f32 = jnp.float32
    any_spec = pl.BlockSpec(memory_space=pl.ANY)
    vmem_spec = pl.BlockSpec(memory_space=pltpu.VMEM)
    return pl.pallas_call(
        functools.partial(finish_kernel, nz),
        out_shape=[
            jax.ShapeDtypeStruct(velocity.shape, f32),
            jax.ShapeDtypeStruct(pressure.shape, f32),
            jax.ShapeDtypeStruct(memory.shape, f32),
            jax.ShapeDtypeStruct(spectra.shape, f32),
            jax.ShapeDtypeStruct((rup_group, share, width), f32),
        ],
        in_specs=[vmem_spec] * len(state),
        out_specs=[any_spec] * 5,
        scratch_shapes=[
            pltpu.VMEM((rup_group, share, width), f32),
            pltpu.VMEM(state[7].shape, jnp.bfloat16),
            pltpu.VMEM((8, state[7].shape[0]), f32),
            pltpu.SemaphoreType.DMA((6,)),
            pltpu.SemaphoreType.DMA((1,)),
        ],
        compiler_params=pltpu.CompilerParams(vmem_limit_bytes=VMEM_LIMIT),
    )(*[pltpu.with_memory_space_constraint(x, pltpu.VMEM) for x in state])


def per_device(
    velocity,
    pressure,
    memory,
    buoyancy,
    modulus,
    relax,
    strength,
    spectra,
    patch_cell,
    rupture_patches,
    slip_weights,
):
    state = advance(
        velocity,
        pressure,
        memory,
        buoyancy,
        modulus,
        relax,
        strength,
        spectra,
        patch_cell,
        rupture_patches,
        slip_weights,
    )
    return tuple(finish(state, velocity, pressure, memory, spectra, slip_weights))


def solution(mesh):
    in_specs = (
        P(None, None, "gy", "gx"),
        P(None, "gy", "gx"),
        P(None, "gy", "gx"),
        P(None, "gy", "gx"),
        P(None, "gy", "gx"),
        P(None, "gy", "gx"),
        P(None, "gy", "gx"),
        P(("gx", "gy"), None),
        P(("gx", "gy")),
        P(),
        P("gx", "gy", None),
    )
    out_specs = (
        P(None, None, "gy", "gx"),
        P(None, "gy", "gx"),
        P(None, "gy", "gx"),
        P(("gx", "gy"), None),
        P("gx", "gy", None),
    )
    return jax.shard_map(
        per_device, mesh=mesh, in_specs=in_specs, out_specs=out_specs, check_vma=False
    )
```

```python
import functools
import math

import jax
import jax.numpy as jnp
import numpy as np
from jax import lax
from jax.experimental import pallas as pl
from jax.experimental.pallas import tpu as pltpu
from jax.sharding import PartitionSpec as P

STEPS = 4
CAP = 2
BATCH = 8


def phase_rows(freqs):
    angle = np.pi * (np.arange(freqs) + 0.5) / freqs
    rows = [np.concatenate([np.cos(angle * n), -np.sin(angle * n)]) for n in range(1, STEPS + 1)]
    rows = rows + [np.zeros(2 * freqs)] * (8 - STEPS)
    return jnp.asarray(np.stack(rows).astype(np.float32))


Y_ROWS = [4, 3] + [2] * (STEPS - 2)
X_PACKS = [3, 2] + [1] * (STEPS - 2)


def quotient(value, size):
    if size & (size - 1):
        return lax.div(value, jnp.full_like(value, size))
    return lax.shift_right_logical(value, jnp.full_like(value, size.bit_length() - 1))


def remainder(value, size):
    if size & (size - 1):
        return lax.rem(value, jnp.full_like(value, size))
    return value & (size - 1)


def step_kernel(dims, *refs):
    nz, ny, nx, chunks, zc, per_dev, ngx, ngy = dims
    refs = list(refs)
    take = lambda count: [refs.pop(0) for _ in range(count)]
    vel_in, p_in, m_in, b_in, mod_in, rel_in, str_in = take(7)
    spectra_in, cell_row_in, phase_in, listed_in, weights = take(5)
    vx, vy, vz, p, m, spectra_out, mixed, rows_out, heard, phase = take(10)
    b, mod, rel, stg, vx_old, vy_old, p_old, b_east = take(8)
    ysend, xsend, csend = take(3)
    yrecv, xrecv, crecv = (take(STEPS), take(STEPS), take(STEPS))
    cell_row, listed, index_made, index = take(4)
    vxh, bwh, bxh, hx, hx_old, vyh, vyx, xj, got, shear, factors = take(11)
    hp, hv, hb, weights_got, table, columns, wide = take(7)
    placing, placed, rows_send, rows_group, told = take(5)
    in_sem, small_sem, send_sem, recv_sem, corner_sem = take(5)
    far_sem, block_sem, tell_sem, hear_sem, index_sem = take(5)

    gx, gy = (lax.axis_index("gx"), lax.axis_index("gy"))
    has = [gy > 0, gy < ngy - 1, gx > 0, gx < ngx - 1]
    has = has + [has[k // 2] & has[2 + k % 2] for k in range(4)]
    peer = [{"gy": gy - 1}, {"gy": gy + 1}, {"gx": gx - 1}, {"gx": gx + 1}]
    peer = peer + [{**peer[k // 2], **peer[2 + k % 2]} for k in range(4)]

    def load(i, h):
        count = nz // 2 if i < 4 else nz
        at = pl.ds(h * count, count)
        moved = pl.ds(h * count + 1, count)
        src, dst = [
            (p_in.at[at], p_old.at[moved]),
            (b_in.at[at], b.at[at]),
            (vel_in.at[0, at], vx_old.at[at]),
            (vel_in.at[1, at], vy_old.at[at]),
            (vel_in.at[2, at], vz.at[moved]),
            (rel_in.at[at], rel.at[at]),
            (m_in.at[at], m.at[at]),
            (str_in.at[at], stg.at[at]),
            (mod_in.at[at], mod.at[at]),
        ][i]
        return pltpu.make_async_copy(src, dst, in_sem.at[i + 9 * h])

    y_row = lambda r, k: sum(Y_ROWS[:r]) + k
    x_row = lambda r, k: sum(X_PACKS[:r]) + k

    smalls = [
        pltpu.make_async_copy(src, dst, small_sem.at[i])
        for i, (src, dst) in enumerate(
            [
                (cell_row_in, cell_row),
                (listed_in, listed),
                (phase_in, phase),
                (spectra_in, spectra_out),
            ]
        )
    ]
    for small in smalls:
        small.start()
    for h in range(2):
        for i in range(4):
            load(i, h).start()
    for i in range(4, 9):
        load(i, 0).start()
    devices = ngx * ngy
    me = gx * ngy + gy
    mine = gy * ngx + gx

    def other_device(k):
        other = lax.rem(me + k, devices)
        return {"gx": lax.div(other, ngy), "gy": lax.rem(other, ngy)}

    def flip(j):
        index = gy
        for bit in range(j.bit_length()):
            if (j >> bit) & 1:
                step = 2**bit
                index = index + step * (1 - 2 * lax.rem(lax.div(index, step), 2))
        return index

    barrier = pltpu.get_barrier_semaphore()

    peers = [{"gx": lax.rem(gx + k, ngx)} for k in range(1, ngx)]
    peers = peers + [{"gy": lax.rem(gy + k, ngy)} for k in range(1, ngy)]
    peers = peers + [
        {"gy": lax.rem(gy + ngy + dy, ngy), "gx": lax.rem(gx + ngx + dx, ngx)}
        for dy in (-1, 1)
        for dx in (-1, 1)
    ]
    for other in peers:
        pl.semaphore_signal(
            barrier, inc=1, device_id=other, device_id_type=pl.DeviceIdType.MESH
        )

    plane = jnp.zeros((ny, nx), jnp.float32)
    for field in (p_old, p):
        field[0] = plane
        field[nz + 1] = plane
        field[nz + 2] = plane
    vz[0] = plane
    vz[nz + 1] = plane
    b[nz] = plane
    for side in range(8):

        @pl.when(jnp.logical_not(has[side]))
        def _():
            for r in range(STEPS):
                if side < 2:
                    yrecv[r][side] = jnp.zeros(yrecv[r].shape[1:], jnp.float32)
                elif side < 4:
                    xrecv[r][side - 2] = jnp.zeros(xrecv[r].shape[1:], jnp.float32)
                else:
                    crecv[r][side - 4] = jnp.zeros(crecv[r].shape[1:], jnp.float32)

    def ends(r, c, side, coming):
        k = side % 4
        if side < 2:
            there = side if coming else 1 - side
            src = ysend.at[side, c, pl.ds(y_row(r, 0), Y_ROWS[r])]
            dst = yrecv[r].at[there, c]
            arrives = there
        elif side < 4:
            there = k - 2 if coming else 3 - k
            src = xsend.at[c, pl.ds(x_row(r, 0), X_PACKS[r])]
            dst = xrecv[r].at[there, c]
            arrives = 2 + there
        else:
            there = k if coming else 3 - k
            src, dst = (csend.at[k // 2, r], crecv[r].at[there])
            arrives = 4 + there
        return pltpu.make_async_remote_copy(
            src_ref=src,
            dst_ref=dst,
            send_sem=send_sem.at[side],
            recv_sem=recv_sem.at[r % 2, c, arrives] if side < 4 else corner_sem.at[r, there],
            device_id=peer[side],
            device_id_type=pl.DeviceIdType.MESH,
        )

    def send(r, c):
        for side in range(8 if c == chunks - 1 else 4):

            @pl.when(has[side])
            def _():
                ends(r, c, side, False).start()

    def receive(r, c, sides=range(4)):
        for side in sides:

            @pl.when(has[side])
            def _():
                ends(r, c, side, True).wait_recv()

    def corners(r):
        receive(r, chunks - 1, range(4, 8))
        for c in range(chunks):
            south = jnp.where(west_half, crecv[r][0, c], crecv[r][1, c])
            north = jnp.where(west_half, crecv[r][2, c], crecv[r][3, c])
            xj[r % 2, c, 7:8, :] = south
            xj[r % 2, c, 8 + ny : 9 + ny, :] = north

    lane = lax.broadcasted_iota(jnp.int32, (ny, nx), 1)
    row = lax.broadcasted_iota(jnp.int32, (ny, nx), 0)
    quad, lane4 = (quotient(lane, 4), remainder(lane, 4))
    last_row, first_row = (row == ny - 1, row == 0)
    west_half = remainder(lax.broadcasted_iota(jnp.int32, (1, nx), 1), 4) < 2

    def pack(total, slab, zl):
        return jnp.where(quad == zl, pltpu.roll(slab, 4 * zl + 2, 1), total)

    def d_y(slab, south, north):
        after = jnp.where(last_row, north, pltpu.roll(slab, ny - 1, 0))
        before = jnp.where(first_row, south, pltpu.roll(slab, 1, 0))
        return after - before

    for c in range(chunks):
        if c % (chunks // 2) == 0:
            for i in range(4):
                load(i, c // (chunks // 2)).wait()

        def edges(i, totals):
            pt, vt, bt = totals
            for j in range(8):
                zl = i * 8 + j
                z = c * zc + zl
                ps, vs, ws, bs = (p_old[z + 1], vx_old[z], vy_old[z], b[z])
                pt, vt, bt = (pack(pt, ps, zl), pack(vt, vs, zl), pack(bt, bs, zl))
                at = pl.ds(zl, 1)
                ysend[0, c, y_row(0, 0), at, :] = ps[0:1]
                ysend[0, c, y_row(0, 1), at, :] = ps[1:2]
                ysend[0, c, y_row(0, 2), at, :] = ws[0:1]
                ysend[0, c, y_row(0, 3), at, :] = bs[0:1]
                ysend[1, c, y_row(0, 0), at, :] = ps[ny - 2 : ny - 1]
                ysend[1, c, y_row(0, 1), at, :] = ps[ny - 1 : ny]
                ysend[1, c, y_row(0, 2), at, :] = ws[ny - 1 : ny]
                ysend[1, c, y_row(0, 3), at, :] = bs[ny - 1 : ny]
            return pt, vt, bt

        totals = lax.fori_loop(0, zc // 8, edges, (plane, plane, plane))
        for i, total in enumerate(totals):
            xsend[c, x_row(0, i)] = total
        csend[0, 0, c] = totals[0][0:1]
        csend[1, 0, c] = totals[0][ny - 1 : ny]
        if c == 0:
            pl.semaphore_wait(barrier, len(peers))
        send(0, c)

    rup_group, slot_dev, variations = weights.shape
    lanes = weights_got.shape[3]
    group_rows = ngy * CAP
    all_rows = ngx * group_rows

    def weight_block(other):
        block = other * (variations // ngy) // lanes
        return weights.at[:, :, pl.ds(pl.multiple_of(block * lanes, lanes), lanes)]

    def far(kind, k, src, dst):
        axis, size = ("gx", ngx) if kind == 1 else ("gy", ngy)
        return pltpu.make_async_remote_copy(
            src_ref=src,
            dst_ref=dst,
            send_sem=far_sem.at[kind, 0],
            recv_sem=far_sem.at[kind, 1],
            device_id={axis: lax.rem(lax.axis_index(axis) + k, size)},
            device_id_type=pl.DeviceIdType.MESH,
        )

    def settle(ref, sem):
        pltpu.make_async_copy(ref, ref, sem).wait()

    def rows_of(ref, index, count):
        return ref.at[pl.ds(pl.multiple_of(index * count, count), count)]

    def weights_to(k):
        return far(0, k, weight_block(lax.rem(gy + k, ngy)), weights_got.at[gy])

    def first_to(k):
        src = rows_of(rows_send, lax.rem(gx + k, ngx), group_rows)
        return far(1, k, src, rows_of(rows_group, gx, group_rows))

    half = all_rows // 2

    def block_rows(owner, h):
        at = pl.multiple_of(owner * all_rows + h * half, half)
        return rows_out.at[pl.ds(at, half)]

    def carry_over(j, h, src, dst, partner):
        return pltpu.make_async_remote_copy(
            src_ref=src,
            dst_ref=dst,
            send_sem=block_sem.at[0, 1],
            recv_sem=block_sem.at[0, 0] if j % 2 else block_sem.at[j // 2, h],
            device_id={"gy": partner},
            device_id_type=pl.DeviceIdType.MESH,
        )

    def direct_to(j, h):
        return carry_over(
            j, h, rows_group.at[pl.ds(h * half, half)], block_rows(gy, h), flip(j)
        )

    def pass_on(j, h):
        block = block_rows(flip(j), h)
        return carry_over(j + 1, h, block, block, flip(1))

    def block_from(j, h):
        block = block_rows(flip(j), h)
        return carry_over(j, h, block, block, flip(1 if j % 2 else j))

    def tell(k):
        where = other_device(k)
        return pltpu.make_async_remote_copy(
            src_ref=told.at[where["gx"]],
            dst_ref=heard.at[mine],
            send_sem=tell_sem.at[0],
            recv_sem=hear_sem.at[0],
            device_id=where,
            device_id_type=pl.DeviceIdType.MESH,
        )

    def tell_all():
        pltpu.make_async_copy(told.at[gx], heard.at[mine], hear_sem.at[0]).start()

        def start(k, carry):
            tell(k).start()
            return carry

        lax.fori_loop(1, devices, start, 0)

    own_weights = pltpu.make_async_copy(weight_block(gy), weights_got.at[gy], far_sem.at[0, 1])

    square = (per_dev, per_dev)
    eye = lax.broadcasted_iota(jnp.int32, square, 0) == lax.broadcasted_iota(jnp.int32, square, 1)

    def to_row(column):
        return jnp.sum(jnp.where(eye, column, 0.0), axis=0, keepdims=True)

    def to_column(line):
        return jnp.sum(jnp.where(eye, line, 0.0), axis=1, keepdims=True)

    def fill_placing():
        ruptures, slots = listed.shape
        shape = (per_dev, slots)
        own_ids = lax.broadcasted_iota(jnp.int32, shape, 0) + (gx * ngy + gy) * per_dev
        slot_owner = quotient(lax.broadcasted_iota(jnp.int32, shape, 1), slot_dev)

        def body(r, best):
            owner = quotient(r, rup_group) * ngy + slot_owner
            return jnp.where(listed[pl.ds(r, 1), :] == own_ids, owner, best)

        best = lax.fori_loop(0, ruptures, body, jnp.full(shape, -1, jnp.int32))
        target = jnp.max(best.astype(jnp.float32), axis=1, keepdims=True)
        before = lax.broadcasted_iota(jnp.int32, square, 1) < lax.broadcasted_iota(
            jnp.int32, square, 0
        )
        same = (to_row(target) == target) & before
        rank = jnp.sum(jnp.where(same, 1.0, 0.0), axis=1, keepdims=True)
        bucket = jnp.where(target >= 0.0, target * CAP + rank, -1.0)
        spot = lax.broadcasted_iota(jnp.int32, placed.shape, 1).astype(jnp.float32)
        placed[...] = jnp.where(spot == bucket, 1.0, 0.0)
        place = lax.broadcasted_iota(jnp.int32, placing.shape, 0).astype(jnp.float32)
        placing[...] = jnp.where(place == to_row(bucket), 1.0, 0.0)

    def fill_table():
        slot_count = listed.shape[1]
        shape = table.shape
        spot = lax.broadcasted_iota(jnp.int32, shape, 1)
        owner, place = (quotient(spot, slot_dev), remainder(spot, slot_dev))
        table[...] = jnp.full(shape, -1, jnp.int32)
        group = pl.ds(pl.multiple_of(gx * rup_group, rup_group), rup_group)
        table[:, :slot_count] = listed[group, :]
        ids = table[...]
        source = quotient(ids, per_dev)

        def earlier(i, rank):
            shift = i - (slot_dev - 1)
            inside = (place >= shift) & (place < shift + slot_dev)
            turned = pltpu.roll(ids, jnp.where(shift < 0, shift + shape[1], shift), 1)
            for k in range(rup_group):
                other = pltpu.roll(turned, k, 0) if k else turned
                found = inside & (other < ids) & (quotient(other, per_dev) == source)
                rank = jnp.where(found, 1, rank)
            return rank

        shifts = 2 * slot_dev - 1
        unroll = max(k for k in range(1, 16) if shifts % k == 0)
        rank = lax.fori_loop(0, shifts, earlier, jnp.zeros(shape, jnp.int32), unroll=unroll)
        block = remainder(source, ngy) * ngx + quotient(source, ngy)
        table[...] = jnp.where(ids >= 0, (block * ngy + owner) * CAP + rank, -1)

    def halos(r, c):
        def joined(i):
            return jnp.where(lane4 < 2, xrecv[r][0, c, i], xrecv[r][1, c, i])

        west, east, own = (xrecv[r][0, c, 0], xrecv[r][1, c, 0], xsend[c, x_row(r, 0)])
        if r == 0:

            def edge(i):
                return jnp.where(lane4 == 1, xrecv[0][0, c, i], xsend[c, x_row(0, i)])

            vh, bh = (pltpu.roll(edge(1), 1, 1), pltpu.roll(edge(2), 1, 1))
            bwh[c] = bh
            bxh[c] = joined(2)
            hx_old[0, c] = pltpu.roll(xrecv[0][1, c, 2], nx - 1, 1)
            hx_old[1, c] = pltpu.roll(xrecv[0][1, c, 1], nx - 1, 1)
            vyh[0, c] = yrecv[0][0, c, 2]
            vyh[1, c] = yrecv[0][1, c, 2]
            for side in range(2):
                hb[side, c] = yrecv[0][side, c, 3]
        else:
            vh, bh = (vxh[c], bwh[c])
            if r == 1:
                vyx[c] = joined(1)
                for side in range(2):
                    hv[side, c] = yrecv[1][side, c, 2]
        for side in range(2):
            hp[r % 2, side, c] = yrecv[r][side, c, 1 - side]
        xj[r % 2, c, 8 : 8 + ny, :] = joined(0)
        vh = vh - bh * (own - pltpu.roll(west, 2, 1))
        vxh[c] = vh
        hx[c] = jnp.where(lane4 < 2, pltpu.roll(east, nx - 2, 1), vh)
        vyh[0, c] = vyh[0, c] - yrecv[0][0, c, 3] * (ysend[0, c, y_row(r, 0)] - yrecv[r][0, c, 0])
        vyh[1, c] = vyh[1, c] - yrecv[0][1, c, 3] * (yrecv[r][1, c, 1] - ysend[1, c, y_row(r, 1)])

    def sweep(r, c):
        last, first = (r == STEPS - 1, r == 0)
        n = r + 1
        p_from, w_from = (p_old, vy_old) if first else (p, vy)

        def body(i, total):
            base = i * BATCH
            z0 = c * zc + base
            ps = [p_from[z0 + 1 + j] for j in range(BATCH + 2)]
            bs = [b[z0 + j] for j in range(BATCH + 1)]
            zs = [vz[z0], vz[z0 + 1]]
            vs, ws, new_p, outer = ([], [], [], [])
            for j in range(BATCH):
                zl = base + j
                at = pl.ds(zl, 1)
                turn = nx - 2 - 4 * zl
                zs.append(vz[z0 + j + 2] - bs[j + 1] * (ps[j + 2] - ps[j]))
                outer.append(pltpu.roll(hx[c], turn, 1))
                ahead = jnp.where(lane >= nx - 2, outer[j], pltpu.roll(ps[j], nx - 2, 1))
                shifted, speed = (b_east[z0 + j], vx[z0 + j])
                if first:
                    edges_in = [pltpu.roll(hx_old[k, c], turn, 1) for k in range(2)]
                    shifted = jnp.where(lane == nx - 1, edges_in[0], shifted)
                    b_east[z0 + j] = shifted
                    speed = jnp.where(lane == nx - 1, edges_in[1], speed)
                vs.append(speed - shifted * (ahead - ps[j]))
                south, north = (yrecv[r][0, c, 1, at, :], yrecv[r][1, c, 0, at, :])
                ws.append(w_from[z0 + j] - bs[j] * d_y(ps[j], south, north))
            for j in range(BATCH):
                zl = base + j
                at = pl.ds(zl, 1)
                turned = pltpu.roll(vs[j], 2, 1)
                spread = vs[j] - jnp.where(lane < 2, outer[j], turned)
                if last:
                    vs[j] = pltpu.roll(jnp.where(lane == 1, outer[j], turned), nx - 1, 1)
                spread = spread + d_y(ws[j], vyh[0, c, at, :], vyh[1, c, at, :])
                spread = spread + (zs[j + 2] - zs[j])
                mem = m[z0 + j]
                mem = mem - rel[z0 + j] * (mem + stg[z0 + j] * spread)
                m[z0 + j] = mem
                new_p.append(ps[j] - mod[z0 + j] * (spread + mem))
            for j in range(BATCH):
                zl = base + j
                at = pl.ds(zl, 1)
                vz[z0 + j + 2] = zs[j + 2]
                vx[z0 + j] = vs[j]
                vy[z0 + j] = ws[j]
                p[z0 + j + 1] = new_p[j]
                if not last:
                    total = pack(total, new_p[j], zl)
                    ysend[0, c, y_row(n, 0), at, :] = new_p[j][0:1]
                    ysend[0, c, y_row(n, 1), at, :] = new_p[j][1:2]
                    ysend[1, c, y_row(n, 0), at, :] = new_p[j][ny - 2 : ny - 1]
                    ysend[1, c, y_row(n, 1), at, :] = new_p[j][ny - 1 : ny]
            return total

        total = lax.fori_loop(0, zc // BATCH, body, plane)
        if not last:
            xsend[c, x_row(n, 0)] = total
            csend[0, n, c] = total[0:1]
            csend[1, n, c] = total[ny - 1 : ny]

    def shift(c):
        def body(i, total):
            for j in range(8):
                zl = i * 8 + j
                z = c * zc + zl
                at = pl.ds(zl, 1)
                old = vx_old[z]
                vx[z] = pltpu.roll(old, nx - 1, 1)
                b_east[z] = pltpu.roll(b[z], nx - 1, 1)
                total = pack(total, vy_old[z], zl)
                ysend[0, c, y_row(1, 2), at, :] = old[0:1]
                ysend[1, c, y_row(1, 2), at, :] = old[ny - 1 : ny]
            return total

        xsend[c, x_row(1, 1)] = lax.fori_loop(0, zc // 8, body, plane)

    told_lane = lax.broadcasted_iota(jnp.int32, (1, 128), 1)
    in_place = quotient(told_lane, group_rows) == remainder(mine, 128 // group_rows)
    patch_lane = lax.broadcasted_iota(jnp.int32, (per_dev, nx), 1)

    def masked(keep, values):
        return jnp.where(keep, values, 0.0)

    def flat(ref):
        return ref.reshape(math.prod(ref.shape[:-1]), ref.shape[-1])

    UP, DOWN, MID, HALO, EDGE, PACK = range(6)

    def make_index():
        cells = cell_row[...]
        z, y = (quotient(cells, ny * nx), remainder(quotient(cells, nx), ny))
        c, zl = (quotient(z, zc), remainder(z, zc))
        side = jnp.where(y == 0, 0, 1)
        rows = [
            z * ny + jnp.minimum(y + 1, ny - 1),
            z * ny + jnp.maximum(y - 1, 0),
            z * ny + y,
            (side * chunks + c) * zc + zl,
            c * (ny + 16) + y,
            c * ny + y,
        ]
        index_made[...] = jnp.zeros(index_made.shape, jnp.int32)
        for k, values in enumerate(rows):
            index_made[k : k + 1, :per_dev] = values

    def gather(*wanted):
        refs = [(slot, flat(ref), which, shift) for slot, ref, which, shift in wanted]

        def body(i, carry):
            at = {which: index[which, i] for which in sorted({w[2] for w in refs})}
            out = pl.ds(i, 1)
            for slot, ref, which, shift in refs:
                got[slot, out, :] = ref[pl.ds(at[which] + shift, 1), :]
            return carry

        lax.fori_loop(0, per_dev, body, 0, unroll=8)

    B_OWN, P_OWN, V_OWN, P_HALO, V_HALO, B_HALO, OLD_OWN, OLD_HALO = (0, 3, 5, 8, 11, 13, 15, 17)

    def own_rows(slot, ref, shift):
        return [(slot, ref, UP, shift), (slot + 1, ref, DOWN, shift)]

    def halo_rows(slot, n):
        edge = xj.at[n % 2]
        return [
            (slot, hp.at[n % 2], HALO, 0),
            (slot + 1, edge, EDGE, 9),
            (slot + 2, edge, EDGE, 7),
        ]

    def places():
        cells = to_column(cell_row[...].astype(jnp.float32)).astype(jnp.int32)
        cell_z, cell_x = (quotient(cells, ny * nx), remainder(cells, nx))
        return cell_x, remainder(quotient(cells, nx), ny), 4 * remainder(cell_z, zc)

    def along(values):
        return jnp.sum(values, axis=1, keepdims=True)

    def note(n, value):
        shear[...] = jnp.broadcast_to(value, shear.shape)
        line = jnp.sum(placed[...] * value, axis=0, keepdims=True)
        for k in range(ngx):
            begin = k * group_rows
            tile = begin - begin % 128
            piece = line[:, tile : tile + 128]
            spread = pltpu.roll(piece, remainder(mine * group_rows + (128 - begin % 128), 128), 1)
            spread = jnp.where(in_place, spread, 0.0)
            told[k, n - 1] = spread
        spectra_out[...] = spectra_out[...] + value * phase[n - 1 : n, :]

    def marks():
        cell_x, cell_y, start = places()
        here = patch_lane == cell_x
        up, down = (cell_y < ny - 1, cell_y > 0)
        ahead, behind = (patch_lane == cell_x + 1, patch_lane == cell_x - 1)
        ahead_out = (patch_lane == start + 2) & (cell_x == nx - 1)
        behind_out = (patch_lane == start + 1) & (cell_x == 0)
        return here, up, down, ahead, behind, ahead_out, behind_out

    def first_shear():
        here, up, down, ahead, behind, ahead_out, behind_out = marks()
        total = masked(here, jnp.where(up, got[V_OWN], got[V_HALO]))
        total = total - masked(here, jnp.where(down, got[V_OWN + 1], got[V_HALO]))
        total = total + masked(ahead, got[V_OWN + 2]) - masked(behind, got[V_OWN + 2])
        total = total + masked(ahead_out, got[V_HALO + 1]) - masked(behind_out, got[V_HALO + 1])
        shear[...] = jnp.broadcast_to(along(total), shear.shape)

    def make_factors():
        here, up, down, ahead, behind, ahead_out, behind_out = marks()
        b_up = along(masked(here, jnp.where(up, got[B_OWN], got[B_HALO])))
        b_down = along(masked(here, jnp.where(down, got[B_OWN + 1], got[B_HALO])))
        b_mid, b_out = (got[B_OWN + 2], got[B_HALO + 1])
        b_ahead = along(masked(ahead, b_mid) + masked(ahead_out, b_out))
        b_behind = along(masked(behind, b_mid) + masked(behind_out, b_out))
        at_up = masked(behind, b_up + b_behind) - masked(ahead, b_up + b_ahead)
        at_down = masked(ahead, b_down + b_ahead) - masked(behind, b_down + b_behind)
        factors[0] = masked(up, at_up)
        factors[1] = masked(down, at_down)
        factors[2] = jnp.where(up, masked(jnp.logical_not(down), at_down), at_up)
        factors[3] = masked(behind_out, b_up + b_behind) - masked(ahead_out, b_up + b_ahead)
        factors[4] = masked(ahead_out, b_down + b_ahead) - masked(behind_out, b_down + b_behind)

    def next_shear(n, own=P_OWN, halo=P_HALO):
        rows = [own, own + 1, halo, halo + 1, halo + 2]
        total = factors[0] * got[rows[0]]
        for k in range(1, 5):
            total = total + factors[k] * got[rows[k]]
        note(n, shear[:, 0:1] + along(total))

    for small in smalls:
        small.wait()
    make_index()
    index_copy = pltpu.make_async_copy(index_made, index, index_sem.at[0])
    index_copy.start()
    for c in range(chunks // 2):
        shift(c)
    for i in range(4, 9):
        load(i, 0).wait()

    def send_rows():
        fill_placing()
        rows_send[...] = jnp.dot(
            placing[...],
            spectra_out[...],
            preferred_element_type=jnp.float32,
            precision=lax.Precision.HIGHEST,
        )
        for k in range(1, ngx):
            first_to(k).start()
        at = pl.ds(pl.multiple_of(gx * group_rows, group_rows), group_rows)
        rows_group[at, :] = rows_send[at, :]

    def mix():
        slot_count = slot_dev * ngy
        lines = min(slot_count, 128)
        depth = min(mixed.shape[1], 512)
        share = mixed.shape[0] // rup_group
        begin = pl.multiple_of(lax.rem(gy * share, lanes), share)
        block = (lines, lines)
        own_line = lax.broadcasted_iota(jnp.int32, block, 0) == lax.broadcasted_iota(
            jnp.int32, block, 1
        )
        row_at = lax.broadcasted_iota(jnp.int32, (slot_count, depth), 1)
        for r in range(rup_group):
            for k in range(slot_count // lines):
                line = table[r : r + 1, k * lines : (k + 1) * lines].astype(jnp.float32)
                column = jnp.sum(jnp.where(own_line, line, 0.0), axis=1, keepdims=True)
                at = pl.ds(k * lines, lines)
                columns[r, at, :] = jnp.broadcast_to(
                    column.astype(jnp.int32), (lines, columns.shape[2])
                )

        def blend(r, k):
            base = k * depth
            chosen = jnp.where(row_at + base == columns[r, :, 0:1], 1.0, 0.0).astype(jnp.bfloat16)
            own = weights_got[:, r].astype(jnp.float32).reshape(slot_count, lanes)
            spread = lax.dot_general(
                own.astype(jnp.bfloat16),
                chosen,
                (((0,), (0,)), ((), ())),
                preferred_element_type=jnp.float32,
            )
            wide[r] = spread
            rows = pl.ds(r * share, share)
            mixed[rows, pl.ds(base, depth)] = wide[r, pl.ds(begin, share), :].astype(jnp.bfloat16)

        for r in range(rup_group):
            if mixed.shape[1] == depth:
                blend(r, 0)
            else:

                @pl.loop(0, mixed.shape[1] // depth)
                def _(k):
                    blend(r, k)

    def work_after(r):
        corners(r)
        if r == 0:
            index_copy.wait()
            gather(
                *own_rows(B_OWN, b, 0),
                (B_OWN + 2, b, MID, 0),
                *own_rows(V_OWN, vx_old, 0),
                (V_OWN + 2, vy_old, MID, 0),
                (B_HALO, hb, HALO, 0),
                (B_HALO + 1, bxh, PACK, 0),
                *own_rows(OLD_OWN, p_old, ny),
                *halo_rows(OLD_HALO, 0),
                *own_rows(P_OWN, p, ny),
            )
            make_factors()
        elif r == 1:
            gather(*halo_rows(P_HALO, 1), (V_HALO, hv, HALO, 0), (V_HALO + 1, vyx, PACK, 0))
            first_shear()
            next_shear(1, OLD_OWN, OLD_HALO)
            next_shear(2)
            gather(*own_rows(P_OWN, p, ny))
        elif r < STEPS - 1:
            gather(*halo_rows(P_HALO, r))
            next_shear(r + 1)
            gather(*own_rows(P_OWN, p, ny))

    def last_shear():
        corners(STEPS - 1)
        gather(*halo_rows(P_HALO, STEPS - 1))
        next_shear(STEPS)
        tell_all()

    gaps = [(r, c) for r in range(STEPS - 1) for c in range(chunks)][chunks + chunks // 2 :]
    jobs = {gap: [] for gap in gaps + [None]}
    order = list(jobs)
    pieces = [(j, h) for j in range(2, ngy, 2) for h in range(2)]

    def enter_rows():
        settle(rows_group.at[pl.ds(0, (ngx - 1) * group_rows)], far_sem.at[1, 1])
        at = pl.ds(pl.multiple_of(gy * all_rows, all_rows), all_rows)
        rows_out[at, :] = rows_group[...]
        for h in range(2):
            direct_to(1, h).start()
        own_weights.start()

    def leave(j, h):
        direct_to(j, h).start()

    def forward(j, h):
        block_from(j, h).wait_recv()
        pass_on(j, h).start()

    jobs[0, 0] = [send_rows]
    jobs[order[0]].append(enter_rows)
    for i, (j, h) in enumerate(pieces):
        place = i * len(gaps) // len(pieces)
        jobs[order[place]].append(functools.partial(leave, j, h))
        after = order[min(place + 5, len(order) - 1)]
        jobs[after].append(functools.partial(forward, j, h))
    for r in range(STEPS):
        above = p_old if r == 0 else p
        vz[1] = vz[1] - b[0] * (above[2] - above[0])
        for c in range(chunks):
            if r == STEPS - 1 and c == 0:
                for k in range(1, ngy):
                    weights_to(k).start()
            receive(r, c)
            halos(r, c)
            if r == 0 and c >= chunks // 2:
                shift(c)
            if r == STEPS - 1 and c == chunks - 1:
                last_shear()
            sweep(r, c)
            if r < STEPS - 1:
                send(r + 1, c)
            for job in jobs.get((r, c), []):
                job()
        if r < STEPS - 1:
            work_after(r)
    for job in jobs[None]:
        job()
    fill_table()
    for side in range(8):

        @pl.when(has[side])
        def _():
            sent = ysend.at[side] if side < 2 else xsend if side < 4 else csend.at[side // 2 - 2]
            settle(sent, send_sem.at[side])

    settle(weights_got.at[pl.ds(0, ngy - 1)], far_sem.at[0, 0])
    settle(weights_got, far_sem.at[0, 1])
    mix()
    settle(rows_group.at[pl.ds(0, (ngx - 1) * group_rows)], far_sem.at[1, 0])
    settle(rows_out.at[pl.ds(0, (ngy - 1) * all_rows)], block_sem.at[0, 1])
    settle(rows_out.at[pl.ds(0, ngy // 2 * all_rows)], block_sem.at[0, 0])
    settle(heard.at[pl.ds(1, devices - 1)], tell_sem.at[0])
    settle(heard, hear_sem.at[0])


def finish_kernel(nz, *refs):
    refs = list(refs)
    take = lambda count: [refs.pop(0) for _ in range(count)]
    vx, vy, vz, p, m, spectra, mixed, rows, heard, phase = take(10)
    vel_out, p_out, m_out, spectra_out, slip_out = take(5)
    slip, exact, lines_in, out_sem, slip_sem = take(5)
    inner = pl.ds(1, nz)
    pairs = [
        (vx, vel_out.at[0]),
        (vy, vel_out.at[1]),
        (vz.at[inner], vel_out.at[2]),
        (p.at[inner], p_out),
        (m, m_out),
        (spectra, spectra_out),
    ]
    stores = [
        pltpu.make_async_copy(src, dst, out_sem.at[i]) for i, (src, dst) in enumerate(pairs)
    ]
    for store in stores:
        store.start()

    count = heard.shape[0]
    per_tile = count * 128 // rows.shape[0]
    lines_in[...] = jnp.zeros(lines_in.shape, jnp.float32)
    for t in range(count // per_tile):
        at, of = (pl.ds(t * 128, 128), pl.ds(t * per_tile, per_tile))
        for n in range(STEPS):
            lines_in[n : n + 1, at] = jnp.sum(heard[of, n], axis=0)
    for t in range(count // per_tile):
        at = pl.ds(t * 128, 128)
        change = lax.dot_general(
            lines_in[:, at],
            phase[...],
            (((0,), (0,)), ((), ())),
            preferred_element_type=jnp.float32,
            precision=lax.Precision.HIGHEST,
        )
        exact[at, :] = (rows[at, :] + change).astype(jnp.bfloat16)
    rup_group, share = slip.shape[:2]
    response = jnp.dot(mixed[...], exact[...], preferred_element_type=jnp.float32)
    slip[...] = response.reshape(slip.shape)
    answer = pltpu.make_async_copy(slip, slip_out, slip_sem.at[0])
    answer.start()
    for store in stores:
        store.wait()
    answer.wait()


VMEM_LIMIT = 40 * 1024 * 1024


def in_hbm(x):
    return pltpu.with_memory_space_constraint(x, pltpu.HBM)


def advance(
    velocity, pressure, memory, buoyancy, modulus, relax, strength, spectra, patch_cell, listed, weights
):
    nz, ny, nx = pressure.shape
    per_dev, width = spectra.shape
    zc = nx // 8
    chunks = nz // zc
    ngx, ngy = (lax.axis_size("gx"), lax.axis_size("gy"))
    dims = (nz, ny, nx, chunks, zc, per_dev, ngx, ngy)
    rup_group, slot_dev, variations = weights.shape
    lanes = max(variations // ngy, 128)
    all_rows = ngx * ngy * CAP
    f32 = jnp.float32
    field = lambda planes: pltpu.VMEM((planes, ny, nx), f32)
    rounds = range(STEPS)
    any_spec = pl.BlockSpec(memory_space=pl.ANY)
    vmem_spec = pl.BlockSpec(memory_space=pltpu.VMEM)
    return pl.pallas_call(
        functools.partial(step_kernel, dims),
        out_shape=[
            field(nz),
            field(nz),
            field(nz + 2),
            field(nz + 3),
            field(nz),
            pltpu.VMEM(spectra.shape, f32),
            pltpu.VMEM((rup_group * (variations // ngy), ngy * all_rows), jnp.bfloat16),
            pltpu.VMEM((ngy * all_rows, width), f32),
            pltpu.VMEM((ngx * ngy, STEPS, 1, 128), f32),
            pltpu.VMEM((8, width), f32),
        ],
        in_specs=[any_spec] * 12,
        out_specs=[vmem_spec] * 10,
        scratch_shapes=[field(nz + 1), field(nz), field(nz), field(nz)]
        + [field(nz), field(nz), field(nz + 3), field(nz)]
        + [
            pltpu.VMEM((2, chunks, sum(Y_ROWS), zc, nx), f32),
            pltpu.VMEM((chunks, sum(X_PACKS), ny, nx), f32),
            pltpu.VMEM((2, STEPS, chunks, 1, nx), f32),
        ]
        + [pltpu.VMEM((2, chunks, Y_ROWS[r], zc, nx), f32) for r in rounds]
        + [pltpu.VMEM((2, chunks, X_PACKS[r], ny, nx), f32) for r in rounds]
        + [pltpu.VMEM((4, chunks, 1, nx), f32) for r in rounds]
        + [
            pltpu.VMEM((1, per_dev), jnp.int32),
            pltpu.VMEM(listed.shape, jnp.int32),
            pltpu.VMEM((8, max(per_dev, 128)), jnp.int32),
            pltpu.SMEM((8, max(per_dev, 128)), jnp.int32),
            pltpu.VMEM((chunks, ny, nx), f32),
            pltpu.VMEM((chunks, ny, nx), f32),
            pltpu.VMEM((chunks, ny, nx), f32),
            pltpu.VMEM((chunks, ny, nx), f32),
            pltpu.VMEM((2, chunks, ny, nx), f32),
            pltpu.VMEM((2, chunks, zc, nx), f32),
            pltpu.VMEM((chunks, ny, nx), f32),
            pltpu.VMEM((2, chunks, ny + 16, nx), f32),
            pltpu.VMEM((20, per_dev, nx), f32),
            pltpu.VMEM((per_dev, nx), f32),
            pltpu.VMEM((5, per_dev, nx), f32),
            pltpu.VMEM((2, 2, chunks, zc, nx), f32),
            pltpu.VMEM((2, chunks, zc, nx), f32),
            pltpu.VMEM((2, chunks, zc, nx), f32),
            pltpu.VMEM((ngy, rup_group, slot_dev, lanes), jnp.bfloat16),
            pltpu.VMEM((rup_group, max(listed.shape[1], 128)), jnp.int32),
            pltpu.VMEM((rup_group, listed.shape[1], 128), jnp.int32),
            pltpu.VMEM((rup_group, lanes, min(ngy * all_rows, 512)), f32),
            pltpu.VMEM((all_rows, per_dev), f32),
            pltpu.VMEM((per_dev, max(all_rows, 128)), f32),
            pltpu.VMEM((all_rows, width), f32),
            pltpu.VMEM((all_rows, width), f32),
            pltpu.VMEM((ngx, STEPS, 1, 128), f32),
            pltpu.SemaphoreType.DMA((13,)),
            pltpu.SemaphoreType.DMA((4,)),
            pltpu.SemaphoreType.DMA((8,)),
            pltpu.SemaphoreType.DMA((2, chunks, 4)),
            pltpu.SemaphoreType.DMA((STEPS, 4)),
            pltpu.SemaphoreType.DMA((2, 2)),
            pltpu.SemaphoreType.DMA((ngy // 2, 2)),
            pltpu.SemaphoreType.DMA((1,)),
            pltpu.SemaphoreType.DMA((1,)),
            pltpu.SemaphoreType.DMA((1,)),
        ],
        compiler_params=pltpu.CompilerParams(
            collective_id=0, has_side_effects=True, vmem_limit_bytes=VMEM_LIMIT
        ),
    )(
        *[in_hbm(x) for x in (velocity, pressure, memory, buoyancy, modulus, relax, strength)],
        in_hbm(spectra),
        in_hbm(patch_cell.reshape(1, -1)),
        in_hbm(phase_rows(width // 2)),
        in_hbm(listed),
        in_hbm(weights),
    )


def finish(state, velocity, pressure, memory, spectra, weights):
    nz = pressure.shape[0]
    width = spectra.shape[1]
    ngy = lax.axis_size("gy")
    rup_group, slot_dev, variations = weights.shape
    share = variations // ngy
    f32 = jnp.float32
    any_spec = pl.BlockSpec(memory_space=pl.ANY)
    vmem_spec = pl.BlockSpec(memory_space=pltpu.VMEM)
    return pl.pallas_call(
        functools.partial(finish_kernel, nz),
        out_shape=[
            jax.ShapeDtypeStruct(velocity.shape, f32),
            jax.ShapeDtypeStruct(pressure.shape, f32),
            jax.ShapeDtypeStruct(memory.shape, f32),
            jax.ShapeDtypeStruct(spectra.shape, f32),
            jax.ShapeDtypeStruct((rup_group, share, width), f32),
        ],
        in_specs=[vmem_spec] * len(state),
        out_specs=[any_spec] * 5,
        scratch_shapes=[
            pltpu.VMEM((rup_group, share, width), f32),
            pltpu.VMEM(state[7].shape, jnp.bfloat16),
            pltpu.VMEM((8, state[7].shape[0]), f32),
            pltpu.SemaphoreType.DMA((6,)),
            pltpu.SemaphoreType.DMA((1,)),
        ],
        compiler_params=pltpu.CompilerParams(vmem_limit_bytes=VMEM_LIMIT),
    )(*[pltpu.with_memory_space_constraint(x, pltpu.VMEM) for x in state])


def per_device(
    velocity,
    pressure,
    memory,
    buoyancy,
    modulus,
    relax,
    strength,
    spectra,
    patch_cell,
    rupture_patches,
    slip_weights,
):
    state = advance(
        velocity,
        pressure,
        memory,
        buoyancy,
        modulus,
        relax,
        strength,
        spectra,
        patch_cell,
        rupture_patches,
        slip_weights,
    )
    return tuple(finish(state, velocity, pressure, memory, spectra, slip_weights))


def solution(mesh):
    in_specs = (
        P(None, None, "gy", "gx"),
        P(None, "gy", "gx"),
        P(None, "gy", "gx"),
        P(None, "gy", "gx"),
        P(None, "gy", "gx"),
        P(None, "gy", "gx"),
        P(None, "gy", "gx"),
        P(("gx", "gy"), None),
        P(("gx", "gy")),
        P(),
        P("gx", "gy", None),
    )
    out_specs = (
        P(None, None, "gy", "gx"),
        P(None, "gy", "gx"),
        P(None, "gy", "gx"),
        P(("gx", "gy"), None),
        P("gx", "gy", None),
    )
    return jax.shard_map(
        per_device, mesh=mesh, in_specs=in_specs, out_specs=out_specs, check_vma=False
    )
```

```python
import functools
import math

import jax
import jax.numpy as jnp
import numpy as np
from jax import lax
from jax.experimental import pallas as pl
from jax.experimental.pallas import tpu as pltpu
from jax.sharding import PartitionSpec as P

STEPS = 4
CAP = 2
BATCH = 8


def phase_rows(freqs):
    angle = np.pi * (np.arange(freqs) + 0.5) / freqs
    rows = [np.concatenate([np.cos(angle * n), -np.sin(angle * n)]) for n in range(1, STEPS + 1)]
    rows = rows + [np.zeros(2 * freqs)] * (8 - STEPS)
    return jnp.asarray(np.stack(rows).astype(np.float32))


Y_ROWS = [4, 3] + [2] * (STEPS - 2)
X_PACKS = [3, 2] + [1] * (STEPS - 2)


def quotient(value, size):
    if size & (size - 1):
        return lax.div(value, jnp.full_like(value, size))
    return lax.shift_right_logical(value, jnp.full_like(value, size.bit_length() - 1))


def remainder(value, size):
    if size & (size - 1):
        return lax.rem(value, jnp.full_like(value, size))
    return value & (size - 1)


def step_kernel(dims, *refs):
    nz, ny, nx, chunks, zc, per_dev, ngx, ngy = dims
    refs = list(refs)
    take = lambda count: [refs.pop(0) for _ in range(count)]
    vel_in, p_in, m_in, b_in, mod_in, rel_in, str_in = take(7)
    spectra_in, cell_row_in, phase_in, listed_in, weights = take(5)
    vx, vy, vz, p, m, spectra_out, mixed, rows_out, heard, phase = take(10)
    b, mod, rel, stg, vx_old, vy_old, p_old, b_east = take(8)
    ysend, xsend, csend = take(3)
    yrecv, xrecv, crecv = (take(STEPS), take(STEPS), take(STEPS))
    cell_row, listed, index_made, index = take(4)
    vxh, bwh, bxh, hx, hx_old, vyh, vyx, xj, got, shear, factors = take(11)
    hp, hv, hb, weights_got, table, columns, wide = take(7)
    placing, placed, rows_send, rows_group, told = take(5)
    in_sem, small_sem, send_sem, recv_sem, corner_sem = take(5)
    far_sem, block_sem, tell_sem, hear_sem, index_sem = take(5)

    gx, gy = (lax.axis_index("gx"), lax.axis_index("gy"))
    has = [gy > 0, gy < ngy - 1, gx > 0, gx < ngx - 1]
    has = has + [has[k // 2] & has[2 + k % 2] for k in range(4)]
    peer = [{"gy": gy - 1}, {"gy": gy + 1}, {"gx": gx - 1}, {"gx": gx + 1}]
    peer = peer + [{**peer[k // 2], **peer[2 + k % 2]} for k in range(4)]

    def load(i, h):
        cuts = [0, zc, 2 * zc, nz] if i < 4 else [0, nz // 2, nz]
        at = pl.ds(cuts[h], cuts[h + 1] - cuts[h])
        moved = pl.ds(cuts[h] + 1, cuts[h + 1] - cuts[h])
        src, dst = [
            (p_in.at[at], p_old.at[moved]),
            (b_in.at[at], b.at[at]),
            (vel_in.at[0, at], vx_old.at[at]),
            (vel_in.at[1, at], vy_old.at[at]),
            (vel_in.at[2, at], vz.at[moved]),
            (rel_in.at[at], rel.at[at]),
            (m_in.at[at], m.at[at]),
            (str_in.at[at], stg.at[at]),
            (mod_in.at[at], mod.at[at]),
        ][i]
        return pltpu.make_async_copy(src, dst, in_sem.at[i + 9 * h if h < 2 else 18 + i])

    y_row = lambda r, k: sum(Y_ROWS[:r]) + k
    x_row = lambda r, k: sum(X_PACKS[:r]) + k

    smalls = [
        pltpu.make_async_copy(src, dst, small_sem.at[i])
        for i, (src, dst) in enumerate(
            [
                (cell_row_in, cell_row),
                (listed_in, listed),
                (phase_in, phase),
                (spectra_in, spectra_out),
            ]
        )
    ]
    for small in smalls:
        small.start()
    for h in range(3):
        for i in range(4):
            load(i, h).start()
    for h in range(2):
        for i in range(4, 9):
            load(i, h).start()
    devices = ngx * ngy
    me = gx * ngy + gy
    mine = gy * ngx + gx

    def flip(j):
        index = gy
        for bit in range(j.bit_length()):
            if (j >> bit) & 1:
                step = 2**bit
                index = index + step * (1 - 2 * lax.rem(lax.div(index, step), 2))
        return index

    barrier = pltpu.get_barrier_semaphore()

    peers = [{"gx": lax.rem(gx + k, ngx)} for k in range(1, ngx)]
    peers = peers + [{"gy": lax.rem(gy + k, ngy)} for k in range(1, ngy)]
    peers = peers + [
        {"gy": lax.rem(gy + ngy + dy, ngy), "gx": lax.rem(gx + ngx + dx, ngx)}
        for dy in (-1, 1)
        for dx in (-1, 1)
    ]
    for other in peers:
        pl.semaphore_signal(
            barrier, inc=1, device_id=other, device_id_type=pl.DeviceIdType.MESH
        )

    plane = jnp.zeros((ny, nx), jnp.float32)
    for field in (p_old, p):
        field[0] = plane
        field[nz + 1] = plane
        field[nz + 2] = plane
    vz[0] = plane
    vz[nz + 1] = plane
    b[nz] = plane
    for side in range(8):

        @pl.when(jnp.logical_not(has[side]))
        def _():
            for r in range(STEPS):
                if side < 2:
                    yrecv[r][side] = jnp.zeros(yrecv[r].shape[1:], jnp.float32)
                elif side < 4:
                    xrecv[r][side - 2] = jnp.zeros(xrecv[r].shape[1:], jnp.float32)
                else:
                    crecv[r][side - 4] = jnp.zeros(crecv[r].shape[1:], jnp.float32)

    def ends(r, c, side, coming):
        k = side % 4
        if side < 2:
            there = side if coming else 1 - side
            src = ysend.at[side, c, pl.ds(y_row(r, 0), Y_ROWS[r])]
            dst = yrecv[r].at[there, c]
            arrives = there
        elif side < 4:
            there = k - 2 if coming else 3 - k
            src = xsend.at[c, pl.ds(x_row(r, 0), X_PACKS[r])]
            dst = xrecv[r].at[there, c]
            arrives = 2 + there
        else:
            there = k if coming else 3 - k
            src, dst = (csend.at[k // 2, r], crecv[r].at[there])
            arrives = 4 + there
        return pltpu.make_async_remote_copy(
            src_ref=src,
            dst_ref=dst,
            send_sem=send_sem.at[side],
            recv_sem=recv_sem.at[r % 2, c, arrives] if side < 4 else corner_sem.at[r, there],
            device_id=peer[side],
            device_id_type=pl.DeviceIdType.MESH,
        )

    def send(r, c):
        for side in range(8 if c == chunks - 1 else 4):

            @pl.when(has[side])
            def _():
                ends(r, c, side, False).start()

    def receive(r, c, sides=range(4)):
        for side in sides:

            @pl.when(has[side])
            def _():
                ends(r, c, side, True).wait_recv()

    def corners(r):
        receive(r, chunks - 1, range(4, 8))
        for c in range(chunks):
            south = jnp.where(west_half, crecv[r][0, c], crecv[r][1, c])
            north = jnp.where(west_half, crecv[r][2, c], crecv[r][3, c])
            xj[r % 2, c, 7:8, :] = south
            xj[r % 2, c, 8 + ny : 9 + ny, :] = north

    lane = lax.broadcasted_iota(jnp.int32, (ny, nx), 1)
    row = lax.broadcasted_iota(jnp.int32, (ny, nx), 0)
    quad, lane4 = (quotient(lane, 4), remainder(lane, 4))
    last_row, first_row = (row == ny - 1, row == 0)
    west_half = remainder(lax.broadcasted_iota(jnp.int32, (1, nx), 1), 4) < 2

    def pack(total, slab, zl):
        return jnp.where(quad == zl, pltpu.roll(slab, 4 * zl + 2, 1), total)

    def d_y(slab, south, north):
        after = jnp.where(last_row, north, pltpu.roll(slab, ny - 1, 0))
        before = jnp.where(first_row, south, pltpu.roll(slab, 1, 0))
        return after - before

    for c in range(chunks):
        if c < 3:
            for i in range(4):
                load(i, c).wait()

        def edges(i, totals):
            pt, vt, bt = totals
            for j in range(8):
                zl = i * 8 + j
                z = c * zc + zl
                ps, vs, ws, bs = (p_old[z + 1], vx_old[z], vy_old[z], b[z])
                pt, vt, bt = (pack(pt, ps, zl), pack(vt, vs, zl), pack(bt, bs, zl))
                at = pl.ds(zl, 1)
                ysend[0, c, y_row(0, 0), at, :] = ps[0:1]
                ysend[0, c, y_row(0, 1), at, :] = ps[1:2]
                ysend[0, c, y_row(0, 2), at, :] = ws[0:1]
                ysend[0, c, y_row(0, 3), at, :] = bs[0:1]
                ysend[1, c, y_row(0, 0), at, :] = ps[ny - 2 : ny - 1]
                ysend[1, c, y_row(0, 1), at, :] = ps[ny - 1 : ny]
                ysend[1, c, y_row(0, 2), at, :] = ws[ny - 1 : ny]
                ysend[1, c, y_row(0, 3), at, :] = bs[ny - 1 : ny]
            return pt, vt, bt

        totals = lax.fori_loop(0, zc // 8, edges, (plane, plane, plane))
        for i, total in enumerate(totals):
            xsend[c, x_row(0, i)] = total
        csend[0, 0, c] = totals[0][0:1]
        csend[1, 0, c] = totals[0][ny - 1 : ny]
        if c == 0:
            pl.semaphore_wait(barrier, len(peers))
        send(0, c)

    rup_group, slot_dev, variations = weights.shape
    lanes = weights_got.shape[3]
    group_rows = ngy * CAP
    all_rows = ngx * group_rows

    def weight_block(other):
        block = other * (variations // ngy) // lanes
        return weights.at[:, :, pl.ds(pl.multiple_of(block * lanes, lanes), lanes)]

    def far(kind, k, src, dst):
        axis, size = ("gx", ngx) if kind == 1 else ("gy", ngy)
        return pltpu.make_async_remote_copy(
            src_ref=src,
            dst_ref=dst,
            send_sem=far_sem.at[kind, 0],
            recv_sem=far_sem.at[kind, 1],
            device_id={axis: lax.rem(lax.axis_index(axis) + k, size)},
            device_id_type=pl.DeviceIdType.MESH,
        )

    def settle(ref, sem):
        pltpu.make_async_copy(ref, ref, sem).wait()

    def rows_of(ref, index, count):
        return ref.at[pl.ds(pl.multiple_of(index * count, count), count)]

    def weights_to(k):
        return far(0, k, weight_block(lax.rem(gy + k, ngy)), weights_got.at[gy])

    def first_to(k):
        src = rows_of(rows_send, lax.rem(gx + k, ngx), group_rows)
        return far(1, k, src, rows_of(rows_group, gx, group_rows))

    half = all_rows // 2

    def block_rows(owner, h):
        at = pl.multiple_of(owner * all_rows + h * half, half)
        return rows_out.at[pl.ds(at, half)]

    def carry_over(j, h, src, dst, partner):
        return pltpu.make_async_remote_copy(
            src_ref=src,
            dst_ref=dst,
            send_sem=block_sem.at[0, 1],
            recv_sem=block_sem.at[0, 0] if j % 2 else block_sem.at[j // 2, h],
            device_id={"gy": partner},
            device_id_type=pl.DeviceIdType.MESH,
        )

    def direct_to(j, h):
        return carry_over(
            j, h, rows_group.at[pl.ds(h * half, half)], block_rows(gy, h), flip(j)
        )

    def pass_on(j, h):
        block = block_rows(flip(j), h)
        return carry_over(j + 1, h, block, block, flip(1))

    def block_from(j, h):
        block = block_rows(flip(j), h)
        return carry_over(j, h, block, block, flip(1 if j % 2 else j))

    def tell_all():
        pltpu.make_async_copy(told.at[gx], heard.at[mine], hear_sem.at[0]).start()
        flips = [flip(j) for j in range(ngy)]

        def tell(x, y):
            pltpu.make_async_remote_copy(
                src_ref=told.at[x],
                dst_ref=heard.at[mine],
                send_sem=tell_sem.at[0],
                recv_sem=hear_sem.at[0],
                device_id={"gx": x, "gy": y},
                device_id_type=pl.DeviceIdType.MESH,
            ).start()

        for i in range(ngx):
            x = jnp.where(gx < ngx // 2, ngx - 1 - i, i)
            for j in range(ngy - 1, 0, -1):
                tell(x, flips[j])

            @pl.when(x != gx)
            def _():
                tell(x, gy)

    own_weights = pltpu.make_async_copy(weight_block(gy), weights_got.at[gy], far_sem.at[0, 1])

    square = (per_dev, per_dev)
    eye = lax.broadcasted_iota(jnp.int32, square, 0) == lax.broadcasted_iota(jnp.int32, square, 1)

    def to_row(column):
        return jnp.sum(jnp.where(eye, column, 0.0), axis=0, keepdims=True)

    def to_column(line):
        return jnp.sum(jnp.where(eye, line, 0.0), axis=1, keepdims=True)

    def fill_placing():
        ruptures, slots = listed.shape
        shape = (per_dev, slots)
        own_ids = lax.broadcasted_iota(jnp.int32, shape, 0) + (gx * ngy + gy) * per_dev
        slot_owner = quotient(lax.broadcasted_iota(jnp.int32, shape, 1), slot_dev)

        def body(r, best):
            owner = quotient(r, rup_group) * ngy + slot_owner
            return jnp.where(listed[pl.ds(r, 1), :] == own_ids, owner, best)

        best = lax.fori_loop(0, ruptures, body, jnp.full(shape, -1, jnp.int32))
        target = jnp.max(best.astype(jnp.float32), axis=1, keepdims=True)
        before = lax.broadcasted_iota(jnp.int32, square, 1) < lax.broadcasted_iota(
            jnp.int32, square, 0
        )
        same = (to_row(target) == target) & before
        rank = jnp.sum(jnp.where(same, 1.0, 0.0), axis=1, keepdims=True)
        bucket = jnp.where(target >= 0.0, target * CAP + rank, -1.0)
        spot = lax.broadcasted_iota(jnp.int32, placed.shape, 1).astype(jnp.float32)
        placed[...] = jnp.where(spot == bucket, 1.0, 0.0)
        place = lax.broadcasted_iota(jnp.int32, placing.shape, 0).astype(jnp.float32)
        placing[...] = jnp.where(place == to_row(bucket), 1.0, 0.0)

    def fill_table():
        slot_count = listed.shape[1]
        shape = table.shape
        spot = lax.broadcasted_iota(jnp.int32, shape, 1)
        owner, place = (quotient(spot, slot_dev), remainder(spot, slot_dev))
        table[...] = jnp.full(shape, -1, jnp.int32)
        group = pl.ds(pl.multiple_of(gx * rup_group, rup_group), rup_group)
        table[:, :slot_count] = listed[group, :]
        ids = table[...]
        source = quotient(ids, per_dev)

        def earlier(i, rank):
            shift = i - (slot_dev - 1)
            inside = (place >= shift) & (place < shift + slot_dev)
            turned = pltpu.roll(ids, jnp.where(shift < 0, shift + shape[1], shift), 1)
            for k in range(rup_group):
                other = pltpu.roll(turned, k, 0) if k else turned
                found = inside & (other < ids) & (quotient(other, per_dev) == source)
                rank = jnp.where(found, 1, rank)
            return rank

        shifts = 2 * slot_dev - 1
        unroll = max(k for k in range(1, 16) if shifts % k == 0)
        rank = lax.fori_loop(0, shifts, earlier, jnp.zeros(shape, jnp.int32), unroll=unroll)
        block = remainder(source, ngy) * ngx + quotient(source, ngy)
        table[...] = jnp.where(ids >= 0, (block * ngy + owner) * CAP + rank, -1)

    def halos(r, c):
        def joined(i):
            return jnp.where(lane4 < 2, xrecv[r][0, c, i], xrecv[r][1, c, i])

        west, east, own = (xrecv[r][0, c, 0], xrecv[r][1, c, 0], xsend[c, x_row(r, 0)])
        if r == 0:

            def edge(i):
                return jnp.where(lane4 == 1, xrecv[0][0, c, i], xsend[c, x_row(0, i)])

            vh, bh = (pltpu.roll(edge(1), 1, 1), pltpu.roll(edge(2), 1, 1))
            bwh[c] = bh
            bxh[c] = joined(2)
            hx_old[0, c] = pltpu.roll(xrecv[0][1, c, 2], nx - 1, 1)
            hx_old[1, c] = pltpu.roll(xrecv[0][1, c, 1], nx - 1, 1)
            vyh[0, c] = yrecv[0][0, c, 2]
            vyh[1, c] = yrecv[0][1, c, 2]
            for side in range(2):
                hb[side, c] = yrecv[0][side, c, 3]
        else:
            vh, bh = (vxh[c], bwh[c])
            if r == 1:
                vyx[c] = joined(1)
                for side in range(2):
                    hv[side, c] = yrecv[1][side, c, 2]
        for side in range(2):
            hp[r % 2, side, c] = yrecv[r][side, c, 1 - side]
        xj[r % 2, c, 8 : 8 + ny, :] = joined(0)
        vh = vh - bh * (own - pltpu.roll(west, 2, 1))
        vxh[c] = vh
        hx[c] = jnp.where(lane4 < 2, pltpu.roll(east, nx - 2, 1), vh)
        vyh[0, c] = vyh[0, c] - yrecv[0][0, c, 3] * (ysend[0, c, y_row(r, 0)] - yrecv[r][0, c, 0])
        vyh[1, c] = vyh[1, c] - yrecv[0][1, c, 3] * (yrecv[r][1, c, 1] - ysend[1, c, y_row(r, 1)])

    def sweep(r, c):
        last, first = (r == STEPS - 1, r == 0)
        n = r + 1
        p_from, w_from = (p_old, vy_old) if first else (p, vy)

        def body(i, total):
            base = i * BATCH
            z0 = c * zc + base
            ps = [p_from[z0 + 1 + j] for j in range(BATCH + 2)]
            bs = [b[z0 + j] for j in range(BATCH + 1)]
            zs = [vz[z0], vz[z0 + 1]]
            vs, ws, new_p, outer = ([], [], [], [])
            for j in range(BATCH):
                zl = base + j
                at = pl.ds(zl, 1)
                turn = nx - 2 - 4 * zl
                zs.append(vz[z0 + j + 2] - bs[j + 1] * (ps[j + 2] - ps[j]))
                outer.append(pltpu.roll(hx[c], turn, 1))
                ahead = jnp.where(lane >= nx - 2, outer[j], pltpu.roll(ps[j], nx - 2, 1))
                shifted, speed = (b_east[z0 + j], vx[z0 + j])
                if first:
                    edges_in = [pltpu.roll(hx_old[k, c], turn, 1) for k in range(2)]
                    shifted = jnp.where(lane == nx - 1, edges_in[0], shifted)
                    b_east[z0 + j] = shifted
                    speed = jnp.where(lane == nx - 1, edges_in[1], speed)
                vs.append(speed - shifted * (ahead - ps[j]))
                south, north = (yrecv[r][0, c, 1, at, :], yrecv[r][1, c, 0, at, :])
                ws.append(w_from[z0 + j] - bs[j] * d_y(ps[j], south, north))
            for j in range(BATCH):
                zl = base + j
                at = pl.ds(zl, 1)
                turned = pltpu.roll(vs[j], 2, 1)
                spread = vs[j] - jnp.where(lane < 2, outer[j], turned)
                if last:
                    vs[j] = pltpu.roll(jnp.where(lane == 1, outer[j], turned), nx - 1, 1)
                spread = spread + d_y(ws[j], vyh[0, c, at, :], vyh[1, c, at, :])
                spread = spread + (zs[j + 2] - zs[j])
                mem = m[z0 + j]
                mem = mem - rel[z0 + j] * (mem + stg[z0 + j] * spread)
                m[z0 + j] = mem
                new_p.append(ps[j] - mod[z0 + j] * (spread + mem))
            for j in range(BATCH):
                zl = base + j
                at = pl.ds(zl, 1)
                vz[z0 + j + 2] = zs[j + 2]
                vx[z0 + j] = vs[j]
                vy[z0 + j] = ws[j]
                p[z0 + j + 1] = new_p[j]
                if not last:
                    total = pack(total, new_p[j], zl)
                    ysend[0, c, y_row(n, 0), at, :] = new_p[j][0:1]
                    ysend[0, c, y_row(n, 1), at, :] = new_p[j][1:2]
                    ysend[1, c, y_row(n, 0), at, :] = new_p[j][ny - 2 : ny - 1]
                    ysend[1, c, y_row(n, 1), at, :] = new_p[j][ny - 1 : ny]
            return total

        total = plane
        for i in range(zc // BATCH):
            total = body(i, total)
        if not last:
            xsend[c, x_row(n, 0)] = total
            csend[0, n, c] = total[0:1]
            csend[1, n, c] = total[ny - 1 : ny]

    def shift(c):
        def body(i, total):
            for j in range(8):
                zl = i * 8 + j
                z = c * zc + zl
                at = pl.ds(zl, 1)
                old = vx_old[z]
                vx[z] = pltpu.roll(old, nx - 1, 1)
                b_east[z] = pltpu.roll(b[z], nx - 1, 1)
                total = pack(total, vy_old[z], zl)
                ysend[0, c, y_row(1, 2), at, :] = old[0:1]
                ysend[1, c, y_row(1, 2), at, :] = old[ny - 1 : ny]
            return total

        xsend[c, x_row(1, 1)] = lax.fori_loop(0, zc // 8, body, plane)

    told_lane = lax.broadcasted_iota(jnp.int32, (1, 128), 1)
    in_place = quotient(told_lane, group_rows) == remainder(mine, 128 // group_rows)
    patch_lane = lax.broadcasted_iota(jnp.int32, (per_dev, nx), 1)

    def masked(keep, values):
        return jnp.where(keep, values, 0.0)

    def flat(ref):
        return ref.reshape(math.prod(ref.shape[:-1]), ref.shape[-1])

    UP, DOWN, MID, HALO, EDGE, PACK = range(6)

    def make_index():
        cells = cell_row[...]
        z, y = (quotient(cells, ny * nx), remainder(quotient(cells, nx), ny))
        c, zl = (quotient(z, zc), remainder(z, zc))
        side = jnp.where(y == 0, 0, 1)
        rows = [
            z * ny + jnp.minimum(y + 1, ny - 1),
            z * ny + jnp.maximum(y - 1, 0),
            z * ny + y,
            (side * chunks + c) * zc + zl,
            c * (ny + 16) + y,
            c * ny + y,
        ]
        index_made[...] = jnp.zeros(index_made.shape, jnp.int32)
        for k, values in enumerate(rows):
            index_made[k : k + 1, :per_dev] = values

    def gather(*wanted):
        refs = [(slot, flat(ref), which, shift) for slot, ref, which, shift in wanted]

        def body(i, carry):
            at = {which: index[which, i] for which in sorted({w[2] for w in refs})}
            out = pl.ds(i, 1)
            for slot, ref, which, shift in refs:
                got[slot, out, :] = ref[pl.ds(at[which] + shift, 1), :]
            return carry

        lax.fori_loop(0, per_dev, body, 0, unroll=8)

    B_OWN, P_OWN, V_OWN, P_HALO, V_HALO, B_HALO, OLD_OWN, OLD_HALO = (0, 3, 5, 8, 11, 13, 15, 17)

    def own_rows(slot, ref, shift):
        return [(slot, ref, UP, shift), (slot + 1, ref, DOWN, shift)]

    def halo_rows(slot, n):
        edge = xj.at[n % 2]
        return [
            (slot, hp.at[n % 2], HALO, 0),
            (slot + 1, edge, EDGE, 9),
            (slot + 2, edge, EDGE, 7),
        ]

    def places():
        cells = to_column(cell_row[...].astype(jnp.float32)).astype(jnp.int32)
        cell_z, cell_x = (quotient(cells, ny * nx), remainder(cells, nx))
        return cell_x, remainder(quotient(cells, nx), ny), 4 * remainder(cell_z, zc)

    def along(values):
        return jnp.sum(values, axis=1, keepdims=True)

    def note(n, value):
        shear[...] = jnp.broadcast_to(value, shear.shape)
        line = jnp.sum(placed[...] * value, axis=0, keepdims=True)
        for k in range(ngx):
            begin = k * group_rows
            tile = begin - begin % 128
            piece = line[:, tile : tile + 128]
            spread = pltpu.roll(piece, remainder(mine * group_rows + (128 - begin % 128), 128), 1)
            spread = jnp.where(in_place, spread, 0.0)
            told[k, n - 1] = spread
        spectra_out[...] = spectra_out[...] + value * phase[n - 1 : n, :]

    def marks():
        cell_x, cell_y, start = places()
        here = patch_lane == cell_x
        up, down = (cell_y < ny - 1, cell_y > 0)
        ahead, behind = (patch_lane == cell_x + 1, patch_lane == cell_x - 1)
        ahead_out = (patch_lane == start + 2) & (cell_x == nx - 1)
        behind_out = (patch_lane == start + 1) & (cell_x == 0)
        return here, up, down, ahead, behind, ahead_out, behind_out

    def first_shear():
        here, up, down, ahead, behind, ahead_out, behind_out = marks()
        total = masked(here, jnp.where(up, got[V_OWN], got[V_HALO]))
        total = total - masked(here, jnp.where(down, got[V_OWN + 1], got[V_HALO]))
        total = total + masked(ahead, got[V_OWN + 2]) - masked(behind, got[V_OWN + 2])
        total = total + masked(ahead_out, got[V_HALO + 1]) - masked(behind_out, got[V_HALO + 1])
        shear[...] = jnp.broadcast_to(along(total), shear.shape)

    def make_factors():
        here, up, down, ahead, behind, ahead_out, behind_out = marks()
        b_up = along(masked(here, jnp.where(up, got[B_OWN], got[B_HALO])))
        b_down = along(masked(here, jnp.where(down, got[B_OWN + 1], got[B_HALO])))
        b_mid, b_out = (got[B_OWN + 2], got[B_HALO + 1])
        b_ahead = along(masked(ahead, b_mid) + masked(ahead_out, b_out))
        b_behind = along(masked(behind, b_mid) + masked(behind_out, b_out))
        at_up = masked(behind, b_up + b_behind) - masked(ahead, b_up + b_ahead)
        at_down = masked(ahead, b_down + b_ahead) - masked(behind, b_down + b_behind)
        factors[0] = masked(up, at_up)
        factors[1] = masked(down, at_down)
        factors[2] = jnp.where(up, masked(jnp.logical_not(down), at_down), at_up)
        factors[3] = masked(behind_out, b_up + b_behind) - masked(ahead_out, b_up + b_ahead)
        factors[4] = masked(ahead_out, b_down + b_ahead) - masked(behind_out, b_down + b_behind)

    def next_shear(n, own=P_OWN, halo=P_HALO):
        rows = [own, own + 1, halo, halo + 1, halo + 2]
        total = factors[0] * got[rows[0]]
        for k in range(1, 5):
            total = total + factors[k] * got[rows[k]]
        note(n, shear[:, 0:1] + along(total))

    for small in smalls:
        small.wait()
    make_index()
    index_copy = pltpu.make_async_copy(index_made, index, index_sem.at[0])
    index_copy.start()
    for c in range(2):
        shift(c)
    for i in range(4, 9):
        load(i, 0).wait()

    def send_rows():
        fill_placing()
        rows_send[...] = jnp.dot(
            placing[...],
            spectra_out[...],
            preferred_element_type=jnp.float32,
            precision=lax.Precision.HIGHEST,
        )
        for k in range(1, ngx):
            first_to(k).start()
        at = pl.ds(pl.multiple_of(gx * group_rows, group_rows), group_rows)
        rows_group[at, :] = rows_send[at, :]

    def mix():
        slot_count = slot_dev * ngy
        lines = min(slot_count, 128)
        depth = min(mixed.shape[1], 512)
        share = mixed.shape[0] // rup_group
        begin = pl.multiple_of(lax.rem(gy * share, lanes), share)
        block = (lines, lines)
        own_line = lax.broadcasted_iota(jnp.int32, block, 0) == lax.broadcasted_iota(
            jnp.int32, block, 1
        )
        row_at = lax.broadcasted_iota(jnp.int32, (slot_count, depth), 1)
        for r in range(rup_group):
            for k in range(slot_count // lines):
                line = table[r : r + 1, k * lines : (k + 1) * lines].astype(jnp.float32)
                column = jnp.sum(jnp.where(own_line, line, 0.0), axis=1, keepdims=True)
                at = pl.ds(k * lines, lines)
                columns[r, at, :] = jnp.broadcast_to(
                    column.astype(jnp.int32), (lines, columns.shape[2])
                )

        def blend(r, k):
            base = k * depth
            chosen = jnp.where(row_at + base == columns[r, :, 0:1], 1.0, 0.0).astype(jnp.bfloat16)
            own = weights_got[:, r].astype(jnp.float32).reshape(slot_count, lanes)
            spread = lax.dot_general(
                own.astype(jnp.bfloat16),
                chosen,
                (((0,), (0,)), ((), ())),
                preferred_element_type=jnp.float32,
            )
            wide[r] = spread
            rows = pl.ds(r * share, share)
            mixed[rows, pl.ds(base, depth)] = wide[r, pl.ds(begin, share), :].astype(jnp.bfloat16)

        for r in range(rup_group):
            if mixed.shape[1] == depth:
                blend(r, 0)
            else:

                @pl.loop(0, mixed.shape[1] // depth)
                def _(k):
                    blend(r, k)

    def work_after(r):
        corners(r)
        if r == 0:
            index_copy.wait()
            gather(
                *own_rows(B_OWN, b, 0),
                (B_OWN + 2, b, MID, 0),
                *own_rows(V_OWN, vx_old, 0),
                (V_OWN + 2, vy_old, MID, 0),
                (B_HALO, hb, HALO, 0),
                (B_HALO + 1, bxh, PACK, 0),
                *own_rows(OLD_OWN, p_old, ny),
                *halo_rows(OLD_HALO, 0),
                *own_rows(P_OWN, p, ny),
            )
            make_factors()
        elif r == 1:
            gather(*halo_rows(P_HALO, 1), (V_HALO, hv, HALO, 0), (V_HALO + 1, vyx, PACK, 0))
            first_shear()
            next_shear(1, OLD_OWN, OLD_HALO)
            next_shear(2)
            gather(*own_rows(P_OWN, p, ny))
        elif r < STEPS - 1:
            gather(*halo_rows(P_HALO, r))
            next_shear(r + 1)
            gather(*own_rows(P_OWN, p, ny))

    def last_shear():
        corners(STEPS - 1)
        gather(*halo_rows(P_HALO, STEPS - 1))
        next_shear(STEPS)
        tell_all()

    gaps = [(r, c) for r in range(STEPS - 1) for c in range(chunks)][chunks + 1 :]
    jobs = {gap: [] for gap in gaps + [None]}
    order = list(jobs)
    pieces = [(j, h) for j in range(2, ngy, 2) for h in range(2)]

    def enter_rows():
        settle(rows_group.at[pl.ds(0, (ngx - 1) * group_rows)], far_sem.at[1, 1])
        at = pl.ds(pl.multiple_of(gy * all_rows, all_rows), all_rows)
        rows_out[at, :] = rows_group[...]
        for h in range(2):
            direct_to(1, h).start()
        own_weights.start()

    def leave(j, h):
        direct_to(j, h).start()

    def forward(j, h):
        block_from(j, h).wait_recv()
        pass_on(j, h).start()

    jobs[order[0]].append(enter_rows)
    for i, (j, h) in enumerate(pieces):
        place = i * len(gaps) // len(pieces)
        jobs[order[place]].append(functools.partial(leave, j, h))
        after = order[min(place + 5, len(order) - 1)]
        jobs[after].append(functools.partial(forward, j, h))
    send_rows()
    for r in range(STEPS):
        above = p_old if r == 0 else p
        vz[1] = vz[1] - b[0] * (above[2] - above[0])
        for c in range(chunks):
            if r == STEPS - 1 and c == 0:
                for k in range(1, ngy):
                    weights_to(k).start()
            receive(r, c)
            halos(r, c)
            if r == 0 and c >= 2:
                shift(c)
            if r == 0 and c == 1:
                for i in range(4, 9):
                    load(i, 1).wait()
            if r == STEPS - 1 and c == chunks - 1:
                last_shear()
            sweep(r, c)
            if r < STEPS - 1:
                send(r + 1, c)
            for job in jobs.get((r, c), []):
                job()
        if r < STEPS - 1:
            work_after(r)
    for job in jobs[None]:
        job()
    fill_table()
    for side in range(8):

        @pl.when(has[side])
        def _():
            sent = ysend.at[side] if side < 2 else xsend if side < 4 else csend.at[side // 2 - 2]
            settle(sent, send_sem.at[side])

    settle(weights_got.at[pl.ds(0, ngy - 1)], far_sem.at[0, 0])
    settle(weights_got, far_sem.at[0, 1])
    mix()
    settle(rows_group.at[pl.ds(0, (ngx - 1) * group_rows)], far_sem.at[1, 0])
    settle(rows_out.at[pl.ds(0, (ngy - 1) * all_rows)], block_sem.at[0, 1])
    settle(rows_out.at[pl.ds(0, ngy // 2 * all_rows)], block_sem.at[0, 0])
    settle(heard.at[pl.ds(1, devices - 1)], tell_sem.at[0])
    settle(heard, hear_sem.at[0])


def finish_kernel(nz, *refs):
    refs = list(refs)
    take = lambda count: [refs.pop(0) for _ in range(count)]
    vx, vy, vz, p, m, spectra, mixed, rows, heard, phase = take(10)
    vel_out, p_out, m_out, spectra_out, slip_out = take(5)
    slip, exact, lines_in, out_sem, slip_sem = take(5)
    inner = pl.ds(1, nz)
    pairs = [
        (vx, vel_out.at[0]),
        (vy, vel_out.at[1]),
        (vz.at[inner], vel_out.at[2]),
        (p.at[inner], p_out),
        (m, m_out),
        (spectra, spectra_out),
    ]
    stores = [
        pltpu.make_async_copy(src, dst, out_sem.at[i]) for i, (src, dst) in enumerate(pairs)
    ]
    for store in stores:
        store.start()

    count = heard.shape[0]
    per_tile = count * 128 // rows.shape[0]
    lines_in[...] = jnp.zeros(lines_in.shape, jnp.float32)
    for t in range(count // per_tile):
        at, of = (pl.ds(t * 128, 128), pl.ds(t * per_tile, per_tile))
        for n in range(STEPS):
            lines_in[n : n + 1, at] = jnp.sum(heard[of, n], axis=0)
    for t in range(count // per_tile):
        at = pl.ds(t * 128, 128)
        change = lax.dot_general(
            lines_in[:, at],
            phase[...],
            (((0,), (0,)), ((), ())),
            preferred_element_type=jnp.float32,
            precision=lax.Precision.HIGHEST,
        )
        exact[at, :] = (rows[at, :] + change).astype(jnp.bfloat16)
    rup_group, share = slip.shape[:2]
    response = jnp.dot(mixed[...], exact[...], preferred_element_type=jnp.float32)
    slip[...] = response.reshape(slip.shape)
    answer = pltpu.make_async_copy(slip, slip_out, slip_sem.at[0])
    answer.start()
    for store in stores:
        store.wait()
    answer.wait()


VMEM_LIMIT = 40 * 1024 * 1024


def in_hbm(x):
    return pltpu.with_memory_space_constraint(x, pltpu.HBM)


def advance(
    velocity, pressure, memory, buoyancy, modulus, relax, strength, spectra, patch_cell, listed, weights
):
    nz, ny, nx = pressure.shape
    per_dev, width = spectra.shape
    zc = nx // 8
    chunks = nz // zc
    ngx, ngy = (lax.axis_size("gx"), lax.axis_size("gy"))
    dims = (nz, ny, nx, chunks, zc, per_dev, ngx, ngy)
    rup_group, slot_dev, variations = weights.shape
    lanes = max(variations // ngy, 128)
    all_rows = ngx * ngy * CAP
    f32 = jnp.float32
    field = lambda planes: pltpu.VMEM((planes, ny, nx), f32)
    rounds = range(STEPS)
    any_spec = pl.BlockSpec(memory_space=pl.ANY)
    vmem_spec = pl.BlockSpec(memory_space=pltpu.VMEM)
    return pl.pallas_call(
        functools.partial(step_kernel, dims),
        out_shape=[
            field(nz),
            field(nz),
            field(nz + 2),
            field(nz + 3),
            field(nz),
            pltpu.VMEM(spectra.shape, f32),
            pltpu.VMEM((rup_group * (variations // ngy), ngy * all_rows), jnp.bfloat16),
            pltpu.VMEM((ngy * all_rows, width), f32),
            pltpu.VMEM((ngx * ngy, STEPS, 1, 128), f32),
            pltpu.VMEM((8, width), f32),
        ],
        in_specs=[any_spec] * 12,
        out_specs=[vmem_spec] * 10,
        scratch_shapes=[field(nz + 1), field(nz), field(nz), field(nz)]
        + [field(nz), field(nz), field(nz + 3), field(nz)]
        + [
            pltpu.VMEM((2, chunks, sum(Y_ROWS), zc, nx), f32),
            pltpu.VMEM((chunks, sum(X_PACKS), ny, nx), f32),
            pltpu.VMEM((2, STEPS, chunks, 1, nx), f32),
        ]
        + [pltpu.VMEM((2, chunks, Y_ROWS[r], zc, nx), f32) for r in rounds]
        + [pltpu.VMEM((2, chunks, X_PACKS[r], ny, nx), f32) for r in rounds]
        + [pltpu.VMEM((4, chunks, 1, nx), f32) for r in rounds]
        + [
            pltpu.VMEM((1, per_dev), jnp.int32),
            pltpu.VMEM(listed.shape, jnp.int32),
            pltpu.VMEM((8, max(per_dev, 128)), jnp.int32),
            pltpu.SMEM((8, max(per_dev, 128)), jnp.int32),
            pltpu.VMEM((chunks, ny, nx), f32),
            pltpu.VMEM((chunks, ny, nx), f32),
            pltpu.VMEM((chunks, ny, nx), f32),
            pltpu.VMEM((chunks, ny, nx), f32),
            pltpu.VMEM((2, chunks, ny, nx), f32),
            pltpu.VMEM((2, chunks, zc, nx), f32),
            pltpu.VMEM((chunks, ny, nx), f32),
            pltpu.VMEM((2, chunks, ny + 16, nx), f32),
            pltpu.VMEM((20, per_dev, nx), f32),
            pltpu.VMEM((per_dev, nx), f32),
            pltpu.VMEM((5, per_dev, nx), f32),
            pltpu.VMEM((2, 2, chunks, zc, nx), f32),
            pltpu.VMEM((2, chunks, zc, nx), f32),
            pltpu.VMEM((2, chunks, zc, nx), f32),
            pltpu.VMEM((ngy, rup_group, slot_dev, lanes), jnp.bfloat16),
            pltpu.VMEM((rup_group, max(listed.shape[1], 128)), jnp.int32),
            pltpu.VMEM((rup_group, listed.shape[1], 128), jnp.int32),
            pltpu.VMEM((rup_group, lanes, min(ngy * all_rows, 512)), f32),
            pltpu.VMEM((all_rows, per_dev), f32),
            pltpu.VMEM((per_dev, max(all_rows, 128)), f32),
            pltpu.VMEM((all_rows, width), f32),
            pltpu.VMEM((all_rows, width), f32),
            pltpu.VMEM((ngx, STEPS, 1, 128), f32),
            pltpu.SemaphoreType.DMA((22,)),
            pltpu.SemaphoreType.DMA((4,)),
            pltpu.SemaphoreType.DMA((8,)),
            pltpu.SemaphoreType.DMA((2, chunks, 4)),
            pltpu.SemaphoreType.DMA((STEPS, 4)),
            pltpu.SemaphoreType.DMA((2, 2)),
            pltpu.SemaphoreType.DMA((ngy // 2, 2)),
            pltpu.SemaphoreType.DMA((1,)),
            pltpu.SemaphoreType.DMA((1,)),
            pltpu.SemaphoreType.DMA((1,)),
        ],
        compiler_params=pltpu.CompilerParams(
            collective_id=0, has_side_effects=True, vmem_limit_bytes=VMEM_LIMIT
        ),
    )(
        *[in_hbm(x) for x in (velocity, pressure, memory, buoyancy, modulus, relax, strength)],
        in_hbm(spectra),
        in_hbm(patch_cell.reshape(1, -1)),
        in_hbm(phase_rows(width // 2)),
        in_hbm(listed),
        in_hbm(weights),
    )


def finish(state, velocity, pressure, memory, spectra, weights):
    nz = pressure.shape[0]
    width = spectra.shape[1]
    ngy = lax.axis_size("gy")
    rup_group, slot_dev, variations = weights.shape
    share = variations // ngy
    f32 = jnp.float32
    any_spec = pl.BlockSpec(memory_space=pl.ANY)
    vmem_spec = pl.BlockSpec(memory_space=pltpu.VMEM)
    return pl.pallas_call(
        functools.partial(finish_kernel, nz),
        out_shape=[
            jax.ShapeDtypeStruct(velocity.shape, f32),
            jax.ShapeDtypeStruct(pressure.shape, f32),
            jax.ShapeDtypeStruct(memory.shape, f32),
            jax.ShapeDtypeStruct(spectra.shape, f32),
            jax.ShapeDtypeStruct((rup_group, share, width), f32),
        ],
        in_specs=[vmem_spec] * len(state),
        out_specs=[any_spec] * 5,
        scratch_shapes=[
            pltpu.VMEM((rup_group, share, width), f32),
            pltpu.VMEM(state[7].shape, jnp.bfloat16),
            pltpu.VMEM((8, state[7].shape[0]), f32),
            pltpu.SemaphoreType.DMA((6,)),
            pltpu.SemaphoreType.DMA((1,)),
        ],
        compiler_params=pltpu.CompilerParams(vmem_limit_bytes=VMEM_LIMIT),
    )(*[pltpu.with_memory_space_constraint(x, pltpu.VMEM) for x in state])


def per_device(
    velocity,
    pressure,
    memory,
    buoyancy,
    modulus,
    relax,
    strength,
    spectra,
    patch_cell,
    rupture_patches,
    slip_weights,
):
    state = advance(
        velocity,
        pressure,
        memory,
        buoyancy,
        modulus,
        relax,
        strength,
        spectra,
        patch_cell,
        rupture_patches,
        slip_weights,
    )
    return tuple(finish(state, velocity, pressure, memory, spectra, slip_weights))


def solution(mesh):
    in_specs = (
        P(None, None, "gy", "gx"),
        P(None, "gy", "gx"),
        P(None, "gy", "gx"),
        P(None, "gy", "gx"),
        P(None, "gy", "gx"),
        P(None, "gy", "gx"),
        P(None, "gy", "gx"),
        P(("gx", "gy"), None),
        P(("gx", "gy")),
        P(),
        P("gx", "gy", None),
    )
    out_specs = (
        P(None, None, "gy", "gx"),
        P(None, "gy", "gx"),
        P(None, "gy", "gx"),
        P(("gx", "gy"), None),
        P("gx", "gy", None),
    )
    return jax.shard_map(
        per_device, mesh=mesh, in_specs=in_specs, out_specs=out_specs, check_vma=False
    )
```

```python
import functools
import math

import jax
import jax.numpy as jnp
import numpy as np
from jax import lax
from jax.experimental import pallas as pl
from jax.experimental.pallas import tpu as pltpu
from jax.sharding import PartitionSpec as P

STEPS = 4
CAP = 2
BATCH = 8


def phase_rows(freqs):
    angle = np.pi * (np.arange(freqs) + 0.5) / freqs
    rows = [np.concatenate([np.cos(angle * n), -np.sin(angle * n)]) for n in range(1, STEPS + 1)]
    rows = rows + [np.zeros(2 * freqs)] * (8 - STEPS)
    return jnp.asarray(np.stack(rows).astype(np.float32))


Y_ROWS = [4, 3] + [2] * (STEPS - 2)
X_PACKS = [2] + [1] * (STEPS - 1)


def quotient(value, size):
    if size & (size - 1):
        return lax.div(value, jnp.full_like(value, size))
    return lax.shift_right_logical(value, jnp.full_like(value, size.bit_length() - 1))


def remainder(value, size):
    if size & (size - 1):
        return lax.rem(value, jnp.full_like(value, size))
    return value & (size - 1)


def step_kernel(dims, *refs):
    nz, ny, nx, chunks, zc, per_dev, ngx, ngy = dims
    refs = list(refs)
    take = lambda count: [refs.pop(0) for _ in range(count)]
    vel_in, p_in, m_in, b_in, mod_in, rel_in, str_in = take(7)
    spectra_in, cell_row_in, phase_in, listed_in, weights = take(5)
    vx, vy, vz, p, m, spectra_out, mixed, rows_out, heard, phase = take(10)
    b, mod, rel, stg, vx_old, vy_old, p_old, b_east = take(8)
    ysend, xsend, csend = take(3)
    yrecv, xrecv, crecv = (take(STEPS), take(STEPS), take(STEPS))
    cell_row, listed, index_made, index = take(4)
    vxh, bwh, bxh, hx, hx_old, vyh, vyx, xj, got, shear, factors = take(11)
    hp, hv, hb, vy_pack, weights_got, table, columns, wide = take(8)
    placing, placed, rows_send, rows_group, told = take(5)
    in_sem, small_sem, send_sem, recv_sem, corner_sem = take(5)
    far_sem, block_sem, tell_sem, hear_sem, index_sem = take(5)

    gx, gy = (lax.axis_index("gx"), lax.axis_index("gy"))
    has = [gy > 0, gy < ngy - 1, gx > 0, gx < ngx - 1]
    has = has + [has[k // 2] & has[2 + k % 2] for k in range(4)]
    peer = [{"gy": gy - 1}, {"gy": gy + 1}, {"gx": gx - 1}, {"gx": gx + 1}]
    peer = peer + [{**peer[k // 2], **peer[2 + k % 2]} for k in range(4)]

    def load(i, h):
        cuts = [0, zc, 2 * zc, nz] if i < 4 else [0, nz // 2, nz]
        at = pl.ds(cuts[h], cuts[h + 1] - cuts[h])
        moved = pl.ds(cuts[h] + 1, cuts[h + 1] - cuts[h])
        src, dst = [
            (p_in.at[at], p_old.at[moved]),
            (b_in.at[at], b.at[at]),
            (vel_in.at[0, at], vx_old.at[at]),
            (vel_in.at[1, at], vy_old.at[at]),
            (vel_in.at[2, at], vz.at[moved]),
            (rel_in.at[at], rel.at[at]),
            (m_in.at[at], m.at[at]),
            (str_in.at[at], stg.at[at]),
            (mod_in.at[at], mod.at[at]),
        ][i]
        return pltpu.make_async_copy(src, dst, in_sem.at[i + 9 * h if h < 2 else 18 + i])

    y_row = lambda r, k: sum(Y_ROWS[:r]) + k
    x_row = lambda r, k: sum(X_PACKS[:r]) + k

    smalls = [
        pltpu.make_async_copy(src, dst, small_sem.at[i])
        for i, (src, dst) in enumerate(
            [
                (cell_row_in, cell_row),
                (listed_in, listed),
                (phase_in, phase),
                (spectra_in, spectra_out),
            ]
        )
    ]
    for small in smalls:
        small.start()
    for h in range(3):
        for i in range(4):
            load(i, h).start()
    for h in range(2):
        for i in range(4, 9):
            load(i, h).start()
    devices = ngx * ngy
    me = gx * ngy + gy
    mine = gy * ngx + gx

    def flip(j):
        index = gy
        for bit in range(j.bit_length()):
            if (j >> bit) & 1:
                step = 2**bit
                index = index + step * (1 - 2 * lax.rem(lax.div(index, step), 2))
        return index

    barrier = pltpu.get_barrier_semaphore()

    peers = [{"gx": lax.rem(gx + k, ngx)} for k in range(1, ngx)]
    peers = peers + [{"gy": lax.rem(gy + k, ngy)} for k in range(1, ngy)]
    peers = peers + [
        {"gy": lax.rem(gy + ngy + dy, ngy), "gx": lax.rem(gx + ngx + dx, ngx)}
        for dy in (-1, 1)
        for dx in (-1, 1)
    ]
    for other in peers:
        pl.semaphore_signal(
            barrier, inc=1, device_id=other, device_id_type=pl.DeviceIdType.MESH
        )

    plane = jnp.zeros((ny, nx), jnp.float32)
    for field in (p_old, p):
        field[0] = plane
        field[nz + 1] = plane
        field[nz + 2] = plane
    vz[0] = plane
    vz[nz + 1] = plane
    b[nz] = plane
    for side in range(8):

        @pl.when(jnp.logical_not(has[side]))
        def _():
            for r in range(STEPS):
                if side < 2:
                    yrecv[r][side] = jnp.zeros(yrecv[r].shape[1:], jnp.float32)
                elif side < 4:
                    xrecv[r][side - 2] = jnp.zeros(xrecv[r].shape[1:], jnp.float32)
                else:
                    crecv[r][side - 4] = jnp.zeros(crecv[r].shape[1:], jnp.float32)

    def ends(r, c, side, coming):
        k = side % 4
        if side < 2:
            there = side if coming else 1 - side
            src = ysend.at[side, c, pl.ds(y_row(r, 0), Y_ROWS[r])]
            dst = yrecv[r].at[there, c]
            arrives = there
        elif side < 4:
            there = k - 2 if coming else 3 - k
            src = xsend.at[c, pl.ds(x_row(r, 0), X_PACKS[r])]
            dst = xrecv[r].at[there, c]
            arrives = 2 + there
        else:
            there = k if coming else 3 - k
            src, dst = (csend.at[k // 2, r], crecv[r].at[there])
            arrives = 4 + there
        return pltpu.make_async_remote_copy(
            src_ref=src,
            dst_ref=dst,
            send_sem=send_sem.at[side],
            recv_sem=recv_sem.at[r % 2, c, arrives] if side < 4 else corner_sem.at[r, there],
            device_id=peer[side],
            device_id_type=pl.DeviceIdType.MESH,
        )

    def send(r, c):
        for side in range(8 if c == chunks - 1 else 4):

            @pl.when(has[side])
            def _():
                ends(r, c, side, False).start()

    def receive(r, c, sides=range(4)):
        for side in sides:

            @pl.when(has[side])
            def _():
                ends(r, c, side, True).wait_recv()

    def corners(r):
        receive(r, chunks - 1, range(4, 8))
        for c in range(chunks):
            south = jnp.where(west_half, crecv[r][0, c], crecv[r][1, c])
            north = jnp.where(west_half, crecv[r][2, c], crecv[r][3, c])
            xj[r % 2, c, 7:8, :] = south
            xj[r % 2, c, 8 + ny : 9 + ny, :] = north

    lane = lax.broadcasted_iota(jnp.int32, (ny, nx), 1)
    row = lax.broadcasted_iota(jnp.int32, (ny, nx), 0)
    quad, lane4 = (quotient(lane, 4), remainder(lane, 4))
    last_row, first_row = (row == ny - 1, row == 0)
    west_half = remainder(lax.broadcasted_iota(jnp.int32, (1, nx), 1), 4) < 2

    def pack(total, slab, zl):
        return jnp.where(quad == zl, pltpu.roll(slab, 4 * zl + 2, 1), total)

    def d_y(slab, south, north):
        after = jnp.where(last_row, north, pltpu.roll(slab, ny - 1, 0))
        before = jnp.where(first_row, south, pltpu.roll(slab, 1, 0))
        return after - before

    for c in range(chunks):
        if c < 3:
            for i in range(4):
                load(i, c).wait()

        def edges(i, totals):
            pt, bt = totals
            for j in range(8):
                zl = i * 8 + j
                z = c * zc + zl
                ps, vs, ws, bs = (p_old[z + 1], vx_old[z], vy_old[z], b[z])
                pt, bt = (pack(pack(pt, ps, zl), vs, zl + zc), pack(bt, bs, zl))
                at = pl.ds(zl, 1)
                ysend[0, c, y_row(0, 0), at, :] = ps[0:1]
                ysend[0, c, y_row(0, 1), at, :] = ps[1:2]
                ysend[0, c, y_row(0, 2), at, :] = ws[0:1]
                ysend[0, c, y_row(0, 3), at, :] = bs[0:1]
                ysend[1, c, y_row(0, 0), at, :] = ps[ny - 2 : ny - 1]
                ysend[1, c, y_row(0, 1), at, :] = ps[ny - 1 : ny]
                ysend[1, c, y_row(0, 2), at, :] = ws[ny - 1 : ny]
                ysend[1, c, y_row(0, 3), at, :] = bs[ny - 1 : ny]
            return pt, bt

        totals = lax.fori_loop(0, zc // 8, edges, (plane, plane))
        for i, total in enumerate(totals):
            xsend[c, x_row(0, i)] = total
        csend[0, 0, c] = totals[0][0:1]
        csend[1, 0, c] = totals[0][ny - 1 : ny]
        if c == 0:
            pl.semaphore_wait(barrier, len(peers))
        send(0, c)

    rup_group, slot_dev, variations = weights.shape
    lanes = weights_got.shape[3]
    group_rows = ngy * CAP
    all_rows = ngx * group_rows

    def weight_block(other):
        block = other * (variations // ngy) // lanes
        return weights.at[:, :, pl.ds(pl.multiple_of(block * lanes, lanes), lanes)]

    def far(kind, k, src, dst):
        axis, size = ("gx", ngx) if kind == 1 else ("gy", ngy)
        return pltpu.make_async_remote_copy(
            src_ref=src,
            dst_ref=dst,
            send_sem=far_sem.at[kind, 0],
            recv_sem=far_sem.at[kind, 1],
            device_id={axis: lax.rem(lax.axis_index(axis) + k, size)},
            device_id_type=pl.DeviceIdType.MESH,
        )

    def settle(ref, sem):
        pltpu.make_async_copy(ref, ref, sem).wait()

    def rows_of(ref, index, count):
        return ref.at[pl.ds(pl.multiple_of(index * count, count), count)]

    def weights_to(k):
        return far(0, k, weight_block(lax.rem(gy + k, ngy)), weights_got.at[gy])

    def first_to(k):
        src = rows_of(rows_send, lax.rem(gx + k, ngx), group_rows)
        return far(1, k, src, rows_of(rows_group, gx, group_rows))

    half = all_rows // 2

    def block_rows(owner, h):
        at = pl.multiple_of(owner * all_rows + h * half, half)
        return rows_out.at[pl.ds(at, half)]

    def carry_over(j, h, src, dst, partner):
        return pltpu.make_async_remote_copy(
            src_ref=src,
            dst_ref=dst,
            send_sem=block_sem.at[0, 1],
            recv_sem=block_sem.at[0, 0] if j % 2 else block_sem.at[j // 2, h],
            device_id={"gy": partner},
            device_id_type=pl.DeviceIdType.MESH,
        )

    def direct_to(j, h):
        return carry_over(
            j, h, rows_group.at[pl.ds(h * half, half)], block_rows(gy, h), flip(j)
        )

    def pass_on(j, h):
        block = block_rows(flip(j), h)
        return carry_over(j + 1, h, block, block, flip(1))

    def block_from(j, h):
        block = block_rows(flip(j), h)
        return carry_over(j, h, block, block, flip(1 if j % 2 else j))

    def tell_all():
        pltpu.make_async_copy(told.at[gx], heard.at[mine], hear_sem.at[0]).start()
        flips = [flip(j) for j in range(ngy)]

        def tell(x, y):
            pltpu.make_async_remote_copy(
                src_ref=told.at[x],
                dst_ref=heard.at[mine],
                send_sem=tell_sem.at[0],
                recv_sem=hear_sem.at[0],
                device_id={"gx": x, "gy": y},
                device_id_type=pl.DeviceIdType.MESH,
            ).start()

        for i in range(ngx):
            x = jnp.where(gx < ngx // 2, ngx - 1 - i, i)
            for j in range(ngy - 1, 0, -1):
                tell(x, flips[j])

            @pl.when(x != gx)
            def _():
                tell(x, gy)

    own_weights = pltpu.make_async_copy(weight_block(gy), weights_got.at[gy], far_sem.at[0, 1])

    square = (per_dev, per_dev)
    eye = lax.broadcasted_iota(jnp.int32, square, 0) == lax.broadcasted_iota(jnp.int32, square, 1)

    def to_row(column):
        return jnp.sum(jnp.where(eye, column, 0.0), axis=0, keepdims=True)

    def to_column(line):
        return jnp.sum(jnp.where(eye, line, 0.0), axis=1, keepdims=True)

    def fill_placing():
        ruptures, slots = listed.shape
        shape = (per_dev, slots)
        own_ids = lax.broadcasted_iota(jnp.int32, shape, 0) + (gx * ngy + gy) * per_dev
        slot_owner = quotient(lax.broadcasted_iota(jnp.int32, shape, 1), slot_dev)

        def body(r, best):
            owner = quotient(r, rup_group) * ngy + slot_owner
            return jnp.where(listed[pl.ds(r, 1), :] == own_ids, owner, best)

        best = lax.fori_loop(0, ruptures, body, jnp.full(shape, -1, jnp.int32))
        target = jnp.max(best.astype(jnp.float32), axis=1, keepdims=True)
        before = lax.broadcasted_iota(jnp.int32, square, 1) < lax.broadcasted_iota(
            jnp.int32, square, 0
        )
        same = (to_row(target) == target) & before
        rank = jnp.sum(jnp.where(same, 1.0, 0.0), axis=1, keepdims=True)
        bucket = jnp.where(target >= 0.0, target * CAP + rank, -1.0)
        spot = lax.broadcasted_iota(jnp.int32, placed.shape, 1).astype(jnp.float32)
        placed[...] = jnp.where(spot == bucket, 1.0, 0.0)
        place = lax.broadcasted_iota(jnp.int32, placing.shape, 0).astype(jnp.float32)
        placing[...] = jnp.where(place == to_row(bucket), 1.0, 0.0)

    def fill_table():
        slot_count = listed.shape[1]
        shape = table.shape
        spot = lax.broadcasted_iota(jnp.int32, shape, 1)
        owner, place = (quotient(spot, slot_dev), remainder(spot, slot_dev))
        table[...] = jnp.full(shape, -1, jnp.int32)
        group = pl.ds(pl.multiple_of(gx * rup_group, rup_group), rup_group)
        table[:, :slot_count] = listed[group, :]
        ids = table[...]
        source = quotient(ids, per_dev)

        def earlier(i, rank):
            shift = i - (slot_dev - 1)
            inside = (place >= shift) & (place < shift + slot_dev)
            turned = pltpu.roll(ids, jnp.where(shift < 0, shift + shape[1], shift), 1)
            for k in range(rup_group):
                other = pltpu.roll(turned, k, 0) if k else turned
                found = inside & (other < ids) & (quotient(other, per_dev) == source)
                rank = jnp.where(found, 1, rank)
            return rank

        shifts = 2 * slot_dev - 1
        unroll = max(k for k in range(1, 16) if shifts % k == 0)
        rank = lax.fori_loop(0, shifts, earlier, jnp.zeros(shape, jnp.int32), unroll=unroll)
        block = remainder(source, ngy) * ngx + quotient(source, ngy)
        table[...] = jnp.where(ids >= 0, (block * ngy + owner) * CAP + rank, -1)

    def halos(r, c):
        def joined(i):
            return jnp.where(lane4 < 2, xrecv[r][0, c, i], xrecv[r][1, c, i])

        west, east, own = (xrecv[r][0, c, 0], xrecv[r][1, c, 0], xsend[c, x_row(r, 0)])
        if r == 0:

            def edge(i):
                return jnp.where(lane4 == 1, xrecv[0][0, c, i], xsend[c, x_row(0, i)])

            vh, bh = (pltpu.roll(edge(0), 4 * zc + 1, 1), pltpu.roll(edge(1), 1, 1))
            bwh[c] = bh
            bxh[c] = joined(1)
            hx_old[0, c] = pltpu.roll(xrecv[0][1, c, 1], nx - 1, 1)
            hx_old[1, c] = pltpu.roll(xrecv[0][1, c, 0], nx - 1 - 4 * zc, 1)
            vyh[0, c] = yrecv[0][0, c, 2]
            vyh[1, c] = yrecv[0][1, c, 2]
            for side in range(2):
                hb[side, c] = yrecv[0][side, c, 3]
        else:
            vh, bh = (vxh[c], bwh[c])
            if r == 1:
                vyx[c] = pltpu.roll(joined(0), nx - 4 * zc, 1)
                for side in range(2):
                    hv[side, c] = yrecv[1][side, c, 2]
        for side in range(2):
            hp[r % 2, side, c] = yrecv[r][side, c, 1 - side]
        xj[r % 2, c, 8 : 8 + ny, :] = joined(0)
        vh = vh - bh * (own - pltpu.roll(west, 2, 1))
        vxh[c] = vh
        hx[c] = jnp.where(lane4 < 2, pltpu.roll(east, nx - 2, 1), vh)
        vyh[0, c] = vyh[0, c] - yrecv[0][0, c, 3] * (ysend[0, c, y_row(r, 0)] - yrecv[r][0, c, 0])
        vyh[1, c] = vyh[1, c] - yrecv[0][1, c, 3] * (yrecv[r][1, c, 1] - ysend[1, c, y_row(r, 1)])

    def sweep(r, c):
        last, first = (r == STEPS - 1, r == 0)
        n = r + 1
        p_from, w_from = (p_old, vy_old) if first else (p, vy)

        def body(i, total):
            base = i * BATCH
            z0 = c * zc + base
            ps = [p_from[z0 + 1 + j] for j in range(BATCH + 2)]
            bs = [b[z0 + j] for j in range(BATCH + 1)]
            zs = [vz[z0], vz[z0 + 1]]
            vs, ws, new_p, outer = ([], [], [], [])
            for j in range(BATCH):
                zl = base + j
                at = pl.ds(zl, 1)
                turn = nx - 2 - 4 * zl
                zs.append(vz[z0 + j + 2] - bs[j + 1] * (ps[j + 2] - ps[j]))
                outer.append(pltpu.roll(hx[c], turn, 1))
                ahead = jnp.where(lane >= nx - 2, outer[j], pltpu.roll(ps[j], nx - 2, 1))
                shifted, speed = (b_east[z0 + j], vx[z0 + j])
                if first:
                    edges_in = [pltpu.roll(hx_old[k, c], turn, 1) for k in range(2)]
                    shifted = jnp.where(lane == nx - 1, edges_in[0], shifted)
                    b_east[z0 + j] = shifted
                    speed = jnp.where(lane == nx - 1, edges_in[1], speed)
                vs.append(speed - shifted * (ahead - ps[j]))
                south, north = (yrecv[r][0, c, 1, at, :], yrecv[r][1, c, 0, at, :])
                ws.append(w_from[z0 + j] - bs[j] * d_y(ps[j], south, north))
            for j in range(BATCH):
                zl = base + j
                at = pl.ds(zl, 1)
                turned = pltpu.roll(vs[j], 2, 1)
                spread = vs[j] - jnp.where(lane < 2, outer[j], turned)
                if last:
                    vs[j] = pltpu.roll(jnp.where(lane == 1, outer[j], turned), nx - 1, 1)
                spread = spread + d_y(ws[j], vyh[0, c, at, :], vyh[1, c, at, :])
                spread = spread + (zs[j + 2] - zs[j])
                mem = m[z0 + j]
                mem = mem - rel[z0 + j] * (mem + stg[z0 + j] * spread)
                m[z0 + j] = mem
                new_p.append(ps[j] - mod[z0 + j] * (spread + mem))
            for j in range(BATCH):
                zl = base + j
                at = pl.ds(zl, 1)
                vz[z0 + j + 2] = zs[j + 2]
                vx[z0 + j] = vs[j]
                vy[z0 + j] = ws[j]
                p[z0 + j + 1] = new_p[j]
                if not last:
                    total = pack(total, new_p[j], zl)
                    ysend[0, c, y_row(n, 0), at, :] = new_p[j][0:1]
                    ysend[0, c, y_row(n, 1), at, :] = new_p[j][1:2]
                    ysend[1, c, y_row(n, 0), at, :] = new_p[j][ny - 2 : ny - 1]
                    ysend[1, c, y_row(n, 1), at, :] = new_p[j][ny - 1 : ny]
            return total

        total = vy_pack[c] if first else plane
        for i in range(zc // BATCH):
            total = body(i, total)
        if not last:
            xsend[c, x_row(n, 0)] = total
            csend[0, n, c] = total[0:1]
            csend[1, n, c] = total[ny - 1 : ny]

    def shift(c):
        def body(i, total):
            for j in range(8):
                zl = i * 8 + j
                z = c * zc + zl
                at = pl.ds(zl, 1)
                old = vx_old[z]
                vx[z] = pltpu.roll(old, nx - 1, 1)
                b_east[z] = pltpu.roll(b[z], nx - 1, 1)
                total = pack(total, vy_old[z], zl + zc)
                ysend[0, c, y_row(1, 2), at, :] = old[0:1]
                ysend[1, c, y_row(1, 2), at, :] = old[ny - 1 : ny]
            return total

        vy_pack[c] = lax.fori_loop(0, zc // 8, body, plane)

    told_lane = lax.broadcasted_iota(jnp.int32, (1, 128), 1)
    in_place = quotient(told_lane, group_rows) == remainder(mine, 128 // group_rows)
    patch_lane = lax.broadcasted_iota(jnp.int32, (per_dev, nx), 1)

    def masked(keep, values):
        return jnp.where(keep, values, 0.0)

    def flat(ref):
        return ref.reshape(math.prod(ref.shape[:-1]), ref.shape[-1])

    UP, DOWN, MID, HALO, EDGE, PACK = range(6)

    def make_index():
        cells = cell_row[...]
        z, y = (quotient(cells, ny * nx), remainder(quotient(cells, nx), ny))
        c, zl = (quotient(z, zc), remainder(z, zc))
        side = jnp.where(y == 0, 0, 1)
        rows = [
            z * ny + jnp.minimum(y + 1, ny - 1),
            z * ny + jnp.maximum(y - 1, 0),
            z * ny + y,
            (side * chunks + c) * zc + zl,
            c * (ny + 16) + y,
            c * ny + y,
        ]
        index_made[...] = jnp.zeros(index_made.shape, jnp.int32)
        for k, values in enumerate(rows):
            index_made[k : k + 1, :per_dev] = values

    def gather(*wanted):
        refs = [(slot, flat(ref), which, shift) for slot, ref, which, shift in wanted]

        def body(i, carry):
            at = {which: index[which, i] for which in sorted({w[2] for w in refs})}
            out = pl.ds(i, 1)
            for slot, ref, which, shift in refs:
                got[slot, out, :] = ref[pl.ds(at[which] + shift, 1), :]
            return carry

        lax.fori_loop(0, per_dev, body, 0, unroll=8)

    B_OWN, P_OWN, V_OWN, P_HALO, V_HALO, B_HALO, OLD_OWN, OLD_HALO = (0, 3, 5, 8, 11, 13, 15, 17)

    def own_rows(slot, ref, shift):
        return [(slot, ref, UP, shift), (slot + 1, ref, DOWN, shift)]

    def halo_rows(slot, n):
        edge = xj.at[n % 2]
        return [
            (slot, hp.at[n % 2], HALO, 0),
            (slot + 1, edge, EDGE, 9),
            (slot + 2, edge, EDGE, 7),
        ]

    def places():
        cells = to_column(cell_row[...].astype(jnp.float32)).astype(jnp.int32)
        cell_z, cell_x = (quotient(cells, ny * nx), remainder(cells, nx))
        return cell_x, remainder(quotient(cells, nx), ny), 4 * remainder(cell_z, zc)

    def along(values):
        return jnp.sum(values, axis=1, keepdims=True)

    def note(n, value):
        shear[...] = jnp.broadcast_to(value, shear.shape)
        line = jnp.sum(placed[...] * value, axis=0, keepdims=True)
        for k in range(ngx):
            begin = k * group_rows
            tile = begin - begin % 128
            piece = line[:, tile : tile + 128]
            spread = pltpu.roll(piece, remainder(mine * group_rows + (128 - begin % 128), 128), 1)
            spread = jnp.where(in_place, spread, 0.0)
            told[k, n - 1] = spread
        spectra_out[...] = spectra_out[...] + value * phase[n - 1 : n, :]

    def marks():
        cell_x, cell_y, start = places()
        here = patch_lane == cell_x
        up, down = (cell_y < ny - 1, cell_y > 0)
        ahead, behind = (patch_lane == cell_x + 1, patch_lane == cell_x - 1)
        ahead_out = (patch_lane == start + 2) & (cell_x == nx - 1)
        behind_out = (patch_lane == start + 1) & (cell_x == 0)
        return here, up, down, ahead, behind, ahead_out, behind_out

    def first_shear():
        here, up, down, ahead, behind, ahead_out, behind_out = marks()
        total = masked(here, jnp.where(up, got[V_OWN], got[V_HALO]))
        total = total - masked(here, jnp.where(down, got[V_OWN + 1], got[V_HALO]))
        total = total + masked(ahead, got[V_OWN + 2]) - masked(behind, got[V_OWN + 2])
        total = total + masked(ahead_out, got[V_HALO + 1]) - masked(behind_out, got[V_HALO + 1])
        shear[...] = jnp.broadcast_to(along(total), shear.shape)

    def make_factors():
        here, up, down, ahead, behind, ahead_out, behind_out = marks()
        b_up = along(masked(here, jnp.where(up, got[B_OWN], got[B_HALO])))
        b_down = along(masked(here, jnp.where(down, got[B_OWN + 1], got[B_HALO])))
        b_mid, b_out = (got[B_OWN + 2], got[B_HALO + 1])
        b_ahead = along(masked(ahead, b_mid) + masked(ahead_out, b_out))
        b_behind = along(masked(behind, b_mid) + masked(behind_out, b_out))
        at_up = masked(behind, b_up + b_behind) - masked(ahead, b_up + b_ahead)
        at_down = masked(ahead, b_down + b_ahead) - masked(behind, b_down + b_behind)
        factors[0] = masked(up, at_up)
        factors[1] = masked(down, at_down)
        factors[2] = jnp.where(up, masked(jnp.logical_not(down), at_down), at_up)
        factors[3] = masked(behind_out, b_up + b_behind) - masked(ahead_out, b_up + b_ahead)
        factors[4] = masked(ahead_out, b_down + b_ahead) - masked(behind_out, b_down + b_behind)

    def next_shear(n, own=P_OWN, halo=P_HALO):
        rows = [own, own + 1, halo, halo + 1, halo + 2]
        total = factors[0] * got[rows[0]]
        for k in range(1, 5):
            total = total + factors[k] * got[rows[k]]
        note(n, shear[:, 0:1] + along(total))

    for small in smalls:
        small.wait()
    make_index()
    index_copy = pltpu.make_async_copy(index_made, index, index_sem.at[0])
    index_copy.start()
    for c in range(2):
        shift(c)
    for i in range(4, 9):
        load(i, 0).wait()

    def send_rows():
        fill_placing()
        rows_send[...] = jnp.dot(
            placing[...],
            spectra_out[...],
            preferred_element_type=jnp.float32,
            precision=lax.Precision.HIGHEST,
        )
        for k in range(1, ngx):
            first_to(k).start()
        at = pl.ds(pl.multiple_of(gx * group_rows, group_rows), group_rows)
        rows_group[at, :] = rows_send[at, :]

    def mix():
        slot_count = slot_dev * ngy
        lines = min(slot_count, 128)
        depth = min(mixed.shape[1], 512)
        share = mixed.shape[0] // rup_group
        begin = pl.multiple_of(lax.rem(gy * share, lanes), share)
        block = (lines, lines)
        own_line = lax.broadcasted_iota(jnp.int32, block, 0) == lax.broadcasted_iota(
            jnp.int32, block, 1
        )
        row_at = lax.broadcasted_iota(jnp.int32, (slot_count, depth), 1)
        for r in range(rup_group):
            for k in range(slot_count // lines):
                line = table[r : r + 1, k * lines : (k + 1) * lines].astype(jnp.float32)
                column = jnp.sum(jnp.where(own_line, line, 0.0), axis=1, keepdims=True)
                at = pl.ds(k * lines, lines)
                columns[r, at, :] = jnp.broadcast_to(
                    column.astype(jnp.int32), (lines, columns.shape[2])
                )

        def blend(r, k):
            base = k * depth
            chosen = jnp.where(row_at + base == columns[r, :, 0:1], 1.0, 0.0).astype(jnp.bfloat16)
            own = weights_got[:, r].astype(jnp.float32).reshape(slot_count, lanes)
            spread = lax.dot_general(
                own.astype(jnp.bfloat16),
                chosen,
                (((0,), (0,)), ((), ())),
                preferred_element_type=jnp.float32,
            )
            wide[r] = spread
            rows = pl.ds(r * share, share)
            mixed[rows, pl.ds(base, depth)] = wide[r, pl.ds(begin, share), :].astype(jnp.bfloat16)

        for r in range(rup_group):
            if mixed.shape[1] == depth:
                blend(r, 0)
            else:

                @pl.loop(0, mixed.shape[1] // depth)
                def _(k):
                    blend(r, k)

    def work_after(r):
        corners(r)
        if r == 0:
            index_copy.wait()
            gather(
                *own_rows(B_OWN, b, 0),
                (B_OWN + 2, b, MID, 0),
                *own_rows(V_OWN, vx_old, 0),
                (V_OWN + 2, vy_old, MID, 0),
                (B_HALO, hb, HALO, 0),
                (B_HALO + 1, bxh, PACK, 0),
                *own_rows(OLD_OWN, p_old, ny),
                *halo_rows(OLD_HALO, 0),
                *own_rows(P_OWN, p, ny),
            )
            make_factors()
        elif r == 1:
            gather(*halo_rows(P_HALO, 1), (V_HALO, hv, HALO, 0), (V_HALO + 1, vyx, PACK, 0))
            first_shear()
            next_shear(1, OLD_OWN, OLD_HALO)
            next_shear(2)
            gather(*own_rows(P_OWN, p, ny))
        elif r < STEPS - 1:
            gather(*halo_rows(P_HALO, r))
            next_shear(r + 1)
            gather(*own_rows(P_OWN, p, ny))

    def last_shear():
        corners(STEPS - 1)
        gather(*halo_rows(P_HALO, STEPS - 1))
        next_shear(STEPS)
        tell_all()

    gaps = [(r, c) for r in range(STEPS - 1) for c in range(chunks)][chunks + 1 :]
    jobs = {gap: [] for gap in gaps + [None]}
    order = list(jobs)
    pieces = [(j, h) for j in range(2, ngy, 2) for h in range(2)]

    def enter_rows():
        settle(rows_group.at[pl.ds(0, (ngx - 1) * group_rows)], far_sem.at[1, 1])
        at = pl.ds(pl.multiple_of(gy * all_rows, all_rows), all_rows)
        rows_out[at, :] = rows_group[...]
        for h in range(2):
            direct_to(1, h).start()
        own_weights.start()

    def leave(j, h):
        direct_to(j, h).start()

    def forward(j, h):
        block_from(j, h).wait_recv()
        pass_on(j, h).start()

    jobs[order[0]].append(enter_rows)
    for i, (j, h) in enumerate(pieces):
        place = i * len(gaps) // len(pieces)
        jobs[order[place]].append(functools.partial(leave, j, h))
        after = order[min(place + 5, len(order) - 1)]
        jobs[after].append(functools.partial(forward, j, h))
    send_rows()
    for r in range(STEPS):
        above = p_old if r == 0 else p
        vz[1] = vz[1] - b[0] * (above[2] - above[0])
        for c in range(chunks):
            if r == STEPS - 1 and c == 0:
                for k in range(1, ngy):
                    weights_to(k).start()
            receive(r, c)
            halos(r, c)
            if r == 0 and c >= 2:
                shift(c)
            if r == 0 and c == 1:
                for i in range(4, 9):
                    load(i, 1).wait()
            if r == STEPS - 1 and c == chunks - 1:
                last_shear()
            sweep(r, c)
            if r < STEPS - 1:
                send(r + 1, c)
            for job in jobs.get((r, c), []):
                job()
        if r < STEPS - 1:
            work_after(r)
    for job in jobs[None]:
        job()
    fill_table()
    for side in range(8):

        @pl.when(has[side])
        def _():
            sent = ysend.at[side] if side < 2 else xsend if side < 4 else csend.at[side // 2 - 2]
            settle(sent, send_sem.at[side])

    settle(weights_got.at[pl.ds(0, ngy - 1)], far_sem.at[0, 0])
    settle(weights_got, far_sem.at[0, 1])
    mix()
    settle(rows_group.at[pl.ds(0, (ngx - 1) * group_rows)], far_sem.at[1, 0])
    settle(rows_out.at[pl.ds(0, (ngy - 1) * all_rows)], block_sem.at[0, 1])
    settle(rows_out.at[pl.ds(0, ngy // 2 * all_rows)], block_sem.at[0, 0])
    settle(heard.at[pl.ds(1, devices - 1)], tell_sem.at[0])
    settle(heard, hear_sem.at[0])


def finish_kernel(nz, *refs):
    refs = list(refs)
    take = lambda count: [refs.pop(0) for _ in range(count)]
    vx, vy, vz, p, m, spectra, mixed, rows, heard, phase = take(10)
    vel_out, p_out, m_out, spectra_out, slip_out = take(5)
    slip, exact, lines_in, out_sem, slip_sem = take(5)
    inner = pl.ds(1, nz)
    pairs = [
        (vx, vel_out.at[0]),
        (vy, vel_out.at[1]),
        (vz.at[inner], vel_out.at[2]),
        (p.at[inner], p_out),
        (m, m_out),
        (spectra, spectra_out),
    ]
    stores = [
        pltpu.make_async_copy(src, dst, out_sem.at[i]) for i, (src, dst) in enumerate(pairs)
    ]
    for store in stores:
        store.start()

    count = heard.shape[0]
    per_tile = count * 128 // rows.shape[0]
    lines_in[...] = jnp.zeros(lines_in.shape, jnp.float32)
    for t in range(count // per_tile):
        at, of = (pl.ds(t * 128, 128), pl.ds(t * per_tile, per_tile))
        for n in range(STEPS):
            lines_in[n : n + 1, at] = jnp.sum(heard[of, n], axis=0)
    for t in range(count // per_tile):
        at = pl.ds(t * 128, 128)
        change = lax.dot_general(
            lines_in[:, at],
            phase[...],
            (((0,), (0,)), ((), ())),
            preferred_element_type=jnp.float32,
            precision=lax.Precision.HIGHEST,
        )
        exact[at, :] = (rows[at, :] + change).astype(jnp.bfloat16)
    rup_group, share = slip.shape[:2]
    response = jnp.dot(mixed[...], exact[...], preferred_element_type=jnp.float32)
    slip[...] = response.reshape(slip.shape)
    answer = pltpu.make_async_copy(slip, slip_out, slip_sem.at[0])
    answer.start()
    for store in stores:
        store.wait()
    answer.wait()


VMEM_LIMIT = 40 * 1024 * 1024


def in_hbm(x):
    return pltpu.with_memory_space_constraint(x, pltpu.HBM)


def advance(
    velocity, pressure, memory, buoyancy, modulus, relax, strength, spectra, patch_cell, listed, weights
):
    nz, ny, nx = pressure.shape
    per_dev, width = spectra.shape
    zc = nx // 8
    chunks = nz // zc
    ngx, ngy = (lax.axis_size("gx"), lax.axis_size("gy"))
    dims = (nz, ny, nx, chunks, zc, per_dev, ngx, ngy)
    rup_group, slot_dev, variations = weights.shape
    lanes = max(variations // ngy, 128)
    all_rows = ngx * ngy * CAP
    f32 = jnp.float32
    field = lambda planes: pltpu.VMEM((planes, ny, nx), f32)
    rounds = range(STEPS)
    any_spec = pl.BlockSpec(memory_space=pl.ANY)
    vmem_spec = pl.BlockSpec(memory_space=pltpu.VMEM)
    return pl.pallas_call(
        functools.partial(step_kernel, dims),
        out_shape=[
            field(nz),
            field(nz),
            field(nz + 2),
            field(nz + 3),
            field(nz),
            pltpu.VMEM(spectra.shape, f32),
            pltpu.VMEM((rup_group * (variations // ngy), ngy * all_rows), jnp.bfloat16),
            pltpu.VMEM((ngy * all_rows, width), f32),
            pltpu.VMEM((ngx * ngy, STEPS, 1, 128), f32),
            pltpu.VMEM((8, width), f32),
        ],
        in_specs=[any_spec] * 12,
        out_specs=[vmem_spec] * 10,
        scratch_shapes=[field(nz + 1), field(nz), field(nz), field(nz)]
        + [field(nz), field(nz), field(nz + 3), field(nz)]
        + [
            pltpu.VMEM((2, chunks, sum(Y_ROWS), zc, nx), f32),
            pltpu.VMEM((chunks, sum(X_PACKS), ny, nx), f32),
            pltpu.VMEM((2, STEPS, chunks, 1, nx), f32),
        ]
        + [pltpu.VMEM((2, chunks, Y_ROWS[r], zc, nx), f32) for r in rounds]
        + [pltpu.VMEM((2, chunks, X_PACKS[r], ny, nx), f32) for r in rounds]
        + [pltpu.VMEM((4, chunks, 1, nx), f32) for r in rounds]
        + [
            pltpu.VMEM((1, per_dev), jnp.int32),
            pltpu.VMEM(listed.shape, jnp.int32),
            pltpu.VMEM((8, max(per_dev, 128)), jnp.int32),
            pltpu.SMEM((8, max(per_dev, 128)), jnp.int32),
            pltpu.VMEM((chunks, ny, nx), f32),
            pltpu.VMEM((chunks, ny, nx), f32),
            pltpu.VMEM((chunks, ny, nx), f32),
            pltpu.VMEM((chunks, ny, nx), f32),
            pltpu.VMEM((2, chunks, ny, nx), f32),
            pltpu.VMEM((2, chunks, zc, nx), f32),
            pltpu.VMEM((chunks, ny, nx), f32),
            pltpu.VMEM((2, chunks, ny + 16, nx), f32),
            pltpu.VMEM((20, per_dev, nx), f32),
            pltpu.VMEM((per_dev, nx), f32),
            pltpu.VMEM((5, per_dev, nx), f32),
            pltpu.VMEM((2, 2, chunks, zc, nx), f32),
            pltpu.VMEM((2, chunks, zc, nx), f32),
            pltpu.VMEM((2, chunks, zc, nx), f32),
            pltpu.VMEM((chunks, ny, nx), f32),
            pltpu.VMEM((ngy, rup_group, slot_dev, lanes), jnp.bfloat16),
            pltpu.VMEM((rup_group, max(listed.shape[1], 128)), jnp.int32),
            pltpu.VMEM((rup_group, listed.shape[1], 128), jnp.int32),
            pltpu.VMEM((rup_group, lanes, min(ngy * all_rows, 512)), f32),
            pltpu.VMEM((all_rows, per_dev), f32),
            pltpu.VMEM((per_dev, max(all_rows, 128)), f32),
            pltpu.VMEM((all_rows, width), f32),
            pltpu.VMEM((all_rows, width), f32),
            pltpu.VMEM((ngx, STEPS, 1, 128), f32),
            pltpu.SemaphoreType.DMA((22,)),
            pltpu.SemaphoreType.DMA((4,)),
            pltpu.SemaphoreType.DMA((8,)),
            pltpu.SemaphoreType.DMA((2, chunks, 4)),
            pltpu.SemaphoreType.DMA((STEPS, 4)),
            pltpu.SemaphoreType.DMA((2, 2)),
            pltpu.SemaphoreType.DMA((ngy // 2, 2)),
            pltpu.SemaphoreType.DMA((1,)),
            pltpu.SemaphoreType.DMA((1,)),
            pltpu.SemaphoreType.DMA((1,)),
        ],
        compiler_params=pltpu.CompilerParams(
            collective_id=0, has_side_effects=True, vmem_limit_bytes=VMEM_LIMIT
        ),
    )(
        *[in_hbm(x) for x in (velocity, pressure, memory, buoyancy, modulus, relax, strength)],
        in_hbm(spectra),
        in_hbm(patch_cell.reshape(1, -1)),
        in_hbm(phase_rows(width // 2)),
        in_hbm(listed),
        in_hbm(weights),
    )


def finish(state, velocity, pressure, memory, spectra, weights):
    nz = pressure.shape[0]
    width = spectra.shape[1]
    ngy = lax.axis_size("gy")
    rup_group, slot_dev, variations = weights.shape
    share = variations // ngy
    f32 = jnp.float32
    any_spec = pl.BlockSpec(memory_space=pl.ANY)
    vmem_spec = pl.BlockSpec(memory_space=pltpu.VMEM)
    return pl.pallas_call(
        functools.partial(finish_kernel, nz),
        out_shape=[
            jax.ShapeDtypeStruct(velocity.shape, f32),
            jax.ShapeDtypeStruct(pressure.shape, f32),
            jax.ShapeDtypeStruct(memory.shape, f32),
            jax.ShapeDtypeStruct(spectra.shape, f32),
            jax.ShapeDtypeStruct((rup_group, share, width), f32),
        ],
        in_specs=[vmem_spec] * len(state),
        out_specs=[any_spec] * 5,
        scratch_shapes=[
            pltpu.VMEM((rup_group, share, width), f32),
            pltpu.VMEM(state[7].shape, jnp.bfloat16),
            pltpu.VMEM((8, state[7].shape[0]), f32),
            pltpu.SemaphoreType.DMA((6,)),
            pltpu.SemaphoreType.DMA((1,)),
        ],
        compiler_params=pltpu.CompilerParams(vmem_limit_bytes=VMEM_LIMIT),
    )(*[pltpu.with_memory_space_constraint(x, pltpu.VMEM) for x in state])


def per_device(
    velocity,
    pressure,
    memory,
    buoyancy,
    modulus,
    relax,
    strength,
    spectra,
    patch_cell,
    rupture_patches,
    slip_weights,
):
    state = advance(
        velocity,
        pressure,
        memory,
        buoyancy,
        modulus,
        relax,
        strength,
        spectra,
        patch_cell,
        rupture_patches,
        slip_weights,
    )
    return tuple(finish(state, velocity, pressure, memory, spectra, slip_weights))


def solution(mesh):
    in_specs = (
        P(None, None, "gy", "gx"),
        P(None, "gy", "gx"),
        P(None, "gy", "gx"),
        P(None, "gy", "gx"),
        P(None, "gy", "gx"),
        P(None, "gy", "gx"),
        P(None, "gy", "gx"),
        P(("gx", "gy"), None),
        P(("gx", "gy")),
        P(),
        P("gx", "gy", None),
    )
    out_specs = (
        P(None, None, "gy", "gx"),
        P(None, "gy", "gx"),
        P(None, "gy", "gx"),
        P(("gx", "gy"), None),
        P("gx", "gy", None),
    )
    return jax.shard_map(
        per_device, mesh=mesh, in_specs=in_specs, out_specs=out_specs, check_vma=False
    )
```

```python
import functools
import math

import jax
import jax.numpy as jnp
import numpy as np
from jax import lax
from jax.experimental import pallas as pl
from jax.experimental.pallas import tpu as pltpu
from jax.sharding import PartitionSpec as P

STEPS = 4
CAP = 2
BATCH = 8


def phase_rows(freqs):
    angle = np.pi * (np.arange(freqs) + 0.5) / freqs
    rows = [np.concatenate([np.cos(angle * n), -np.sin(angle * n)]) for n in range(1, STEPS + 1)]
    rows = rows + [np.zeros(2 * freqs)] * (8 - STEPS)
    return jnp.asarray(np.stack(rows).astype(np.float32))


Y_ROWS = [4, 3] + [2] * (STEPS - 2)
X_PACKS = [2] + [1] * (STEPS - 1)


def quotient(value, size):
    if size & (size - 1):
        return lax.div(value, jnp.full_like(value, size))
    return lax.shift_right_logical(value, jnp.full_like(value, size.bit_length() - 1))


def remainder(value, size):
    if size & (size - 1):
        return lax.rem(value, jnp.full_like(value, size))
    return value & (size - 1)


def step_kernel(dims, *refs):
    nz, ny, nx, chunks, zc, per_dev, ngx, ngy = dims
    refs = list(refs)
    take = lambda count: [refs.pop(0) for _ in range(count)]
    vel_in, p_in, m_in, b_in, mod_in, rel_in, str_in = take(7)
    spectra_in, cell_row_in, phase_in, listed_in, weights = take(5)
    vx, vy, vz, p, m, spectra_out, mixed, rows_out, heard, phase = take(10)
    b, mod, rel, stg, vx_old, vy_old, p_old, b_east = take(8)
    ysend, xsend, csend = take(3)
    yrecv, xrecv, crecv = (take(STEPS), take(STEPS), take(STEPS))
    cell_row, listed, index_made, index = take(4)
    vxh, bwh, bxh, hx, hx_old, vyh, vyx, xj, got, shear, factors = take(11)
    hp, hv, hb, vy_pack, weights_got, table, columns, wide = take(8)
    placing, placed, rows_send, rows_group, told = take(5)
    in_sem, small_sem, send_sem, recv_sem, corner_sem = take(5)
    far_sem, block_sem, tell_sem, hear_sem, index_sem = take(5)

    gx, gy = (lax.axis_index("gx"), lax.axis_index("gy"))
    has = [gy > 0, gy < ngy - 1, gx > 0, gx < ngx - 1]
    has = has + [has[k // 2] & has[2 + k % 2] for k in range(4)]
    peer = [{"gy": gy - 1}, {"gy": gy + 1}, {"gx": gx - 1}, {"gx": gx + 1}]
    peer = peer + [{**peer[k // 2], **peer[2 + k % 2]} for k in range(4)]

    def load(i, h):
        cuts = [0, zc, nz] if i < 4 else [0, nz // 2, nz]
        at = pl.ds(cuts[h], cuts[h + 1] - cuts[h])
        moved = pl.ds(cuts[h] + 1, cuts[h + 1] - cuts[h])
        src, dst = [
            (p_in.at[at], p_old.at[moved]),
            (b_in.at[at], b.at[at]),
            (vel_in.at[0, at], vx_old.at[at]),
            (vel_in.at[1, at], vy_old.at[at]),
            (vel_in.at[2, at], vz.at[moved]),
            (rel_in.at[at], rel.at[at]),
            (m_in.at[at], m.at[at]),
            (str_in.at[at], stg.at[at]),
            (mod_in.at[at], mod.at[at]),
        ][i]
        return pltpu.make_async_copy(src, dst, in_sem.at[i + 9 * h])

    y_row = lambda r, k: sum(Y_ROWS[:r]) + k
    x_row = lambda r, k: sum(X_PACKS[:r]) + k

    smalls = [
        pltpu.make_async_copy(src, dst, small_sem.at[i])
        for i, (src, dst) in enumerate(
            [
                (cell_row_in, cell_row),
                (listed_in, listed),
                (phase_in, phase),
                (spectra_in, spectra_out),
            ]
        )
    ]
    for small in smalls:
        small.start()
    for h in range(2):
        for i in range(4):
            load(i, h).start()
    for h in range(2):
        for i in range(4, 9):
            load(i, h).start()
    devices = ngx * ngy
    me = gx * ngy + gy
    mine = gy * ngx + gx

    def flip(j):
        index = gy
        for bit in range(j.bit_length()):
            if (j >> bit) & 1:
                step = 2**bit
                index = index + step * (1 - 2 * lax.rem(lax.div(index, step), 2))
        return index

    barrier = pltpu.get_barrier_semaphore()

    peers = [{"gx": lax.rem(gx + k, ngx)} for k in range(1, ngx)]
    peers = peers + [{"gy": lax.rem(gy + k, ngy)} for k in range(1, ngy)]
    peers = peers + [
        {"gy": lax.rem(gy + ngy + dy, ngy), "gx": lax.rem(gx + ngx + dx, ngx)}
        for dy in (-1, 1)
        for dx in (-1, 1)
    ]
    for other in peers:
        pl.semaphore_signal(
            barrier, inc=1, device_id=other, device_id_type=pl.DeviceIdType.MESH
        )

    plane = jnp.zeros((ny, nx), jnp.float32)
    for field in (p_old, p):
        field[0] = plane
        field[nz + 1] = plane
        field[nz + 2] = plane
    vz[0] = plane
    vz[nz + 1] = plane
    b[nz] = plane
    for side in range(8):

        @pl.when(jnp.logical_not(has[side]))
        def _():
            for r in range(STEPS):
                if side < 2:
                    yrecv[r][side] = jnp.zeros(yrecv[r].shape[1:], jnp.float32)
                elif side < 4:
                    xrecv[r][side - 2] = jnp.zeros(xrecv[r].shape[1:], jnp.float32)
                else:
                    crecv[r][side - 4] = jnp.zeros(crecv[r].shape[1:], jnp.float32)

    def ends(r, c, side, coming):
        k = side % 4
        if side < 2:
            there = side if coming else 1 - side
            src = ysend.at[side, c, pl.ds(y_row(r, 0), Y_ROWS[r])]
            dst = yrecv[r].at[there, c]
            arrives = there
        elif side < 4:
            there = k - 2 if coming else 3 - k
            src = xsend.at[c, pl.ds(x_row(r, 0), X_PACKS[r])]
            dst = xrecv[r].at[there, c]
            arrives = 2 + there
        else:
            there = k if coming else 3 - k
            src, dst = (csend.at[k // 2, r], crecv[r].at[there])
            arrives = 4 + there
        return pltpu.make_async_remote_copy(
            src_ref=src,
            dst_ref=dst,
            send_sem=send_sem.at[side],
            recv_sem=recv_sem.at[r % 2, c, arrives] if side < 4 else corner_sem.at[r, there],
            device_id=peer[side],
            device_id_type=pl.DeviceIdType.MESH,
        )

    def send(r, c):
        for side in range(8 if c == chunks - 1 else 4):

            @pl.when(has[side])
            def _():
                ends(r, c, side, False).start()

    def receive(r, c, sides=range(4)):
        for side in sides:

            @pl.when(has[side])
            def _():
                ends(r, c, side, True).wait_recv()

    def corners(r):
        receive(r, chunks - 1, range(4, 8))
        for c in range(chunks):
            south = jnp.where(west_half, crecv[r][0, c], crecv[r][1, c])
            north = jnp.where(west_half, crecv[r][2, c], crecv[r][3, c])
            xj[r % 2, c, 7:8, :] = south
            xj[r % 2, c, 8 + ny : 9 + ny, :] = north

    lane = lax.broadcasted_iota(jnp.int32, (ny, nx), 1)
    row = lax.broadcasted_iota(jnp.int32, (ny, nx), 0)
    quad, lane4 = (quotient(lane, 4), remainder(lane, 4))
    last_row, first_row = (row == ny - 1, row == 0)
    west_half = remainder(lax.broadcasted_iota(jnp.int32, (1, nx), 1), 4) < 2

    def pack(total, slab, zl):
        return jnp.where(quad == zl, pltpu.roll(slab, 4 * zl + 2, 1), total)

    def d_y(slab, south, north):
        after = jnp.where(last_row, north, pltpu.roll(slab, ny - 1, 0))
        before = jnp.where(first_row, south, pltpu.roll(slab, 1, 0))
        return after - before

    for c in range(chunks):
        if c < 2:
            for i in range(4):
                load(i, c).wait()

        def edges(i, totals):
            pt, bt = totals
            for j in range(8):
                zl = i * 8 + j
                z = c * zc + zl
                ps, vs, ws, bs = (p_old[z + 1], vx_old[z], vy_old[z], b[z])
                pt, bt = (pack(pack(pt, ps, zl), vs, zl + zc), pack(bt, bs, zl))
                at = pl.ds(zl, 1)
                ysend[0, c, y_row(0, 0), at, :] = ps[0:1]
                ysend[0, c, y_row(0, 1), at, :] = ps[1:2]
                ysend[0, c, y_row(0, 2), at, :] = ws[0:1]
                ysend[0, c, y_row(0, 3), at, :] = bs[0:1]
                ysend[1, c, y_row(0, 0), at, :] = ps[ny - 2 : ny - 1]
                ysend[1, c, y_row(0, 1), at, :] = ps[ny - 1 : ny]
                ysend[1, c, y_row(0, 2), at, :] = ws[ny - 1 : ny]
                ysend[1, c, y_row(0, 3), at, :] = bs[ny - 1 : ny]
            return pt, bt

        totals = lax.fori_loop(0, zc // 8, edges, (plane, plane))
        for i, total in enumerate(totals):
            xsend[c, x_row(0, i)] = total
        csend[0, 0, c] = totals[0][0:1]
        csend[1, 0, c] = totals[0][ny - 1 : ny]
        if c == 0:
            pl.semaphore_wait(barrier, len(peers))
        send(0, c)

    rup_group, slot_dev, variations = weights.shape
    lanes = weights_got.shape[3]
    group_rows = ngy * CAP
    all_rows = ngx * group_rows

    def weight_block(other):
        block = other * (variations // ngy) // lanes
        return weights.at[:, :, pl.ds(pl.multiple_of(block * lanes, lanes), lanes)]

    def far(kind, k, src, dst):
        axis, size = ("gx", ngx) if kind == 1 else ("gy", ngy)
        return pltpu.make_async_remote_copy(
            src_ref=src,
            dst_ref=dst,
            send_sem=far_sem.at[kind, 0],
            recv_sem=far_sem.at[kind, 1],
            device_id={axis: lax.rem(lax.axis_index(axis) + k, size)},
            device_id_type=pl.DeviceIdType.MESH,
        )

    def settle(ref, sem):
        pltpu.make_async_copy(ref, ref, sem).wait()

    def rows_of(ref, index, count):
        return ref.at[pl.ds(pl.multiple_of(index * count, count), count)]

    def weights_to(k):
        return far(0, k, weight_block(lax.rem(gy + k, ngy)), weights_got.at[gy])

    def first_to(k):
        src = rows_of(rows_send, lax.rem(gx + k, ngx), group_rows)
        return far(1, k, src, rows_of(rows_group, gx, group_rows))

    half = all_rows // 2

    def block_rows(owner, h):
        at = pl.multiple_of(owner * all_rows + h * half, half)
        return rows_out.at[pl.ds(at, half)]

    def carry_over(j, h, src, dst, partner):
        return pltpu.make_async_remote_copy(
            src_ref=src,
            dst_ref=dst,
            send_sem=block_sem.at[0, 1],
            recv_sem=block_sem.at[0, 0] if j % 2 else block_sem.at[j // 2, h],
            device_id={"gy": partner},
            device_id_type=pl.DeviceIdType.MESH,
        )

    def direct_to(j, h):
        return carry_over(
            j, h, rows_group.at[pl.ds(h * half, half)], block_rows(gy, h), flip(j)
        )

    def pass_on(j, h):
        block = block_rows(flip(j), h)
        return carry_over(j + 1, h, block, block, flip(1))

    def block_from(j, h):
        block = block_rows(flip(j), h)
        return carry_over(j, h, block, block, flip(1 if j % 2 else j))

    def tell_all():
        pltpu.make_async_copy(told.at[gx], heard.at[mine], hear_sem.at[0]).start()
        flips = [flip(j) for j in range(ngy)]

        def tell(x, y):
            pltpu.make_async_remote_copy(
                src_ref=told.at[x],
                dst_ref=heard.at[mine],
                send_sem=tell_sem.at[0],
                recv_sem=hear_sem.at[0],
                device_id={"gx": x, "gy": y},
                device_id_type=pl.DeviceIdType.MESH,
            ).start()

        for i in range(ngx):
            x = jnp.where(gx < ngx // 2, ngx - 1 - i, i)
            for j in range(ngy - 1, 0, -1):
                tell(x, flips[j])

            @pl.when(x != gx)
            def _():
                tell(x, gy)

    own_weights = pltpu.make_async_copy(weight_block(gy), weights_got.at[gy], far_sem.at[0, 1])

    square = (per_dev, per_dev)
    eye = lax.broadcasted_iota(jnp.int32, square, 0) == lax.broadcasted_iota(jnp.int32, square, 1)

    def to_row(column):
        return jnp.sum(jnp.where(eye, column, 0.0), axis=0, keepdims=True)

    def to_column(line):
        return jnp.sum(jnp.where(eye, line, 0.0), axis=1, keepdims=True)

    def fill_placing():
        ruptures, slots = listed.shape
        shape = (per_dev, slots)
        own_ids = lax.broadcasted_iota(jnp.int32, shape, 0) + (gx * ngy + gy) * per_dev
        slot_owner = quotient(lax.broadcasted_iota(jnp.int32, shape, 1), slot_dev)

        def body(r, best):
            owner = quotient(r, rup_group) * ngy + slot_owner
            return jnp.where(listed[pl.ds(r, 1), :] == own_ids, owner, best)

        best = lax.fori_loop(0, ruptures, body, jnp.full(shape, -1, jnp.int32))
        target = jnp.max(best.astype(jnp.float32), axis=1, keepdims=True)
        before = lax.broadcasted_iota(jnp.int32, square, 1) < lax.broadcasted_iota(
            jnp.int32, square, 0
        )
        same = (to_row(target) == target) & before
        rank = jnp.sum(jnp.where(same, 1.0, 0.0), axis=1, keepdims=True)
        bucket = jnp.where(target >= 0.0, target * CAP + rank, -1.0)
        spot = lax.broadcasted_iota(jnp.int32, placed.shape, 1).astype(jnp.float32)
        placed[...] = jnp.where(spot == bucket, 1.0, 0.0)
        place = lax.broadcasted_iota(jnp.int32, placing.shape, 0).astype(jnp.float32)
        placing[...] = jnp.where(place == to_row(bucket), 1.0, 0.0)

    def fill_table():
        slot_count = listed.shape[1]
        shape = table.shape
        spot = lax.broadcasted_iota(jnp.int32, shape, 1)
        owner, place = (quotient(spot, slot_dev), remainder(spot, slot_dev))
        table[...] = jnp.full(shape, -1, jnp.int32)
        group = pl.ds(pl.multiple_of(gx * rup_group, rup_group), rup_group)
        table[:, :slot_count] = listed[group, :]
        ids = table[...]
        source = quotient(ids, per_dev)

        def earlier(i, rank):
            shift = i - (slot_dev - 1)
            inside = (place >= shift) & (place < shift + slot_dev)
            turned = pltpu.roll(ids, jnp.where(shift < 0, shift + shape[1], shift), 1)
            for k in range(rup_group):
                other = pltpu.roll(turned, k, 0) if k else turned
                found = inside & (other < ids) & (quotient(other, per_dev) == source)
                rank = jnp.where(found, 1, rank)
            return rank

        shifts = 2 * slot_dev - 1
        unroll = max(k for k in range(1, 16) if shifts % k == 0)
        rank = lax.fori_loop(0, shifts, earlier, jnp.zeros(shape, jnp.int32), unroll=unroll)
        block = remainder(source, ngy) * ngx + quotient(source, ngy)
        table[...] = jnp.where(ids >= 0, (block * ngy + owner) * CAP + rank, -1)

    def halos(r, c):
        def joined(i):
            return jnp.where(lane4 < 2, xrecv[r][0, c, i], xrecv[r][1, c, i])

        west, east, own = (xrecv[r][0, c, 0], xrecv[r][1, c, 0], xsend[c, x_row(r, 0)])
        if r == 0:

            def edge(i):
                return jnp.where(lane4 == 1, xrecv[0][0, c, i], xsend[c, x_row(0, i)])

            vh, bh = (pltpu.roll(edge(0), 4 * zc + 1, 1), pltpu.roll(edge(1), 1, 1))
            bwh[c] = bh
            bxh[c] = joined(1)
            hx_old[0, c] = pltpu.roll(xrecv[0][1, c, 1], nx - 1, 1)
            hx_old[1, c] = pltpu.roll(xrecv[0][1, c, 0], nx - 1 - 4 * zc, 1)
            vyh[0, c] = yrecv[0][0, c, 2]
            vyh[1, c] = yrecv[0][1, c, 2]
            for side in range(2):
                hb[side, c] = yrecv[0][side, c, 3]
        else:
            vh, bh = (vxh[c], bwh[c])
            if r == 1:
                vyx[c] = pltpu.roll(joined(0), nx - 4 * zc, 1)
                for side in range(2):
                    hv[side, c] = yrecv[1][side, c, 2]
        for side in range(2):
            hp[r % 2, side, c] = yrecv[r][side, c, 1 - side]
        xj[r % 2, c, 8 : 8 + ny, :] = joined(0)
        vh = vh - bh * (own - pltpu.roll(west, 2, 1))
        vxh[c] = vh
        hx[c] = jnp.where(lane4 < 2, pltpu.roll(east, nx - 2, 1), vh)
        vyh[0, c] = vyh[0, c] - yrecv[0][0, c, 3] * (ysend[0, c, y_row(r, 0)] - yrecv[r][0, c, 0])
        vyh[1, c] = vyh[1, c] - yrecv[0][1, c, 3] * (yrecv[r][1, c, 1] - ysend[1, c, y_row(r, 1)])

    def sweep(r, c):
        last, first = (r == STEPS - 1, r == 0)
        n = r + 1
        batch = zc if first else BATCH
        p_from, w_from = (p_old, vy_old) if first else (p, vy)

        def body(i, total):
            base = i * batch
            z0 = c * zc + base
            ps = [p_from[z0 + 1 + j] for j in range(batch + 2)]
            bs = [b[z0 + j] for j in range(batch + 1)]
            zs = [vz[z0], vz[z0 + 1]]
            vs, ws, new_p, outer = ([], [], [], [])
            for j in range(batch):
                zl = base + j
                at = pl.ds(zl, 1)
                turn = nx - 2 - 4 * zl
                zs.append(vz[z0 + j + 2] - bs[j + 1] * (ps[j + 2] - ps[j]))
                outer.append(pltpu.roll(hx[c], turn, 1))
                ahead = jnp.where(lane >= nx - 2, outer[j], pltpu.roll(ps[j], nx - 2, 1))
                shifted, speed = (b_east[z0 + j], vx[z0 + j])
                if first:
                    edges_in = [pltpu.roll(hx_old[k, c], turn, 1) for k in range(2)]
                    shifted = jnp.where(lane == nx - 1, edges_in[0], shifted)
                    b_east[z0 + j] = shifted
                    speed = jnp.where(lane == nx - 1, edges_in[1], speed)
                vs.append(speed - shifted * (ahead - ps[j]))
                south, north = (yrecv[r][0, c, 1, at, :], yrecv[r][1, c, 0, at, :])
                ws.append(w_from[z0 + j] - bs[j] * d_y(ps[j], south, north))
            for j in range(batch):
                zl = base + j
                at = pl.ds(zl, 1)
                turned = pltpu.roll(vs[j], 2, 1)
                spread = vs[j] - jnp.where(lane < 2, outer[j], turned)
                if last:
                    vs[j] = pltpu.roll(jnp.where(lane == 1, outer[j], turned), nx - 1, 1)
                spread = spread + d_y(ws[j], vyh[0, c, at, :], vyh[1, c, at, :])
                spread = spread + (zs[j + 2] - zs[j])
                mem = m[z0 + j]
                mem = mem - rel[z0 + j] * (mem + stg[z0 + j] * spread)
                m[z0 + j] = mem
                new_p.append(ps[j] - mod[z0 + j] * (spread + mem))
            for j in range(batch):
                zl = base + j
                at = pl.ds(zl, 1)
                vz[z0 + j + 2] = zs[j + 2]
                vx[z0 + j] = vs[j]
                vy[z0 + j] = ws[j]
                p[z0 + j + 1] = new_p[j]
                if not last:
                    total = pack(total, new_p[j], zl)
                    ysend[0, c, y_row(n, 0), at, :] = new_p[j][0:1]
                    ysend[0, c, y_row(n, 1), at, :] = new_p[j][1:2]
                    ysend[1, c, y_row(n, 0), at, :] = new_p[j][ny - 2 : ny - 1]
                    ysend[1, c, y_row(n, 1), at, :] = new_p[j][ny - 1 : ny]
            return total

        total = vy_pack[c] if first else plane
        for i in range(zc // batch):
            total = body(i, total)
        if not last:
            xsend[c, x_row(n, 0)] = total
            csend[0, n, c] = total[0:1]
            csend[1, n, c] = total[ny - 1 : ny]

    def shift(c):
        def body(i, total):
            for j in range(8):
                zl = i * 8 + j
                z = c * zc + zl
                at = pl.ds(zl, 1)
                old = vx_old[z]
                vx[z] = pltpu.roll(old, nx - 1, 1)
                b_east[z] = pltpu.roll(b[z], nx - 1, 1)
                total = pack(total, vy_old[z], zl + zc)
                ysend[0, c, y_row(1, 2), at, :] = old[0:1]
                ysend[1, c, y_row(1, 2), at, :] = old[ny - 1 : ny]
            return total

        vy_pack[c] = lax.fori_loop(0, zc // 8, body, plane)

    told_lane = lax.broadcasted_iota(jnp.int32, (1, 128), 1)
    in_place = quotient(told_lane, group_rows) == remainder(mine, 128 // group_rows)
    patch_lane = lax.broadcasted_iota(jnp.int32, (per_dev, nx), 1)

    def masked(keep, values):
        return jnp.where(keep, values, 0.0)

    def flat(ref):
        return ref.reshape(math.prod(ref.shape[:-1]), ref.shape[-1])

    UP, DOWN, MID, HALO, EDGE, PACK = range(6)

    def make_index():
        cells = cell_row[...]
        z, y = (quotient(cells, ny * nx), remainder(quotient(cells, nx), ny))
        c, zl = (quotient(z, zc), remainder(z, zc))
        side = jnp.where(y == 0, 0, 1)
        rows = [
            z * ny + jnp.minimum(y + 1, ny - 1),
            z * ny + jnp.maximum(y - 1, 0),
            z * ny + y,
            (side * chunks + c) * zc + zl,
            c * (ny + 16) + y,
            c * ny + y,
        ]
        index_made[...] = jnp.zeros(index_made.shape, jnp.int32)
        for k, values in enumerate(rows):
            index_made[k : k + 1, :per_dev] = values

    def gather(*wanted):
        refs = [(slot, flat(ref), which, shift) for slot, ref, which, shift in wanted]

        def body(i, carry):
            at = {which: index[which, i] for which in sorted({w[2] for w in refs})}
            out = pl.ds(i, 1)
            for slot, ref, which, shift in refs:
                got[slot, out, :] = ref[pl.ds(at[which] + shift, 1), :]
            return carry

        lax.fori_loop(0, per_dev, body, 0, unroll=8)

    B_OWN, P_OWN, V_OWN, P_HALO, V_HALO, B_HALO, OLD_OWN, OLD_HALO = (0, 3, 5, 8, 11, 13, 15, 17)

    def own_rows(slot, ref, shift):
        return [(slot, ref, UP, shift), (slot + 1, ref, DOWN, shift)]

    def halo_rows(slot, n):
        edge = xj.at[n % 2]
        return [
            (slot, hp.at[n % 2], HALO, 0),
            (slot + 1, edge, EDGE, 9),
            (slot + 2, edge, EDGE, 7),
        ]

    def places():
        cells = to_column(cell_row[...].astype(jnp.float32)).astype(jnp.int32)
        cell_z, cell_x = (quotient(cells, ny * nx), remainder(cells, nx))
        return cell_x, remainder(quotient(cells, nx), ny), 4 * remainder(cell_z, zc)

    def along(values):
        return jnp.sum(values, axis=1, keepdims=True)

    def note(n, value):
        shear[...] = jnp.broadcast_to(value, shear.shape)
        line = jnp.sum(placed[...] * value, axis=0, keepdims=True)
        for k in range(ngx):
            begin = k * group_rows
            tile = begin - begin % 128
            piece = line[:, tile : tile + 128]
            spread = pltpu.roll(piece, remainder(mine * group_rows + (128 - begin % 128), 128), 1)
            spread = jnp.where(in_place, spread, 0.0)
            told[k, n - 1] = spread
        spectra_out[...] = spectra_out[...] + value * phase[n - 1 : n, :]

    def marks():
        cell_x, cell_y, start = places()
        here = patch_lane == cell_x
        up, down = (cell_y < ny - 1, cell_y > 0)
        ahead, behind = (patch_lane == cell_x + 1, patch_lane == cell_x - 1)
        ahead_out = (patch_lane == start + 2) & (cell_x == nx - 1)
        behind_out = (patch_lane == start + 1) & (cell_x == 0)
        return here, up, down, ahead, behind, ahead_out, behind_out

    def first_shear():
        here, up, down, ahead, behind, ahead_out, behind_out = marks()
        total = masked(here, jnp.where(up, got[V_OWN], got[V_HALO]))
        total = total - masked(here, jnp.where(down, got[V_OWN + 1], got[V_HALO]))
        total = total + masked(ahead, got[V_OWN + 2]) - masked(behind, got[V_OWN + 2])
        total = total + masked(ahead_out, got[V_HALO + 1]) - masked(behind_out, got[V_HALO + 1])
        shear[...] = jnp.broadcast_to(along(total), shear.shape)

    def make_factors():
        here, up, down, ahead, behind, ahead_out, behind_out = marks()
        b_up = along(masked(here, jnp.where(up, got[B_OWN], got[B_HALO])))
        b_down = along(masked(here, jnp.where(down, got[B_OWN + 1], got[B_HALO])))
        b_mid, b_out = (got[B_OWN + 2], got[B_HALO + 1])
        b_ahead = along(masked(ahead, b_mid) + masked(ahead_out, b_out))
        b_behind = along(masked(behind, b_mid) + masked(behind_out, b_out))
        at_up = masked(behind, b_up + b_behind) - masked(ahead, b_up + b_ahead)
        at_down = masked(ahead, b_down + b_ahead) - masked(behind, b_down + b_behind)
        factors[0] = masked(up, at_up)
        factors[1] = masked(down, at_down)
        factors[2] = jnp.where(up, masked(jnp.logical_not(down), at_down), at_up)
        factors[3] = masked(behind_out, b_up + b_behind) - masked(ahead_out, b_up + b_ahead)
        factors[4] = masked(ahead_out, b_down + b_ahead) - masked(behind_out, b_down + b_behind)

    def next_shear(n, own=P_OWN, halo=P_HALO):
        rows = [own, own + 1, halo, halo + 1, halo + 2]
        total = factors[0] * got[rows[0]]
        for k in range(1, 5):
            total = total + factors[k] * got[rows[k]]
        note(n, shear[:, 0:1] + along(total))

    for small in smalls:
        small.wait()
    make_index()
    index_copy = pltpu.make_async_copy(index_made, index, index_sem.at[0])
    index_copy.start()
    for c in range(2):
        shift(c)
    for i in range(4, 9):
        load(i, 0).wait()

    def send_rows():
        fill_placing()
        rows_send[...] = jnp.dot(
            placing[...],
            spectra_out[...],
            preferred_element_type=jnp.float32,
            precision=lax.Precision.HIGHEST,
        )
        for k in range(1, ngx):
            first_to(k).start()
        at = pl.ds(pl.multiple_of(gx * group_rows, group_rows), group_rows)
        rows_group[at, :] = rows_send[at, :]

    def mix():
        slot_count = slot_dev * ngy
        lines = min(slot_count, 128)
        depth = min(mixed.shape[1], 512)
        share = mixed.shape[0] // rup_group
        begin = pl.multiple_of(lax.rem(gy * share, lanes), share)
        block = (lines, lines)
        own_line = lax.broadcasted_iota(jnp.int32, block, 0) == lax.broadcasted_iota(
            jnp.int32, block, 1
        )
        row_at = lax.broadcasted_iota(jnp.int32, (slot_count, depth), 1)
        for r in range(rup_group):
            for k in range(slot_count // lines):
                line = table[r : r + 1, k * lines : (k + 1) * lines].astype(jnp.float32)
                column = jnp.sum(jnp.where(own_line, line, 0.0), axis=1, keepdims=True)
                at = pl.ds(k * lines, lines)
                columns[r, at, :] = jnp.broadcast_to(
                    column.astype(jnp.int32), (lines, columns.shape[2])
                )

        def blend(r, k):
            base = k * depth
            chosen = jnp.where(row_at + base == columns[r, :, 0:1], 1.0, 0.0).astype(jnp.bfloat16)
            own = weights_got[:, r].astype(jnp.float32).reshape(slot_count, lanes)
            spread = lax.dot_general(
                own.astype(jnp.bfloat16),
                chosen,
                (((0,), (0,)), ((), ())),
                preferred_element_type=jnp.float32,
            )
            wide[r] = spread
            rows = pl.ds(r * share, share)
            mixed[rows, pl.ds(base, depth)] = wide[r, pl.ds(begin, share), :].astype(jnp.bfloat16)

        for r in range(rup_group):
            if mixed.shape[1] == depth:
                blend(r, 0)
            else:

                @pl.loop(0, mixed.shape[1] // depth)
                def _(k):
                    blend(r, k)

    def work_after(r):
        corners(r)
        if r == 0:
            index_copy.wait()
            gather(
                *own_rows(B_OWN, b, 0),
                (B_OWN + 2, b, MID, 0),
                *own_rows(V_OWN, vx_old, 0),
                (V_OWN + 2, vy_old, MID, 0),
                (B_HALO, hb, HALO, 0),
                (B_HALO + 1, bxh, PACK, 0),
                *own_rows(OLD_OWN, p_old, ny),
                *halo_rows(OLD_HALO, 0),
                *own_rows(P_OWN, p, ny),
            )
            make_factors()
        elif r == 1:
            gather(*halo_rows(P_HALO, 1), (V_HALO, hv, HALO, 0), (V_HALO + 1, vyx, PACK, 0))
            first_shear()
            next_shear(1, OLD_OWN, OLD_HALO)
            next_shear(2)
            gather(*own_rows(P_OWN, p, ny))
        elif r < STEPS - 1:
            gather(*halo_rows(P_HALO, r))
            next_shear(r + 1)
            gather(*own_rows(P_OWN, p, ny))

    def last_shear():
        corners(STEPS - 1)
        gather(*halo_rows(P_HALO, STEPS - 1))
        next_shear(STEPS)
        tell_all()

    gaps = [(r, c) for r in range(STEPS - 1) for c in range(chunks)][chunks + 1 :]
    jobs = {gap: [] for gap in gaps + [None]}
    order = list(jobs)
    pieces = [(j, h) for j in range(2, ngy, 2) for h in range(2)]

    def enter_rows():
        settle(rows_group.at[pl.ds(0, (ngx - 1) * group_rows)], far_sem.at[1, 1])
        at = pl.ds(pl.multiple_of(gy * all_rows, all_rows), all_rows)
        rows_out[at, :] = rows_group[...]
        for h in range(2):
            direct_to(1, h).start()
        own_weights.start()

    def leave(j, h):
        direct_to(j, h).start()

    def forward(j, h):
        block_from(j, h).wait_recv()
        pass_on(j, h).start()

    jobs[order[0]].append(enter_rows)
    for i, (j, h) in enumerate(pieces):
        place = i * len(gaps) // len(pieces)
        jobs[order[place]].append(functools.partial(leave, j, h))
        after = order[min(place + 5, len(order) - 1)]
        jobs[after].append(functools.partial(forward, j, h))
    send_rows()
    for r in range(STEPS):
        above = p_old if r == 0 else p
        vz[1] = vz[1] - b[0] * (above[2] - above[0])
        for c in range(chunks):
            if r == STEPS - 1 and c == 0:
                for k in range(1, ngy):
                    weights_to(k).start()
            receive(r, c)
            halos(r, c)
            if r == 0 and c >= 2:
                shift(c)
            if r == 0 and c == 1:
                for i in range(4, 9):
                    load(i, 1).wait()
            if r == STEPS - 1 and c == chunks - 1:
                last_shear()
            sweep(r, c)
            if r < STEPS - 1:
                send(r + 1, c)
            for job in jobs.get((r, c), []):
                job()
        if r < STEPS - 1:
            work_after(r)
    for job in jobs[None]:
        job()
    fill_table()
    for side in range(8):

        @pl.when(has[side])
        def _():
            sent = ysend.at[side] if side < 2 else xsend if side < 4 else csend.at[side // 2 - 2]
            settle(sent, send_sem.at[side])

    settle(weights_got.at[pl.ds(0, ngy - 1)], far_sem.at[0, 0])
    settle(weights_got, far_sem.at[0, 1])
    mix()
    settle(rows_group.at[pl.ds(0, (ngx - 1) * group_rows)], far_sem.at[1, 0])
    settle(rows_out.at[pl.ds(0, (ngy - 1) * all_rows)], block_sem.at[0, 1])
    settle(rows_out.at[pl.ds(0, ngy // 2 * all_rows)], block_sem.at[0, 0])
    settle(heard.at[pl.ds(1, devices - 1)], tell_sem.at[0])
    settle(heard, hear_sem.at[0])


def finish_kernel(nz, *refs):
    refs = list(refs)
    take = lambda count: [refs.pop(0) for _ in range(count)]
    vx, vy, vz, p, m, spectra, mixed, rows, heard, phase = take(10)
    vel_out, p_out, m_out, spectra_out, slip_out = take(5)
    slip, exact, lines_in, out_sem, slip_sem = take(5)
    inner = pl.ds(1, nz)
    pairs = [
        (vx, vel_out.at[0]),
        (vy, vel_out.at[1]),
        (vz.at[inner], vel_out.at[2]),
        (p.at[inner], p_out),
        (m, m_out),
        (spectra, spectra_out),
    ]
    stores = [
        pltpu.make_async_copy(src, dst, out_sem.at[i]) for i, (src, dst) in enumerate(pairs)
    ]
    for store in stores:
        store.start()

    count = heard.shape[0]
    per_tile = count * 128 // rows.shape[0]
    lines_in[...] = jnp.zeros(lines_in.shape, jnp.float32)
    for t in range(count // per_tile):
        at, of = (pl.ds(t * 128, 128), pl.ds(t * per_tile, per_tile))
        for n in range(STEPS):
            lines_in[n : n + 1, at] = jnp.sum(heard[of, n], axis=0)
    for t in range(count // per_tile):
        at = pl.ds(t * 128, 128)
        change = lax.dot_general(
            lines_in[:, at],
            phase[...],
            (((0,), (0,)), ((), ())),
            preferred_element_type=jnp.float32,
            precision=lax.Precision.HIGHEST,
        )
        exact[at, :] = (rows[at, :] + change).astype(jnp.bfloat16)
    rup_group, share = slip.shape[:2]
    response = jnp.dot(mixed[...], exact[...], preferred_element_type=jnp.float32)
    slip[...] = response.reshape(slip.shape)
    answer = pltpu.make_async_copy(slip, slip_out, slip_sem.at[0])
    answer.start()
    for store in stores:
        store.wait()
    answer.wait()


VMEM_LIMIT = 40 * 1024 * 1024


def in_hbm(x):
    return pltpu.with_memory_space_constraint(x, pltpu.HBM)


def advance(
    velocity, pressure, memory, buoyancy, modulus, relax, strength, spectra, patch_cell, listed, weights
):
    nz, ny, nx = pressure.shape
    per_dev, width = spectra.shape
    zc = nx // 8
    chunks = nz // zc
    ngx, ngy = (lax.axis_size("gx"), lax.axis_size("gy"))
    dims = (nz, ny, nx, chunks, zc, per_dev, ngx, ngy)
    rup_group, slot_dev, variations = weights.shape
    lanes = max(variations // ngy, 128)
    all_rows = ngx * ngy * CAP
    f32 = jnp.float32
    field = lambda planes: pltpu.VMEM((planes, ny, nx), f32)
    rounds = range(STEPS)
    any_spec = pl.BlockSpec(memory_space=pl.ANY)
    vmem_spec = pl.BlockSpec(memory_space=pltpu.VMEM)
    return pl.pallas_call(
        functools.partial(step_kernel, dims),
        out_shape=[
            field(nz),
            field(nz),
            field(nz + 2),
            field(nz + 3),
            field(nz),
            pltpu.VMEM(spectra.shape, f32),
            pltpu.VMEM((rup_group * (variations // ngy), ngy * all_rows), jnp.bfloat16),
            pltpu.VMEM((ngy * all_rows, width), f32),
            pltpu.VMEM((ngx * ngy, STEPS, 1, 128), f32),
            pltpu.VMEM((8, width), f32),
        ],
        in_specs=[any_spec] * 12,
        out_specs=[vmem_spec] * 10,
        scratch_shapes=[field(nz + 1), field(nz), field(nz), field(nz)]
        + [field(nz), field(nz), field(nz + 3), field(nz)]
        + [
            pltpu.VMEM((2, chunks, sum(Y_ROWS), zc, nx), f32),
            pltpu.VMEM((chunks, sum(X_PACKS), ny, nx), f32),
            pltpu.VMEM((2, STEPS, chunks, 1, nx), f32),
        ]
        + [pltpu.VMEM((2, chunks, Y_ROWS[r], zc, nx), f32) for r in rounds]
        + [pltpu.VMEM((2, chunks, X_PACKS[r], ny, nx), f32) for r in rounds]
        + [pltpu.VMEM((4, chunks, 1, nx), f32) for r in rounds]
        + [
            pltpu.VMEM((1, per_dev), jnp.int32),
            pltpu.VMEM(listed.shape, jnp.int32),
            pltpu.VMEM((8, max(per_dev, 128)), jnp.int32),
            pltpu.SMEM((8, max(per_dev, 128)), jnp.int32),
            pltpu.VMEM((chunks, ny, nx), f32),
            pltpu.VMEM((chunks, ny, nx), f32),
            pltpu.VMEM((chunks, ny, nx), f32),
            pltpu.VMEM((chunks, ny, nx), f32),
            pltpu.VMEM((2, chunks, ny, nx), f32),
            pltpu.VMEM((2, chunks, zc, nx), f32),
            pltpu.VMEM((chunks, ny, nx), f32),
            pltpu.VMEM((2, chunks, ny + 16, nx), f32),
            pltpu.VMEM((20, per_dev, nx), f32),
            pltpu.VMEM((per_dev, nx), f32),
            pltpu.VMEM((5, per_dev, nx), f32),
            pltpu.VMEM((2, 2, chunks, zc, nx), f32),
            pltpu.VMEM((2, chunks, zc, nx), f32),
            pltpu.VMEM((2, chunks, zc, nx), f32),
            pltpu.VMEM((chunks, ny, nx), f32),
            pltpu.VMEM((ngy, rup_group, slot_dev, lanes), jnp.bfloat16),
            pltpu.VMEM((rup_group, max(listed.shape[1], 128)), jnp.int32),
            pltpu.VMEM((rup_group, listed.shape[1], 128), jnp.int32),
            pltpu.VMEM((rup_group, lanes, min(ngy * all_rows, 512)), f32),
            pltpu.VMEM((all_rows, per_dev), f32),
            pltpu.VMEM((per_dev, max(all_rows, 128)), f32),
            pltpu.VMEM((all_rows, width), f32),
            pltpu.VMEM((all_rows, width), f32),
            pltpu.VMEM((ngx, STEPS, 1, 128), f32),
            pltpu.SemaphoreType.DMA((18,)),
            pltpu.SemaphoreType.DMA((4,)),
            pltpu.SemaphoreType.DMA((8,)),
            pltpu.SemaphoreType.DMA((2, chunks, 4)),
            pltpu.SemaphoreType.DMA((STEPS, 4)),
            pltpu.SemaphoreType.DMA((2, 2)),
            pltpu.SemaphoreType.DMA((ngy // 2, 2)),
            pltpu.SemaphoreType.DMA((1,)),
            pltpu.SemaphoreType.DMA((1,)),
            pltpu.SemaphoreType.DMA((1,)),
        ],
        compiler_params=pltpu.CompilerParams(
            collective_id=0, has_side_effects=True, vmem_limit_bytes=VMEM_LIMIT
        ),
    )(
        *[in_hbm(x) for x in (velocity, pressure, memory, buoyancy, modulus, relax, strength)],
        in_hbm(spectra),
        in_hbm(patch_cell.reshape(1, -1)),
        in_hbm(phase_rows(width // 2)),
        in_hbm(listed),
        in_hbm(weights),
    )


def finish(state, velocity, pressure, memory, spectra, weights):
    nz = pressure.shape[0]
    width = spectra.shape[1]
    ngy = lax.axis_size("gy")
    rup_group, slot_dev, variations = weights.shape
    share = variations // ngy
    f32 = jnp.float32
    any_spec = pl.BlockSpec(memory_space=pl.ANY)
    vmem_spec = pl.BlockSpec(memory_space=pltpu.VMEM)
    return pl.pallas_call(
        functools.partial(finish_kernel, nz),
        out_shape=[
            jax.ShapeDtypeStruct(velocity.shape, f32),
            jax.ShapeDtypeStruct(pressure.shape, f32),
            jax.ShapeDtypeStruct(memory.shape, f32),
            jax.ShapeDtypeStruct(spectra.shape, f32),
            jax.ShapeDtypeStruct((rup_group, share, width), f32),
        ],
        in_specs=[vmem_spec] * len(state),
        out_specs=[any_spec] * 5,
        scratch_shapes=[
            pltpu.VMEM((rup_group, share, width), f32),
            pltpu.VMEM(state[7].shape, jnp.bfloat16),
            pltpu.VMEM((8, state[7].shape[0]), f32),
            pltpu.SemaphoreType.DMA((6,)),
            pltpu.SemaphoreType.DMA((1,)),
        ],
        compiler_params=pltpu.CompilerParams(vmem_limit_bytes=VMEM_LIMIT),
    )(*[pltpu.with_memory_space_constraint(x, pltpu.VMEM) for x in state])


def per_device(
    velocity,
    pressure,
    memory,
    buoyancy,
    modulus,
    relax,
    strength,
    spectra,
    patch_cell,
    rupture_patches,
    slip_weights,
):
    state = advance(
        velocity,
        pressure,
        memory,
        buoyancy,
        modulus,
        relax,
        strength,
        spectra,
        patch_cell,
        rupture_patches,
        slip_weights,
    )
    return tuple(finish(state, velocity, pressure, memory, spectra, slip_weights))


def solution(mesh):
    in_specs = (
        P(None, None, "gy", "gx"),
        P(None, "gy", "gx"),
        P(None, "gy", "gx"),
        P(None, "gy", "gx"),
        P(None, "gy", "gx"),
        P(None, "gy", "gx"),
        P(None, "gy", "gx"),
        P(("gx", "gy"), None),
        P(("gx", "gy")),
        P(),
        P("gx", "gy", None),
    )
    out_specs = (
        P(None, None, "gy", "gx"),
        P(None, "gy", "gx"),
        P(None, "gy", "gx"),
        P(("gx", "gy"), None),
        P("gx", "gy", None),
    )
    return jax.shard_map(
        per_device, mesh=mesh, in_specs=in_specs, out_specs=out_specs, check_vma=False
    )
```
